32 devices in a mesh: dp: 8 (over z, y), expert: 4 (over x, core).
Axes of the slice: x: 2, y: 2, z: 4, core: 2. Of those that a mesh axis runs over, the one named last changes fastest.
Arguments:
- tokens: bfloat16 [16, 2048, 1536], P('dp', 'expert')
- segments: int32 [16, 1024], P('dp'), may hold values from 0 to 7, never falling along the last dimension, each value on 1 to 256 neighbouring positions
- routes: int32 [16, 2048, 8], P('dp', 'expert'), may hold values from 0 to 19, as said below
- cotangent: bfloat16 [16, 2048, 1536], P('dp', 'expert'), may hold values from -6 to 6
- attention_gain: float32 [1536], replicated, may hold values from 0.25 to 1.75
- query_weight: bfloat16 [1536, 1536], replicated, may hold values from -0.15625 to 0.15625
- key_weight: bfloat16 [1536, 512], replicated, may hold values from -0.15625 to 0.15625
- value_weight: bfloat16 [1536, 512], replicated, may hold values from -0.15625 to 0.15625
- out_weight: bfloat16 [1536, 1536], replicated, may hold values from -1.25 to 1.25
- mixture_gain: float32 [1536], replicated, may hold values from 0.25 to 1.75
- router_weight: bfloat16 [1536, 20], replicated, may hold values from -0.078125 to 0.078125
- gate_weight: bfloat16 [20, 1536, 512], P('expert'), may hold values from -0.15625 to 0.15625
- up_weight: bfloat16 [20, 1536, 512], P('expert'), may hold values from -0.15625 to 0.15625
- down_weight: bfloat16 [20, 1536, 512], P('expert'), may hold values from -1 to 1
Outputs:
- output: bfloat16 [16, 2048, 1536], P('dp', 'expert')
- input_grad: float32 [16, 2048, 1536], P('dp', 'expert')
- attention_gain_grad: float32 [1536], P('dp')
- query_weight_grad: float32 [1536, 1536], P('dp')
- key_weight_grad: float32 [1536, 512], P('dp')
- value_weight_grad: float32 [1536, 512], P('dp')
- out_weight_grad: float32 [1536, 1536], P('dp')
- mixture_gain_grad: float32 [1536], P('dp')
- router_weight_grad: float32 [1536, 20], P('dp')
- gate_weight_grad: float32 [20, 1536, 512], P('expert', 'dp')
- up_weight_grad: float32 [20, 1536, 512], P('expert', 'dp')
- down_weight_grad: float32 [20, 1536, 512], P('expert', 'dp')
- expert_load: float32 [20], replicated
- prob_mean: float32 [20], replicated
- balance_loss: float32 [], replicated
The draws below stay inside these ranges and needn't reach their ends.
Inputs may be any that keep to these rules, and one draw needn't show every extreme that they name: `routes`: each token names 8 different experts. `segments`: along a group the ids never fall, every id appears, each continuation has 1 to 256 tokens, 128 on average, and one has exactly 256.
All inputs are finite; a program needn't handle non-finite values.
Results may differ from the reference program's by a relative error of at most 0.02.
Values may be sent and summed in bfloat16 or wider, within the bound.
A program may use at most 576 MiB of HBM per device.

```python
import math
import jax
import jax.numpy as jnp
import numpy as np
from jax import lax

D = 1536
H = 24
KVH = 8
HD = 64
FF = 512
TOPK = 8
PROMPT = 1024
NCONT = 8
CMOST = 256
GRP_DP = 2
EXPERTS = 20
CONT = 1024
GLEN = 2048
GROUPS = 16
QLEN = 512
TOK_DEV = 1024
TOKENS = 32768
CAP = 512
N_DP = 8
N_EXPERT = 4


def draw_tokens(key, part):
    noise_key, common_key = jax.random.split(key, 2)
    row_count = GROUPS * GLEN
    placing = (jnp.arange(row_count, dtype=jnp.float32) + 0.5) / row_count
    tilting = 1.2 * (2.0 * placing - 1.0)
    common = jax.random.normal(common_key, (D,), jnp.float32)
    jitter = jax.random.normal(noise_key, (row_count, D), jnp.float32)
    values = jitter + tilting[:, None] * common[None, :]
    return values.reshape(GROUPS, GLEN, D).astype(jnp.bfloat16)


def draw_routes(key, part):
    noise_key, favour_key, slope_key = jax.random.split(key, 3)
    row_count = GROUPS * GLEN
    jitter = jax.random.randint(noise_key, (row_count, EXPERTS), 0, 1000, dtype=jnp.int32)
    favour = jax.random.randint(favour_key, (EXPERTS,), 0, 600, dtype=jnp.int32)
    slopes = jax.random.randint(slope_key, (EXPERTS,), -1, 2, dtype=jnp.int32)
    placing = 2 * jnp.arange(row_count, dtype=jnp.int32) - row_count + 1
    leaning = placing[:, None] * slopes[None, :] * 400 // row_count
    expert_ids = jnp.arange(EXPERTS, dtype=jnp.int32)
    forced = (jnp.arange(row_count, dtype=jnp.int32)[:, None] == expert_ids[None, :]).astype(jnp.int32) * 5000
    scores = (jitter + favour[None, :] + leaning + forced) * EXPERTS + expert_ids[None, :]
    chosen = lax.top_k(scores, TOPK)[1]
    return chosen.astype(jnp.int32).reshape(GROUPS, GLEN, TOPK)


def levels(own_key, extent, cuts, low, largest):
    loudness = 1.0
    for position, shards_of in cuts:
        heights = jax.random.uniform(jax.random.fold_in(jax.random.fold_in(own_key, 6), position), (shards_of,), jnp.float32, low / len(cuts), largest / len(cuts))
        loudness = loudness * jnp.repeat(jnp.exp(heights), extent[position] // shards_of).reshape((-1,) + (1,) * (len(extent) - 1 - position))
    return loudness


def profile(count, total, reach, lean):
    loads = [(1 << 20) // math.isqrt(grade ** lean) + 1 for grade in range(2, count + 1)]
    spare, given = total - reach - (count - 1), [1] * (count - 1)
    while spare > 0:
        candidates = [i for i in range(count - 1) if given[i] < reach]
        mass, budget = sum([loads[i] for i in candidates]), spare
        for i in candidates:
            extra = min(reach - given[i], max(1, budget * loads[i] // mass), spare)
            given[i] = given[i] + extra
            spare = spare - extra
    return np.array([reach] + given)


def ragged(own_key, number_of, total, limit, skew):
    if number_of == 2:
        one = jax.random.randint(own_key, (), max(1, total - limit), min(limit, total - 1) + 1)
        return jnp.stack([one, total - one])
    sizes = jnp.asarray(profile(number_of, total, limit, skew), jnp.int32)
    twos = (number_of - 1) // 2
    source_of, receiver = sizes[1:1 + 2 * twos:2], sizes[2:2 + 2 * twos:2]
    slack = jnp.minimum(source_of - 1, limit - receiver)
    moved = jax.random.randint(jax.random.fold_in(own_key, 1), (twos,), 0, 1 << 20) % (slack + 1)
    sizes = sizes.at[1:1 + 2 * twos:2].set(source_of - moved).at[2:2 + 2 * twos:2].set(receiver + moved)
    return sizes[jax.random.permutation(jax.random.fold_in(own_key, 2), number_of)]


def normal_values(rng, shape, spread, most, pieces=(), kind=jnp.bfloat16):
    array = spread * jax.random.normal(rng, shape, jnp.float32)
    if pieces:
        array = array * levels(rng, shape, pieces, -0.22, 0.18)
    return jnp.clip(array, -most, most).astype(kind)


def setup_inputs(seed: int = 0) -> dict:
    splits = jax.random.split(jax.random.key(seed), 15)
    tokens = draw_tokens(jax.random.fold_in(splits[14], 71), 0)
    segments = jax.vmap(lambda own: jnp.searchsorted(jnp.cumsum(ragged(own, NCONT, CONT, CMOST, 2)), jnp.arange(CONT), side="right"))(jax.random.split(splits[1], GROUPS)).reshape((GROUPS, CONT)).astype(jnp.int32)
    routes = draw_routes(jax.random.fold_in(splits[14], 71), 0)
    cotangent = normal_values(splits[3], (GROUPS, GLEN, D), 1.0, 6.0, ((0, 8), (1, 4)))
    attention_gain = jnp.clip(1.0 + 0.15 * jax.random.normal(splits[4], (D,), jnp.float32), 0.25, 1.75)
    query_weight = normal_values(splits[5], (D, H * HD), D ** -0.5, 0.15625)
    key_weight = normal_values(splits[6], (D, KVH * HD), D ** -0.5, 0.15625)
    value_weight = normal_values(splits[7], (D, KVH * HD), D ** -0.5, 0.15625)
    out_weight = normal_values(splits[8], (H * HD, D), (H * HD // 64) ** -0.5, 1.25)
    mixture_gain = jnp.clip(1.0 + 0.15 * jax.random.normal(splits[9], (D,), jnp.float32), 0.25, 1.75)
    router_weight = normal_values(splits[10], (D, EXPERTS), (4 * D) ** -0.5, 0.078125)
    gate_weight = normal_values(splits[11], (EXPERTS, D, FF), D ** -0.5, 0.15625, ((0, 4),))
    up_weight = normal_values(splits[12], (EXPERTS, D, FF), D ** -0.5, 0.15625, ((0, 4),))
    down_weight = normal_values(splits[13], (EXPERTS, D, FF), (FF // 16) ** -0.5, 1.0, ((0, 4),))
    return dict(tokens=tokens, segments=segments, routes=routes, cotangent=cotangent, attention_gain=attention_gain, query_weight=query_weight, key_weight=key_weight, value_weight=value_weight, out_weight=out_weight, mixture_gain=mixture_gain, router_weight=router_weight, gate_weight=gate_weight, up_weight=up_weight, down_weight=down_weight)


epsilon = 1e-05
rope_base = 10000.0
highest = lax.Precision.HIGHEST

@jax.custom_vjp
def low(v):
    return lax.optimization_barrier(v.astype(jnp.bfloat16)).astype(jnp.float32)

@jax.custom_vjp
def low_back(v):
    return v

def low_keep(v):
    return (low(v), None)

def low_pass(kept, grad):
    return (grad,)

def back_keep(v):
    return (v, None)

def back_low(kept, grad):
    return (low(grad),)
low.defvjp(low_keep, low_pass)
low_back.defvjp(back_keep, back_low)

def rotate(values, cosine, sine_table):
    half_width = values.shape[-1] // 2
    first_half = values[..., :half_width]
    second_half = values[..., half_width:]
    return jnp.concatenate([first_half * cosine - second_half * sine_table, second_half * cosine + first_half * sine_table], axis=-1)

def rms_scaled(values, gain):
    factor = lax.rsqrt(lax.optimization_barrier(jnp.mean(values * values, axis=-1, keepdims=True)) + epsilon)
    return values * factor * gain

def to_sources(values):
    trailing = values.shape[2:]
    shaped = values.reshape((GRP_DP, N_EXPERT, QLEN) + trailing)
    return jnp.swapaxes(shaped, 0, 1).reshape((N_EXPERT, TOK_DEV) + trailing)

def from_sources(values):
    trailing = values.shape[2:]
    shaped = values.reshape((N_EXPERT, GRP_DP, QLEN) + trailing)
    return jnp.swapaxes(shaped, 0, 1).reshape((GRP_DP, GLEN) + trailing)

def slot_tables(routes):
    source_routes = jax.vmap(to_sources)(routes.reshape(N_DP, GRP_DP, GLEN, TOPK)).reshape(N_DP, N_EXPERT, TOK_DEV * TOPK)
    hot_table = (source_routes[..., None] == jnp.arange(EXPERTS, dtype=jnp.int32)).astype(jnp.int32)
    earlier = (jnp.cumsum(hot_table, axis=2) - hot_table).astype(jnp.int32)
    slot_index = lax.optimization_barrier(jnp.sum(earlier * hot_table, axis=3)).astype(jnp.int32)
    target = jnp.where(slot_index < CAP, source_routes * CAP + slot_index, EXPERTS * CAP).astype(jnp.int32)
    pair_ids = jnp.broadcast_to(jnp.arange(TOK_DEV * TOPK, dtype=jnp.int32), target.shape)
    owner_pair = jnp.full((N_DP, N_EXPERT, EXPERTS * CAP + 1), TOK_DEV * TOPK, jnp.int32)
    owner_pair = owner_pair.at[jnp.arange(N_DP)[:, None, None], jnp.arange(N_EXPERT)[None, :, None], target].set(pair_ids)
    token_slot = (owner_pair[:, :, :EXPERTS * CAP] // TOPK).astype(jnp.int32)
    return (target, token_slot.reshape(N_DP, N_EXPERT, EXPERTS, CAP))

def attend(head_item):
    query_one, key_one, value_one, seg_one = head_item
    places = jnp.arange(GLEN, dtype=jnp.int32)
    allowed = (places[None, :] <= places[:, None]) & ((seg_one[None, :] < 0) | (seg_one[None, :] == seg_one[:, None]))
    raw_scores = low_back(jnp.einsum('rqd,kd->rqk', query_one, key_one, precision=highest) * 0.125)
    attention_probs = jax.nn.softmax(jnp.where(allowed[None], raw_scores, -1e+30), axis=-1)
    return low_back(low(jnp.einsum('rqk,kd->rqd', low(attention_probs), value_one, precision=highest)))

def reference(tokens, segments, routes, cotangent, attention_gain, query_weight, key_weight, value_weight, out_weight, mixture_gain, router_weight, gate_weight, up_weight, down_weight):
    sharing = H // KVH
    half_width = HD // 2
    seg_full = jnp.concatenate([jnp.full((GROUPS, PROMPT), -1, jnp.int32), segments.astype(jnp.int32)], axis=1)
    earlier_ids = lax.optimization_barrier(jnp.sum((segments[:, None, :] < seg_full[:, :, None]).astype(jnp.int32), axis=2)).astype(jnp.int32)
    rope_place = jnp.arange(GLEN, dtype=jnp.int32)[None, :] - earlier_ids
    frequency = jnp.exp(-math.log(rope_base) * jnp.arange(half_width, dtype=jnp.float32) / half_width)
    angles = rope_place.astype(jnp.float32)[:, :, None] * frequency
    cosine_all = jnp.cos(angles)[:, :, None, :]
    sine_all = jnp.sin(angles)[:, :, None, :]
    target, token_slot = slot_tables(routes)

    def forward(x_all, gain_a, weight_q, weight_k, weight_v, weight_o, gain_b, weight_r, weight_g, weight_u, weight_d):

        def one_index(index_item):
            block, seg_block, cos_block, sin_block, route_block, target_block, slot_block = index_item
            normed = low(rms_scaled(block, gain_a))
            query_rot = low(rotate(low_back(jnp.einsum('gtd,de->gte', normed, weight_q, precision=highest)).reshape(GRP_DP, GLEN, H, HD), cos_block, sin_block))
            key_rot = low(rotate(low_back(jnp.einsum('gtd,de->gte', normed, weight_k, precision=highest)).reshape(GRP_DP, GLEN, KVH, HD), cos_block, sin_block))
            value_rows = low_back(low(jnp.einsum('gtd,de->gte', normed, weight_v, precision=highest)))
            query_heads = query_rot.reshape(GRP_DP, GLEN, KVH, sharing, HD).transpose(0, 2, 3, 1, 4).reshape(GRP_DP * KVH, sharing, GLEN, HD)
            key_heads = key_rot.transpose(0, 2, 1, 3).reshape(GRP_DP * KVH, GLEN, HD)
            value_heads = value_rows.reshape(GRP_DP, GLEN, KVH, HD).transpose(0, 2, 1, 3).reshape(GRP_DP * KVH, GLEN, HD)
            seg_heads = jnp.repeat(seg_block, KVH, axis=0)
            mixed_heads = lax.map(jax.checkpoint(attend), (query_heads, key_heads, value_heads, seg_heads))
            attended = mixed_heads.reshape(GRP_DP, KVH, sharing, GLEN, HD).transpose(0, 3, 1, 2, 4).reshape(GRP_DP, GLEN, H * HD)
            middle = block + low_back(jnp.einsum('gte,ed->gtd', attended, weight_o, precision=highest))
            hidden_norm = low(rms_scaled(middle, gain_b))
            router_probs = jax.nn.softmax(jnp.einsum('gtd,de->gte', hidden_norm, weight_r, precision=highest), axis=-1)
            source_norm = to_sources(hidden_norm)
            source_probs = to_sources(router_probs)
            source_routes = to_sources(route_block)
            picked = jnp.take_along_axis(source_probs, source_routes, axis=2)
            gate_share = picked / lax.optimization_barrier(jnp.sum(picked, axis=2, keepdims=True))
            padded = jnp.concatenate([source_norm, jnp.zeros((N_EXPERT, 1, D), source_norm.dtype)], axis=1)

            def expert_pass(expert_item):
                slot_rows, gate_one, up_one, down_one = expert_item
                inputs = low_back(jnp.take_along_axis(padded, slot_rows[:, :, None], axis=1))
                gate_pre = low_back(jnp.einsum('scd,df->scf', inputs, gate_one, precision=highest))
                up_pre = low_back(jnp.einsum('scd,df->scf', inputs, up_one, precision=highest))
                hidden = low_back(low(jax.nn.silu(gate_pre) * up_pre))
                return low_back(low(jnp.einsum('scf,df->scd', hidden, down_one, precision=highest)))
            expert_out = lax.map(jax.checkpoint(expert_pass), (jnp.swapaxes(slot_block, 0, 1), weight_g, weight_u, weight_d))
            returned = jnp.swapaxes(expert_out, 0, 1).reshape(N_EXPERT, EXPERTS * CAP, D)
            returned = jnp.concatenate([returned, jnp.zeros((N_EXPERT, 1, D), returned.dtype)], axis=1)
            pair_rows = jnp.take_along_axis(returned, target_block[:, :, None], axis=1).reshape(N_EXPERT, TOK_DEV, TOPK, D)
            mixture = lax.optimization_barrier(jnp.sum(gate_share[..., None] * pair_rows, axis=2))
            return (middle + from_sources(mixture), lax.optimization_barrier(jnp.sum(router_probs, axis=(0, 1))))
        index_items = (x_all.reshape(N_DP, GRP_DP, GLEN, D), seg_full.reshape(N_DP, GRP_DP, GLEN), cosine_all.reshape(N_DP, GRP_DP, GLEN, 1, half_width), sine_all.reshape(N_DP, GRP_DP, GLEN, 1, half_width), routes.reshape(N_DP, GRP_DP, GLEN, TOPK), target, token_slot)
        results, prob_parts = lax.map(jax.checkpoint(one_index), index_items)
        return (results.reshape(GROUPS, GLEN, D), lax.optimization_barrier(jnp.sum(prob_parts, axis=0)))
    primals = (tokens.astype(jnp.float32), attention_gain.astype(jnp.float32), query_weight.astype(jnp.float32), key_weight.astype(jnp.float32), value_weight.astype(jnp.float32), out_weight.astype(jnp.float32), mixture_gain.astype(jnp.float32), router_weight.astype(jnp.float32), gate_weight.astype(jnp.float32), up_weight.astype(jnp.float32), down_weight.astype(jnp.float32))
    (result, prob_total), pullback = jax.vjp(forward, *primals)
    gradients = pullback((cotangent.astype(jnp.float32), jnp.zeros_like(prob_total)))
    counts = lax.optimization_barrier(jnp.sum((routes.reshape(-1, TOPK)[:, :, None] == jnp.arange(EXPERTS, dtype=jnp.int32)).astype(jnp.float32), axis=(0, 1)))
    expert_load = counts * EXPERTS / (TOKENS * TOPK)
    prob_mean = prob_total * EXPERTS / TOKENS
    balance_loss = jnp.sum(expert_load * prob_mean) / EXPERTS
    return (result.astype(jnp.bfloat16), gradients[0], gradients[1], gradients[2], gradients[3], gradients[4], gradients[5], gradients[6], gradients[7], gradients[8], gradients[9], gradients[10], expert_load, prob_mean, balance_loss)
```

```python
import functools
import math

import jax
import jax.numpy as jnp
from jax import lax
from jax.experimental import pallas as pl
from jax.experimental.pallas import tpu as pltpu
from jax.sharding import Mesh
from jax.sharding import PartitionSpec as P

D = 1536
H = 24
KVH = 8
HD = 64
FF = 512
TOPK = 8
EXP_DEV = 5
PROMPT = 1024
LANES = 128
PAIRS = KVH // 2
SHARE = H // KVH
PAIR_Q = 2 * SHARE * HD
ROWS = 256
STACK = SHARE * ROWS
EXPERT = ("eh", "el")
DATA = ("dh", "dl")
VMEM_LIMIT = 63 * 1024 * 1024

epsilon = 1e-05
rope_base = 10000.0
f32 = jnp.float32
bf16 = jnp.bfloat16


def dot(a, b):
    return lax.dot_general(a, b, (((1,), (0,)), ((), ())), preferred_element_type=f32)


def dot_nt(a, b):
    return lax.dot_general(a, b, (((1,), (1,)), ((), ())), preferred_element_type=f32)


def dot_tn(a, b):
    return lax.dot_general(a, b, (((0,), (0,)), ((), ())), preferred_element_type=f32)


def expert_rank():
    return lax.axis_index("eh") * 2 + lax.axis_index("el")


def call(kernel, name, micros, **more):
    cost = pl.CostEstimate(flops=int(micros * 9e8), bytes_accessed=0, transcendentals=0)
    return pl.pallas_call(
        kernel,
        name=name,
        cost_estimate=cost,
        compiler_params=pltpu.CompilerParams(vmem_limit_bytes=VMEM_LIMIT),
        **more,
    )


def shaped(shape, dtype):
    return jax.ShapeDtypeStruct(shape, dtype)


def lane_of(shape):
    return lax.broadcasted_iota(jnp.int32, shape, len(shape) - 1)


def half_swap(values):
    lower = lane_of(values.shape) % HD < HD // 2
    return jnp.where(
        lower, pltpu.roll(values, LANES - HD // 2, 1), pltpu.roll(values, HD // 2, 1)
    )


def resident(shape):
    zeros = (0,) * len(shape)
    return pl.BlockSpec(shape, lambda *_: zeros, pipeline_mode=pl.Buffered(1))


def row_block(width, first=0):
    return pl.BlockSpec((ROWS, width), lambda i: (first + i, 0))


def naming_kernel(capacity, r_ref, o_ref):
    groups, length, _ = r_ref.shape
    rows = groups * length
    lane = lane_of((rows, LANES))
    chosen = r_ref[...].reshape(rows, TOPK)
    named = jnp.zeros((rows, LANES), f32)
    for k in range(TOPK):
        named = jnp.where(chosen[:, k : k + 1] == lane, 1.0, named)
    earlier = lax.broadcasted_iota(jnp.int32, (rows, rows), 1) < lax.broadcasted_iota(
        jnp.int32, (rows, rows), 0
    )
    slot = dot(jnp.where(earlier, 1.0, 0.0).astype(bf16), named.astype(bf16))
    level = named * jnp.where(slot < capacity, 2.0, 1.0)
    o_ref[...] = level.reshape(groups, length, LANES).astype(bf16)


def naming(routes, capacity, ranks):
    groups, total, _ = routes.shape
    length = total // ranks
    return call(
        functools.partial(naming_kernel, capacity),
        "naming",
        5,
        grid=(ranks,),
        in_specs=[pl.BlockSpec((groups, length, TOPK), lambda s: (0, s, 0))],
        out_specs=pl.BlockSpec((groups, length, LANES), lambda s: (0, s, 0)),
        out_shape=shaped((groups, total, LANES), bf16),
    )(routes)


def project_kernel(x_ref, gain_ref, wq_ref, wk_ref, wv_ref, cos_ref, sin_ref, n_ref, q_ref, kv_ref):
    x = x_ref[...].astype(f32)
    factor = lax.rsqrt(jnp.mean(x * x, axis=1, keepdims=True) + epsilon)
    normed = (x * factor * gain_ref[...]).astype(bf16)
    n_ref[...] = normed
    cosine, sine = cos_ref[...], sin_ref[...]
    key = dot(normed, wk_ref[...])
    for c in range(KVH * HD // LANES):
        part = key[:, c * LANES : (c + 1) * LANES]
        turned = part * cosine + half_swap(part) * sine
        kv_ref[:, c * LANES : (c + 1) * LANES] = turned.astype(bf16)
    kv_ref[:, KVH * HD :] = dot(normed, wv_ref[...]).astype(bf16)
    query = dot(normed, wq_ref[...])
    for c in range(H * HD // LANES):
        part = query[:, c * LANES : (c + 1) * LANES]
        turned = part * cosine + half_swap(part) * sine
        q_ref[:, c * LANES : (c + 1) * LANES] = turned.astype(bf16) * jnp.asarray(0.125, bf16)


def project(group, length, x, gain, wq, wk, wv, cosine, sine):
    first = group * length // ROWS
    return call(
        project_kernel,
        "project",
        8,
        grid=(length // ROWS,),
        in_specs=[
            row_block(D, first),
            resident((1, D)),
            resident((D, H * HD)),
            resident((D, KVH * HD)),
            resident((D, KVH * HD)),
            row_block(LANES, first),
            row_block(LANES, first),
        ],
        out_specs=[row_block(D), row_block(H * HD), row_block(2 * KVH * HD)],
        out_shape=[
            shaped((length, D), bf16),
            shaped((length, H * HD), bf16),
            shaped((length, 2 * KVH * HD), bf16),
        ],
    )(x, gain, wq, wk, wv, cosine, sine)


def stack_heads(ref):
    low = lane_of((ROWS, LANES)) < HD
    parts = [ref[:, c * LANES : (c + 1) * LANES].astype(f32) for c in range(SHARE)]
    rolled0, rolled2 = pltpu.roll(parts[0], HD, 1), pltpu.roll(parts[2], HD, 1)
    zero = jnp.zeros((ROWS, LANES), f32)
    first = [parts[0], rolled0, parts[1]]
    second = [parts[1], rolled2, parts[2]]
    return (
        jnp.concatenate([jnp.where(low, v, zero).astype(bf16) for v in first], axis=0),
        jnp.concatenate([jnp.where(low, zero, v).astype(bf16) for v in second], axis=0),
    )


def unstack_heads(first, second):
    low = lane_of((ROWS, LANES)) < HD
    return (
        jnp.where(low, first[:ROWS], pltpu.roll(first[ROWS : 2 * ROWS], HD, 1)),
        jnp.where(low, first[2 * ROWS :], second[:ROWS]),
        jnp.where(low, pltpu.roll(second[ROWS : 2 * ROWS], HD, 1), second[2 * ROWS :]),
    )


def visit_chunks(block, chunk):
    prompt_blocks = PROMPT // ROWS

    @pl.when(block >= prompt_blocks)
    def _():
        for c in range(PROMPT // (2 * ROWS)):
            chunk(c * 2 * ROWS, 2 * ROWS, False)

    @pl.when(block < prompt_blocks)
    def _():
        def step(c, carry):
            chunk(pl.multiple_of(c * ROWS, ROWS), ROWS, False)
            return carry

        lax.fori_loop(0, block, step, 0)

    @pl.when(block > prompt_blocks)
    def _():
        chunk(pl.multiple_of((block - 1) * ROWS, ROWS), ROWS, True)

    chunk(pl.multiple_of(block * ROWS, ROWS), ROWS, True)


def mask_bias(block, begin, size, start_ref):
    place = begin + lax.broadcasted_iota(jnp.int32, (size, ROWS), 0)
    own = block * ROWS + lax.broadcasted_iota(jnp.int32, (size, ROWS), 1)
    ok = (place <= own) & (place >= start_ref[0, :1, :])
    bias = jnp.where(ok, 0.0, -1e30)
    return jnp.concatenate([bias] * SHARE, axis=1)


def attend_kernel(blocks, q_ref, k_ref, v_ref, start_ref, o_ref, lse_ref, vt_ref, m_ref, l_ref, acc_ref):
    block = expert_rank() * blocks + pl.program_id(1)

    @pl.when(pl.program_id(1) == 0)
    def _():
        vt_ref[...] = jnp.transpose(v_ref[...].astype(f32)).astype(bf16)

    queries = stack_heads(q_ref)
    m_ref[...] = jnp.full_like(m_ref, -1e30)
    l_ref[...] = jnp.zeros_like(l_ref)
    acc_ref[...] = jnp.zeros_like(acc_ref)

    def chunk(begin, size, masked):
        keys = k_ref[pl.ds(begin, size), :]
        values = vt_ref[:, pl.ds(begin, size)]
        bias = mask_bias(block, begin, size, start_ref) if masked else None
        for h in range(2):
            scores = dot_nt(keys, queries[h])
            if masked:
                scores = scores + bias
            before = m_ref[h, :1]
            peak = jnp.maximum(before, jnp.max(scores, axis=0, keepdims=True))
            weight = jnp.exp(scores - peak)
            shrink = jnp.exp(before - peak)
            m_ref[h, :1] = peak
            l_ref[h, :1] = l_ref[h, :1] * shrink + jnp.sum(weight, axis=0, keepdims=True)
            acc_ref[h] = acc_ref[h] * shrink + dot(values, weight.astype(bf16))

    visit_chunks(block, chunk)
    mixed = [jnp.transpose(acc_ref[h] / l_ref[h, :1]) for h in range(2)]
    for c, part in enumerate(unstack_heads(*mixed)):
        o_ref[:, c * LANES : (c + 1) * LANES] = part.astype(bf16)
    for h in range(2):
        total = m_ref[h, :1] + jnp.log(l_ref[h, :1])
        lse_ref[0, 0, h] = jnp.broadcast_to(total, (8, STACK))


def attend(group, query, kv, start_row):
    length = query.shape[0]
    total = kv.shape[0]
    blocks = length // ROWS
    heads = pl.BlockSpec((ROWS, PAIR_Q), lambda p, i: (i, p))
    return call(
        functools.partial(attend_kernel, blocks),
        "attend",
        45,
        grid=(PAIRS, blocks),
        in_specs=[
            heads,
            pl.BlockSpec((total, LANES), lambda p, i: (0, p)),
            pl.BlockSpec((total, LANES), lambda p, i: (0, PAIRS + p)),
            pl.BlockSpec((1, 8, ROWS), lambda p, i: (group, 0, i)),
        ],
        out_specs=[
            heads,
            pl.BlockSpec((1, 1, 2, 8, STACK), lambda p, i: (p, i, 0, 0, 0)),
        ],
        out_shape=[
            shaped(query.shape, bf16),
            shaped((PAIRS, blocks, 2, 8, STACK), f32),
        ],
        scratch_shapes=[
            pltpu.VMEM((LANES, total), bf16),
            pltpu.VMEM((2, 8, STACK), f32),
            pltpu.VMEM((2, 8, STACK), f32),
            pltpu.VMEM((2, LANES, STACK), f32),
        ],
    )(query, kv, kv, start_row)


def attend_back_kernel(
    blocks,
    q_ref,
    g_ref,
    o_ref,
    k_ref,
    v_ref,
    lse_ref,
    start_ref,
    cos_ref,
    sin_ref,
    dq_ref,
    dkv_ref,
    dq_acc,
    dkv_acc,
):
    step = pl.program_id(1)
    block = expert_rank() * blocks + step

    @pl.when(step == 0)
    def _():
        dkv_acc[...] = jnp.zeros_like(dkv_acc)

    dq_acc[...] = jnp.zeros_like(dq_acc)
    queries = stack_heads(q_ref)
    grads = stack_heads(g_ref)
    halves = []
    for c in range(SHARE):
        cols = slice(c * LANES, (c + 1) * LANES)
        product = jnp.transpose(g_ref[:, cols].astype(f32) * o_ref[:, cols].astype(f32))
        halves.append(jnp.sum(product[:HD], axis=0, keepdims=True))
        halves.append(jnp.sum(product[HD:], axis=0, keepdims=True))
    inner = [jnp.concatenate(halves[:SHARE], axis=1), jnp.concatenate(halves[SHARE:], axis=1)]

    def chunk(begin, size, masked):
        keys = k_ref[pl.ds(begin, size), :]
        values = v_ref[pl.ds(begin, size), :]
        bias = mask_bias(block, begin, size, start_ref) if masked else None
        key_sum, value_sum = None, None
        for h in range(2):
            scores = dot_nt(keys, queries[h]) - lse_ref[0, 0, h, :1, :]
            if masked:
                scores = scores + bias
            probs = jnp.exp(scores)
            probs_grad = dot_nt(values, grads[h])
            scores_grad = (probs * (probs_grad - inner[h])).astype(bf16)
            value_part = dot(probs.astype(bf16), grads[h])
            key_part = dot(scores_grad, queries[h])
            key_sum = key_part if key_sum is None else key_sum + key_part
            value_sum = value_part if value_sum is None else value_sum + value_part
            dq_acc[h] += dot_tn(scores_grad, keys)
        dkv_acc[0, pl.ds(begin, size), :] += key_sum
        dkv_acc[1, pl.ds(begin, size), :] += value_sum

    visit_chunks(block, chunk)
    cosine, sine = cos_ref[...], sin_ref[...]
    for c, part in enumerate(unstack_heads(dq_acc[0], dq_acc[1])):
        part = part * 0.125
        turned = part * cosine - half_swap(part) * sine
        dq_ref[:, c * LANES : (c + 1) * LANES] = turned.astype(bf16)

    @pl.when(step == blocks - 1)
    def _():
        dkv_ref[...] = dkv_acc[...].astype(bf16)


def attend_back(group, query, grad, mixed, kv, lse, start_row, cosine, sine):
    length = query.shape[0]
    total = kv.shape[0]
    blocks = length // ROWS
    first = group * blocks
    heads = pl.BlockSpec((ROWS, PAIR_Q), lambda p, i: (i, p))
    table = pl.BlockSpec((ROWS, LANES), lambda p, i: (first + i, 0))
    return call(
        functools.partial(attend_back_kernel, blocks),
        "attend_back",
        64,
        grid=(PAIRS, blocks),
        in_specs=[
            heads,
            heads,
            heads,
            pl.BlockSpec((total, LANES), lambda p, i: (0, p)),
            pl.BlockSpec((total, LANES), lambda p, i: (0, PAIRS + p)),
            pl.BlockSpec((1, 1, 2, 8, STACK), lambda p, i: (p, i, 0, 0, 0)),
            pl.BlockSpec((1, 8, ROWS), lambda p, i: (group, 0, i)),
            table,
            table,
        ],
        out_specs=[
            heads,
            pl.BlockSpec((2, total, LANES), lambda p, i: (0, 0, p)),
        ],
        out_shape=[
            shaped(query.shape, bf16),
            shaped((2, total, KVH * HD), bf16),
        ],
        scratch_shapes=[
            pltpu.VMEM((2, STACK, LANES), f32),
            pltpu.VMEM((2, total, LANES), f32),
        ],
    )(query, grad, mixed, kv, kv, lse, start_row, cosine, sine)


def branch_kernel(a_ref, x_ref, wo_ref, gain_ref, m_ref, n_ref):
    middle = x_ref[...].astype(f32) + dot(a_ref[...], wo_ref[...])
    m_ref[...] = middle
    factor = lax.rsqrt(jnp.mean(middle * middle, axis=1, keepdims=True) + epsilon)
    n_ref[...] = (middle * factor * gain_ref[...]).astype(bf16)


def branch(group, attended, x, wo, gain):
    length = attended.shape[0]
    return call(
        branch_kernel,
        "branch",
        6,
        grid=(length // ROWS,),
        in_specs=[
            row_block(H * HD),
            row_block(D, group * length // ROWS),
            resident((H * HD, D)),
            resident((1, D)),
        ],
        out_specs=[row_block(D), row_block(D)],
        out_shape=[shaped((length, D), f32), shaped((length, D), bf16)],
    )(attended, x, wo, gain)


def router(normed, weight):
    count = EXP_DEV * 2 * lax.axis_size("eh")
    logits = dot(normed, weight)
    logits = jnp.where(lane_of(logits.shape) < count, logits, -1e30)
    powers = jnp.exp(logits - jnp.max(logits, axis=1, keepdims=True))
    return powers / jnp.sum(powers, axis=1, keepdims=True)


def experts_kernel(
    x_ref, c_ref, t_ref, wr_ref, wg_ref, wu_ref, wd_ref, *refs
):
    mix_ref, rows_ref, x_out, c_out, hid_ref, gate_ref, up_ref = refs[-7:]
    x, cot = x_ref[...], c_ref[...]
    x_out[...] = x
    c_out[...] = cot
    level = t_ref[0].astype(f32)
    picked = jnp.where(level > 0.5, router(x, wr_ref[...]), 0.0)
    share = picked / jnp.sum(picked, axis=1, keepdims=True)
    share = jnp.where(level > 1.5, share, 0.0)
    lane = lane_of(share.shape)
    base = EXP_DEV * expert_rank()
    share = pltpu.roll(share, lax.rem(LANES - base, LANES), 1)
    mix, rows = None, None
    gate_grads = jnp.zeros(share.shape, bf16)
    for e in range(EXP_DEV):
        gate = dot(x, wg_ref[e])
        up = dot(x, wu_ref[e])
        hidden_grad = dot(cot, wd_ref[e])
        sigmoid = jax.nn.sigmoid(gate)
        active = gate * sigmoid
        hidden = active * up
        inner = jnp.sum(hidden * hidden_grad, axis=1, keepdims=True)
        coarse = inner.astype(bf16)
        fine = (inner - coarse.astype(f32)).astype(bf16)
        gate_grads = jnp.where(lane == base + e, coarse, gate_grads)
        gate_grads = jnp.where(lane == LANES // 2 + base + e, fine, gate_grads)
        weight = share[:, e : e + 1]
        scaled = (hidden * weight).astype(bf16)
        hidden_grad = hidden_grad * weight
        up_grad = (hidden_grad * active).astype(bf16)
        gate_grad = (hidden_grad * up * sigmoid * (1.0 + gate * (1.0 - sigmoid))).astype(bf16)
        cols = slice(e * FF, (e + 1) * FF)
        hid_ref[:, cols] = scaled
        gate_ref[:, cols] = gate_grad
        up_ref[:, cols] = up_grad
        mix_part = dot_nt(scaled, wd_ref[e])
        rows_part = dot_nt(gate_grad, wg_ref[e]) + dot_nt(up_grad, wu_ref[e])
        mix = mix_part if mix is None else mix + mix_part
        rows = rows_part if rows is None else rows + rows_part
    mix_ref[...] = mix.astype(bf16)
    rows_ref[:, :D] = rows.astype(bf16)
    rows_ref[:, D:] = gate_grads


def experts_pass(group, groups, x, cot, level, wr, wg, wu, wd, kept):
    count = x.shape[0]
    first = group * count // ROWS
    whole = groups * count
    side = pl.BlockSpec(memory_space=pl.ANY)
    widths = [D, D, EXP_DEV * FF, EXP_DEV * FF, EXP_DEV * FF]
    return call(
        experts_kernel,
        "experts",
        113,
        grid=(count // ROWS,),
        in_specs=[
            row_block(D),
            row_block(D),
            pl.BlockSpec((1, ROWS, LANES), lambda i: (group, i, 0)),
            resident((D, LANES)),
            resident((EXP_DEV, D, FF)),
            resident((EXP_DEV, D, FF)),
            resident((EXP_DEV, D, FF)),
        ]
        + [side] * len(kept),
        out_specs=[row_block(D), row_block(D + LANES)]
        + [row_block(width, first) for width in widths],
        out_shape=[
            shaped((count, D), bf16),
            shaped((count, D + LANES), bf16),
        ]
        + [shaped((whole, width), bf16) for width in widths],
        input_output_aliases={7 + i: 2 + i for i in range(len(kept))},
    )(x, cot, level, wr, wg, wu, wd, *kept)


def norm_back(grad, normed, factor, gain):
    scaled = grad * gain
    return factor * (scaled - normed * jnp.mean(scaled * normed, axis=1, keepdims=True))


def fold_rows(values):
    return jnp.sum(values.reshape(values.shape[0] // 8, 8, values.shape[1]), axis=0)


def add_up(ref, part):
    @pl.when(pl.program_id(0) == 0)
    def _():
        ref[...] = part

    @pl.when(pl.program_id(0) > 0)
    def _():
        ref[...] += part


def middle_kernel(
    r_ref, t_ref, m_ref, n_ref, c_ref, gain_ref, wr_ref, wo_ref,
    mg_ref, b_ref, ag_ref, l_ref, dg_ref, ps_ref,
):
    probs = router(n_ref[...], wr_ref[...])
    add_up(ps_ref, fold_rows(probs))
    level = t_ref[0].astype(f32)
    sel = jnp.where(level > 0.5, 1.0, 0.0)
    gate_grad = r_ref[:, D:].astype(f32)
    gate_grad = gate_grad + pltpu.roll(gate_grad, LANES // 2, 1)
    gate_grad = jnp.where(level > 1.5, gate_grad, 0.0)
    picked = probs * sel
    total = jnp.sum(picked, axis=1, keepdims=True)
    share = picked / total
    inner = jnp.sum(gate_grad * share, axis=1, keepdims=True)
    probs_grad = (gate_grad - inner) / total * sel
    logits_grad = probs * (probs_grad - jnp.sum(probs_grad * probs, axis=1, keepdims=True))
    coarse = logits_grad.astype(bf16)
    fine = (logits_grad - coarse.astype(f32)).astype(bf16)
    l_ref[:, :LANES] = coarse
    l_ref[:, LANES:] = fine
    grad = r_ref[:, :D].astype(f32) + dot_nt(coarse, wr_ref[...]) + dot_nt(fine, wr_ref[...])
    middle = m_ref[...]
    factor = lax.rsqrt(jnp.mean(middle * middle, axis=1, keepdims=True) + epsilon)
    normed = middle * factor
    add_up(dg_ref, fold_rows(grad * normed))
    middle_grad = c_ref[...].astype(f32) + norm_back(grad, normed, factor, gain_ref[...])
    mg_ref[...] = middle_grad
    low = middle_grad.astype(bf16)
    b_ref[...] = low
    ag_ref[...] = dot_nt(low, wo_ref[...]).astype(bf16)


def middle_back(group, rows, level, middle, normed, cot, gain, wr, wo):
    length = rows.shape[0]
    first = group * length // ROWS
    corner = lambda width: pl.BlockSpec((8, width), lambda i: (0, 0))
    return call(
        middle_kernel,
        "middle_back",
        8,
        grid=(length // ROWS,),
        in_specs=[
            row_block(D + LANES),
            pl.BlockSpec((1, ROWS, LANES), lambda i: (group, i, 0)),
            row_block(D), row_block(D), row_block(D, first),
            resident((1, D)), resident((D, LANES)), resident((H * HD, D)),
        ],
        out_specs=[
            row_block(D), row_block(D), row_block(H * HD), row_block(2 * LANES),
            corner(D), corner(LANES),
        ],
        out_shape=[
            shaped((length, D), f32),
            shaped((length, D), bf16),
            shaped((length, H * HD), bf16),
            shaped((length, 2 * LANES), bf16),
            shaped((8, D), f32),
            shaped((8, LANES), f32),
        ],
    )(rows, level, middle, normed, cot, gain, wr, wo)


def input_kernel(
    dq_ref, dk_ref, dv_ref, x_ref, mg_ref, cos_ref, sin_ref, gain_ref, wq_ref, wk_ref, wv_ref,
    out_ref, dk_out, dg_ref,
):
    cosine, sine = cos_ref[...], sin_ref[...]
    for c in range(KVH * HD // LANES):
        part = dk_ref[0, :, c * LANES : (c + 1) * LANES].astype(f32)
        turned = part * cosine - half_swap(part) * sine
        dk_out[:, c * LANES : (c + 1) * LANES] = turned.astype(bf16)
    grad = dot_nt(dq_ref[...], wq_ref[...])
    grad = grad + dot_nt(dk_out[...], wk_ref[...])
    grad = grad + dot_nt(dv_ref[0], wv_ref[...])
    x = x_ref[...].astype(f32)
    factor = lax.rsqrt(jnp.mean(x * x, axis=1, keepdims=True) + epsilon)
    normed = x * factor
    add_up(dg_ref, fold_rows(grad * normed))
    out_ref[...] = mg_ref[...] + norm_back(grad, normed, factor, gain_ref[...])


def input_back(group, groups, dq, dkv, x, middle_grad, cosine, sine, gain, wq, wk, wv, kept):
    length = dq.shape[0]
    first = group * length // ROWS
    kernel = lambda *refs: input_kernel(*refs[:11], *refs[-3:])
    return call(
        kernel,
        "input_back",
        8,
        grid=(length // ROWS,),
        in_specs=[
            row_block(H * HD),
            pl.BlockSpec((1, ROWS, KVH * HD), lambda i: (0, i, 0)),
            pl.BlockSpec((1, ROWS, KVH * HD), lambda i: (1, i, 0)),
            row_block(D, first),
            row_block(D),
            row_block(LANES, first),
            row_block(LANES, first),
            resident((1, D)),
            resident((D, H * HD)),
            resident((D, KVH * HD)),
            resident((D, KVH * HD)),
        ]
        + [pl.BlockSpec(memory_space=pl.ANY)] * len(kept),
        out_specs=[
            row_block(D, first),
            row_block(KVH * HD),
            pl.BlockSpec((8, D), lambda i: (0, 0)),
        ],
        out_shape=[
            shaped((groups * length, D), f32),
            shaped((length, KVH * HD), bf16),
            shaped((8, D), f32),
        ],
        input_output_aliases={11: 0} if kept else {},
    )(dq, dkv, dkv, x, middle_grad, cosine, sine, gain, wq, wk, wv, *kept)


def dense_kernel(groups, plan, *refs):
    lefts, rights = refs[:groups], refs[groups:-2]
    out_ref, turned = refs[-2:]
    length = lefts[0].shape[0]
    step = pl.program_id(0)

    @pl.when(step == 0)
    def _():
        for g in range(groups):
            for c in range(0, D, 2 * LANES):
                part = lefts[g][:, c : c + 2 * LANES].astype(f32)
                turned[c : c + 2 * LANES, g * length : (g + 1) * length] = jnp.transpose(
                    part
                ).astype(bf16)

    at = 0
    for first, blocks, kind in plan:

        @pl.when((step >= first) & (step < first + blocks))
        def _(at=at, kind=kind):
            if kind == "narrow":
                out_ref[...] = jnp.zeros_like(out_ref)
                out_ref[:, :LANES] = jnp.transpose(rights[at][...]).astype(bf16)
            else:
                total = None
                for g in range(groups):
                    block = rights[at + g]
                    block = block[...] if len(block.shape) == 2 else block[0]
                    part = dot(turned[:, g * length : (g + 1) * length], block)
                    total = part if total is None else total + part
                out_ref[...] = total.astype(bf16)

        at += 1 if kind == "narrow" else groups


def dense_grad(lefts, families, name):
    width = KVH * HD
    groups = len(lefts)
    length = lefts[0].shape[0]
    plan, specs, operands, first = [], [], [], 0
    for kind, arrays in families:
        if kind == "narrow":
            blocks = 1
            specs.append(resident((LANES, D)))
            operands.append(arrays)
        else:
            blocks = arrays[0].shape[-1] // width
            for array in arrays:
                def column(i, first=first, blocks=blocks):
                    return jnp.clip(i - first, 0, blocks - 1)

                if array.ndim == 2:
                    spec = pl.BlockSpec((length, width), lambda i, f=column: (0, f(i)))
                else:
                    spec = pl.BlockSpec((1, length, width), lambda i, f=column: (1, 0, f(i)))
                specs.append(spec)
                operands.append(array)
        plan.append((first, blocks, kind))
        first += blocks
    return call(
        functools.partial(dense_kernel, groups, plan),
        name,
        3 * first,
        grid=(first,),
        in_specs=[resident((length, D))] * groups + specs,
        out_specs=pl.BlockSpec((D, width), lambda i: (0, i)),
        out_shape=shaped((D, first * width), bf16),
        scratch_shapes=[pltpu.VMEM((D, groups * length), bf16)],
    )(*lefts, *operands)


def widen(values):
    return jnp.pad(values, ((0, 0), (0, LANES - values.shape[1])))


def swap(values, axis):
    return lax.ppermute(values, axis, [(0, 1), (1, 0)])


def pick(values, index):
    return lax.dynamic_index_in_dim(values, index, 1, keepdims=False)


def pair_sum(values, shard):
    parts = values.reshape(-1, 2, shard, values.shape[1])
    own = lax.axis_index("dl")
    met = pick(parts, own) + swap(pick(parts, 1 - own), "dl")
    return met.reshape(-1, values.shape[1])


def take(values, axis, index):
    return lax.dynamic_index_in_dim(values, index, axis, keepdims=False)


def expert_sum(values, axis):
    chips = lax.axis_size("eh")
    size = values.shape[axis] // (2 * chips)
    parts = values.reshape(values.shape[:axis] + (chips, 2, size) + values.shape[axis + 1 :])
    own = lax.axis_index("el")
    met = take(parts, axis + 1, own) + swap(take(parts, axis + 1, 1 - own), "el")
    chip = lax.axis_index("eh")
    total = take(met, axis, chip)
    for hop in range(1, chips):
        order = [(i, (i + hop) % chips) for i in range(chips)]
        away = take(met, axis, lax.rem(chip + hop, chips))
        total = total + lax.ppermute(away, "eh", order)
    return total


def column_sum(values):
    chips = lax.axis_size("eh")
    own, chip = lax.axis_index("el"), lax.axis_index("eh")
    half = values.shape[1] // 2

    def cut(array, index, size):
        return lax.dynamic_slice_in_dim(array, index * size, size, 1)

    met = cut(values, own, half) + swap(cut(values, 1 - own, half), "el")
    size = half // chips
    total = cut(met, chip, size)
    for hop in range(1, chips):
        order = [(i, (i + hop) % chips) for i in range(chips)]
        away = cut(met, lax.rem(chip + hop, chips), size)
        total = total + lax.ppermute(away, "eh", order)
    return total


def everywhere_sum(values):
    for axis in ("el", "eh", "dl", "dh"):
        count = lax.axis_size(axis)
        hop = 1
        while hop < count:
            values = values + lax.ppermute(values, axis, [(i, i ^ hop) for i in range(count)])
            hop *= 2
    return values


def together(*values):
    return lax.optimization_barrier(values)


def on_device(
    tokens,
    segments,
    routes,
    cotangent,
    attention_gain,
    query_weight,
    key_weight,
    value_weight,
    out_weight,
    mixture_gain,
    router_weight,
    gate_weight,
    up_weight,
    down_weight,
):
    groups, length, _ = tokens.shape
    each = range(groups)
    rows = groups * length
    ranks = lax.axis_size("eh") * 2
    dp_ranks = lax.axis_size("dh") * 2
    rank = expert_rank()
    experts = EXP_DEV * ranks
    capacity = (rows * TOPK * 5 // (4 * experts) + 7) // 8 * 8
    all_tokens = rows * dp_ranks * ranks
    first_row = rank * length
    shard = D // dp_ranks

    seg_full = jnp.concatenate([jnp.full((groups, PROMPT), -1, jnp.int32), segments], axis=1)
    seg_own = lax.dynamic_slice_in_dim(seg_full, first_row, length, 1)
    earlier = jnp.sum((segments[:, None, :] < seg_own[:, :, None]).astype(jnp.int32), axis=2)
    position = first_row + jnp.arange(length, dtype=jnp.int32)[None, :]
    place = position - earlier
    start = jnp.where(position >= PROMPT, PROMPT + earlier, 0)
    half = HD // 2
    lane = jnp.arange(LANES, dtype=jnp.int32)
    frequency = jnp.exp(-math.log(rope_base) * (lane % half).astype(f32) / half)
    angles = place.astype(f32).reshape(rows, 1) * frequency
    cosine = jnp.cos(angles)
    sine = jnp.sin(angles) * jnp.where(lane % HD < half, -1.0, 1.0)
    start_row = jnp.broadcast_to(start[:, None, :], (groups, 8, length))

    routes_all = lax.all_gather(routes, EXPERT, axis=1, tiled=True)
    level = naming(routes_all, capacity, ranks)
    level_own = lax.dynamic_slice_in_dim(level, first_row, length, 1)
    cot_rows = cotangent.reshape(rows, D)
    cot_all = [lax.all_gather(cotangent[g], EXPERT, axis=0, tiled=True) for g in each]

    x = tokens.reshape(rows, D)
    gain_a = attention_gain.reshape(1, D)
    gain_b = mixture_gain.reshape(1, D)
    router_wide = widen(router_weight)
    normed, query, kv = [None] * groups, [None] * groups, [None] * groups
    for g in each:
        normed[g], query[g], kv_own = project(
            g, length, x, gain_a, query_weight, key_weight, value_weight, cosine, sine
        )
        kv[g] = lax.all_gather(kv_own, EXPERT, axis=0, tiled=True)
    kv[0], level = together(kv[0], level)
    attended, lse = [None] * groups, [None] * groups
    middle, hidden_low, hidden_all = [None] * groups, [None] * groups, [None] * groups
    for g in each:
        attended[g], lse[g] = attend(g, query[g], kv[g], start_row)
        if g == groups - 1:
            attended[g], cot_all[0] = together(attended[g], cot_all[0])
        middle[g], hidden_low[g] = branch(g, attended[g], x, out_weight, gain_b)
        hidden_all[g] = lax.all_gather(hidden_low[g], EXPERT, axis=0, tiled=True)

    kept, rows_back, mixture = [], [], []
    for g in each:
        if g > 0:
            kept[0], cot_all[g] = together(kept[0], cot_all[g])
        mix, rows_grad, *kept = experts_pass(
            g, groups, hidden_all[g], cot_all[g], level, router_wide,
            gate_weight, up_weight, down_weight, kept,
        )
        rows_back.append(lax.psum_scatter(rows_grad, EXPERT, scatter_dimension=0, tiled=True))
        mixture.append(lax.psum_scatter(mix, EXPERT, scatter_dimension=0, tiled=True))
    x_all, cot_both, hidden, gate_back, up_back = kept
    hidden, mixture[0] = together(hidden, mixture[0])
    down_local = dot_tn(cot_both, hidden).astype(bf16)
    x_all, down_local = together(x_all, down_local)
    gate_local = dot_tn(x_all, gate_back).astype(bf16)
    up_local = dot_tn(x_all, up_back).astype(bf16)
    rows_back[0], gate_local, up_local = together(rows_back[0], gate_local, up_local)

    def by_expert(part):
        return jnp.stack([part[:, e * FF : (e + 1) * FF] for e in range(EXP_DEV)]).astype(f32)

    def far_sum(met):
        return lax.psum_scatter(met, "dh", scatter_dimension=0, tiled=True)

    middle_grad, branch_grad, logits_grad, dq, dkv = ([None] * groups for _ in range(5))
    gain_b_local, probs_local = 0.0, 0.0
    down_met = pair_sum(down_local, shard)
    gate_met = pair_sum(gate_local, shard)
    up_met = pair_sum(up_local, shard)
    for g in each:
        middle_grad[g], branch_grad[g], attended_grad, logits_grad[g], gain_part, probs_part = (
            middle_back(
                g, rows_back[g], level_own, middle[g], hidden_low[g], cot_rows,
                gain_b, router_wide, out_weight,
            )
        )
        gain_b_local += jnp.sum(gain_part, axis=0)
        probs_local += jnp.sum(probs_part, axis=0)
        if g == 0:
            attended_grad, down_met, mixture[1] = together(attended_grad, down_met, mixture[1])
            down_part = far_sum(down_met)
        if g == 1:
            out_local = dense_grad(attended, [("out", branch_grad)], "out_grad")
            attended_grad, gate_met, down_part, out_local = together(
                attended_grad, gate_met, down_part, out_local
            )
            gate_part = far_sum(gate_met)
            out_part = column_sum(out_local)
        dq[g], dkv_all = attend_back(
            g, query[g], attended_grad, attended[g], kv[g], lse[g], start_row, cosine, sine
        )
        if g == 1:
            dkv_all, up_met = together(dkv_all, up_met)
            up_part = far_sum(up_met)
        dkv[g] = expert_sum(dkv_all, 1)
    output = jnp.stack(
        [(middle[g] + mixture[g].astype(f32)).astype(bf16) for g in each]
    )

    counts = jnp.sum((level_own > 0.5).astype(f32), axis=(0, 1))
    stats_all = everywhere_sum(jnp.stack([counts, probs_local])[:, :experts])
    dq[0], gate_part, out_part = together(dq[0], gate_part, out_part)
    kept, turned_dk, gain_a_local = [], [None] * groups, 0.0
    for g in each:
        input_grad, turned_dk[g], gain_part = input_back(
            g, groups, dq[g], dkv[g], x, middle_grad[g], cosine, sine,
            gain_a, query_weight, key_weight, value_weight, kept,
        )
        kept = [input_grad]
        gain_a_local += jnp.sum(gain_part, axis=0)
    router_parts = sum(dot_tn(logits_grad[g], hidden_low[g]) for g in each)
    router_local = (router_parts[:LANES] + router_parts[LANES:])[:experts]
    narrow = jnp.concatenate(
        [
            router_local,
            gain_a_local[None, :],
            gain_b_local[None, :],
            jnp.zeros((LANES - experts - 2, D), f32),
        ],
        axis=0,
    )
    dense = dense_grad(
        normed,
        [("query", dq), ("key", turned_dk), ("value", dkv), ("narrow", narrow)],
        "dense_grad",
    )
    dense, up_part, stats_all = together(column_sum(dense), up_part, stats_all)
    expert_load = stats_all[0] * experts / (all_tokens * TOPK)
    prob_mean = stats_all[1] * experts / all_tokens
    balance_loss = jnp.sum(expert_load * prob_mean) / experts
    dense = jnp.concatenate([dense, out_part], axis=1)
    dense = lax.psum_scatter(dense, DATA, scatter_dimension=0, tiled=True)
    dense = lax.all_gather(dense, EXPERT, axis=0, tiled=False).astype(f32)
    width = dense.shape[2] - D // ranks
    blocks = [dense[chip * 2 + core] for core in range(2) for chip in range(ranks // 2)]
    out_grad = jnp.concatenate([block[:, width:] for block in blocks], axis=1)
    dense = jnp.concatenate([block[:, :width] for block in blocks], axis=1)
    down_weight_grad, gate_weight_grad, up_weight_grad = (
        by_expert(part) for part in (down_part, gate_part, up_part)
    )
    spans = [H * HD, KVH * HD, KVH * HD, experts, 1, 1]
    pieces, begin = [], 0
    for span in spans:
        pieces.append(dense[:, begin : begin + span])
        begin += span
    query_grad, key_grad, value_grad, router_grad, gain_a_grad, gain_b_grad = pieces
    return (
        output,
        input_grad.reshape(groups, length, D),
        gain_a_grad[:, 0],
        query_grad,
        key_grad,
        value_grad,
        out_grad,
        gain_b_grad[:, 0],
        router_grad,
        gate_weight_grad,
        up_weight_grad,
        down_weight_grad,
        expert_load,
        prob_mean,
        balance_loss,
    )


def solution(mesh):
    dp_ranks, ranks = mesh.devices.shape
    fine = Mesh(
        mesh.devices.reshape(dp_ranks // 2, 2, ranks // 2, 2), ("dh", "dl", "eh", "el")
    )
    return jax.shard_map(
        on_device,
        mesh=fine,
        in_specs=(
            P(DATA, EXPERT, None),
            P(DATA, None),
            P(DATA, EXPERT, None),
            P(DATA, EXPERT, None),
            P(),
            P(),
            P(),
            P(),
            P(),
            P(),
            P(),
            P(EXPERT, None, None),
            P(EXPERT, None, None),
            P(EXPERT, None, None),
        ),
        out_specs=(
            P(DATA, EXPERT, None),
            P(DATA, EXPERT, None),
            P(DATA),
            P(DATA, None),
            P(DATA, None),
            P(DATA, None),
            P(DATA, None),
            P(DATA),
            P(DATA, None),
            P(EXPERT, DATA, None),
            P(EXPERT, DATA, None),
            P(EXPERT, DATA, None),
            P(),
            P(),
            P(),
        ),
        check_vma=False,
    )
```

```python
import functools
import math

import jax
import jax.numpy as jnp
from jax import lax
from jax.experimental import pallas as pl
from jax.experimental.pallas import tpu as pltpu
from jax.sharding import Mesh
from jax.sharding import PartitionSpec as P

D = 1536
H = 24
KVH = 8
HD = 64
FF = 512
TOPK = 8
EXP_DEV = 5
PROMPT = 1024
LANES = 128
PAIRS = KVH // 2
SHARE = H // KVH
PAIR_Q = 2 * SHARE * HD
ROWS = 256
STACK = SHARE * ROWS
EXPERT = ("eh", "el")
DATA = ("dh", "dl")
VMEM_LIMIT = 63 * 1024 * 1024

epsilon = 1e-05
rope_base = 10000.0
f32 = jnp.float32
bf16 = jnp.bfloat16


def dot(a, b):
    return lax.dot_general(a, b, (((1,), (0,)), ((), ())), preferred_element_type=f32)


def dot_nt(a, b):
    return lax.dot_general(a, b, (((1,), (1,)), ((), ())), preferred_element_type=f32)


def dot_tn(a, b):
    return lax.dot_general(a, b, (((0,), (0,)), ((), ())), preferred_element_type=f32)


def expert_rank():
    return lax.axis_index("eh") * 2 + lax.axis_index("el")


def call(kernel, name, micros, **more):
    cost = pl.CostEstimate(flops=int(micros * 9e8), bytes_accessed=0, transcendentals=0)
    return pl.pallas_call(
        kernel,
        name=name,
        cost_estimate=cost,
        compiler_params=pltpu.CompilerParams(vmem_limit_bytes=VMEM_LIMIT),
        **more,
    )


def shaped(shape, dtype):
    return jax.ShapeDtypeStruct(shape, dtype)


def lane_of(shape):
    return lax.broadcasted_iota(jnp.int32, shape, len(shape) - 1)


def half_swap(values):
    lower = lane_of(values.shape) % HD < HD // 2
    return jnp.where(
        lower, pltpu.roll(values, LANES - HD // 2, 1), pltpu.roll(values, HD // 2, 1)
    )


def resident(shape):
    zeros = (0,) * len(shape)
    return pl.BlockSpec(shape, lambda *_: zeros, pipeline_mode=pl.Buffered(1))


def row_block(width, first=0):
    return pl.BlockSpec((ROWS, width), lambda i: (first + i, 0))


def naming_kernel(capacity, groups, r_ref, o_ref):
    length = r_ref.shape[0]
    rows = groups * length
    lane = lane_of((rows, LANES))
    packed = r_ref[...].astype(jnp.int32)
    chosen = jnp.concatenate(
        [packed[:, g * TOPK : (g + 1) * TOPK] for g in range(groups)], axis=0
    )
    named = jnp.zeros((rows, LANES), f32)
    for k in range(TOPK):
        named = jnp.where(chosen[:, k : k + 1] == lane, 1.0, named)
    earlier = lax.broadcasted_iota(jnp.int32, (rows, rows), 1) < lax.broadcasted_iota(
        jnp.int32, (rows, rows), 0
    )
    slot = dot(jnp.where(earlier, 1.0, 0.0).astype(bf16), named.astype(bf16))
    level = named * jnp.where(slot < capacity, 2.0, 1.0)
    o_ref[...] = level.reshape(groups, length, LANES).astype(bf16)


def naming(kv, capacity, groups, ranks):
    total = kv.shape[0]
    length = total // ranks
    return call(
        functools.partial(naming_kernel, capacity, groups),
        "naming",
        9,
        grid=(ranks,),
        in_specs=[pl.BlockSpec((length, LANES), lambda s: (s, 2 * PAIRS))],
        out_specs=pl.BlockSpec((groups, length, LANES), lambda s: (0, s, 0)),
        out_shape=shaped((groups, total, LANES), bf16),
    )(kv)


def key_value_kernel(x_ref, gain_ref, wk_ref, wv_ref, cos_ref, sin_ref, r_ref, n_ref, kv_ref):
    x = x_ref[...].astype(f32)
    factor = lax.rsqrt(jnp.mean(x * x, axis=1, keepdims=True) + epsilon)
    normed = (x * factor * gain_ref[...]).astype(bf16)
    n_ref[...] = normed
    cosine, sine = cos_ref[...], sin_ref[...]
    key = dot(normed, wk_ref[...])
    for c in range(KVH * HD // LANES):
        part = key[:, c * LANES : (c + 1) * LANES]
        turned = part * cosine + half_swap(part) * sine
        kv_ref[:, c * LANES : (c + 1) * LANES] = turned.astype(bf16)
    kv_ref[:, KVH * HD : 2 * KVH * HD] = dot(normed, wv_ref[...]).astype(bf16)
    kv_ref[:, 2 * KVH * HD :] = r_ref[...]


def key_value(group, length, x, gain, wk, wv, cosine, sine, names):
    first = group * length // ROWS
    width = 2 * KVH * HD + LANES
    return call(
        key_value_kernel,
        "key_value",
        5,
        grid=(length // ROWS,),
        in_specs=[
            row_block(D, first),
            resident((1, D)),
            resident((D, KVH * HD)),
            resident((D, KVH * HD)),
            row_block(LANES, first),
            row_block(LANES, first),
            row_block(LANES),
        ],
        out_specs=[row_block(D), row_block(width)],
        out_shape=[shaped((length, D), bf16), shaped((length, width), bf16)],
    )(x, gain, wk, wv, cosine, sine, names)


def query_kernel(n_ref, wq_ref, cos_ref, sin_ref, q_ref):
    cosine, sine = cos_ref[...], sin_ref[...]
    query = dot(n_ref[...], wq_ref[...])
    for c in range(H * HD // LANES):
        part = query[:, c * LANES : (c + 1) * LANES]
        turned = part * cosine + half_swap(part) * sine
        q_ref[:, c * LANES : (c + 1) * LANES] = turned.astype(bf16) * jnp.asarray(0.125, bf16)


def project_query(group, normed, wq, cosine, sine):
    length = normed.shape[0]
    first = group * length // ROWS
    return call(
        query_kernel,
        "query",
        6,
        grid=(length // ROWS,),
        in_specs=[
            row_block(D),
            resident((D, H * HD)),
            row_block(LANES, first),
            row_block(LANES, first),
        ],
        out_specs=row_block(H * HD),
        out_shape=shaped((length, H * HD), bf16),
    )(normed, wq, cosine, sine)


def stack_heads(ref):
    low = lane_of((ROWS, LANES)) < HD
    parts = [ref[:, c * LANES : (c + 1) * LANES].astype(f32) for c in range(SHARE)]
    rolled0, rolled2 = pltpu.roll(parts[0], HD, 1), pltpu.roll(parts[2], HD, 1)
    zero = jnp.zeros((ROWS, LANES), f32)
    first = [parts[0], rolled0, parts[1]]
    second = [parts[1], rolled2, parts[2]]
    return (
        jnp.concatenate([jnp.where(low, v, zero).astype(bf16) for v in first], axis=0),
        jnp.concatenate([jnp.where(low, zero, v).astype(bf16) for v in second], axis=0),
    )


def unstack_heads(first, second):
    low = lane_of((ROWS, LANES)) < HD
    return (
        jnp.where(low, first[:ROWS], pltpu.roll(first[ROWS : 2 * ROWS], HD, 1)),
        jnp.where(low, first[2 * ROWS :], second[:ROWS]),
        jnp.where(low, pltpu.roll(second[ROWS : 2 * ROWS], HD, 1), second[2 * ROWS :]),
    )


def visit_chunks(block, chunk):
    prompt_blocks = PROMPT // ROWS

    @pl.when(block >= prompt_blocks)
    def _():
        for c in range(PROMPT // (2 * ROWS)):
            chunk(c * 2 * ROWS, 2 * ROWS, False)

    @pl.when(block < prompt_blocks)
    def _():
        def step(c, carry):
            chunk(pl.multiple_of(c * ROWS, ROWS), ROWS, False)
            return carry

        lax.fori_loop(0, block, step, 0)

    @pl.when(block > prompt_blocks)
    def _():
        chunk(pl.multiple_of((block - 1) * ROWS, ROWS), ROWS, True)

    chunk(pl.multiple_of(block * ROWS, ROWS), ROWS, True)


def mask_bias(block, begin, size, start_ref):
    place = begin + lax.broadcasted_iota(jnp.int32, (size, ROWS), 0)
    own = block * ROWS + lax.broadcasted_iota(jnp.int32, (size, ROWS), 1)
    ok = (place <= own) & (place >= start_ref[0, :1, :])
    bias = jnp.where(ok, 0.0, -1e30)
    return jnp.concatenate([bias] * SHARE, axis=1)


def attend_kernel(blocks, q_ref, k_ref, v_ref, start_ref, o_ref, lse_ref, vt_ref, m_ref, l_ref, acc_ref):
    block = expert_rank() * blocks + pl.program_id(1)

    @pl.when(pl.program_id(1) == 0)
    def _():
        vt_ref[...] = jnp.transpose(v_ref[...].astype(f32)).astype(bf16)

    queries = stack_heads(q_ref)
    m_ref[...] = jnp.full_like(m_ref, -1e30)
    l_ref[...] = jnp.zeros_like(l_ref)
    acc_ref[...] = jnp.zeros_like(acc_ref)

    def chunk(begin, size, masked):
        keys = k_ref[pl.ds(begin, size), :]
        values = vt_ref[:, pl.ds(begin, size)]
        bias = mask_bias(block, begin, size, start_ref) if masked else None
        for h in range(2):
            scores = dot_nt(keys, queries[h])
            if masked:
                scores = scores + bias
            before = m_ref[h, :1]
            peak = jnp.maximum(before, jnp.max(scores, axis=0, keepdims=True))
            weight = jnp.exp(scores - peak)
            shrink = jnp.exp(before - peak)
            m_ref[h, :1] = peak
            l_ref[h, :1] = l_ref[h, :1] * shrink + jnp.sum(weight, axis=0, keepdims=True)
            acc_ref[h] = acc_ref[h] * shrink + dot(values, weight.astype(bf16))

    visit_chunks(block, chunk)
    mixed = [jnp.transpose(acc_ref[h] / l_ref[h, :1]) for h in range(2)]
    for c, part in enumerate(unstack_heads(*mixed)):
        o_ref[:, c * LANES : (c + 1) * LANES] = part.astype(bf16)
    for h in range(2):
        total = m_ref[h, :1] + jnp.log(l_ref[h, :1])
        lse_ref[0, 0, h] = jnp.broadcast_to(total, (8, STACK))


def attend(group, query, kv, start_row):
    length = query.shape[0]
    total = kv.shape[0]
    blocks = length // ROWS
    heads = pl.BlockSpec((ROWS, PAIR_Q), lambda p, i: (i, p))
    return call(
        functools.partial(attend_kernel, blocks),
        "attend",
        45,
        grid=(PAIRS, blocks),
        in_specs=[
            heads,
            pl.BlockSpec((total, LANES), lambda p, i: (0, p)),
            pl.BlockSpec((total, LANES), lambda p, i: (0, PAIRS + p)),
            pl.BlockSpec((1, 8, ROWS), lambda p, i: (group, 0, i)),
        ],
        out_specs=[
            heads,
            pl.BlockSpec((1, 1, 2, 8, STACK), lambda p, i: (p, i, 0, 0, 0)),
        ],
        out_shape=[
            shaped(query.shape, bf16),
            shaped((PAIRS, blocks, 2, 8, STACK), f32),
        ],
        scratch_shapes=[
            pltpu.VMEM((LANES, total), bf16),
            pltpu.VMEM((2, 8, STACK), f32),
            pltpu.VMEM((2, 8, STACK), f32),
            pltpu.VMEM((2, LANES, STACK), f32),
        ],
    )(query, kv, kv, start_row)


def attend_back_kernel(
    blocks,
    q_ref,
    g_ref,
    o_ref,
    k_ref,
    v_ref,
    lse_ref,
    start_ref,
    cos_ref,
    sin_ref,
    dq_ref,
    keep_ref,
    send_ref,
    dq_acc,
    dkv_acc,
):
    step = pl.program_id(1)
    block = expert_rank() * blocks + step

    @pl.when(step == 0)
    def _():
        dkv_acc[...] = jnp.zeros_like(dkv_acc)

    dq_acc[...] = jnp.zeros_like(dq_acc)
    queries = stack_heads(q_ref)
    grads = stack_heads(g_ref)
    halves = []
    for c in range(SHARE):
        cols = slice(c * LANES, (c + 1) * LANES)
        product = jnp.transpose(g_ref[:, cols].astype(f32) * o_ref[:, cols].astype(f32))
        halves.append(jnp.sum(product[:HD], axis=0, keepdims=True))
        halves.append(jnp.sum(product[HD:], axis=0, keepdims=True))
    inner = [jnp.concatenate(halves[:SHARE], axis=1), jnp.concatenate(halves[SHARE:], axis=1)]

    def chunk(begin, size, masked):
        keys = k_ref[pl.ds(begin, size), :]
        values = v_ref[pl.ds(begin, size), :]
        bias = mask_bias(block, begin, size, start_ref) if masked else None
        key_sum, value_sum = None, None
        for h in range(2):
            scores = dot_nt(keys, queries[h]) - lse_ref[0, 0, h, :1, :]
            if masked:
                scores = scores + bias
            probs = jnp.exp(scores)
            probs_grad = dot_nt(values, grads[h])
            scores_grad = (probs * (probs_grad - inner[h])).astype(bf16)
            value_part = dot(probs.astype(bf16), grads[h])
            key_part = dot(scores_grad, queries[h])
            key_sum = key_part if key_sum is None else key_sum + key_part
            value_sum = value_part if value_sum is None else value_sum + value_part
            dq_acc[h] += dot_tn(scores_grad, keys)
        dkv_acc[0, pl.ds(begin, size), :] += key_sum
        dkv_acc[1, pl.ds(begin, size), :] += value_sum

    visit_chunks(block, chunk)
    cosine, sine = cos_ref[...], sin_ref[...]
    for c, part in enumerate(unstack_heads(dq_acc[0], dq_acc[1])):
        part = part * 0.125
        turned = part * cosine - half_swap(part) * sine
        dq_ref[:, c * LANES : (c + 1) * LANES] = turned.astype(bf16)

    @pl.when(step == blocks - 1)
    def _():
        length = blocks * ROWS
        own = lax.axis_index("el")
        for chip in range(dkv_acc.shape[1] // (2 * length)):
            mine = pl.multiple_of((2 * chip + own) * length, length)
            other = pl.multiple_of((2 * chip + 1 - own) * length, length)
            for i in range(2):
                keep_ref[chip, i] = dkv_acc[i, pl.ds(mine, length), :].astype(bf16)
                send_ref[chip, i] = dkv_acc[i, pl.ds(other, length), :].astype(bf16)


def attend_back(group, query, grad, mixed, kv, lse, start_row, cosine, sine):
    length = query.shape[0]
    total = kv.shape[0]
    blocks = length // ROWS
    first = group * blocks
    chips = total // (2 * length)
    side = pl.BlockSpec((chips, 2, length, LANES), lambda p, i: (0, 0, 0, p))
    heads = pl.BlockSpec((ROWS, PAIR_Q), lambda p, i: (i, p))
    table = pl.BlockSpec((ROWS, LANES), lambda p, i: (first + i, 0))
    return call(
        functools.partial(attend_back_kernel, blocks),
        "attend_back",
        64,
        grid=(PAIRS, blocks),
        in_specs=[
            heads,
            heads,
            heads,
            pl.BlockSpec((total, LANES), lambda p, i: (0, p)),
            pl.BlockSpec((total, LANES), lambda p, i: (0, PAIRS + p)),
            pl.BlockSpec((1, 1, 2, 8, STACK), lambda p, i: (p, i, 0, 0, 0)),
            pl.BlockSpec((1, 8, ROWS), lambda p, i: (group, 0, i)),
            table,
            table,
        ],
        out_specs=[
            heads,
            side,
            side,
        ],
        out_shape=[
            shaped(query.shape, bf16),
            shaped((chips, 2, length, KVH * HD), bf16),
            shaped((chips, 2, length, KVH * HD), bf16),
        ],
        scratch_shapes=[
            pltpu.VMEM((2, STACK, LANES), f32),
            pltpu.VMEM((2, total, LANES), f32),
        ],
    )(query, grad, mixed, kv, kv, lse, start_row, cosine, sine)


def branch_kernel(a_ref, x_ref, wo_ref, gain_ref, m_ref, n_ref):
    middle = x_ref[...].astype(f32) + dot(a_ref[...], wo_ref[...])
    m_ref[...] = middle
    factor = lax.rsqrt(jnp.mean(middle * middle, axis=1, keepdims=True) + epsilon)
    n_ref[...] = (middle * factor * gain_ref[...]).astype(bf16)


def branch(group, attended, x, wo, gain):
    length = attended.shape[0]
    return call(
        branch_kernel,
        "branch",
        6,
        grid=(length // ROWS,),
        in_specs=[
            row_block(H * HD),
            row_block(D, group * length // ROWS),
            resident((H * HD, D)),
            resident((1, D)),
        ],
        out_specs=[row_block(D), row_block(D)],
        out_shape=[shaped((length, D), f32), shaped((length, D), bf16)],
    )(attended, x, wo, gain)


def router(normed, weight):
    count = EXP_DEV * 2 * lax.axis_size("eh")
    logits = dot(normed, weight)
    logits = jnp.where(lane_of(logits.shape) < count, logits, -1e30)
    powers = jnp.exp(logits - jnp.max(logits, axis=1, keepdims=True))
    return powers / jnp.sum(powers, axis=1, keepdims=True)


def experts_kernel(
    x_ref, c_ref, t_ref, wr_ref, wg_ref, wu_ref, wd_ref, *refs
):
    mix_ref, rows_ref, x_out, c_out, hid_ref, gate_ref, up_ref = refs[-7:]
    x, cot = x_ref[...], c_ref[...]
    x_out[...] = x
    c_out[...] = cot
    level = t_ref[0].astype(f32)
    picked = jnp.where(level > 0.5, router(x, wr_ref[...]), 0.0)
    share = picked / jnp.sum(picked, axis=1, keepdims=True)
    share = jnp.where(level > 1.5, share, 0.0)
    lane = lane_of(share.shape)
    base = EXP_DEV * expert_rank()
    share = pltpu.roll(share, lax.rem(LANES - base, LANES), 1)
    mix, rows = None, None
    gate_grads = jnp.zeros(share.shape, bf16)
    for e in range(EXP_DEV):
        gate = dot(x, wg_ref[e])
        up = dot(x, wu_ref[e])
        hidden_grad = dot(cot, wd_ref[e])
        sigmoid = jax.nn.sigmoid(gate)
        active = gate * sigmoid
        hidden = active * up
        inner = jnp.sum(hidden * hidden_grad, axis=1, keepdims=True)
        coarse = inner.astype(bf16)
        fine = (inner - coarse.astype(f32)).astype(bf16)
        gate_grads = jnp.where(lane == base + e, coarse, gate_grads)
        gate_grads = jnp.where(lane == LANES // 2 + base + e, fine, gate_grads)
        weight = share[:, e : e + 1]
        scaled = (hidden * weight).astype(bf16)
        hidden_grad = hidden_grad * weight
        up_grad = (hidden_grad * active).astype(bf16)
        gate_grad = (hidden_grad * up * sigmoid * (1.0 + gate * (1.0 - sigmoid))).astype(bf16)
        cols = slice(e * FF, (e + 1) * FF)
        hid_ref[:, cols] = scaled
        gate_ref[:, cols] = gate_grad
        up_ref[:, cols] = up_grad
        mix_part = dot_nt(scaled, wd_ref[e])
        rows_part = dot_nt(gate_grad, wg_ref[e]) + dot_nt(up_grad, wu_ref[e])
        mix = mix_part if mix is None else mix + mix_part
        rows = rows_part if rows is None else rows + rows_part
    mix_ref[...] = mix.astype(bf16)
    rows_ref[:, :D] = rows.astype(bf16)
    rows_ref[:, D:] = gate_grads


def experts_pass(group, groups, x, cot, level, wr, wg, wu, wd, kept):
    count = x.shape[0]
    first = group * count // ROWS
    whole = groups * count
    side = pl.BlockSpec(memory_space=pl.ANY)
    widths = [D, D, EXP_DEV * FF, EXP_DEV * FF, EXP_DEV * FF]
    return call(
        experts_kernel,
        "experts",
        113,
        grid=(count // ROWS,),
        in_specs=[
            row_block(D),
            row_block(D),
            pl.BlockSpec((1, ROWS, LANES), lambda i: (group, i, 0)),
            resident((D, LANES)),
            resident((EXP_DEV, D, FF)),
            resident((EXP_DEV, D, FF)),
            resident((EXP_DEV, D, FF)),
        ]
        + [side] * len(kept),
        out_specs=[row_block(D), row_block(D + LANES)]
        + [row_block(width, first) for width in widths],
        out_shape=[
            shaped((count, D), bf16),
            shaped((count, D + LANES), bf16),
        ]
        + [shaped((whole, width), bf16) for width in widths],
        input_output_aliases={7 + i: 2 + i for i in range(len(kept))},
    )(x, cot, level, wr, wg, wu, wd, *kept)


def norm_back(grad, normed, factor, gain):
    scaled = grad * gain
    return factor * (scaled - normed * jnp.mean(scaled * normed, axis=1, keepdims=True))


def fold_rows(values):
    return jnp.sum(values.reshape(values.shape[0] // 8, 8, values.shape[1]), axis=0)


def add_up(ref, part):
    @pl.when(pl.program_id(0) == 0)
    def _():
        ref[...] = part

    @pl.when(pl.program_id(0) > 0)
    def _():
        ref[...] += part


def middle_kernel(
    r_ref, t_ref, m_ref, n_ref, c_ref, gain_ref, wr_ref, wo_ref,
    mg_ref, b_ref, ag_ref, l_ref, dg_ref, ps_ref,
):
    probs = router(n_ref[...], wr_ref[...])
    add_up(ps_ref, fold_rows(probs))
    level = t_ref[0].astype(f32)
    sel = jnp.where(level > 0.5, 1.0, 0.0)
    gate_grad = r_ref[:, D:].astype(f32)
    gate_grad = gate_grad + pltpu.roll(gate_grad, LANES // 2, 1)
    gate_grad = jnp.where(level > 1.5, gate_grad, 0.0)
    picked = probs * sel
    total = jnp.sum(picked, axis=1, keepdims=True)
    share = picked / total
    inner = jnp.sum(gate_grad * share, axis=1, keepdims=True)
    probs_grad = (gate_grad - inner) / total * sel
    logits_grad = probs * (probs_grad - jnp.sum(probs_grad * probs, axis=1, keepdims=True))
    coarse = logits_grad.astype(bf16)
    fine = (logits_grad - coarse.astype(f32)).astype(bf16)
    l_ref[:, :LANES] = coarse
    l_ref[:, LANES:] = fine
    grad = r_ref[:, :D].astype(f32) + dot_nt(coarse, wr_ref[...]) + dot_nt(fine, wr_ref[...])
    middle = m_ref[...]
    factor = lax.rsqrt(jnp.mean(middle * middle, axis=1, keepdims=True) + epsilon)
    normed = middle * factor
    add_up(dg_ref, fold_rows(grad * normed))
    middle_grad = c_ref[...].astype(f32) + norm_back(grad, normed, factor, gain_ref[...])
    mg_ref[...] = middle_grad
    low = middle_grad.astype(bf16)
    b_ref[...] = low
    ag_ref[...] = dot_nt(low, wo_ref[...]).astype(bf16)


def middle_back(group, rows, level, middle, normed, cot, gain, wr, wo):
    length = rows.shape[0]
    first = group * length // ROWS
    corner = lambda width: pl.BlockSpec((8, width), lambda i: (0, 0))
    return call(
        middle_kernel,
        "middle_back",
        8,
        grid=(length // ROWS,),
        in_specs=[
            row_block(D + LANES),
            pl.BlockSpec((1, ROWS, LANES), lambda i: (group, i, 0)),
            row_block(D), row_block(D), row_block(D, first),
            resident((1, D)), resident((D, LANES)), resident((H * HD, D)),
        ],
        out_specs=[
            row_block(D), row_block(D), row_block(H * HD), row_block(2 * LANES),
            corner(D), corner(LANES),
        ],
        out_shape=[
            shaped((length, D), f32),
            shaped((length, D), bf16),
            shaped((length, H * HD), bf16),
            shaped((length, 2 * LANES), bf16),
            shaped((8, D), f32),
            shaped((8, LANES), f32),
        ],
    )(rows, level, middle, normed, cot, gain, wr, wo)


def input_kernel(
    dq_ref, dk_ref, dv_ref, x_ref, mg_ref, cos_ref, sin_ref, gain_ref, wq_ref, wk_ref, wv_ref,
    out_ref, dk_out, dg_ref,
):
    cosine, sine = cos_ref[...], sin_ref[...]
    for c in range(KVH * HD // LANES):
        part = dk_ref[0, :, c * LANES : (c + 1) * LANES].astype(f32)
        turned = part * cosine - half_swap(part) * sine
        dk_out[:, c * LANES : (c + 1) * LANES] = turned.astype(bf16)
    grad = dot_nt(dq_ref[...], wq_ref[...])
    grad = grad + dot_nt(dk_out[...], wk_ref[...])
    grad = grad + dot_nt(dv_ref[0], wv_ref[...])
    x = x_ref[...].astype(f32)
    factor = lax.rsqrt(jnp.mean(x * x, axis=1, keepdims=True) + epsilon)
    normed = x * factor
    add_up(dg_ref, fold_rows(grad * normed))
    out_ref[...] = mg_ref[...] + norm_back(grad, normed, factor, gain_ref[...])


def input_back(group, groups, dq, dkv, x, middle_grad, cosine, sine, gain, wq, wk, wv, kept):
    length = dq.shape[0]
    first = group * length // ROWS
    kernel = lambda *refs: input_kernel(*refs[:11], *refs[-3:])
    return call(
        kernel,
        "input_back",
        8,
        grid=(length // ROWS,),
        in_specs=[
            row_block(H * HD),
            pl.BlockSpec((1, ROWS, KVH * HD), lambda i: (0, i, 0)),
            pl.BlockSpec((1, ROWS, KVH * HD), lambda i: (1, i, 0)),
            row_block(D, first),
            row_block(D),
            row_block(LANES, first),
            row_block(LANES, first),
            resident((1, D)),
            resident((D, H * HD)),
            resident((D, KVH * HD)),
            resident((D, KVH * HD)),
        ]
        + [pl.BlockSpec(memory_space=pl.ANY)] * len(kept),
        out_specs=[
            row_block(D, first),
            row_block(KVH * HD),
            pl.BlockSpec((8, D), lambda i: (0, 0)),
        ],
        out_shape=[
            shaped((groups * length, D), f32),
            shaped((length, KVH * HD), bf16),
            shaped((8, D), f32),
        ],
        input_output_aliases={11: 0} if kept else {},
    )(dq, dkv, dkv, x, middle_grad, cosine, sine, gain, wq, wk, wv, *kept)


def transpose_into(turned, lefts):
    length = lefts[0].shape[0]
    for g, left in enumerate(lefts):
        for c in range(0, D, 2 * LANES):
            part = left[:, c : c + 2 * LANES].astype(f32)
            turned[c : c + 2 * LANES, g * length : (g + 1) * length] = jnp.transpose(part).astype(
                bf16
            )


def out_kernel(groups, *refs):
    lefts, rights = refs[:groups], refs[groups : 2 * groups]
    out_ref, turned = refs[-2:]
    length = lefts[0].shape[0]

    @pl.when(pl.program_id(0) == 0)
    def _():
        transpose_into(turned, lefts)

    total = None
    for g in range(groups):
        part = dot(turned[:, g * length : (g + 1) * length], rights[g][...])
        total = part if total is None else total + part
    out_ref[...] = total.astype(bf16)


def out_gradient(lefts, rights):
    groups, length = len(lefts), lefts[0].shape[0]
    width = 4 * LANES
    return call(
        functools.partial(out_kernel, groups),
        "out_grad",
        10,
        grid=(D // width,),
        in_specs=[resident((length, D))] * groups
        + [pl.BlockSpec((length, width), lambda i: (0, i))] * groups,
        out_specs=pl.BlockSpec((D, width), lambda i: (0, i)),
        out_shape=shaped((D, D), bf16),
        scratch_shapes=[pltpu.VMEM((D, groups * length), bf16)],
    )(*lefts, *rights)


def dense_kernel(groups, sizes, *refs):
    data, chips, shard, width, full, late = sizes
    lefts, queries, keys, values = (refs[i * groups : (i + 1) * groups] for i in range(4))
    narrow_ref, late_ref, out_ref = refs[4 * groups : 4 * groups + 3]
    turned, keep1, send1, got1, keep2, send2, got2, sum2, got3, sum3, got4, sum4, got5 = refs[
        4 * groups + 3 : 4 * groups + 16
    ]
    sems = refs[4 * groups + 16 :]
    half = width // 2
    length = lefts[0].shape[0]
    ranks = 2 * chips
    dh, dl, eh, el = (lax.axis_index(name) for name in ("dh", "dl", "eh", "el"))

    def near(hop, core):
        return {"eh": lax.rem(eh + hop, chips), "el": core}

    peers = [{"el": 1 - el}, {"dl": 1 - dl}]
    for hop in range(1, chips):
        peers += [near(hop, el), near(hop, 1 - el)]
    for hop in range(1, data):
        peers.append({"dh": lax.rem(dh + hop, data)})
    barrier = pltpu.get_barrier_semaphore()
    for peer in peers:
        pl.semaphore_signal(barrier, inc=1, device_id=peer, device_id_type=pl.DeviceIdType.MESH)
    pl.semaphore_wait(barrier, len(peers))

    transpose_into(turned, lefts)

    def copy(source, target, phase, k, lane, peer):
        return pltpu.make_async_remote_copy(
            src_ref=source,
            dst_ref=target,
            send_sem=sems[2 * phase].at[k, lane],
            recv_sem=sems[2 * phase + 1].at[k, lane],
            device_id=peer,
            device_id_type=pl.DeviceIdType.MESH,
        )

    def copies(phase, k):
        if phase == 0:
            return [copy(send1.at[k], got1.at[k], 0, k, 0, {"el": 1 - el})]
        if phase == 1:
            return [
                copy(send2.at[k, hop - 1], got2.at[k, hop - 1], 1, k, hop - 1, near(hop, el))
                for hop in range(1, chips)
            ]
        if phase == 2:
            return [copy(sum2.at[k, 1 - dl], got3.at[k], 2, k, 0, {"dl": 1 - dl})]
        if phase == 3:
            found = []
            for hop in range(1, data):
                away = lax.rem(dh + hop, data)
                found.append(
                    copy(sum3.at[k, away], got4.at[k, hop - 1], 3, k, hop - 1, {"dh": away})
                )
            return found
        found = []
        for hop in range(chips):
            for side in range(2):
                if hop or side:
                    lane = 2 * hop + side - 1
                    peer = near(hop, el if side == 0 else 1 - el)
                    found.append(copy(sum4.at[k], got5.at[k, lane], 4, k, lane, peer))
        return found

    def start(phase, k):
        for one in copies(phase, k):
            one.start()

    def arrived(phase, k):
        for one in copies(phase, k):
            one.wait_recv()

    def finish_shard(k, c):
        base = c * width if k < full else full * width + (k - full) * LANES

        def put(side, chip, block):
            place = side * chips + chip
            place = place * LANES if k < full else place * late * LANES
            at = pl.multiple_of(base + place, LANES)
            out_ref[:, pl.ds(at, LANES)] = block.astype(f32)

        put(el, eh, sum4[k])
        for hop in range(chips):
            for side in range(2):
                if hop or side:
                    chip = lax.rem(eh + chips - hop, chips)
                    put(el if side == 0 else 1 - el, chip, got5[k, 2 * hop + side - 1])

    def piece(column):
        size = KVH * HD
        if column >= H * HD + 2 * size:
            if column > H * HD + 2 * size:
                return jnp.zeros((D, size), bf16)
            part = jnp.transpose(narrow_ref[...])
            return jnp.concatenate([part, jnp.zeros((D, size - LANES), f32)], axis=1).astype(bf16)
        total = None
        for g in range(groups):
            if column < H * HD:
                block = queries[g][:, column : column + size]
            elif column < H * HD + size:
                block = keys[g][...]
            else:
                block = values[g][1]
            one = dot(turned[:, g * length : (g + 1) * length], block)
            total = one if total is None else total + one
        return total.astype(bf16)

    def stage_compute(k):
        if k < full:
            part = [piece(k * width + c) for c in range(0, width, KVH * HD)]
            part = part[0] if len(part) == 1 else jnp.concatenate(part, axis=1)

            @pl.when(el == 0)
            def _():
                keep1[k] = part[:, :half]
                send1[k] = part[:, half:]

            @pl.when(el == 1)
            def _():
                keep1[k] = part[:, half:]
                send1[k] = part[:, :half]

            start(0, k)

    def stage_core(k):
        arrived(0, k)
        met = keep1[k].astype(f32) + got1[k].astype(f32)
        met = met.astype(bf16)
        for chip in range(chips):
            block = met[:, chip * LANES : (chip + 1) * LANES]
            hop = lax.rem(chip + chips - eh, chips)

            @pl.when(hop == 0)
            def _(block=block):
                keep2[k] = block

            @pl.when(hop > 0)
            def _(block=block, hop=hop):
                send2[k, hop - 1] = block

        start(1, k)

    def stage_chip(k):
        arrived(1, k)
        total = keep2[k].astype(f32)
        for hop in range(1, chips):
            total = total + got2[k, hop - 1].astype(f32)
        spread(k, total.astype(bf16))

    def spread(k, total):
        for far in range(data):
            for side in range(2):
                first = (2 * far + side) * shard
                sum2[k, side, far] = total[first : first + shard]
        start(2, k)

    def stage_pair(k):
        arrived(2, k)
        sum3[k] = (sum2[k, dl].astype(f32) + got3[k].astype(f32)).astype(bf16)
        start(3, k)

    def stage_far(k):
        arrived(3, k)
        total = sum3[k, dh].astype(f32)
        for hop in range(1, data):
            total = total + got4[k, hop - 1].astype(f32)
        sum4[k] = total.astype(bf16)
        start(4, k)

    def stage_last(k):
        arrived(4, k)
        finish_shard(k, k)

    everything = list(range(full, full + late)) + list(range(full))
    for k in range(full, full + late):
        first = (k - full) * LANES
        spread(k, late_ref[:, first : first + LANES])
    for step in range(full + 5):
        for stage, delay in (
            (stage_compute, 0),
            (stage_core, 1),
            (stage_chip, 2),
            (stage_pair, 3),
            (stage_far, 4),
            (stage_last, 5),
        ):
            k = step - delay
            if 0 <= k < full:
                stage(k)
        if step == 0:
            for k in range(full, full + late):
                stage_pair(k)
        if step == 1:
            for k in range(full, full + late):
                stage_far(k)
        if step == 2:
            for k in range(full, full + late):
                stage_last(k)
    for k in everything:
        for phase in range(5):
            if k < full or phase > 1:
                for one in copies(phase, k):
                    one.wait_send()


def dense_gradient(lefts, queries, keys, values, narrow, late_part):
    groups = len(lefts)
    data, chips = lax.axis_size("dh"), lax.axis_size("eh")
    shard = D // (2 * data)
    width = 2 * chips * LANES
    columns = H * HD + 2 * KVH * HD
    full = -(-(columns + LANES) // width)
    late = late_part.shape[1] // LANES
    total = full + late
    half, ranks = width // 2, 2 * chips
    sizes = (data, chips, shard, width, full, late)
    lanes = [1, chips - 1, 1, data - 1, ranks - 1]
    sems = []
    for count in lanes:
        sems += [pltpu.SemaphoreType.DMA((total, count))] * 2
    operands = [*lefts, *queries, *keys, *values, narrow, late_part]
    whole = pl.BlockSpec(memory_space=pltpu.VMEM)
    return pl.pallas_call(
        functools.partial(dense_kernel, groups, sizes),
        name="dense_grad",
        in_specs=[whole] * len(operands),
        out_specs=whole,
        out_shape=shaped((shard, full * width + late * ranks * LANES), f32),
        scratch_shapes=[
            pltpu.VMEM((D, groups * lefts[0].shape[0]), bf16),
            pltpu.VMEM((full, D, half), bf16),
            pltpu.VMEM((full, D, half), bf16),
            pltpu.VMEM((full, D, half), bf16),
            pltpu.VMEM((full, D, LANES), bf16),
            pltpu.VMEM((full, chips - 1, D, LANES), bf16),
            pltpu.VMEM((full, chips - 1, D, LANES), bf16),
            pltpu.VMEM((total, 2, data, shard, LANES), bf16),
            pltpu.VMEM((total, data, shard, LANES), bf16),
            pltpu.VMEM((total, data, shard, LANES), bf16),
            pltpu.VMEM((total, data - 1, shard, LANES), bf16),
            pltpu.VMEM((total, shard, LANES), bf16),
            pltpu.VMEM((total, ranks - 1, shard, LANES), bf16),
        ]
        + sems,
        cost_estimate=pl.CostEstimate(
            flops=int(80 * 9e8), bytes_accessed=0, transcendentals=0
        ),
        compiler_params=pltpu.CompilerParams(
            vmem_limit_bytes=VMEM_LIMIT, collective_id=0, has_side_effects=True
        ),
    )(*operands)


def widen(values):
    return jnp.pad(values, ((0, 0), (0, LANES - values.shape[1])))


def swap(values, axis):
    return lax.ppermute(values, axis, [(0, 1), (1, 0)])


def pick(values, index):
    return lax.dynamic_index_in_dim(values, index, 1, keepdims=False)


def pair_sum(values, shard):
    parts = values.reshape(-1, 2, shard, values.shape[1])
    own = lax.axis_index("dl")
    met = pick(parts, own) + swap(pick(parts, 1 - own), "dl")
    return met.reshape(-1, values.shape[1])


def take(values, axis, index):
    return lax.dynamic_index_in_dim(values, index, axis, keepdims=False)


def expert_sum(keep, send):
    chips = lax.axis_size("eh")
    met = keep + swap(send, "el")
    chip = lax.axis_index("eh")
    total = take(met, 0, chip)
    for hop in range(1, chips):
        order = [(i, (i + hop) % chips) for i in range(chips)]
        away = take(met, 0, lax.rem(chip + hop, chips))
        total = total + lax.ppermute(away, "eh", order)
    return total


def column_sum(values):
    chips = lax.axis_size("eh")
    own, chip = lax.axis_index("el"), lax.axis_index("eh")
    half = values.shape[1] // 2

    def cut(array, index, size):
        return lax.dynamic_slice_in_dim(array, index * size, size, 1)

    met = cut(values, own, half) + swap(cut(values, 1 - own, half), "el")
    size = half // chips
    total = cut(met, chip, size)
    for hop in range(1, chips):
        order = [(i, (i + hop) % chips) for i in range(chips)]
        away = cut(met, lax.rem(chip + hop, chips), size)
        total = total + lax.ppermute(away, "eh", order)
    return total


def everywhere_sum(values):
    for axis in ("el", "eh", "dl", "dh"):
        count = lax.axis_size(axis)
        hop = 1
        while hop < count:
            values = values + lax.ppermute(values, axis, [(i, i ^ hop) for i in range(count)])
            hop *= 2
    return values


def together(*values):
    return lax.optimization_barrier(values)


def on_device(
    tokens,
    segments,
    routes,
    cotangent,
    attention_gain,
    query_weight,
    key_weight,
    value_weight,
    out_weight,
    mixture_gain,
    router_weight,
    gate_weight,
    up_weight,
    down_weight,
):
    groups, length, _ = tokens.shape
    each = range(groups)
    rows = groups * length
    ranks = lax.axis_size("eh") * 2
    dp_ranks = lax.axis_size("dh") * 2
    rank = expert_rank()
    experts = EXP_DEV * ranks
    capacity = (rows * TOPK * 5 // (4 * experts) + 7) // 8 * 8
    all_tokens = rows * dp_ranks * ranks
    first_row = rank * length
    shard = D // dp_ranks

    seg_full = jnp.concatenate([jnp.full((groups, PROMPT), -1, jnp.int32), segments], axis=1)
    seg_own = lax.dynamic_slice_in_dim(seg_full, first_row, length, 1)
    earlier = jnp.sum((segments[:, None, :] < seg_own[:, :, None]).astype(jnp.int32), axis=2)
    position = first_row + jnp.arange(length, dtype=jnp.int32)[None, :]
    place = position - earlier
    start = jnp.where(position >= PROMPT, PROMPT + earlier, 0)
    half = HD // 2
    lane = jnp.arange(LANES, dtype=jnp.int32)
    frequency = jnp.exp(-math.log(rope_base) * (lane % half).astype(f32) / half)
    angles = place.astype(f32).reshape(rows, 1) * frequency
    cosine = jnp.cos(angles)
    sine = jnp.sin(angles) * jnp.where(lane % HD < half, -1.0, 1.0)
    start_row = jnp.broadcast_to(start[:, None, :], (groups, 8, length))

    names = jnp.concatenate([routes[g] for g in each], axis=1).astype(bf16)
    names = widen(names)
    cot_rows = cotangent.reshape(rows, D)
    cot_all = [lax.all_gather(cotangent[g], EXPERT, axis=0, tiled=True) for g in each]

    x = tokens.reshape(rows, D)
    gain_a = attention_gain.reshape(1, D)
    gain_b = mixture_gain.reshape(1, D)
    router_wide = widen(router_weight)
    normed, query, kv = [None] * groups, [None] * groups, [None] * groups
    for g in each:
        normed[g], kv_own = key_value(
            g, length, x, gain_a, key_weight, value_weight, cosine, sine, names
        )
        kv[g] = lax.all_gather(kv_own, EXPERT, axis=0, tiled=True)
    for g in each:
        query[g] = project_query(g, normed[g], query_weight, cosine, sine)
    level = naming(kv[groups - 1], capacity, groups, ranks)
    level_own = lax.dynamic_slice_in_dim(level, first_row, length, 1)
    kv[0], query = together(kv[0], query)
    attended, lse = [None] * groups, [None] * groups
    middle, hidden_low, hidden_all = [None] * groups, [None] * groups, [None] * groups
    for g in each:
        attended[g], lse[g] = attend(g, query[g], kv[g], start_row)
        if g == groups - 1:
            attended[g], cot_all[0] = together(attended[g], cot_all[0])
        middle[g], hidden_low[g] = branch(g, attended[g], x, out_weight, gain_b)
        hidden_all[g] = lax.all_gather(hidden_low[g], EXPERT, axis=0, tiled=True)

    kept, rows_back, mixture = [], [], []
    for g in each:
        if g > 0:
            kept[0], cot_all[g] = together(kept[0], cot_all[g])
        mix, rows_grad, *kept = experts_pass(
            g, groups, hidden_all[g], cot_all[g], level, router_wide,
            gate_weight, up_weight, down_weight, kept,
        )
        rows_back.append(lax.psum_scatter(rows_grad, EXPERT, scatter_dimension=0, tiled=True))
        mixture.append(lax.psum_scatter(mix, EXPERT, scatter_dimension=0, tiled=True))
    x_all, cot_both, hidden, gate_back, up_back = kept
    hidden, mixture[0] = together(hidden, mixture[0])
    down_local = dot_tn(cot_both, hidden).astype(bf16)
    x_all, down_local = together(x_all, down_local)
    gate_local = dot_tn(x_all, gate_back).astype(bf16)
    up_local = dot_tn(x_all, up_back).astype(bf16)
    rows_back[0], gate_local, up_local = together(rows_back[0], gate_local, up_local)

    def by_expert(part):
        return jnp.stack([part[:, e * FF : (e + 1) * FF] for e in range(EXP_DEV)]).astype(f32)

    def far_sum(met):
        return lax.psum_scatter(met, "dh", scatter_dimension=0, tiled=True)

    middle_grad, branch_grad, logits_grad, dq, dkv = ([None] * groups for _ in range(5))
    gain_b_local, probs_local = 0.0, 0.0
    down_met = pair_sum(down_local, shard)
    gate_met = pair_sum(gate_local, shard)
    for g in each:
        middle_grad[g], branch_grad[g], attended_grad, logits_grad[g], gain_part, probs_part = (
            middle_back(
                g, rows_back[g], level_own, middle[g], hidden_low[g], cot_rows,
                gain_b, router_wide, out_weight,
            )
        )
        gain_b_local += jnp.sum(gain_part, axis=0)
        probs_local += jnp.sum(probs_part, axis=0)
        if g == 0:
            attended_grad, down_met, mixture[1] = together(attended_grad, down_met, mixture[1])
            down_part = far_sum(down_met)
        if g == 1:
            out_local = out_gradient(attended, branch_grad)
            attended_grad, gate_met, down_part, out_local, dkv[0] = together(
                attended_grad, gate_met, down_part, out_local, dkv[0]
            )
            gate_part = far_sum(gate_met)
            up_local, out_local, gate_met = together(up_local, out_local, gate_met)
            up_met = pair_sum(up_local, shard)
            fill = -D % (ranks * LANES)
            out_part = column_sum(jnp.pad(out_local, ((0, 0), (0, fill))))
        dq[g], keep_part, send_part = attend_back(
            g, query[g], attended_grad, attended[g], kv[g], lse[g], start_row, cosine, sine
        )
        if g == 1:
            keep_part, up_met = together(keep_part, up_met)
            up_part = far_sum(up_met)
        dkv[g] = expert_sum(keep_part, send_part)
    output = jnp.stack(
        [(middle[g] + mixture[g].astype(f32)).astype(bf16) for g in each]
    )

    counts = jnp.sum((level_own > 0.5).astype(f32), axis=(0, 1))
    stats_all = everywhere_sum(jnp.stack([counts, probs_local])[:, :experts])
    dq[0], gate_part, out_part = together(dq[0], gate_part, out_part)
    kept, turned_dk, gain_a_local = [], [None] * groups, 0.0
    for g in each:
        input_grad, turned_dk[g], gain_part = input_back(
            g, groups, dq[g], dkv[g], x, middle_grad[g], cosine, sine,
            gain_a, query_weight, key_weight, value_weight, kept,
        )
        kept = [input_grad]
        gain_a_local += jnp.sum(gain_part, axis=0)
    router_parts = sum(dot_tn(logits_grad[g], hidden_low[g]) for g in each)
    router_local = (router_parts[:LANES] + router_parts[LANES:])[:experts]
    narrow = jnp.concatenate(
        [
            router_local,
            gain_a_local[None, :],
            gain_b_local[None, :],
            jnp.zeros((LANES - experts - 2, D), f32),
        ],
        axis=0,
    )
    dense = dense_gradient(normed, dq, turned_dk, dkv, narrow, out_part)
    dense, stats_all = together(dense, stats_all)
    expert_load = stats_all[0] * experts / (all_tokens * TOPK)
    prob_mean = stats_all[1] * experts / all_tokens
    balance_loss = jnp.sum(expert_load * prob_mean) / experts
    first = dense.shape[1] - D - fill
    out_grad = dense[:, first : first + D]
    down_weight_grad, gate_weight_grad, up_weight_grad = (
        by_expert(part) for part in (down_part, gate_part, up_part)
    )
    spans = [H * HD, KVH * HD, KVH * HD, experts, 1, 1]
    pieces, begin = [], 0
    for span in spans:
        pieces.append(dense[:, begin : begin + span])
        begin += span
    query_grad, key_grad, value_grad, router_grad, gain_a_grad, gain_b_grad = pieces
    return (
        output,
        input_grad.reshape(groups, length, D),
        gain_a_grad[:, 0],
        query_grad,
        key_grad,
        value_grad,
        out_grad,
        gain_b_grad[:, 0],
        router_grad,
        gate_weight_grad,
        up_weight_grad,
        down_weight_grad,
        expert_load,
        prob_mean,
        balance_loss,
    )


def solution(mesh):
    dp_ranks, ranks = mesh.devices.shape
    fine = Mesh(
        mesh.devices.reshape(dp_ranks // 2, 2, ranks // 2, 2), ("dh", "dl", "eh", "el")
    )
    return jax.shard_map(
        on_device,
        mesh=fine,
        in_specs=(
            P(DATA, EXPERT, None),
            P(DATA, None),
            P(DATA, EXPERT, None),
            P(DATA, EXPERT, None),
            P(),
            P(),
            P(),
            P(),
            P(),
            P(),
            P(),
            P(EXPERT, None, None),
            P(EXPERT, None, None),
            P(EXPERT, None, None),
        ),
        out_specs=(
            P(DATA, EXPERT, None),
            P(DATA, EXPERT, None),
            P(DATA),
            P(DATA, None),
            P(DATA, None),
            P(DATA, None),
            P(DATA, None),
            P(DATA),
            P(DATA, None),
            P(EXPERT, DATA, None),
            P(EXPERT, DATA, None),
            P(EXPERT, DATA, None),
            P(),
            P(),
            P(),
        ),
        check_vma=False,
    )
```

```python
import functools
import math

import jax
import jax.numpy as jnp
from jax import lax
from jax.experimental import pallas as pl
from jax.experimental.pallas import tpu as pltpu
from jax.sharding import Mesh
from jax.sharding import PartitionSpec as P

D = 1536
H = 24
KVH = 8
HD = 64
FF = 512
TOPK = 8
EXP_DEV = 5
PROMPT = 1024
LANES = 128
PAIRS = KVH // 2
SHARE = H // KVH
PAIR_Q = 2 * SHARE * HD
ROWS = 256
STACK = SHARE * ROWS
EXPERT = ("eh", "el")
DATA = ("dh", "dl")
VMEM_LIMIT = 63 * 1024 * 1024

epsilon = 1e-05
rope_base = 10000.0
f32 = jnp.float32
bf16 = jnp.bfloat16


def dot(a, b):
    return lax.dot_general(a, b, (((1,), (0,)), ((), ())), preferred_element_type=f32)


def dot_nt(a, b):
    return lax.dot_general(a, b, (((1,), (1,)), ((), ())), preferred_element_type=f32)


def dot_tn(a, b):
    return lax.dot_general(a, b, (((0,), (0,)), ((), ())), preferred_element_type=f32)


def expert_rank():
    return lax.axis_index("eh") * 2 + lax.axis_index("el")


def call(kernel, name, micros, **more):
    cost = pl.CostEstimate(flops=int(micros * 2.5e8), bytes_accessed=0, transcendentals=0)
    return pl.pallas_call(
        kernel,
        name=name,
        cost_estimate=cost,
        compiler_params=pltpu.CompilerParams(vmem_limit_bytes=VMEM_LIMIT),
        **more,
    )


def shaped(shape, dtype):
    return jax.ShapeDtypeStruct(shape, dtype)


def lane_of(shape):
    return lax.broadcasted_iota(jnp.int32, shape, len(shape) - 1)


def half_swap(values):
    lower = lane_of(values.shape) % HD < HD // 2
    return jnp.where(
        lower, pltpu.roll(values, LANES - HD // 2, 1), pltpu.roll(values, HD // 2, 1)
    )


def resident(shape):
    zeros = (0,) * len(shape)
    return pl.BlockSpec(shape, lambda *_: zeros, pipeline_mode=pl.Buffered(1))


def row_block(width, first=0):
    return pl.BlockSpec((ROWS, width), lambda i: (first + i, 0))


def naming_kernel(capacity, groups, r_ref, o_ref):
    length = r_ref.shape[0]
    rows = groups * length
    lane = lane_of((rows, LANES))
    packed = r_ref[...].astype(jnp.int32)
    chosen = jnp.concatenate(
        [packed[:, g * TOPK : (g + 1) * TOPK] for g in range(groups)], axis=0
    )
    named = jnp.zeros((rows, LANES), f32)
    for k in range(TOPK):
        named = jnp.where(chosen[:, k : k + 1] == lane, 1.0, named)
    earlier = lax.broadcasted_iota(jnp.int32, (rows, rows), 1) < lax.broadcasted_iota(
        jnp.int32, (rows, rows), 0
    )
    slot = dot(jnp.where(earlier, 1.0, 0.0).astype(bf16), named.astype(bf16))
    level = named * jnp.where(slot < capacity, 2.0, 1.0)
    o_ref[...] = level.reshape(groups, length, LANES).astype(bf16)


def naming(kv, capacity, groups, ranks):
    total = kv.shape[0]
    length = total // ranks
    return call(
        functools.partial(naming_kernel, capacity, groups),
        "naming",
        9,
        grid=(ranks,),
        in_specs=[pl.BlockSpec((length, LANES), lambda s: (s, 2 * PAIRS))],
        out_specs=pl.BlockSpec((groups, length, LANES), lambda s: (0, s, 0)),
        out_shape=shaped((groups, total, LANES), bf16),
    )(kv)


def key_value_kernel(x_ref, gain_ref, wk_ref, wv_ref, cos_ref, sin_ref, r_ref, n_ref, kv_ref):
    x = x_ref[...].astype(f32)
    factor = lax.rsqrt(jnp.mean(x * x, axis=1, keepdims=True) + epsilon)
    normed = (x * factor * gain_ref[...]).astype(bf16)
    n_ref[...] = normed
    cosine, sine = cos_ref[...], sin_ref[...]
    key = dot(normed, wk_ref[...])
    for c in range(KVH * HD // LANES):
        part = key[:, c * LANES : (c + 1) * LANES]
        turned = part * cosine + half_swap(part) * sine
        kv_ref[:, c * LANES : (c + 1) * LANES] = turned.astype(bf16)
    kv_ref[:, KVH * HD : 2 * KVH * HD] = dot(normed, wv_ref[...]).astype(bf16)
    kv_ref[:, 2 * KVH * HD :] = r_ref[...]


def key_value(group, length, x, gain, wk, wv, cosine, sine, names):
    first = group * length // ROWS
    width = 2 * KVH * HD + LANES
    return call(
        key_value_kernel,
        "key_value",
        5,
        grid=(length // ROWS,),
        in_specs=[
            row_block(D, first),
            resident((1, D)),
            resident((D, KVH * HD)),
            resident((D, KVH * HD)),
            row_block(LANES, first),
            row_block(LANES, first),
            row_block(LANES),
        ],
        out_specs=[row_block(D), row_block(width)],
        out_shape=[shaped((length, D), bf16), shaped((length, width), bf16)],
    )(x, gain, wk, wv, cosine, sine, names)


def query_kernel(n_ref, wq_ref, cos_ref, sin_ref, q_ref):
    cosine, sine = cos_ref[...], sin_ref[...]
    query = dot(n_ref[...], wq_ref[...])
    for c in range(H * HD // LANES):
        part = query[:, c * LANES : (c + 1) * LANES]
        turned = part * cosine + half_swap(part) * sine
        q_ref[:, c * LANES : (c + 1) * LANES] = turned.astype(bf16) * jnp.asarray(0.125, bf16)


def project_query(group, normed, wq, cosine, sine):
    length = normed.shape[0]
    first = group * length // ROWS
    return call(
        query_kernel,
        "query",
        6,
        grid=(length // ROWS,),
        in_specs=[
            row_block(D),
            resident((D, H * HD)),
            row_block(LANES, first),
            row_block(LANES, first),
        ],
        out_specs=row_block(H * HD),
        out_shape=shaped((length, H * HD), bf16),
    )(normed, wq, cosine, sine)


def stack_heads(ref):
    low = lane_of((ROWS, LANES)) < HD
    parts = [ref[:, c * LANES : (c + 1) * LANES].astype(f32) for c in range(SHARE)]
    rolled0, rolled2 = pltpu.roll(parts[0], HD, 1), pltpu.roll(parts[2], HD, 1)
    zero = jnp.zeros((ROWS, LANES), f32)
    first = [parts[0], rolled0, parts[1]]
    second = [parts[1], rolled2, parts[2]]
    return (
        jnp.concatenate([jnp.where(low, v, zero).astype(bf16) for v in first], axis=0),
        jnp.concatenate([jnp.where(low, zero, v).astype(bf16) for v in second], axis=0),
    )


def unstack_heads(first, second):
    low = lane_of((ROWS, LANES)) < HD
    return (
        jnp.where(low, first[:ROWS], pltpu.roll(first[ROWS : 2 * ROWS], HD, 1)),
        jnp.where(low, first[2 * ROWS :], second[:ROWS]),
        jnp.where(low, pltpu.roll(second[ROWS : 2 * ROWS], HD, 1), second[2 * ROWS :]),
    )


def visit_chunks(block, chunk):
    prompt_blocks = PROMPT // ROWS

    @pl.when(block >= prompt_blocks)
    def _():
        for c in range(PROMPT // (2 * ROWS)):
            chunk(c * 2 * ROWS, 2 * ROWS, False)

    @pl.when(block < prompt_blocks)
    def _():
        def step(c, carry):
            chunk(pl.multiple_of(c * ROWS, ROWS), ROWS, False)
            return carry

        lax.fori_loop(0, block, step, 0)

    @pl.when(block > prompt_blocks)
    def _():
        chunk(pl.multiple_of((block - 1) * ROWS, ROWS), ROWS, True)

    chunk(pl.multiple_of(block * ROWS, ROWS), ROWS, True)


def mask_bias(block, begin, size, start_ref):
    place = begin + lax.broadcasted_iota(jnp.int32, (size, ROWS), 0)
    own = block * ROWS + lax.broadcasted_iota(jnp.int32, (size, ROWS), 1)
    ok = (place <= own) & (place >= start_ref[0, :1, :])
    bias = jnp.where(ok, 0.0, -1e30)
    return jnp.concatenate([bias] * SHARE, axis=1)


def attend_kernel(blocks, q_ref, k_ref, v_ref, start_ref, o_ref, lse_ref, vt_ref, m_ref, l_ref, acc_ref):
    block = expert_rank() * blocks + pl.program_id(1)

    @pl.when(pl.program_id(1) == 0)
    def _():
        vt_ref[...] = jnp.transpose(v_ref[...].astype(f32)).astype(bf16)

    queries = stack_heads(q_ref)
    m_ref[...] = jnp.full_like(m_ref, -1e30)
    l_ref[...] = jnp.zeros_like(l_ref)
    acc_ref[...] = jnp.zeros_like(acc_ref)

    def chunk(begin, size, masked):
        keys = k_ref[pl.ds(begin, size), :]
        values = vt_ref[:, pl.ds(begin, size)]
        bias = mask_bias(block, begin, size, start_ref) if masked else None
        for h in range(2):
            scores = dot_nt(keys, queries[h])
            if masked:
                scores = scores + bias
            before = m_ref[h, :1]
            peak = jnp.maximum(before, jnp.max(scores, axis=0, keepdims=True))
            weight = jnp.exp(scores - peak)
            shrink = jnp.exp(before - peak)
            m_ref[h, :1] = peak
            l_ref[h, :1] = l_ref[h, :1] * shrink + jnp.sum(weight, axis=0, keepdims=True)
            acc_ref[h] = acc_ref[h] * shrink + dot(values, weight.astype(bf16))

    visit_chunks(block, chunk)
    mixed = [jnp.transpose(acc_ref[h] / l_ref[h, :1]) for h in range(2)]
    for c, part in enumerate(unstack_heads(*mixed)):
        o_ref[:, c * LANES : (c + 1) * LANES] = part.astype(bf16)
    for h in range(2):
        total = m_ref[h, :1] + jnp.log(l_ref[h, :1])
        lse_ref[0, 0, h] = jnp.broadcast_to(total, (8, STACK))


def attend(group, query, kv, start_row):
    length = query.shape[0]
    total = kv.shape[0]
    blocks = length // ROWS
    heads = pl.BlockSpec((ROWS, PAIR_Q), lambda p, i: (i, p))
    return call(
        functools.partial(attend_kernel, blocks),
        "attend",
        45,
        grid=(PAIRS, blocks),
        in_specs=[
            heads,
            pl.BlockSpec((total, LANES), lambda p, i: (0, p)),
            pl.BlockSpec((total, LANES), lambda p, i: (0, PAIRS + p)),
            pl.BlockSpec((1, 8, ROWS), lambda p, i: (group, 0, i)),
        ],
        out_specs=[
            heads,
            pl.BlockSpec((1, 1, 2, 8, STACK), lambda p, i: (p, i, 0, 0, 0)),
        ],
        out_shape=[
            shaped(query.shape, bf16),
            shaped((PAIRS, blocks, 2, 8, STACK), f32),
        ],
        scratch_shapes=[
            pltpu.VMEM((LANES, total), bf16),
            pltpu.VMEM((2, 8, STACK), f32),
            pltpu.VMEM((2, 8, STACK), f32),
            pltpu.VMEM((2, LANES, STACK), f32),
        ],
    )(query, kv, kv, start_row)


def attend_back_kernel(
    blocks,
    q_ref,
    g_ref,
    o_ref,
    k_ref,
    v_ref,
    lse_ref,
    start_ref,
    cos_ref,
    sin_ref,
    dq_ref,
    keep_ref,
    send_ref,
    dq_acc,
    dkv_acc,
):
    step = pl.program_id(1)
    block = expert_rank() * blocks + step

    @pl.when(step == 0)
    def _():
        dkv_acc[...] = jnp.zeros_like(dkv_acc)

    dq_acc[...] = jnp.zeros_like(dq_acc)
    queries = stack_heads(q_ref)
    grads = stack_heads(g_ref)
    halves = []
    for c in range(SHARE):
        cols = slice(c * LANES, (c + 1) * LANES)
        product = jnp.transpose(g_ref[:, cols].astype(f32) * o_ref[:, cols].astype(f32))
        halves.append(jnp.sum(product[:HD], axis=0, keepdims=True))
        halves.append(jnp.sum(product[HD:], axis=0, keepdims=True))
    inner = [jnp.concatenate(halves[:SHARE], axis=1), jnp.concatenate(halves[SHARE:], axis=1)]

    def chunk(begin, size, masked):
        keys = k_ref[pl.ds(begin, size), :]
        values = v_ref[pl.ds(begin, size), :]
        bias = mask_bias(block, begin, size, start_ref) if masked else None
        key_sum, value_sum = None, None
        for h in range(2):
            scores = dot_nt(keys, queries[h]) - lse_ref[0, 0, h, :1, :]
            if masked:
                scores = scores + bias
            probs = jnp.exp(scores)
            probs_grad = dot_nt(values, grads[h])
            scores_grad = (probs * (probs_grad - inner[h])).astype(bf16)
            value_part = dot(probs.astype(bf16), grads[h])
            key_part = dot(scores_grad, queries[h])
            key_sum = key_part if key_sum is None else key_sum + key_part
            value_sum = value_part if value_sum is None else value_sum + value_part
            dq_acc[h] += dot_tn(scores_grad, keys)
        dkv_acc[0, pl.ds(begin, size), :] += key_sum
        dkv_acc[1, pl.ds(begin, size), :] += value_sum

    visit_chunks(block, chunk)
    cosine, sine = cos_ref[...], sin_ref[...]
    for c, part in enumerate(unstack_heads(dq_acc[0], dq_acc[1])):
        part = part * 0.125
        turned = part * cosine - half_swap(part) * sine
        dq_ref[:, c * LANES : (c + 1) * LANES] = turned.astype(bf16)

    @pl.when(step == blocks - 1)
    def _():
        length = blocks * ROWS
        own = lax.axis_index("el")
        for chip in range(dkv_acc.shape[1] // (2 * length)):
            mine = pl.multiple_of((2 * chip + own) * length, length)
            other = pl.multiple_of((2 * chip + 1 - own) * length, length)
            for i in range(2):
                keep_ref[chip, i] = dkv_acc[i, pl.ds(mine, length), :].astype(bf16)
                send_ref[chip, i] = dkv_acc[i, pl.ds(other, length), :].astype(bf16)


def attend_back(group, span, query, grad, mixed, kv, lse, start_row, cosine, sine, kept):
    length = query.shape[0]
    total = kv.shape[0]
    blocks = length // ROWS
    first = group * blocks
    chips = total // (2 * length)
    base, pairs = span
    side = pl.BlockSpec((chips, 2, length, LANES), lambda p, i: (0, 0, 0, p))
    heads = pl.BlockSpec((ROWS, PAIR_Q), lambda p, i: (i, base + p))
    table = pl.BlockSpec((ROWS, LANES), lambda p, i: (first + i, 0))
    return call(
        lambda *refs: attend_back_kernel(blocks, *refs[:9], *refs[-5:]),
        "attend_back",
        16 * pairs,
        grid=(pairs, blocks),
        in_specs=[
            heads,
            heads,
            heads,
            pl.BlockSpec((total, LANES), lambda p, i: (0, base + p)),
            pl.BlockSpec((total, LANES), lambda p, i: (0, PAIRS + base + p)),
            pl.BlockSpec((1, 1, 2, 8, STACK), lambda p, i: (base + p, i, 0, 0, 0)),
            pl.BlockSpec((1, 8, ROWS), lambda p, i: (group, 0, i)),
            table,
            table,
        ]
        + [pl.BlockSpec(memory_space=pl.ANY)] * len(kept),
        out_specs=[
            heads,
            side,
            side,
        ],
        input_output_aliases={9: 0} if kept else {},
        out_shape=[
            shaped(query.shape, bf16),
            shaped((chips, 2, length, pairs * LANES), bf16),
            shaped((chips, 2, length, pairs * LANES), bf16),
        ],
        scratch_shapes=[
            pltpu.VMEM((2, STACK, LANES), f32),
            pltpu.VMEM((2, total, LANES), f32),
        ],
    )(query, grad, mixed, kv, kv, lse, start_row, cosine, sine, *kept)


def branch_kernel(a_ref, x_ref, wo_ref, gain_ref, wr_ref, m_ref, n_ref, ps_ref):
    middle = x_ref[...].astype(f32) + dot(a_ref[...], wo_ref[...])
    m_ref[...] = middle
    factor = lax.rsqrt(jnp.mean(middle * middle, axis=1, keepdims=True) + epsilon)
    normed = (middle * factor * gain_ref[...]).astype(bf16)
    n_ref[...] = normed
    add_up(ps_ref, fold_rows(router(normed, wr_ref[...])))


def branch(group, attended, x, wo, gain, wr):
    length = attended.shape[0]
    return call(
        branch_kernel,
        "branch",
        6,
        grid=(length // ROWS,),
        in_specs=[
            row_block(H * HD),
            row_block(D, group * length // ROWS),
            resident((H * HD, D)),
            resident((1, D)),
            resident((D, LANES)),
        ],
        out_specs=[row_block(D), row_block(D), pl.BlockSpec((8, LANES), lambda i: (0, 0))],
        out_shape=[
            shaped((length, D), f32),
            shaped((length, D), bf16),
            shaped((8, LANES), f32),
        ],
    )(attended, x, wo, gain, wr)


def router(normed, weight):
    count = EXP_DEV * 2 * lax.axis_size("eh")
    logits = dot(normed, weight)
    logits = jnp.where(lane_of(logits.shape) < count, logits, -1e30)
    powers = jnp.exp(logits - jnp.max(logits, axis=1, keepdims=True))
    return powers / jnp.sum(powers, axis=1, keepdims=True)


def experts_kernel(
    x_ref, c_ref, t_ref, wr_ref, wg_ref, wu_ref, wd_ref, *refs
):
    mix_ref, rows_ref, x_out, c_out, hid_ref, gate_ref, up_ref = refs[-7:]
    x, cot = x_ref[...], c_ref[...]
    x_out[...] = x
    c_out[...] = cot
    level = t_ref[0].astype(f32)
    picked = jnp.where(level > 0.5, router(x, wr_ref[...]), 0.0)
    share = picked / jnp.sum(picked, axis=1, keepdims=True)
    share = jnp.where(level > 1.5, share, 0.0)
    lane = lane_of(share.shape)
    base = EXP_DEV * expert_rank()
    share = pltpu.roll(share, lax.rem(LANES - base, LANES), 1)
    mix, rows = None, None
    gate_grads = jnp.zeros(share.shape, bf16)
    for e in range(EXP_DEV):
        gate = dot(x, wg_ref[e])
        up = dot(x, wu_ref[e])
        hidden_grad = dot(cot, wd_ref[e])
        sigmoid = jax.nn.sigmoid(gate)
        active = gate * sigmoid
        hidden = active * up
        inner = jnp.sum(hidden * hidden_grad, axis=1, keepdims=True)
        coarse = inner.astype(bf16)
        fine = (inner - coarse.astype(f32)).astype(bf16)
        gate_grads = jnp.where(lane == base + e, coarse, gate_grads)
        gate_grads = jnp.where(lane == LANES // 2 + base + e, fine, gate_grads)
        weight = share[:, e : e + 1]
        scaled = (hidden * weight).astype(bf16)
        hidden_grad = hidden_grad * weight
        up_grad = (hidden_grad * active).astype(bf16)
        gate_grad = (hidden_grad * up * sigmoid * (1.0 + gate * (1.0 - sigmoid))).astype(bf16)
        cols = slice(e * FF, (e + 1) * FF)
        hid_ref[:, cols] = scaled
        gate_ref[:, cols] = gate_grad
        up_ref[:, cols] = up_grad
    for e in range(EXP_DEV):
        cols = slice(e * FF, (e + 1) * FF)
        mix_part = dot_nt(hid_ref[:, cols], wd_ref[e])
        rows_part = dot_nt(gate_ref[:, cols], wg_ref[e]) + dot_nt(up_ref[:, cols], wu_ref[e])
        mix = mix_part if mix is None else mix + mix_part
        rows = rows_part if rows is None else rows + rows_part
    mix_ref[...] = mix.astype(bf16)
    rows_ref[:, :D] = rows.astype(bf16)
    rows_ref[:, D:] = gate_grads


def experts_pass(group, groups, x, cot, level, wr, wg, wu, wd, kept):
    count = x.shape[0]
    first = group * count // ROWS
    whole = groups * count
    side = pl.BlockSpec(memory_space=pl.ANY)
    widths = [D, D, EXP_DEV * FF, EXP_DEV * FF, EXP_DEV * FF]
    return call(
        experts_kernel,
        "experts",
        113,
        grid=(count // ROWS,),
        in_specs=[
            row_block(D),
            row_block(D),
            pl.BlockSpec((1, ROWS, LANES), lambda i: (group, i, 0)),
            resident((D, LANES)),
            resident((EXP_DEV, D, FF)),
            resident((EXP_DEV, D, FF)),
            resident((EXP_DEV, D, FF)),
        ]
        + [side] * len(kept),
        out_specs=[row_block(D), row_block(D + LANES)]
        + [row_block(width, first) for width in widths],
        out_shape=[
            shaped((count, D), bf16),
            shaped((count, D + LANES), bf16),
        ]
        + [shaped((whole, width), bf16) for width in widths],
        input_output_aliases={7 + i: 2 + i for i in range(len(kept))},
    )(x, cot, level, wr, wg, wu, wd, *kept)


def norm_back(grad, normed, factor, gain):
    scaled = grad * gain
    return factor * (scaled - normed * jnp.mean(scaled * normed, axis=1, keepdims=True))


def fold_rows(values):
    return jnp.sum(values.reshape(values.shape[0] // 8, 8, values.shape[1]), axis=0)


def add_up(ref, part):
    @pl.when(pl.program_id(0) == 0)
    def _():
        ref[...] = part

    @pl.when(pl.program_id(0) > 0)
    def _():
        ref[...] += part


def middle_kernel(
    r_ref, t_ref, m_ref, n_ref, c_ref, gain_ref, wr_ref, wo_ref,
    mg_ref, b_ref, ag_ref, l_ref, dg_ref,
):
    probs = router(n_ref[...], wr_ref[...])
    level = t_ref[0].astype(f32)
    sel = jnp.where(level > 0.5, 1.0, 0.0)
    gate_grad = r_ref[:, D:].astype(f32)
    gate_grad = gate_grad + pltpu.roll(gate_grad, LANES // 2, 1)
    gate_grad = jnp.where(level > 1.5, gate_grad, 0.0)
    picked = probs * sel
    total = jnp.sum(picked, axis=1, keepdims=True)
    share = picked / total
    inner = jnp.sum(gate_grad * share, axis=1, keepdims=True)
    probs_grad = (gate_grad - inner) / total * sel
    logits_grad = probs * (probs_grad - jnp.sum(probs_grad * probs, axis=1, keepdims=True))
    coarse = logits_grad.astype(bf16)
    fine = (logits_grad - coarse.astype(f32)).astype(bf16)
    l_ref[:, :LANES] = coarse
    l_ref[:, LANES:] = fine
    grad = r_ref[:, :D].astype(f32) + dot_nt(coarse, wr_ref[...]) + dot_nt(fine, wr_ref[...])
    middle = m_ref[...]
    factor = lax.rsqrt(jnp.mean(middle * middle, axis=1, keepdims=True) + epsilon)
    normed = middle * factor
    add_up(dg_ref, fold_rows(grad * normed))
    middle_grad = c_ref[...].astype(f32) + norm_back(grad, normed, factor, gain_ref[...])
    mg_ref[...] = middle_grad
    low = middle_grad.astype(bf16)
    b_ref[...] = low
    ag_ref[...] = dot_nt(low, wo_ref[...]).astype(bf16)


def middle_back(group, rows, level, middle, normed, cot, gain, wr, wo):
    length = rows.shape[0]
    first = group * length // ROWS
    corner = lambda width: pl.BlockSpec((8, width), lambda i: (0, 0))
    return call(
        middle_kernel,
        "middle_back",
        8,
        grid=(length // ROWS,),
        in_specs=[
            row_block(D + LANES),
            pl.BlockSpec((1, ROWS, LANES), lambda i: (group, i, 0)),
            row_block(D), row_block(D), row_block(D, first),
            resident((1, D)), resident((D, LANES)), resident((H * HD, D)),
        ],
        out_specs=[
            row_block(D), row_block(D), row_block(H * HD), row_block(2 * LANES),
            corner(D),
        ],
        out_shape=[
            shaped((length, D), f32),
            shaped((length, D), bf16),
            shaped((length, H * HD), bf16),
            shaped((length, 2 * LANES), bf16),
            shaped((8, D), f32),
        ],
    )(rows, level, middle, normed, cot, gain, wr, wo)


def input_kernel(
    dq_ref, dk_ref, dv_ref, x_ref, mg_ref, cos_ref, sin_ref, gain_ref, wq_ref, wk_ref, wv_ref,
    out_ref, dk_out, dg_ref,
):
    cosine, sine = cos_ref[...], sin_ref[...]
    for c in range(KVH * HD // LANES):
        part = dk_ref[0, :, c * LANES : (c + 1) * LANES].astype(f32)
        turned = part * cosine - half_swap(part) * sine
        dk_out[:, c * LANES : (c + 1) * LANES] = turned.astype(bf16)
    grad = dot_nt(dq_ref[...], wq_ref[...])
    grad = grad + dot_nt(dk_out[...], wk_ref[...])
    grad = grad + dot_nt(dv_ref[0], wv_ref[...])
    x = x_ref[...].astype(f32)
    factor = lax.rsqrt(jnp.mean(x * x, axis=1, keepdims=True) + epsilon)
    normed = x * factor
    add_up(dg_ref, fold_rows(grad * normed))
    out_ref[...] = mg_ref[...] + norm_back(grad, normed, factor, gain_ref[...])


def input_back(group, groups, dq, dkv, x, middle_grad, cosine, sine, gain, wq, wk, wv, kept):
    length = dq.shape[0]
    first = group * length // ROWS
    kernel = lambda *refs: input_kernel(*refs[:11], *refs[-3:])
    return call(
        kernel,
        "input_back",
        8,
        grid=(length // ROWS,),
        in_specs=[
            row_block(H * HD),
            pl.BlockSpec((1, ROWS, KVH * HD), lambda i: (0, i, 0)),
            pl.BlockSpec((1, ROWS, KVH * HD), lambda i: (1, i, 0)),
            row_block(D, first),
            row_block(D),
            row_block(LANES, first),
            row_block(LANES, first),
            resident((1, D)),
            resident((D, H * HD)),
            resident((D, KVH * HD)),
            resident((D, KVH * HD)),
        ]
        + [pl.BlockSpec(memory_space=pl.ANY)] * len(kept),
        out_specs=[
            row_block(D, first),
            row_block(KVH * HD),
            pl.BlockSpec((8, D), lambda i: (0, 0)),
        ],
        out_shape=[
            shaped((groups * length, D), f32),
            shaped((length, KVH * HD), bf16),
            shaped((8, D), f32),
        ],
        input_output_aliases={11: 0} if kept else {},
    )(dq, dkv, dkv, x, middle_grad, cosine, sine, gain, wq, wk, wv, *kept)


def transpose_into(turned, lefts):
    length = lefts[0].shape[0]
    for g, left in enumerate(lefts):
        for c in range(0, D, 2 * LANES):
            part = left[:, c : c + 2 * LANES].astype(f32)
            turned[c : c + 2 * LANES, g * length : (g + 1) * length] = jnp.transpose(part).astype(
                bf16
            )


def out_kernel(groups, *refs):
    lefts, rights = refs[:groups], refs[groups : 2 * groups]
    out_ref, turned = refs[-2:]
    length = lefts[0].shape[0]

    @pl.when(pl.program_id(0) == 0)
    def _():
        transpose_into(turned, lefts)

    total = None
    for g in range(groups):
        part = dot(turned[:, g * length : (g + 1) * length], rights[g][...])
        total = part if total is None else total + part
    out_ref[...] = total.astype(bf16)


def out_gradient(lefts, rights):
    groups, length = len(lefts), lefts[0].shape[0]
    width = 4 * LANES
    return call(
        functools.partial(out_kernel, groups),
        "out_grad",
        10,
        grid=(D // width,),
        in_specs=[resident((length, D))] * groups
        + [pl.BlockSpec((length, width), lambda i: (0, i))] * groups,
        out_specs=pl.BlockSpec((D, width), lambda i: (0, i)),
        out_shape=shaped((D, D), bf16),
        scratch_shapes=[pltpu.VMEM((D, groups * length), bf16)],
    )(*lefts, *rights)


def dense_kernel(groups, sizes, *refs):
    data, chips, shard, width, full, late = sizes
    lefts, queries, keys, values = (refs[i * groups : (i + 1) * groups] for i in range(4))
    narrow_ref, late_ref, out_ref = refs[4 * groups : 4 * groups + 3]
    (turned, keep1, send1, got1, keep2, send2, got2, sum2, got3, sum3, got4, sum4, near5, far5,
     wide2, wide3, keep6, send6, got6) = refs[4 * groups + 3 : 4 * groups + 22]
    sems = refs[4 * groups + 22 :]
    half = width // 2
    length = lefts[0].shape[0]
    ranks = 2 * chips
    dh, dl, eh, el = (lax.axis_index(name) for name in ("dh", "dl", "eh", "el"))

    def near(hop, core):
        return {"eh": lax.rem(eh + hop, chips), "el": core}

    peers = [{"el": 1 - el}, {"dl": 1 - dl}]
    for hop in range(1, chips):
        peers.append(near(hop, el))
    for hop in range(1, data):
        peers.append({"dh": lax.rem(dh + hop, data)})
    barrier = pltpu.get_barrier_semaphore()
    for peer in peers:
        pl.semaphore_signal(barrier, inc=1, device_id=peer, device_id_type=pl.DeviceIdType.MESH)
    transpose_into(turned, lefts)
    pl.semaphore_wait(barrier, len(peers))

    def copy(source, target, phase, k, lane, peer):
        return pltpu.make_async_remote_copy(
            src_ref=source,
            dst_ref=target,
            send_sem=sems[2 * phase].at[k, lane],
            recv_sem=sems[2 * phase + 1].at[k, lane],
            device_id=peer,
            device_id_type=pl.DeviceIdType.MESH,
        )

    def crossed(k):
        return k < full and k % 2 == 1

    def slot(k):
        return k // 2 if k < full else (full + 1) // 2 + k - full

    def copies(phase, k):
        if phase == 0:
            return [copy(send1.at[k], got1.at[k], 0, k, 0, {"el": 1 - el})]
        if phase == 1:
            source, target = (send6, got6) if crossed(k) else (send2, got2)
            at = k // 2
            return [
                copy(source.at[at, hop - 1], target.at[at, hop - 1], 1, k, hop - 1, near(hop, el))
                for hop in range(1, chips)
            ]
        if phase == 2:
            if crossed(k):
                at = k // 2
                return [copy(wide2.at[at, 1 - dl], wide3.at[at], 2, k, 0, {"dl": 1 - dl})]
            at = slot(k)
            return [copy(sum2.at[at, 1 - dl], got3.at[at], 2, k, 0, {"dl": 1 - dl})]
        if phase == 3:
            found = []
            for hop in range(1, data):
                away = lax.rem(dh + hop, data)
                found.append(
                    copy(sum3.at[k, away], got4.at[k, hop - 1], 3, k, hop - 1, {"dh": away})
                )
            return found
        if phase == 4:
            return [
                copy(sum4.at[k], near5.at[k, eh], 4, k, hop - 1, near(hop, el))
                for hop in range(1, chips)
            ]
        return [copy(near5.at[k], far5.at[k], 5, k, 0, {"el": 1 - el})]

    def start(phase, k):
        for one in copies(phase, k):
            one.start()

    def arrived(phase, k):
        for one in copies(phase, k):
            one.wait_recv()

    def finish_shard(k):
        base = k * width if k < full else full * width + (k - full) * LANES

        def put(side, chip, block):
            place = side * chips + chip
            place = place * LANES if k < full else place * late * LANES
            at = pl.multiple_of(base + place, LANES)
            out_ref[:, pl.ds(at, LANES)] = block.astype(f32)

        for chip in range(chips):
            put(el, chip, near5[k, chip])
            put(1 - el, chip, far5[k, chip])

    def piece(column):
        size = KVH * HD
        if column >= H * HD + 2 * size:
            if column > H * HD + 2 * size:
                return jnp.zeros((D, size), bf16)
            part = jnp.transpose(narrow_ref[...])
            return jnp.concatenate([part, jnp.zeros((D, size - LANES), f32)], axis=1).astype(bf16)
        total = None
        for g in range(groups):
            if column < H * HD:
                block = queries[g][:, column : column + size]
            elif column < H * HD + size:
                block = keys[g][...]
            else:
                block = values[g][1]
            one = dot(turned[:, g * length : (g + 1) * length], block)
            total = one if total is None else total + one
        return total.astype(bf16)

    def stage_compute(k):
        if k < full:
            part = [piece(k * width + c) for c in range(0, width, KVH * HD)]
            part = part[0] if len(part) == 1 else jnp.concatenate(part, axis=1)

            @pl.when(el == 0)
            def _():
                keep1[k] = part[:, :half]
                send1[k] = part[:, half:]

            @pl.when(el == 1)
            def _():
                keep1[k] = part[:, half:]
                send1[k] = part[:, :half]

            start(0, k)

    def hand_out(block, chip, keep, send):
        hop = lax.rem(chip + chips - eh, chips)

        @pl.when(hop == 0)
        def _():
            keep[...] = block

        @pl.when(hop > 0)
        def _():
            send[hop - 1] = block

    def chip_columns(chip):
        return slice(chip * LANES, (chip + 1) * LANES)

    def stage_core(k):
        arrived(0, k)
        met = (keep1[k].astype(f32) + got1[k].astype(f32)).astype(bf16)
        at = k // 2
        if crossed(k):
            for far in range(data):
                for side in range(2):
                    first = (2 * far + side) * shard
                    wide2[at, side, far] = met[first : first + shard]
            start(2, k)
        else:
            for chip in range(chips):
                hand_out(met[:, chip_columns(chip)], chip, keep2.at[at], send2.at[at])
            start(1, k)

    def stage_second(k):
        at = k // 2
        if crossed(k):
            arrived(2, k)
            met = (wide2[at, dl].astype(f32) + wide3[at].astype(f32)).astype(bf16)
            for chip in range(chips):
                hand_out(met[:, :, chip_columns(chip)], chip, keep6.at[at], send6.at[at])
            start(1, k)
        else:
            arrived(1, k)
            total = keep2[at].astype(f32)
            for hop in range(1, chips):
                total = total + got2[at, hop - 1].astype(f32)
            spread(k, total.astype(bf16))

    def spread(k, total):
        for far in range(data):
            for side in range(2):
                first = (2 * far + side) * shard
                sum2[slot(k), side, far] = total[first : first + shard]
        start(2, k)

    def stage_third(k):
        if crossed(k):
            at = k // 2
            arrived(1, k)
            total = keep6[at].astype(f32)
            for hop in range(1, chips):
                total = total + got6[at, hop - 1].astype(f32)
        else:
            at = slot(k)
            arrived(2, k)
            total = sum2[at, dl].astype(f32) + got3[at].astype(f32)
        sum3[k] = total.astype(bf16)
        start(3, k)

    def stage_far(k):
        arrived(3, k)
        total = sum3[k, dh].astype(f32)
        for hop in range(1, data):
            total = total + got4[k, hop - 1].astype(f32)
        total = total.astype(bf16)
        sum4[k] = total
        near5[k, eh] = total
        start(4, k)

    def stage_gather(k):
        arrived(4, k)
        start(5, k)

    def stage_last(k):
        arrived(5, k)
        finish_shard(k)

    everything = list(range(full, full + late)) + list(range(full))
    for k in range(full, full + late):
        first = (k - full) * LANES
        spread(k, late_ref[:, first : first + LANES])
    stages = (
        stage_compute,
        stage_core,
        stage_second,
        stage_third,
        stage_far,
        stage_gather,
        stage_last,
    )
    for step in range(full + len(stages) - 1):
        for delay, stage in enumerate(stages):
            if 0 <= step - delay < full:
                stage(step - delay)
        if step < 4:
            for k in range(full, full + late):
                stages[3 + step](k)
    for k in everything:
        for phase in range(6):
            if k < full or phase > 1:
                for one in copies(phase, k):
                    one.wait_send()


def dense_gradient(lefts, queries, keys, values, narrow, late_part):
    groups = len(lefts)
    data, chips = lax.axis_size("dh"), lax.axis_size("eh")
    shard = D // (2 * data)
    width = 2 * chips * LANES
    columns = H * HD + 2 * KVH * HD
    full = -(-(columns + LANES) // width)
    late = late_part.shape[1] // LANES
    total = full + late
    half, ranks = width // 2, 2 * chips
    sizes = (data, chips, shard, width, full, late)
    lanes = [1, chips - 1, 1, data - 1, chips - 1, 1]
    even, odd = (full + 1) // 2, full // 2
    sems = []
    for count in lanes:
        sems += [pltpu.SemaphoreType.DMA((total, count))] * 2
    operands = [*lefts, *queries, *keys, *values, narrow, late_part]
    whole = pl.BlockSpec(memory_space=pltpu.VMEM)
    return pl.pallas_call(
        functools.partial(dense_kernel, groups, sizes),
        name="dense_grad",
        in_specs=[whole] * len(operands),
        out_specs=whole,
        out_shape=shaped((shard, full * width + late * ranks * LANES), f32),
        scratch_shapes=[
            pltpu.VMEM((D, groups * lefts[0].shape[0]), bf16),
            pltpu.VMEM((full, D, half), bf16),
            pltpu.VMEM((full, D, half), bf16),
            pltpu.VMEM((full, D, half), bf16),
            pltpu.VMEM((even, D, LANES), bf16),
            pltpu.VMEM((even, chips - 1, D, LANES), bf16),
            pltpu.VMEM((even, chips - 1, D, LANES), bf16),
            pltpu.VMEM((even + late, 2, data, shard, LANES), bf16),
            pltpu.VMEM((even + late, data, shard, LANES), bf16),
            pltpu.VMEM((total, data, shard, LANES), bf16),
            pltpu.VMEM((total, data - 1, shard, LANES), bf16),
            pltpu.VMEM((total, shard, LANES), bf16),
            pltpu.VMEM((total, chips, shard, LANES), bf16),
            pltpu.VMEM((total, chips, shard, LANES), bf16),
            pltpu.VMEM((odd, 2, data, shard, half), bf16),
            pltpu.VMEM((odd, data, shard, half), bf16),
            pltpu.VMEM((odd, data, shard, LANES), bf16),
            pltpu.VMEM((odd, chips - 1, data, shard, LANES), bf16),
            pltpu.VMEM((odd, chips - 1, data, shard, LANES), bf16),
        ]
        + sems,
        cost_estimate=pl.CostEstimate(
            flops=int(80 * 9e8), bytes_accessed=0, transcendentals=0
        ),
        compiler_params=pltpu.CompilerParams(
            vmem_limit_bytes=VMEM_LIMIT, collective_id=0, has_side_effects=True
        ),
    )(*operands)


def widen(values):
    return jnp.pad(values, ((0, 0), (0, LANES - values.shape[1])))


def swap(values, axis):
    return lax.ppermute(values, axis, [(0, 1), (1, 0)])


def pick(values, index):
    return lax.dynamic_index_in_dim(values, index, 1, keepdims=False)


def pair_parts(values, shard):
    parts = values.reshape(-1, 2, shard, values.shape[1])
    own = lax.axis_index("dl")
    return pick(parts, own), swap(pick(parts, 1 - own), "dl")


def far_sum(own, met):
    met = (own + met).reshape(-1, own.shape[2])
    return lax.psum_scatter(met, "dh", scatter_dimension=0, tiled=True)


def take(values, axis, index):
    return lax.dynamic_index_in_dim(values, index, axis, keepdims=False)


def chip_sum(met):
    chips = lax.axis_size("eh")
    chip = lax.axis_index("eh")
    total = take(met, 0, chip)
    for hop in range(1, chips):
        order = [(i, (i + hop) % chips) for i in range(chips)]
        away = take(met, 0, lax.rem(chip + hop, chips))
        total = total + lax.ppermute(away, "eh", order)
    return total


def cut(array, index, size):
    return lax.dynamic_slice_in_dim(array, index * size, size, 1)


def column_core_sum(values):
    half = values.shape[1] // 2
    own = lax.axis_index("el")
    return cut(values, own, half) + swap(cut(values, 1 - own, half), "el")


def column_chip_sum(met):
    chips, chip = lax.axis_size("eh"), lax.axis_index("eh")
    size = met.shape[1] // chips
    total = cut(met, chip, size)
    for hop in range(1, chips):
        order = [(i, (i + hop) % chips) for i in range(chips)]
        away = cut(met, lax.rem(chip + hop, chips), size)
        total = total + lax.ppermute(away, "eh", order)
    return total


def sum_steps():
    for axis in ("el", "eh", "dl", "dh"):
        count = lax.axis_size(axis)
        hop = 1
        while hop < count:
            order = [(i, i ^ hop) for i in range(count)]
            yield lambda v, axis=axis, order=order: v + lax.ppermute(v, axis, order)
            hop *= 2


def together(*values):
    return lax.optimization_barrier(values)


def on_device(
    tokens,
    segments,
    routes,
    cotangent,
    attention_gain,
    query_weight,
    key_weight,
    value_weight,
    out_weight,
    mixture_gain,
    router_weight,
    gate_weight,
    up_weight,
    down_weight,
):
    groups, length, _ = tokens.shape
    each = range(groups)
    rows = groups * length
    ranks = lax.axis_size("eh") * 2
    dp_ranks = lax.axis_size("dh") * 2
    rank = expert_rank()
    experts = EXP_DEV * ranks
    capacity = (rows * TOPK * 5 // (4 * experts) + 7) // 8 * 8
    all_tokens = rows * dp_ranks * ranks
    first_row = rank * length
    shard = D // dp_ranks

    seg_full = jnp.concatenate([jnp.full((groups, PROMPT), -1, jnp.int32), segments], axis=1)
    seg_own = lax.dynamic_slice_in_dim(seg_full, first_row, length, 1)
    earlier = jnp.sum((segments[:, None, :] < seg_own[:, :, None]).astype(jnp.int32), axis=2)
    position = first_row + jnp.arange(length, dtype=jnp.int32)[None, :]
    place = position - earlier
    start = jnp.where(position >= PROMPT, PROMPT + earlier, 0)
    half = HD // 2
    lane = jnp.arange(LANES, dtype=jnp.int32)
    frequency = jnp.exp(-math.log(rope_base) * (lane % half).astype(f32) / half)
    angles = place.astype(f32).reshape(rows, 1) * frequency
    cosine = jnp.cos(angles)
    sine = jnp.sin(angles) * jnp.where(lane % HD < half, -1.0, 1.0)
    start_row = jnp.broadcast_to(start[:, None, :], (groups, 8, length))

    names = jnp.concatenate([routes[g] for g in each], axis=1).astype(bf16)
    names = widen(names)
    cot_rows = cotangent.reshape(rows, D)
    cot_all = [lax.all_gather(cotangent[g], EXPERT, axis=0, tiled=True) for g in each]

    x = tokens.reshape(rows, D)
    gain_a = attention_gain.reshape(1, D)
    gain_b = mixture_gain.reshape(1, D)
    router_wide = widen(router_weight)
    normed, query, kv = [None] * groups, [None] * groups, [None] * groups
    for g in each:
        normed[g], kv_own = key_value(
            g, length, x, gain_a, key_weight, value_weight, cosine, sine, names
        )
        kv[g] = lax.all_gather(kv_own, EXPERT, axis=0, tiled=True)
    for g in each:
        query[g] = project_query(g, normed[g], query_weight, cosine, sine)
    level = naming(kv[groups - 1], capacity, groups, ranks)
    level_own = lax.dynamic_slice_in_dim(level, first_row, length, 1)
    kv[0], query = together(kv[0], query)
    attended, lse = [None] * groups, [None] * groups
    middle, hidden_low, hidden_all = [None] * groups, [None] * groups, [None] * groups
    probs_local = 0.0
    for g in each:
        attended[g], lse[g] = attend(g, query[g], kv[g], start_row)
        if g == groups - 1:
            attended[g], cot_all[0] = together(attended[g], cot_all[0])
        middle[g], hidden_low[g], probs_part = branch(
            g, attended[g], x, out_weight, gain_b, router_wide
        )
        probs_local += jnp.sum(probs_part, axis=0)
        hidden_all[g] = lax.all_gather(hidden_low[g], EXPERT, axis=0, tiled=True)

    counts = jnp.sum((level_own > 0.5).astype(f32), axis=(0, 1))
    stats = jnp.stack([counts, probs_local])[:, :experts]
    steps = sum_steps()

    def beside(value, stats):
        step = next(steps, None)
        return (value, stats) if step is None else together(value, step(stats))

    kept, rows_back, mixture = [], [], []
    for g in each:
        if g > 0:
            kept[0], cot_all[g] = together(kept[0], cot_all[g])
            hidden_all[g], stats = beside(hidden_all[g], stats)
        mix, rows_grad, *kept = experts_pass(
            g, groups, hidden_all[g], cot_all[g], level, router_wide,
            gate_weight, up_weight, down_weight, kept,
        )
        rows_back.append(lax.psum_scatter(rows_grad, EXPERT, scatter_dimension=0, tiled=True))
        mixture.append(lax.psum_scatter(mix, EXPERT, scatter_dimension=0, tiled=True))
    x_all, cot_both, hidden, gate_back, up_back = kept
    hidden, mixture[0] = together(hidden, mixture[0])
    hidden, stats = beside(hidden, stats)
    down_local = dot_tn(cot_both, hidden).astype(bf16)
    x_all, down_local = together(x_all, down_local)
    gate_back, stats = beside(gate_back, stats)
    gate_local = dot_tn(x_all, gate_back).astype(bf16)
    up_back, gate_local = together(up_back, gate_local)
    gate_own, gate_met = pair_parts(gate_local, shard)
    up_back, stats = beside(up_back, stats)
    up_local = dot_tn(x_all, up_back).astype(bf16)
    rows_back[0], up_local = together(rows_back[0], up_local)
    rows_back[0], stats = beside(rows_back[0], stats)
    for step in steps:
        stats = step(stats)
    expert_load = stats[0] * experts / (all_tokens * TOPK)
    prob_mean = stats[1] * experts / all_tokens
    balance_loss = jnp.sum(expert_load * prob_mean) / experts

    def by_expert(part):
        return jnp.stack([part[:, e * FF : (e + 1) * FF] for e in range(EXP_DEV)]).astype(f32)

    middle_grad, branch_grad, attended_grad, logits_grad, dq, dkv = (
        [None] * groups for _ in range(6)
    )
    gain_b_local, last = 0.0, groups - 1
    down_far = lax.psum_scatter(down_local, "dh", scatter_dimension=0, tiled=True)
    for g in each:
        middle_grad[g], branch_grad[g], attended_grad[g], logits_grad[g], gain_part = middle_back(
            g, rows_back[g], level_own, middle[g], hidden_low[g], cot_rows,
            gain_b, router_wide, out_weight,
        )
        gain_b_local += jnp.sum(gain_part, axis=0)
    out_local = out_gradient(attended, branch_grad)
    fill = -D % (ranks * LANES)
    out_local = jnp.pad(out_local, ((0, 0), (0, fill)))
    out_local, up_local = together(out_local, up_local)
    up_own, up_met = pair_parts(up_local, shard)
    attended_grad[0], out_local, mixture[last] = together(
        attended_grad[0], out_local, mixture[last]
    )
    out_met = column_core_sum(out_local)
    for g in each:
        pieces, kept = [], []
        spans = [(0, PAIRS)] if g < last else [(0, PAIRS // 2), (PAIRS // 2, PAIRS // 2)]
        for at, span in enumerate(spans):
            if g == last and at == 0:
                dq[0], gate_own = together(dq[0], gate_own)
                attended_grad[g], out_met, dq[0], gate_own, gate_met, down_far = together(
                    attended_grad[g], out_met, dq[0], gate_own, gate_met, down_far
                )
                gate_part = far_sum(gate_own, gate_met)
                out_part = column_chip_sum(out_met)
            if g == last and at == 1:
                kept, dkv[0], pieces[0] = together(kept, dkv[0], pieces[0])
            grad, keep_part, send_part = attend_back(
                g, span, query[g], attended_grad[g], attended[g], kv[g], lse[g], start_row,
                cosine, sine, kept,
            )
            kept = [grad]
            if g == last and at == 1:
                keep_part, dq[0], down_far, up_own = together(keep_part, dq[0], down_far, up_own)
                up_part = far_sum(up_own, up_met)
                down_own, down_met = pair_parts(down_far, shard)
                down_part = (down_own + down_met)[0]
            pieces.append(keep_part + swap(send_part, "el"))
        dq[g] = kept[0]
        pieces = [chip_sum(piece) for piece in pieces]
        dkv[g] = pieces[0] if len(pieces) == 1 else jnp.concatenate(pieces, axis=2)
    output = jnp.stack(
        [(middle[g] + mixture[g].astype(f32)).astype(bf16) for g in each]
    )

    kept, turned_dk, gain_a_local = [], [None] * groups, 0.0
    for g in each:
        input_grad, turned_dk[g], gain_part = input_back(
            g, groups, dq[g], dkv[g], x, middle_grad[g], cosine, sine,
            gain_a, query_weight, key_weight, value_weight, kept,
        )
        kept = [input_grad]
        gain_a_local += jnp.sum(gain_part, axis=0)
    router_parts = sum(dot_tn(logits_grad[g], hidden_low[g]) for g in each)
    router_local = (router_parts[:LANES] + router_parts[LANES:])[:experts]
    narrow = jnp.concatenate(
        [
            router_local,
            gain_a_local[None, :],
            gain_b_local[None, :],
            jnp.zeros((LANES - experts - 2, D), f32),
        ],
        axis=0,
    )
    dense = dense_gradient(normed, dq, turned_dk, dkv, narrow, out_part)
    first = dense.shape[1] - D - fill
    out_grad = dense[:, first : first + D]
    down_weight_grad, gate_weight_grad, up_weight_grad = (
        by_expert(part) for part in (down_part, gate_part, up_part)
    )
    spans = [H * HD, KVH * HD, KVH * HD, experts, 1, 1]
    pieces, begin = [], 0
    for span in spans:
        pieces.append(dense[:, begin : begin + span])
        begin += span
    query_grad, key_grad, value_grad, router_grad, gain_a_grad, gain_b_grad = pieces
    return (
        output,
        input_grad.reshape(groups, length, D),
        gain_a_grad[:, 0],
        query_grad,
        key_grad,
        value_grad,
        out_grad,
        gain_b_grad[:, 0],
        router_grad,
        gate_weight_grad,
        up_weight_grad,
        down_weight_grad,
        expert_load,
        prob_mean,
        balance_loss,
    )


def solution(mesh):
    dp_ranks, ranks = mesh.devices.shape
    fine = Mesh(
        mesh.devices.reshape(dp_ranks // 2, 2, ranks // 2, 2), ("dh", "dl", "eh", "el")
    )
    return jax.shard_map(
        on_device,
        mesh=fine,
        in_specs=(
            P(DATA, EXPERT, None),
            P(DATA, None),
            P(DATA, EXPERT, None),
            P(DATA, EXPERT, None),
            P(),
            P(),
            P(),
            P(),
            P(),
            P(),
            P(),
            P(EXPERT, None, None),
            P(EXPERT, None, None),
            P(EXPERT, None, None),
        ),
        out_specs=(
            P(DATA, EXPERT, None),
            P(DATA, EXPERT, None),
            P(DATA),
            P(DATA, None),
            P(DATA, None),
            P(DATA, None),
            P(DATA, None),
            P(DATA),
            P(DATA, None),
            P(EXPERT, DATA, None),
            P(EXPERT, DATA, None),
            P(EXPERT, DATA, None),
            P(),
            P(),
            P(),
        ),
        check_vma=False,
    )
```

```python
import functools
import math

import jax
import jax.numpy as jnp
from jax import lax
from jax.experimental import pallas as pl
from jax.experimental.pallas import tpu as pltpu
from jax.sharding import Mesh
from jax.sharding import PartitionSpec as P

D = 1536
H = 24
KVH = 8
HD = 64
FF = 512
TOPK = 8
EXP_DEV = 5
PROMPT = 1024
LANES = 128
PAIRS = KVH // 2
SHARE = H // KVH
PAIR_Q = 2 * SHARE * HD
ROWS = 256
STACK = SHARE * ROWS
EXPERT = ("eh", "el")
DATA = ("dh", "dl")
VMEM_LIMIT = 63 * 1024 * 1024

epsilon = 1e-05
rope_base = 10000.0
f32 = jnp.float32
bf16 = jnp.bfloat16


def dot(a, b):
    return lax.dot_general(a, b, (((1,), (0,)), ((), ())), preferred_element_type=f32)


def dot_nt(a, b):
    return lax.dot_general(a, b, (((1,), (1,)), ((), ())), preferred_element_type=f32)


def dot_tn(a, b):
    return lax.dot_general(a, b, (((0,), (0,)), ((), ())), preferred_element_type=f32)


def expert_rank():
    return lax.axis_index("eh") * 2 + lax.axis_index("el")


def call(kernel, name, micros, extra=None, **more):
    cost = pl.CostEstimate(flops=int(micros * 2.5e8), bytes_accessed=0, transcendentals=0)
    return pl.pallas_call(
        kernel,
        name=name,
        cost_estimate=cost,
        compiler_params=pltpu.CompilerParams(vmem_limit_bytes=VMEM_LIMIT, **(extra or {})),
        **more,
    )


def shaped(shape, dtype):
    return jax.ShapeDtypeStruct(shape, dtype)


def lane_of(shape):
    return lax.broadcasted_iota(jnp.int32, shape, len(shape) - 1)


def half_swap(values):
    lower = lane_of(values.shape) % HD < HD // 2
    return jnp.where(
        lower, pltpu.roll(values, LANES - HD // 2, 1), pltpu.roll(values, HD // 2, 1)
    )


def resident(shape):
    zeros = (0,) * len(shape)
    return pl.BlockSpec(shape, lambda *_: zeros, pipeline_mode=pl.Buffered(1))


def row_block(width, first=0):
    return pl.BlockSpec((ROWS, width), lambda i: (first + i, 0))


def naming_kernel(capacity, groups, r_ref, o_ref):
    length = r_ref.shape[0]
    rows = groups * length
    lane = lane_of((rows, LANES))
    packed = r_ref[...].astype(jnp.int32)
    chosen = jnp.concatenate(
        [packed[:, g * TOPK : (g + 1) * TOPK] for g in range(groups)], axis=0
    )
    named = jnp.zeros((rows, LANES), f32)
    for k in range(TOPK):
        named = jnp.where(chosen[:, k : k + 1] == lane, 1.0, named)
    earlier = lax.broadcasted_iota(jnp.int32, (rows, rows), 1) < lax.broadcasted_iota(
        jnp.int32, (rows, rows), 0
    )
    slot = dot(jnp.where(earlier, 1.0, 0.0).astype(bf16), named.astype(bf16))
    level = named * jnp.where(slot < capacity, 2.0, 1.0)
    o_ref[...] = level.reshape(groups, length, LANES).astype(bf16)


def naming(kv, capacity, groups, ranks):
    total = kv.shape[0]
    length = total // ranks
    return call(
        functools.partial(naming_kernel, capacity, groups),
        "naming",
        9,
        grid=(ranks,),
        in_specs=[pl.BlockSpec((length, LANES), lambda s: (s, 2 * PAIRS))],
        out_specs=pl.BlockSpec((groups, length, LANES), lambda s: (0, s, 0)),
        out_shape=shaped((groups, total, LANES), bf16),
    )(kv)


def key_value_kernel(x_ref, gain_ref, wk_ref, wv_ref, cos_ref, sin_ref, r_ref, n_ref, kv_ref):
    x = x_ref[...].astype(f32)
    factor = lax.rsqrt(jnp.mean(x * x, axis=1, keepdims=True) + epsilon)
    normed = (x * factor * gain_ref[...]).astype(bf16)
    n_ref[...] = normed
    cosine, sine = cos_ref[...], sin_ref[...]
    key = dot(normed, wk_ref[...])
    for c in range(KVH * HD // LANES):
        part = key[:, c * LANES : (c + 1) * LANES]
        turned = part * cosine + half_swap(part) * sine
        kv_ref[:, c * LANES : (c + 1) * LANES] = turned.astype(bf16)
    kv_ref[:, KVH * HD : 2 * KVH * HD] = dot(normed, wv_ref[...]).astype(bf16)
    kv_ref[:, 2 * KVH * HD :] = r_ref[...]


def key_value(group, length, x, gain, wk, wv, cosine, sine, names):
    first = group * length // ROWS
    width = 2 * KVH * HD + LANES
    return call(
        key_value_kernel,
        "key_value",
        5,
        grid=(length // ROWS,),
        in_specs=[
            row_block(D, first),
            resident((1, D)),
            resident((D, KVH * HD)),
            resident((D, KVH * HD)),
            row_block(LANES, first),
            row_block(LANES, first),
            row_block(LANES),
        ],
        out_specs=[row_block(D), row_block(width)],
        out_shape=[shaped((length, D), bf16), shaped((length, width), bf16)],
    )(x, gain, wk, wv, cosine, sine, names)


def query_kernel(n_ref, wq_ref, cos_ref, sin_ref, q_ref):
    cosine, sine = cos_ref[...], sin_ref[...]
    query = dot(n_ref[...], wq_ref[...])
    for c in range(H * HD // LANES):
        part = query[:, c * LANES : (c + 1) * LANES]
        turned = part * cosine + half_swap(part) * sine
        q_ref[:, c * LANES : (c + 1) * LANES] = turned.astype(bf16) * jnp.asarray(0.125, bf16)


def project_query(group, normed, wq, cosine, sine):
    length = normed.shape[0]
    first = group * length // ROWS
    return call(
        query_kernel,
        "query",
        6,
        grid=(length // ROWS,),
        in_specs=[
            row_block(D),
            resident((D, H * HD)),
            row_block(LANES, first),
            row_block(LANES, first),
        ],
        out_specs=row_block(H * HD),
        out_shape=shaped((length, H * HD), bf16),
    )(normed, wq, cosine, sine)


def stack_heads(ref):
    low = lane_of((ROWS, LANES)) < HD
    parts = [ref[:, c * LANES : (c + 1) * LANES].astype(f32) for c in range(SHARE)]
    rolled0, rolled2 = pltpu.roll(parts[0], HD, 1), pltpu.roll(parts[2], HD, 1)
    zero = jnp.zeros((ROWS, LANES), f32)
    first = [parts[0], rolled0, parts[1]]
    second = [parts[1], rolled2, parts[2]]
    return (
        jnp.concatenate([jnp.where(low, v, zero).astype(bf16) for v in first], axis=0),
        jnp.concatenate([jnp.where(low, zero, v).astype(bf16) for v in second], axis=0),
    )


def unstack_heads(first, second):
    low = lane_of((ROWS, LANES)) < HD
    return (
        jnp.where(low, first[:ROWS], pltpu.roll(first[ROWS : 2 * ROWS], HD, 1)),
        jnp.where(low, first[2 * ROWS :], second[:ROWS]),
        jnp.where(low, pltpu.roll(second[ROWS : 2 * ROWS], HD, 1), second[2 * ROWS :]),
    )


def visit_chunks(block, chunk):
    prompt_blocks = PROMPT // ROWS

    @pl.when(block >= prompt_blocks)
    def _():
        for c in range(PROMPT // (2 * ROWS)):
            chunk(c * 2 * ROWS, 2 * ROWS, False)

    @pl.when(block < prompt_blocks)
    def _():
        def step(c, carry):
            chunk(pl.multiple_of(c * ROWS, ROWS), ROWS, False)
            return carry

        lax.fori_loop(0, block, step, 0)

    @pl.when(block > prompt_blocks)
    def _():
        chunk(pl.multiple_of((block - 1) * ROWS, ROWS), ROWS, True)

    chunk(pl.multiple_of(block * ROWS, ROWS), ROWS, True)


def mask_bias(block, begin, size, start_ref):
    place = begin + lax.broadcasted_iota(jnp.int32, (size, ROWS), 0)
    own = block * ROWS + lax.broadcasted_iota(jnp.int32, (size, ROWS), 1)
    ok = (place <= own) & (place >= start_ref[0, :1, :])
    bias = jnp.where(ok, 0.0, -1e30)
    return jnp.concatenate([bias] * SHARE, axis=1)


def attend_kernel(blocks, q_ref, k_ref, v_ref, start_ref, o_ref, lse_ref, vt_ref, m_ref, l_ref, acc_ref):
    block = expert_rank() * blocks + pl.program_id(1)

    @pl.when(pl.program_id(1) == 0)
    def _():
        vt_ref[...] = jnp.transpose(v_ref[...].astype(f32)).astype(bf16)

    queries = stack_heads(q_ref)
    m_ref[...] = jnp.full_like(m_ref, -1e30)
    l_ref[...] = jnp.zeros_like(l_ref)
    acc_ref[...] = jnp.zeros_like(acc_ref)

    def chunk(begin, size, masked):
        keys = k_ref[pl.ds(begin, size), :]
        values = vt_ref[:, pl.ds(begin, size)]
        bias = mask_bias(block, begin, size, start_ref) if masked else None
        for h in range(2):
            scores = dot_nt(keys, queries[h])
            if masked:
                scores = scores + bias
            before = m_ref[h, :1]
            peak = jnp.maximum(before, jnp.max(scores, axis=0, keepdims=True))
            weight = jnp.exp(scores - peak)
            shrink = jnp.exp(before - peak)
            m_ref[h, :1] = peak
            l_ref[h, :1] = l_ref[h, :1] * shrink + jnp.sum(weight, axis=0, keepdims=True)
            acc_ref[h] = acc_ref[h] * shrink + dot(values, weight.astype(bf16))

    visit_chunks(block, chunk)
    mixed = [jnp.transpose(acc_ref[h] / l_ref[h, :1]) for h in range(2)]
    for c, part in enumerate(unstack_heads(*mixed)):
        o_ref[:, c * LANES : (c + 1) * LANES] = part.astype(bf16)
    for h in range(2):
        total = m_ref[h, :1] + jnp.log(l_ref[h, :1])
        lse_ref[0, 0, h] = jnp.broadcast_to(total, (8, STACK))


def attend(group, query, kv, start_row):
    length = query.shape[0]
    total = kv.shape[0]
    blocks = length // ROWS
    heads = pl.BlockSpec((ROWS, PAIR_Q), lambda p, i: (i, p))
    return call(
        functools.partial(attend_kernel, blocks),
        "attend",
        45,
        grid=(PAIRS, blocks),
        in_specs=[
            heads,
            pl.BlockSpec((total, LANES), lambda p, i: (0, p)),
            pl.BlockSpec((total, LANES), lambda p, i: (0, PAIRS + p)),
            pl.BlockSpec((1, 8, ROWS), lambda p, i: (group, 0, i)),
        ],
        out_specs=[
            heads,
            pl.BlockSpec((1, 1, 2, 8, STACK), lambda p, i: (p, i, 0, 0, 0)),
        ],
        out_shape=[
            shaped(query.shape, bf16),
            shaped((PAIRS, blocks, 2, 8, STACK), f32),
        ],
        scratch_shapes=[
            pltpu.VMEM((LANES, total), bf16),
            pltpu.VMEM((2, 8, STACK), f32),
            pltpu.VMEM((2, 8, STACK), f32),
            pltpu.VMEM((2, LANES, STACK), f32),
        ],
    )(query, kv, kv, start_row)


def attend_back_kernel(
    blocks,
    q_ref,
    g_ref,
    o_ref,
    k_ref,
    v_ref,
    lse_ref,
    start_ref,
    cos_ref,
    sin_ref,
    dq_ref,
    keep_ref,
    send_ref,
    dq_acc,
    dkv_acc,
):
    step = pl.program_id(1)
    block = expert_rank() * blocks + step

    @pl.when(step == 0)
    def _():
        dkv_acc[...] = jnp.zeros_like(dkv_acc)

    dq_acc[...] = jnp.zeros_like(dq_acc)
    queries = stack_heads(q_ref)
    grads = stack_heads(g_ref)
    halves = []
    for c in range(SHARE):
        cols = slice(c * LANES, (c + 1) * LANES)
        product = jnp.transpose(g_ref[:, cols].astype(f32) * o_ref[:, cols].astype(f32))
        halves.append(jnp.sum(product[:HD], axis=0, keepdims=True))
        halves.append(jnp.sum(product[HD:], axis=0, keepdims=True))
    inner = [jnp.concatenate(halves[:SHARE], axis=1), jnp.concatenate(halves[SHARE:], axis=1)]

    def chunk(begin, size, masked):
        keys = k_ref[pl.ds(begin, size), :]
        values = v_ref[pl.ds(begin, size), :]
        bias = mask_bias(block, begin, size, start_ref) if masked else None
        key_sum, value_sum = None, None
        for h in range(2):
            scores = dot_nt(keys, queries[h]) - lse_ref[0, 0, h, :1, :]
            if masked:
                scores = scores + bias
            probs = jnp.exp(scores)
            probs_grad = dot_nt(values, grads[h])
            scores_grad = (probs * (probs_grad - inner[h])).astype(bf16)
            value_part = dot(probs.astype(bf16), grads[h])
            key_part = dot(scores_grad, queries[h])
            key_sum = key_part if key_sum is None else key_sum + key_part
            value_sum = value_part if value_sum is None else value_sum + value_part
            dq_acc[h] += dot_tn(scores_grad, keys)
        dkv_acc[0, pl.ds(begin, size), :] += key_sum
        dkv_acc[1, pl.ds(begin, size), :] += value_sum

    visit_chunks(block, chunk)
    cosine, sine = cos_ref[...], sin_ref[...]
    for c, part in enumerate(unstack_heads(dq_acc[0], dq_acc[1])):
        part = part * 0.125
        turned = part * cosine - half_swap(part) * sine
        dq_ref[:, c * LANES : (c + 1) * LANES] = turned.astype(bf16)

    @pl.when(step == blocks - 1)
    def _():
        length = blocks * ROWS
        own = lax.axis_index("el")
        for chip in range(dkv_acc.shape[1] // (2 * length)):
            mine = pl.multiple_of((2 * chip + own) * length, length)
            other = pl.multiple_of((2 * chip + 1 - own) * length, length)
            for i in range(2):
                keep_ref[chip, i] = dkv_acc[i, pl.ds(mine, length), :].astype(bf16)
                send_ref[chip, i] = dkv_acc[i, pl.ds(other, length), :].astype(bf16)


def attend_back_and_swap(blocks, pairs, *refs):
    away_ref = refs[9]
    here_ref = refs[-5]
    send_sem, recv_sem = refs[-2:]
    at = pl.program_id(0) * blocks + pl.program_id(1)
    peer = {"dl": 1 - lax.axis_index("dl")}
    exchange = pltpu.make_async_remote_copy(
        src_ref=away_ref,
        dst_ref=here_ref,
        send_sem=send_sem,
        recv_sem=recv_sem,
        device_id=peer,
        device_id_type=pl.DeviceIdType.MESH,
    )

    @pl.when(at == 0)
    def _():
        barrier = pltpu.get_barrier_semaphore()
        pl.semaphore_signal(barrier, inc=1, device_id=peer, device_id_type=pl.DeviceIdType.MESH)
        pl.semaphore_wait(barrier, 1)
        exchange.start()

    attend_back_kernel(blocks, *refs[:9], *refs[-8:-5], *refs[-4:-2])

    @pl.when(at == pairs * blocks - 1)
    def _():
        exchange.wait()


def attend_back(
    group, span, query, grad, mixed, kv, lse, start_row, cosine, sine, away, collective, kept
):
    length = query.shape[0]
    total = kv.shape[0]
    blocks = length // ROWS
    first = group * blocks
    chips = total // (2 * length)
    base, pairs = span
    side = pl.BlockSpec((chips, 2, length, LANES), lambda p, i: (0, 0, 0, p))
    heads = pl.BlockSpec((ROWS, PAIR_Q), lambda p, i: (i, base + p))
    table = pl.BlockSpec((ROWS, LANES), lambda p, i: (first + i, 0))
    swaps = [] if away is None else [away]
    if away is None:
        kernel = lambda *refs: attend_back_kernel(blocks, *refs[:9], *refs[-5:])
        extra = {}
    else:
        kernel = functools.partial(attend_back_and_swap, blocks, pairs)
        extra = dict(collective_id=collective, has_side_effects=True)
    anywhere = pl.BlockSpec(memory_space=pl.ANY)
    return call(
        kernel,
        "attend_back",
        16 * pairs,
        extra,
        grid=(pairs, blocks),
        in_specs=[
            heads,
            heads,
            heads,
            pl.BlockSpec((total, LANES), lambda p, i: (0, base + p)),
            pl.BlockSpec((total, LANES), lambda p, i: (0, PAIRS + base + p)),
            pl.BlockSpec((1, 1, 2, 8, STACK), lambda p, i: (base + p, i, 0, 0, 0)),
            pl.BlockSpec((1, 8, ROWS), lambda p, i: (group, 0, i)),
            table,
            table,
        ]
        + [anywhere] * len(swaps + kept),
        out_specs=[
            heads,
            side,
            side,
        ]
        + [anywhere] * len(swaps),
        input_output_aliases={9 + len(swaps): 0} if kept else {},
        out_shape=[
            shaped(query.shape, bf16),
            shaped((chips, 2, length, pairs * LANES), bf16),
            shaped((chips, 2, length, pairs * LANES), bf16),
        ]
        + [shaped(one.shape, one.dtype) for one in swaps],
        scratch_shapes=[
            pltpu.VMEM((2, STACK, LANES), f32),
            pltpu.VMEM((2, total, LANES), f32),
        ]
        + [pltpu.SemaphoreType.DMA] * (2 * len(swaps)),
    )(query, grad, mixed, kv, kv, lse, start_row, cosine, sine, *swaps, *kept)


def branch_kernel(a_ref, x_ref, wo_ref, gain_ref, wr_ref, m_ref, n_ref, ps_ref):
    middle = x_ref[...].astype(f32) + dot(a_ref[...], wo_ref[...])
    m_ref[...] = middle
    factor = lax.rsqrt(jnp.mean(middle * middle, axis=1, keepdims=True) + epsilon)
    normed = (middle * factor * gain_ref[...]).astype(bf16)
    n_ref[...] = normed
    add_up(ps_ref, fold_rows(router(normed, wr_ref[...])))


def branch(group, attended, x, wo, gain, wr):
    length = attended.shape[0]
    return call(
        branch_kernel,
        "branch",
        6,
        grid=(length // ROWS,),
        in_specs=[
            row_block(H * HD),
            row_block(D, group * length // ROWS),
            resident((H * HD, D)),
            resident((1, D)),
            resident((D, LANES)),
        ],
        out_specs=[row_block(D), row_block(D), pl.BlockSpec((8, LANES), lambda i: (0, 0))],
        out_shape=[
            shaped((length, D), f32),
            shaped((length, D), bf16),
            shaped((8, LANES), f32),
        ],
    )(attended, x, wo, gain, wr)


def router(normed, weight):
    count = EXP_DEV * 2 * lax.axis_size("eh")
    logits = dot(normed, weight)
    logits = jnp.where(lane_of(logits.shape) < count, logits, -1e30)
    powers = jnp.exp(logits - jnp.max(logits, axis=1, keepdims=True))
    return powers / jnp.sum(powers, axis=1, keepdims=True)


def experts_kernel(
    x_ref, c_ref, t_ref, wr_ref, wg_ref, wu_ref, wd_ref, *refs
):
    mix_ref, rows_ref, x_out, c_out, hid_ref, gate_ref, up_ref = refs[-7:]
    x, cot = x_ref[...], c_ref[...]
    x_out[...] = x
    c_out[...] = cot
    level = t_ref[0].astype(f32)
    picked = jnp.where(level > 0.5, router(x, wr_ref[...]), 0.0)
    share = picked / jnp.sum(picked, axis=1, keepdims=True)
    share = jnp.where(level > 1.5, share, 0.0)
    lane = lane_of(share.shape)
    base = EXP_DEV * expert_rank()
    share = pltpu.roll(share, lax.rem(LANES - base, LANES), 1)
    mix, rows = None, None
    gate_grads = jnp.zeros(share.shape, bf16)
    for e in range(EXP_DEV):
        gate = dot(x, wg_ref[e])
        up = dot(x, wu_ref[e])
        hidden_grad = dot(cot, wd_ref[e])
        sigmoid = jax.nn.sigmoid(gate)
        active = gate * sigmoid
        hidden = active * up
        inner = jnp.sum(hidden * hidden_grad, axis=1, keepdims=True)
        coarse = inner.astype(bf16)
        fine = (inner - coarse.astype(f32)).astype(bf16)
        gate_grads = jnp.where(lane == base + e, coarse, gate_grads)
        gate_grads = jnp.where(lane == LANES // 2 + base + e, fine, gate_grads)
        weight = share[:, e : e + 1]
        scaled = (hidden * weight).astype(bf16)
        hidden_grad = hidden_grad * weight
        up_grad = (hidden_grad * active).astype(bf16)
        gate_grad = (hidden_grad * up * sigmoid * (1.0 + gate * (1.0 - sigmoid))).astype(bf16)
        cols = slice(e * FF, (e + 1) * FF)
        hid_ref[:, cols] = scaled
        gate_ref[:, cols] = gate_grad
        up_ref[:, cols] = up_grad
    for e in range(EXP_DEV):
        cols = slice(e * FF, (e + 1) * FF)
        mix_part = dot_nt(hid_ref[:, cols], wd_ref[e])
        rows_part = dot_nt(gate_ref[:, cols], wg_ref[e]) + dot_nt(up_ref[:, cols], wu_ref[e])
        mix = mix_part if mix is None else mix + mix_part
        rows = rows_part if rows is None else rows + rows_part
    mix_ref[...] = mix.astype(bf16)
    rows_ref[:, :D] = rows.astype(bf16)
    rows_ref[:, D:] = gate_grads


def experts_pass(group, groups, x, cot, level, wr, wg, wu, wd, kept):
    count = x.shape[0]
    first = group * count // ROWS
    whole = groups * count
    side = pl.BlockSpec(memory_space=pl.ANY)
    widths = [D, D, EXP_DEV * FF, EXP_DEV * FF, EXP_DEV * FF]
    return call(
        experts_kernel,
        "experts",
        113,
        grid=(count // ROWS,),
        in_specs=[
            row_block(D),
            row_block(D),
            pl.BlockSpec((1, ROWS, LANES), lambda i: (group, i, 0)),
            resident((D, LANES)),
            resident((EXP_DEV, D, FF)),
            resident((EXP_DEV, D, FF)),
            resident((EXP_DEV, D, FF)),
        ]
        + [side] * len(kept),
        out_specs=[row_block(D), row_block(D + LANES)]
        + [row_block(width, first) for width in widths],
        out_shape=[
            shaped((count, D), bf16),
            shaped((count, D + LANES), bf16),
        ]
        + [shaped((whole, width), bf16) for width in widths],
        input_output_aliases={7 + i: 2 + i for i in range(len(kept))},
    )(x, cot, level, wr, wg, wu, wd, *kept)


def norm_back(grad, normed, factor, gain):
    scaled = grad * gain
    return factor * (scaled - normed * jnp.mean(scaled * normed, axis=1, keepdims=True))


def fold_rows(values):
    return jnp.sum(values.reshape(values.shape[0] // 8, 8, values.shape[1]), axis=0)


def add_up(ref, part):
    @pl.when(pl.program_id(0) == 0)
    def _():
        ref[...] = part

    @pl.when(pl.program_id(0) > 0)
    def _():
        ref[...] += part


def middle_kernel(
    r_ref, t_ref, m_ref, n_ref, c_ref, gain_ref, wr_ref, wo_ref,
    mg_ref, b_ref, ag_ref, l_ref, dg_ref,
):
    probs = router(n_ref[...], wr_ref[...])
    level = t_ref[0].astype(f32)
    sel = jnp.where(level > 0.5, 1.0, 0.0)
    gate_grad = r_ref[:, D:].astype(f32)
    gate_grad = gate_grad + pltpu.roll(gate_grad, LANES // 2, 1)
    gate_grad = jnp.where(level > 1.5, gate_grad, 0.0)
    picked = probs * sel
    total = jnp.sum(picked, axis=1, keepdims=True)
    share = picked / total
    inner = jnp.sum(gate_grad * share, axis=1, keepdims=True)
    probs_grad = (gate_grad - inner) / total * sel
    logits_grad = probs * (probs_grad - jnp.sum(probs_grad * probs, axis=1, keepdims=True))
    coarse = logits_grad.astype(bf16)
    fine = (logits_grad - coarse.astype(f32)).astype(bf16)
    l_ref[:, :LANES] = coarse
    l_ref[:, LANES:] = fine
    grad = r_ref[:, :D].astype(f32) + dot_nt(coarse, wr_ref[...]) + dot_nt(fine, wr_ref[...])
    middle = m_ref[...]
    factor = lax.rsqrt(jnp.mean(middle * middle, axis=1, keepdims=True) + epsilon)
    normed = middle * factor
    add_up(dg_ref, fold_rows(grad * normed))
    middle_grad = c_ref[...].astype(f32) + norm_back(grad, normed, factor, gain_ref[...])
    mg_ref[...] = middle_grad
    low = middle_grad.astype(bf16)
    b_ref[...] = low
    ag_ref[...] = dot_nt(low, wo_ref[...]).astype(bf16)


def middle_back(group, rows, level, middle, normed, cot, gain, wr, wo):
    length = rows.shape[0]
    first = group * length // ROWS
    corner = lambda width: pl.BlockSpec((8, width), lambda i: (0, 0))
    return call(
        middle_kernel,
        "middle_back",
        8,
        grid=(length // ROWS,),
        in_specs=[
            row_block(D + LANES),
            pl.BlockSpec((1, ROWS, LANES), lambda i: (group, i, 0)),
            row_block(D), row_block(D), row_block(D, first),
            resident((1, D)), resident((D, LANES)), resident((H * HD, D)),
        ],
        out_specs=[
            row_block(D), row_block(D), row_block(H * HD), row_block(2 * LANES),
            corner(D),
        ],
        out_shape=[
            shaped((length, D), f32),
            shaped((length, D), bf16),
            shaped((length, H * HD), bf16),
            shaped((length, 2 * LANES), bf16),
            shaped((8, D), f32),
        ],
    )(rows, level, middle, normed, cot, gain, wr, wo)


def input_kernel(
    dq_ref, dk_ref, dv_ref, x_ref, mg_ref, cos_ref, sin_ref, gain_ref, wq_ref, wk_ref, wv_ref,
    out_ref, dk_out, dg_ref,
):
    cosine, sine = cos_ref[...], sin_ref[...]
    for c in range(KVH * HD // LANES):
        part = dk_ref[0, :, c * LANES : (c + 1) * LANES].astype(f32)
        turned = part * cosine - half_swap(part) * sine
        dk_out[:, c * LANES : (c + 1) * LANES] = turned.astype(bf16)
    grad = dot_nt(dq_ref[...], wq_ref[...])
    grad = grad + dot_nt(dk_out[...], wk_ref[...])
    grad = grad + dot_nt(dv_ref[0], wv_ref[...])
    x = x_ref[...].astype(f32)
    factor = lax.rsqrt(jnp.mean(x * x, axis=1, keepdims=True) + epsilon)
    normed = x * factor
    add_up(dg_ref, fold_rows(grad * normed))
    out_ref[...] = mg_ref[...] + norm_back(grad, normed, factor, gain_ref[...])


def input_back(group, groups, dq, dkv, x, middle_grad, cosine, sine, gain, wq, wk, wv, kept):
    length = dq.shape[0]
    first = group * length // ROWS
    kernel = lambda *refs: input_kernel(*refs[:11], *refs[-3:])
    return call(
        kernel,
        "input_back",
        8,
        grid=(length // ROWS,),
        in_specs=[
            row_block(H * HD),
            pl.BlockSpec((1, ROWS, KVH * HD), lambda i: (0, i, 0)),
            pl.BlockSpec((1, ROWS, KVH * HD), lambda i: (1, i, 0)),
            row_block(D, first),
            row_block(D),
            row_block(LANES, first),
            row_block(LANES, first),
            resident((1, D)),
            resident((D, H * HD)),
            resident((D, KVH * HD)),
            resident((D, KVH * HD)),
        ]
        + [pl.BlockSpec(memory_space=pl.ANY)] * len(kept),
        out_specs=[
            row_block(D, first),
            row_block(KVH * HD),
            pl.BlockSpec((8, D), lambda i: (0, 0)),
        ],
        out_shape=[
            shaped((groups * length, D), f32),
            shaped((length, KVH * HD), bf16),
            shaped((8, D), f32),
        ],
        input_output_aliases={11: 0} if kept else {},
    )(dq, dkv, dkv, x, middle_grad, cosine, sine, gain, wq, wk, wv, *kept)


def transpose_into(turned, lefts):
    length = lefts[0].shape[0]
    for g, left in enumerate(lefts):
        for c in range(0, D, 2 * LANES):
            part = left[:, c : c + 2 * LANES].astype(f32)
            turned[c : c + 2 * LANES, g * length : (g + 1) * length] = jnp.transpose(part).astype(
                bf16
            )


def out_kernel(groups, *refs):
    lefts, rights = refs[:groups], refs[groups : 2 * groups]
    out_ref, turned = refs[-2:]
    length = lefts[0].shape[0]

    @pl.when(pl.program_id(0) == 0)
    def _():
        transpose_into(turned, lefts)

    total = None
    for g in range(groups):
        part = dot(turned[:, g * length : (g + 1) * length], rights[g][...])
        total = part if total is None else total + part
    out_ref[...] = total.astype(bf16)


def out_gradient(lefts, rights):
    groups, length = len(lefts), lefts[0].shape[0]
    width = 4 * LANES
    return call(
        functools.partial(out_kernel, groups),
        "out_grad",
        10,
        grid=(D // width,),
        in_specs=[resident((length, D))] * groups
        + [pl.BlockSpec((length, width), lambda i: (0, i))] * groups,
        out_specs=pl.BlockSpec((D, width), lambda i: (0, i)),
        out_shape=shaped((D, D), bf16),
        scratch_shapes=[pltpu.VMEM((D, groups * length), bf16)],
    )(*lefts, *rights)


def dense_kernel(groups, sizes, *refs):
    data, chips, shard, width, full, late = sizes
    lefts, queries, keys, values = (refs[i * groups : (i + 1) * groups] for i in range(4))
    narrow_ref, late_ref, out_ref = refs[4 * groups : 4 * groups + 3]
    (turned, keep1, send1, got1, keep2, send2, got2, sum2, got3, sum3, got4, sum4, near5, far5,
     wide2, wide3, keep6, send6, got6) = refs[4 * groups + 3 : 4 * groups + 22]
    sems = refs[4 * groups + 22 :]
    half = width // 2
    length = lefts[0].shape[0]
    ranks = 2 * chips
    dh, dl, eh, el = (lax.axis_index(name) for name in ("dh", "dl", "eh", "el"))

    def near(hop, core):
        return {"eh": lax.rem(eh + hop, chips), "el": core}

    peers = [{"el": 1 - el}, {"dl": 1 - dl}]
    for hop in range(1, chips):
        peers.append(near(hop, el))
    for hop in range(1, data):
        peers.append({"dh": lax.rem(dh + hop, data)})
    barrier = pltpu.get_barrier_semaphore()
    for peer in peers:
        pl.semaphore_signal(barrier, inc=1, device_id=peer, device_id_type=pl.DeviceIdType.MESH)
    transpose_into(turned, lefts)
    pl.semaphore_wait(barrier, len(peers))

    def copy(source, target, phase, k, lane, peer):
        return pltpu.make_async_remote_copy(
            src_ref=source,
            dst_ref=target,
            send_sem=sems[2 * phase].at[k, lane],
            recv_sem=sems[2 * phase + 1].at[k, lane],
            device_id=peer,
            device_id_type=pl.DeviceIdType.MESH,
        )

    def crossed(k):
        return k < full and k % 2 == 1

    def slot(k):
        return k // 2 if k < full else (full + 1) // 2 + k - full

    def copies(phase, k):
        if phase == 0:
            return [copy(send1.at[k], got1.at[k], 0, k, 0, {"el": 1 - el})]
        if phase == 1:
            source, target = (send6, got6) if crossed(k) else (send2, got2)
            at = k // 2
            return [
                copy(source.at[at, hop - 1], target.at[at, hop - 1], 1, k, hop - 1, near(hop, el))
                for hop in range(1, chips)
            ]
        if phase == 2:
            if crossed(k):
                at = k // 2
                return [copy(wide2.at[at, 1 - dl], wide3.at[at], 2, k, 0, {"dl": 1 - dl})]
            at = slot(k)
            return [copy(sum2.at[at, 1 - dl], got3.at[at], 2, k, 0, {"dl": 1 - dl})]
        if phase == 3:
            found = []
            for hop in range(1, data):
                away = lax.rem(dh + hop, data)
                found.append(
                    copy(sum3.at[k, away], got4.at[k, hop - 1], 3, k, hop - 1, {"dh": away})
                )
            return found
        if phase == 4:
            return [
                copy(sum4.at[k], near5.at[k, eh], 4, k, hop - 1, near(hop, el))
                for hop in range(1, chips)
            ]
        return [copy(near5.at[k], far5.at[k], 5, k, 0, {"el": 1 - el})]

    def start(phase, k):
        for one in copies(phase, k):
            one.start()

    def arrived(phase, k):
        for one in copies(phase, k):
            one.wait_recv()

    def finish_shard(k):
        base = k * width if k < full else full * width + (k - full) * LANES

        def put(side, chip, block):
            place = side * chips + chip
            place = place * LANES if k < full else place * late * LANES
            at = pl.multiple_of(base + place, LANES)
            out_ref[:, pl.ds(at, LANES)] = block.astype(f32)

        for chip in range(chips):
            put(el, chip, near5[k, chip])
            put(1 - el, chip, far5[k, chip])

    def piece(column):
        size = KVH * HD
        if column >= H * HD + 2 * size:
            if column > H * HD + 2 * size:
                return jnp.zeros((D, size), bf16)
            part = jnp.transpose(narrow_ref[...])
            return jnp.concatenate([part, jnp.zeros((D, size - LANES), f32)], axis=1).astype(bf16)
        total = None
        for g in range(groups):
            if column < H * HD:
                block = queries[g][:, column : column + size]
            elif column < H * HD + size:
                block = keys[g][...]
            else:
                block = values[g][1]
            one = dot(turned[:, g * length : (g + 1) * length], block)
            total = one if total is None else total + one
        return total.astype(bf16)

    def stage_compute(k):
        if k < full:
            part = [piece(k * width + c) for c in range(0, width, KVH * HD)]
            part = part[0] if len(part) == 1 else jnp.concatenate(part, axis=1)

            @pl.when(el == 0)
            def _():
                keep1[k] = part[:, :half]
                send1[k] = part[:, half:]

            @pl.when(el == 1)
            def _():
                keep1[k] = part[:, half:]
                send1[k] = part[:, :half]

            start(0, k)

    def hand_out(block, chip, keep, send):
        hop = lax.rem(chip + chips - eh, chips)

        @pl.when(hop == 0)
        def _():
            keep[...] = block

        @pl.when(hop > 0)
        def _():
            send[hop - 1] = block

    def chip_columns(chip):
        return slice(chip * LANES, (chip + 1) * LANES)

    def stage_core(k):
        arrived(0, k)
        met = (keep1[k].astype(f32) + got1[k].astype(f32)).astype(bf16)
        at = k // 2
        if crossed(k):
            for far in range(data):
                for side in range(2):
                    first = (2 * far + side) * shard
                    wide2[at, side, far] = met[first : first + shard]
            start(2, k)
        else:
            for chip in range(chips):
                hand_out(met[:, chip_columns(chip)], chip, keep2.at[at], send2.at[at])
            start(1, k)

    def stage_second(k):
        at = k // 2
        if crossed(k):
            arrived(2, k)
            met = (wide2[at, dl].astype(f32) + wide3[at].astype(f32)).astype(bf16)
            for chip in range(chips):
                hand_out(met[:, :, chip_columns(chip)], chip, keep6.at[at], send6.at[at])
            start(1, k)
        else:
            arrived(1, k)
            total = keep2[at].astype(f32)
            for hop in range(1, chips):
                total = total + got2[at, hop - 1].astype(f32)
            spread(k, total.astype(bf16))

    def spread(k, total):
        for far in range(data):
            for side in range(2):
                first = (2 * far + side) * shard
                sum2[slot(k), side, far] = total[first : first + shard]
        start(2, k)

    def stage_third(k):
        if crossed(k):
            at = k // 2
            arrived(1, k)
            total = keep6[at].astype(f32)
            for hop in range(1, chips):
                total = total + got6[at, hop - 1].astype(f32)
        else:
            at = slot(k)
            arrived(2, k)
            total = sum2[at, dl].astype(f32) + got3[at].astype(f32)
        sum3[k] = total.astype(bf16)
        start(3, k)

    def stage_far(k):
        arrived(3, k)
        total = sum3[k, dh].astype(f32)
        for hop in range(1, data):
            total = total + got4[k, hop - 1].astype(f32)
        total = total.astype(bf16)
        sum4[k] = total
        near5[k, eh] = total
        start(4, k)

    def stage_gather(k):
        arrived(4, k)
        start(5, k)

    def stage_last(k):
        arrived(5, k)
        finish_shard(k)

    everything = list(range(full, full + late)) + list(range(full))
    for k in range(full, full + late):
        first = (k - full) * LANES
        spread(k, late_ref[:, first : first + LANES])
    stages = (
        stage_compute,
        stage_core,
        stage_second,
        stage_third,
        stage_far,
        stage_gather,
        stage_last,
    )
    for step in range(full + len(stages) - 1):
        for delay, stage in enumerate(stages):
            if 0 <= step - delay < full:
                stage(step - delay)
        if step < 4:
            for k in range(full, full + late):
                stages[3 + step](k)
    for k in everything:
        for phase in range(6):
            if k < full or phase > 1:
                for one in copies(phase, k):
                    one.wait_send()


def dense_gradient(lefts, queries, keys, values, narrow, late_part):
    groups = len(lefts)
    data, chips = lax.axis_size("dh"), lax.axis_size("eh")
    shard = D // (2 * data)
    width = 2 * chips * LANES
    columns = H * HD + 2 * KVH * HD
    full = -(-(columns + LANES) // width)
    late = late_part.shape[1] // LANES
    total = full + late
    half, ranks = width // 2, 2 * chips
    sizes = (data, chips, shard, width, full, late)
    lanes = [1, chips - 1, 1, data - 1, chips - 1, 1]
    even, odd = (full + 1) // 2, full // 2
    sems = []
    for count in lanes:
        sems += [pltpu.SemaphoreType.DMA((total, count))] * 2
    operands = [*lefts, *queries, *keys, *values, narrow, late_part]
    whole = pl.BlockSpec(memory_space=pltpu.VMEM)
    return pl.pallas_call(
        functools.partial(dense_kernel, groups, sizes),
        name="dense_grad",
        in_specs=[whole] * len(operands),
        out_specs=whole,
        out_shape=shaped((shard, full * width + late * ranks * LANES), f32),
        scratch_shapes=[
            pltpu.VMEM((D, groups * lefts[0].shape[0]), bf16),
            pltpu.VMEM((full, D, half), bf16),
            pltpu.VMEM((full, D, half), bf16),
            pltpu.VMEM((full, D, half), bf16),
            pltpu.VMEM((even, D, LANES), bf16),
            pltpu.VMEM((even, chips - 1, D, LANES), bf16),
            pltpu.VMEM((even, chips - 1, D, LANES), bf16),
            pltpu.VMEM((even + late, 2, data, shard, LANES), bf16),
            pltpu.VMEM((even + late, data, shard, LANES), bf16),
            pltpu.VMEM((total, data, shard, LANES), bf16),
            pltpu.VMEM((total, data - 1, shard, LANES), bf16),
            pltpu.VMEM((total, shard, LANES), bf16),
            pltpu.VMEM((total, chips, shard, LANES), bf16),
            pltpu.VMEM((total, chips, shard, LANES), bf16),
            pltpu.VMEM((odd, 2, data, shard, half), bf16),
            pltpu.VMEM((odd, data, shard, half), bf16),
            pltpu.VMEM((odd, data, shard, LANES), bf16),
            pltpu.VMEM((odd, chips - 1, data, shard, LANES), bf16),
            pltpu.VMEM((odd, chips - 1, data, shard, LANES), bf16),
        ]
        + sems,
        cost_estimate=pl.CostEstimate(
            flops=int(80 * 9e8), bytes_accessed=0, transcendentals=0
        ),
        compiler_params=pltpu.CompilerParams(
            vmem_limit_bytes=VMEM_LIMIT, collective_id=0, has_side_effects=True
        ),
    )(*operands)


def widen(values):
    return jnp.pad(values, ((0, 0), (0, LANES - values.shape[1])))


def swap(values, axis):
    return lax.ppermute(values, axis, [(0, 1), (1, 0)])


def pick(values, index):
    return lax.dynamic_index_in_dim(values, index, 1, keepdims=False)


def pair_slices(values, shard):
    parts = values.reshape(-1, 2, shard, values.shape[1])
    own = lax.axis_index("dl")
    return pick(parts, own), pick(parts, 1 - own)


def pair_parts(values, shard):
    own, away = pair_slices(values, shard)
    return own, swap(away, "dl")


def far_sum(own, met):
    met = (own + met).reshape(-1, own.shape[2])
    return lax.psum_scatter(met, "dh", scatter_dimension=0, tiled=True)


def take(values, axis, index):
    return lax.dynamic_index_in_dim(values, index, axis, keepdims=False)


def chip_sum(met):
    chips = lax.axis_size("eh")
    chip = lax.axis_index("eh")
    total = take(met, 0, chip)
    for hop in range(1, chips):
        order = [(i, (i + hop) % chips) for i in range(chips)]
        away = take(met, 0, lax.rem(chip + hop, chips))
        total = total + lax.ppermute(away, "eh", order)
    return total


def cut(array, index, size):
    return lax.dynamic_slice_in_dim(array, index * size, size, 1)


def column_core_sum(values):
    half = values.shape[1] // 2
    own = lax.axis_index("el")
    return cut(values, own, half) + swap(cut(values, 1 - own, half), "el")


def column_chip_sum(met):
    chips, chip = lax.axis_size("eh"), lax.axis_index("eh")
    size = met.shape[1] // chips
    total = cut(met, chip, size)
    for hop in range(1, chips):
        order = [(i, (i + hop) % chips) for i in range(chips)]
        away = cut(met, lax.rem(chip + hop, chips), size)
        total = total + lax.ppermute(away, "eh", order)
    return total


def sum_steps():
    for axis in ("el", "eh", "dl", "dh"):
        count = lax.axis_size(axis)
        hop = 1
        while hop < count:
            order = [(i, i ^ hop) for i in range(count)]
            yield lambda v, axis=axis, order=order: v + lax.ppermute(v, axis, order)
            hop *= 2


def together(*values):
    return lax.optimization_barrier(values)


def on_device(
    tokens,
    segments,
    routes,
    cotangent,
    attention_gain,
    query_weight,
    key_weight,
    value_weight,
    out_weight,
    mixture_gain,
    router_weight,
    gate_weight,
    up_weight,
    down_weight,
):
    groups, length, _ = tokens.shape
    each = range(groups)
    rows = groups * length
    ranks = lax.axis_size("eh") * 2
    dp_ranks = lax.axis_size("dh") * 2
    rank = expert_rank()
    experts = EXP_DEV * ranks
    capacity = (rows * TOPK * 5 // (4 * experts) + 7) // 8 * 8
    all_tokens = rows * dp_ranks * ranks
    first_row = rank * length
    shard = D // dp_ranks

    seg_full = jnp.concatenate([jnp.full((groups, PROMPT), -1, jnp.int32), segments], axis=1)
    seg_own = lax.dynamic_slice_in_dim(seg_full, first_row, length, 1)
    earlier = jnp.sum((segments[:, None, :] < seg_own[:, :, None]).astype(jnp.int32), axis=2)
    position = first_row + jnp.arange(length, dtype=jnp.int32)[None, :]
    place = position - earlier
    start = jnp.where(position >= PROMPT, PROMPT + earlier, 0)
    half = HD // 2
    lane = jnp.arange(LANES, dtype=jnp.int32)
    frequency = jnp.exp(-math.log(rope_base) * (lane % half).astype(f32) / half)
    angles = place.astype(f32).reshape(rows, 1) * frequency
    cosine = jnp.cos(angles)
    sine = jnp.sin(angles) * jnp.where(lane % HD < half, -1.0, 1.0)
    start_row = jnp.broadcast_to(start[:, None, :], (groups, 8, length))

    names = jnp.concatenate([routes[g] for g in each], axis=1).astype(bf16)
    names = widen(names)
    cot_rows = cotangent.reshape(rows, D)
    cot_all = [lax.all_gather(cotangent[g], EXPERT, axis=0, tiled=True) for g in each]

    x = tokens.reshape(rows, D)
    gain_a = attention_gain.reshape(1, D)
    gain_b = mixture_gain.reshape(1, D)
    router_wide = widen(router_weight)
    normed, query, kv = [None] * groups, [None] * groups, [None] * groups
    for g in each:
        normed[g], kv_own = key_value(
            g, length, x, gain_a, key_weight, value_weight, cosine, sine, names
        )
        kv[g] = lax.all_gather(kv_own, EXPERT, axis=0, tiled=True)
    for g in each:
        query[g] = project_query(g, normed[g], query_weight, cosine, sine)
    level = naming(kv[groups - 1], capacity, groups, ranks)
    level_own = lax.dynamic_slice_in_dim(level, first_row, length, 1)
    kv[0], query = together(kv[0], query)
    attended, lse = [None] * groups, [None] * groups
    middle, hidden_low, hidden_all = [None] * groups, [None] * groups, [None] * groups
    probs_local = 0.0
    for g in each:
        attended[g], lse[g] = attend(g, query[g], kv[g], start_row)
        if g == groups - 1:
            attended[g], cot_all[0] = together(attended[g], cot_all[0])
        middle[g], hidden_low[g], probs_part = branch(
            g, attended[g], x, out_weight, gain_b, router_wide
        )
        probs_local += jnp.sum(probs_part, axis=0)
        hidden_all[g] = lax.all_gather(hidden_low[g], EXPERT, axis=0, tiled=True)

    counts = jnp.sum((level_own > 0.5).astype(f32), axis=(0, 1))
    stats = jnp.stack([counts, probs_local])[:, :experts]
    steps = sum_steps()

    def beside(value, stats):
        step = next(steps, None)
        return (value, stats) if step is None else together(value, step(stats))

    kept, rows_back, mixture = [], [], []
    for g in each:
        if g > 0:
            kept[0], cot_all[g] = together(kept[0], cot_all[g])
            hidden_all[g], stats = beside(hidden_all[g], stats)
        mix, rows_grad, *kept = experts_pass(
            g, groups, hidden_all[g], cot_all[g], level, router_wide,
            gate_weight, up_weight, down_weight, kept,
        )
        rows_back.append(lax.psum_scatter(rows_grad, EXPERT, scatter_dimension=0, tiled=True))
        mixture.append(mix)
        if g < groups - 1:
            mixture[g] = lax.psum_scatter(mix, EXPERT, scatter_dimension=0, tiled=True)
    x_all, cot_both, hidden, gate_back, up_back = kept
    hidden, mixture[0] = together(hidden, mixture[0])
    hidden, stats = beside(hidden, stats)
    down_local = dot_tn(cot_both, hidden).astype(bf16)
    x_all, down_local = together(x_all, down_local)
    gate_back, stats = beside(gate_back, stats)
    gate_local = dot_tn(x_all, gate_back).astype(bf16)
    up_back, gate_local = together(up_back, gate_local)
    gate_own, gate_met = pair_parts(gate_local, shard)
    up_back, mix = together(up_back, mixture[-1])
    mixture[-1] = lax.psum_scatter(mix, EXPERT, scatter_dimension=0, tiled=True)
    up_back, stats = beside(up_back, stats)
    up_local = dot_tn(x_all, up_back).astype(bf16)
    rows_back[0], up_local = together(rows_back[0], up_local)
    rows_back[0], stats = beside(rows_back[0], stats)
    for step in steps:
        stats = step(stats)
    expert_load = stats[0] * experts / (all_tokens * TOPK)
    prob_mean = stats[1] * experts / all_tokens
    balance_loss = jnp.sum(expert_load * prob_mean) / experts

    def by_expert(part):
        return jnp.stack([part[:, e * FF : (e + 1) * FF] for e in range(EXP_DEV)]).astype(f32)

    middle_grad, branch_grad, attended_grad, logits_grad, dq, dkv = (
        [None] * groups for _ in range(6)
    )
    gain_b_local, last = 0.0, groups - 1
    down_far = lax.psum_scatter(down_local, "dh", scatter_dimension=0, tiled=True)
    for g in each:
        middle_grad[g], branch_grad[g], attended_grad[g], logits_grad[g], gain_part = middle_back(
            g, rows_back[g], level_own, middle[g], hidden_low[g], cot_rows,
            gain_b, router_wide, out_weight,
        )
        gain_b_local += jnp.sum(gain_part, axis=0)
    out_local = out_gradient(attended, branch_grad)
    fill = -D % (ranks * LANES)
    out_local = jnp.pad(out_local, ((0, 0), (0, fill)))
    attended_grad[0], out_local = together(attended_grad[0], out_local)
    cut_at = 3 * FF
    slices = [pair_slices(up_local[:, :cut_at], shard), pair_slices(up_local[:, cut_at:], shard)]
    out_met = column_core_sum(out_local)
    for g in each:
        pieces, kept = [], []
        here = [] if g == 0 else here
        spans = [(0, PAIRS)] if g < last else [(0, PAIRS // 2), (PAIRS // 2, PAIRS // 2)]
        for at, span in enumerate(spans):
            if g == last and at == 0:
                dq[0], gate_own = together(dq[0], gate_own)
                attended_grad[g], out_met, dq[0], gate_own, gate_met, down_far = together(
                    attended_grad[g], out_met, dq[0], gate_own, gate_met, down_far
                )
                gate_part = far_sum(gate_own, gate_met)
                out_part = column_chip_sum(out_met)
            if g == last and at == 1:
                up_met = jnp.concatenate([slices[i][0] + here[i] for i in range(2)], axis=2)
                kept, dkv[0], pieces[0], up_met, mixture[last] = together(
                    kept, dkv[0], pieces[0], up_met, mixture[last]
                )
                up_part = lax.psum_scatter(
                    up_met.reshape(-1, up_met.shape[2]), "dh", scatter_dimension=0, tiled=True
                )
            turn = len(here)
            grad, keep_part, send_part, *arrived = attend_back(
                g, span, query[g], attended_grad[g], attended[g], kv[g], lse[g], start_row,
                cosine, sine, slices[turn][1] if turn < 2 else None, 1 + turn, kept,
            )
            here += arrived
            kept = [grad]
            if g == last and at == 1:
                keep_part, dq[0], down_far = together(keep_part, dq[0], down_far)
                down_own, down_met = pair_parts(down_far, shard)
                down_part = (down_own + down_met)[0]
            pieces.append(keep_part + swap(send_part, "el"))
        dq[g] = kept[0]
        pieces = [chip_sum(piece) for piece in pieces]
        dkv[g] = pieces[0] if len(pieces) == 1 else jnp.concatenate(pieces, axis=2)
    output = jnp.stack(
        [(middle[g] + mixture[g].astype(f32)).astype(bf16) for g in each]
    )

    kept, turned_dk, gain_a_local = [], [None] * groups, 0.0
    for g in each:
        input_grad, turned_dk[g], gain_part = input_back(
            g, groups, dq[g], dkv[g], x, middle_grad[g], cosine, sine,
            gain_a, query_weight, key_weight, value_weight, kept,
        )
        kept = [input_grad]
        gain_a_local += jnp.sum(gain_part, axis=0)
    router_parts = sum(dot_tn(logits_grad[g], hidden_low[g]) for g in each)
    router_local = (router_parts[:LANES] + router_parts[LANES:])[:experts]
    narrow = jnp.concatenate(
        [
            router_local,
            gain_a_local[None, :],
            gain_b_local[None, :],
            jnp.zeros((LANES - experts - 2, D), f32),
        ],
        axis=0,
    )
    narrow, up_part = together(narrow, up_part)
    dense = dense_gradient(normed, dq, turned_dk, dkv, narrow, out_part)
    first = dense.shape[1] - D - fill
    out_grad = dense[:, first : first + D]
    down_weight_grad, gate_weight_grad, up_weight_grad = (
        by_expert(part) for part in (down_part, gate_part, up_part)
    )
    spans = [H * HD, KVH * HD, KVH * HD, experts, 1, 1]
    pieces, begin = [], 0
    for span in spans:
        pieces.append(dense[:, begin : begin + span])
        begin += span
    query_grad, key_grad, value_grad, router_grad, gain_a_grad, gain_b_grad = pieces
    return (
        output,
        input_grad.reshape(groups, length, D),
        gain_a_grad[:, 0],
        query_grad,
        key_grad,
        value_grad,
        out_grad,
        gain_b_grad[:, 0],
        router_grad,
        gate_weight_grad,
        up_weight_grad,
        down_weight_grad,
        expert_load,
        prob_mean,
        balance_loss,
    )


def solution(mesh):
    dp_ranks, ranks = mesh.devices.shape
    fine = Mesh(
        mesh.devices.reshape(dp_ranks // 2, 2, ranks // 2, 2), ("dh", "dl", "eh", "el")
    )
    return jax.shard_map(
        on_device,
        mesh=fine,
        in_specs=(
            P(DATA, EXPERT, None),
            P(DATA, None),
            P(DATA, EXPERT, None),
            P(DATA, EXPERT, None),
            P(),
            P(),
            P(),
            P(),
            P(),
            P(),
            P(),
            P(EXPERT, None, None),
            P(EXPERT, None, None),
            P(EXPERT, None, None),
        ),
        out_specs=(
            P(DATA, EXPERT, None),
            P(DATA, EXPERT, None),
            P(DATA),
            P(DATA, None),
            P(DATA, None),
            P(DATA, None),
            P(DATA, None),
            P(DATA),
            P(DATA, None),
            P(EXPERT, DATA, None),
            P(EXPERT, DATA, None),
            P(EXPERT, DATA, None),
            P(),
            P(),
            P(),
        ),
        check_vma=False,
    )
```

```python
import functools
import math

import jax
import jax.numpy as jnp
from jax import lax
from jax.experimental import pallas as pl
from jax.experimental.pallas import tpu as pltpu
from jax.sharding import Mesh
from jax.sharding import PartitionSpec as P

D = 1536
H = 24
KVH = 8
HD = 64
FF = 512
TOPK = 8
EXP_DEV = 5
PROMPT = 1024
LANES = 128
PAIRS = KVH // 2
SHARE = H // KVH
PAIR_Q = 2 * SHARE * HD
ROWS = 256
STACK = SHARE * ROWS
EXPERT = ("eh", "el")
DATA = ("dh", "dl")
VMEM_LIMIT = 63 * 1024 * 1024

epsilon = 1e-05
rope_base = 10000.0
f32 = jnp.float32
bf16 = jnp.bfloat16


def dot(a, b):
    return lax.dot_general(a, b, (((1,), (0,)), ((), ())), preferred_element_type=f32)


def dot_nt(a, b):
    return lax.dot_general(a, b, (((1,), (1,)), ((), ())), preferred_element_type=f32)


def dot_tn(a, b):
    return lax.dot_general(a, b, (((0,), (0,)), ((), ())), preferred_element_type=f32)


def expert_rank():
    return lax.axis_index("eh") * 2 + lax.axis_index("el")


def call(kernel, name, micros, extra=None, **more):
    cost = pl.CostEstimate(flops=int(micros * 2.5e8), bytes_accessed=0, transcendentals=0)
    return pl.pallas_call(
        kernel,
        name=name,
        cost_estimate=cost,
        compiler_params=pltpu.CompilerParams(vmem_limit_bytes=VMEM_LIMIT, **(extra or {})),
        **more,
    )


def shaped(shape, dtype):
    return jax.ShapeDtypeStruct(shape, dtype)


def lane_of(shape):
    return lax.broadcasted_iota(jnp.int32, shape, len(shape) - 1)


def half_swap(values):
    lower = lane_of(values.shape) % HD < HD // 2
    return jnp.where(
        lower, pltpu.roll(values, LANES - HD // 2, 1), pltpu.roll(values, HD // 2, 1)
    )


def resident(shape):
    zeros = (0,) * len(shape)
    return pl.BlockSpec(shape, lambda *_: zeros, pipeline_mode=pl.Buffered(1))


def row_block(width, first=0):
    return pl.BlockSpec((ROWS, width), lambda i: (first + i, 0))


def naming_kernel(capacity, groups, r_ref, o_ref):
    length = r_ref.shape[0]
    rows = groups * length
    lane = lane_of((rows, LANES))
    packed = r_ref[...].astype(jnp.int32)
    chosen = jnp.concatenate(
        [packed[:, g * TOPK : (g + 1) * TOPK] for g in range(groups)], axis=0
    )
    named = jnp.zeros((rows, LANES), f32)
    for k in range(TOPK):
        named = jnp.where(chosen[:, k : k + 1] == lane, 1.0, named)
    earlier = lax.broadcasted_iota(jnp.int32, (rows, rows), 1) < lax.broadcasted_iota(
        jnp.int32, (rows, rows), 0
    )
    slot = dot(jnp.where(earlier, 1.0, 0.0).astype(bf16), named.astype(bf16))
    level = named * jnp.where(slot < capacity, 2.0, 1.0)
    o_ref[...] = level.reshape(groups, length, LANES).astype(bf16)


def naming(kv, capacity, groups, ranks):
    total = kv.shape[0]
    length = total // ranks
    return call(
        functools.partial(naming_kernel, capacity, groups),
        "naming",
        9,
        grid=(ranks,),
        in_specs=[pl.BlockSpec((length, LANES), lambda s: (s, 2 * PAIRS))],
        out_specs=pl.BlockSpec((groups, length, LANES), lambda s: (0, s, 0)),
        out_shape=shaped((groups, total, LANES), bf16),
    )(kv)


def key_value_kernel(x_ref, gain_ref, wk_ref, wv_ref, cos_ref, sin_ref, r_ref, n_ref, kv_ref):
    x = x_ref[...].astype(f32)
    factor = lax.rsqrt(jnp.mean(x * x, axis=1, keepdims=True) + epsilon)
    normed = (x * factor * gain_ref[...]).astype(bf16)
    n_ref[...] = normed
    cosine, sine = cos_ref[...], sin_ref[...]
    key = dot(normed, wk_ref[...])
    for c in range(KVH * HD // LANES):
        part = key[:, c * LANES : (c + 1) * LANES]
        turned = part * cosine + half_swap(part) * sine
        kv_ref[:, c * LANES : (c + 1) * LANES] = turned.astype(bf16)
    kv_ref[:, KVH * HD : 2 * KVH * HD] = dot(normed, wv_ref[...]).astype(bf16)
    kv_ref[:, 2 * KVH * HD :] = r_ref[...]


def key_value(group, length, x, gain, wk, wv, cosine, sine, names):
    first = group * length // ROWS
    width = 2 * KVH * HD + LANES
    return call(
        key_value_kernel,
        "key_value",
        5,
        grid=(length // ROWS,),
        in_specs=[
            row_block(D, first),
            resident((1, D)),
            resident((D, KVH * HD)),
            resident((D, KVH * HD)),
            row_block(LANES, first),
            row_block(LANES, first),
            row_block(LANES),
        ],
        out_specs=[row_block(D), row_block(width)],
        out_shape=[shaped((length, D), bf16), shaped((length, width), bf16)],
    )(x, gain, wk, wv, cosine, sine, names)


def query_kernel(n_ref, wq_ref, cos_ref, sin_ref, q_ref):
    cosine, sine = cos_ref[...], sin_ref[...]
    query = dot(n_ref[...], wq_ref[...])
    for c in range(H * HD // LANES):
        part = query[:, c * LANES : (c + 1) * LANES]
        turned = part * cosine + half_swap(part) * sine
        q_ref[:, c * LANES : (c + 1) * LANES] = turned.astype(bf16) * jnp.asarray(0.125, bf16)


def project_query(group, normed, wq, cosine, sine):
    length = normed.shape[0]
    first = group * length // ROWS
    return call(
        query_kernel,
        "query",
        6,
        grid=(length // ROWS,),
        in_specs=[
            row_block(D),
            resident((D, H * HD)),
            row_block(LANES, first),
            row_block(LANES, first),
        ],
        out_specs=row_block(H * HD),
        out_shape=shaped((length, H * HD), bf16),
    )(normed, wq, cosine, sine)


def stack_heads(ref):
    low = lane_of((ROWS, LANES)) < HD
    parts = [ref[:, c * LANES : (c + 1) * LANES].astype(f32) for c in range(SHARE)]
    rolled0, rolled2 = pltpu.roll(parts[0], HD, 1), pltpu.roll(parts[2], HD, 1)
    zero = jnp.zeros((ROWS, LANES), f32)
    first = [parts[0], rolled0, parts[1]]
    second = [parts[1], rolled2, parts[2]]
    return (
        jnp.concatenate([jnp.where(low, v, zero).astype(bf16) for v in first], axis=0),
        jnp.concatenate([jnp.where(low, zero, v).astype(bf16) for v in second], axis=0),
    )


def unstack_heads(first, second):
    low = lane_of((ROWS, LANES)) < HD
    return (
        jnp.where(low, first[:ROWS], pltpu.roll(first[ROWS : 2 * ROWS], HD, 1)),
        jnp.where(low, first[2 * ROWS :], second[:ROWS]),
        jnp.where(low, pltpu.roll(second[ROWS : 2 * ROWS], HD, 1), second[2 * ROWS :]),
    )


def visit_chunks(block, chunk):
    prompt_blocks = PROMPT // ROWS

    @pl.when(block >= prompt_blocks)
    def _():
        for c in range(PROMPT // (2 * ROWS)):
            chunk(c * 2 * ROWS, 2 * ROWS, False)

    @pl.when(block < prompt_blocks)
    def _():
        def step(c, carry):
            chunk(pl.multiple_of(c * ROWS, ROWS), ROWS, False)
            return carry

        lax.fori_loop(0, block, step, 0)

    @pl.when(block > prompt_blocks)
    def _():
        chunk(pl.multiple_of((block - 1) * ROWS, ROWS), ROWS, True)

    chunk(pl.multiple_of(block * ROWS, ROWS), ROWS, True)


def mask_bias(block, begin, size, start_ref):
    place = begin + lax.broadcasted_iota(jnp.int32, (size, ROWS), 0)
    own = block * ROWS + lax.broadcasted_iota(jnp.int32, (size, ROWS), 1)
    ok = (place <= own) & (place >= start_ref[0, :1, :])
    bias = jnp.where(ok, 0.0, -1e30)
    return jnp.concatenate([bias] * SHARE, axis=1)


def attend_kernel(blocks, q_ref, k_ref, v_ref, start_ref, o_ref, lse_ref, vt_ref, m_ref, l_ref, acc_ref):
    block = expert_rank() * blocks + pl.program_id(1)

    @pl.when(pl.program_id(1) == 0)
    def _():
        vt_ref[...] = jnp.transpose(v_ref[...].astype(f32)).astype(bf16)

    queries = stack_heads(q_ref)
    m_ref[...] = jnp.full_like(m_ref, -1e30)
    l_ref[...] = jnp.zeros_like(l_ref)
    acc_ref[...] = jnp.zeros_like(acc_ref)

    def chunk(begin, size, masked):
        keys = k_ref[pl.ds(begin, size), :]
        values = vt_ref[:, pl.ds(begin, size)]
        bias = mask_bias(block, begin, size, start_ref) if masked else None
        for h in range(2):
            scores = dot_nt(keys, queries[h])
            if masked:
                scores = scores + bias
            before = m_ref[h, :1]
            peak = jnp.maximum(before, jnp.max(scores, axis=0, keepdims=True))
            weight = jnp.exp(scores - peak)
            shrink = jnp.exp(before - peak)
            m_ref[h, :1] = peak
            l_ref[h, :1] = l_ref[h, :1] * shrink + jnp.sum(weight, axis=0, keepdims=True)
            acc_ref[h] = acc_ref[h] * shrink + dot(values, weight.astype(bf16))

    visit_chunks(block, chunk)
    mixed = [jnp.transpose(acc_ref[h] / l_ref[h, :1]) for h in range(2)]
    for c, part in enumerate(unstack_heads(*mixed)):
        o_ref[:, c * LANES : (c + 1) * LANES] = part.astype(bf16)
    for h in range(2):
        total = m_ref[h, :1] + jnp.log(l_ref[h, :1])
        lse_ref[0, 0, h] = jnp.broadcast_to(total, (8, STACK))


def attend(group, query, kv, start_row):
    length = query.shape[0]
    total = kv.shape[0]
    blocks = length // ROWS
    heads = pl.BlockSpec((ROWS, PAIR_Q), lambda p, i: (i, p))
    return call(
        functools.partial(attend_kernel, blocks),
        "attend",
        45,
        grid=(PAIRS, blocks),
        in_specs=[
            heads,
            pl.BlockSpec((total, LANES), lambda p, i: (0, p)),
            pl.BlockSpec((total, LANES), lambda p, i: (0, PAIRS + p)),
            pl.BlockSpec((1, 8, ROWS), lambda p, i: (group, 0, i)),
        ],
        out_specs=[
            heads,
            pl.BlockSpec((1, 1, 2, 8, STACK), lambda p, i: (p, i, 0, 0, 0)),
        ],
        out_shape=[
            shaped(query.shape, bf16),
            shaped((PAIRS, blocks, 2, 8, STACK), f32),
        ],
        scratch_shapes=[
            pltpu.VMEM((LANES, total), bf16),
            pltpu.VMEM((2, 8, STACK), f32),
            pltpu.VMEM((2, 8, STACK), f32),
            pltpu.VMEM((2, LANES, STACK), f32),
        ],
    )(query, kv, kv, start_row)


def attend_back_kernel(
    blocks,
    q_ref,
    g_ref,
    o_ref,
    k_ref,
    v_ref,
    lse_ref,
    start_ref,
    cos_ref,
    sin_ref,
    dq_ref,
    keep_ref,
    send_ref,
    dq_acc,
    dkv_acc,
):
    step = pl.program_id(1)
    block = expert_rank() * blocks + step

    @pl.when(step == 0)
    def _():
        dkv_acc[...] = jnp.zeros_like(dkv_acc)

    dq_acc[...] = jnp.zeros_like(dq_acc)
    queries = stack_heads(q_ref)
    grads = stack_heads(g_ref)
    halves = []
    for c in range(SHARE):
        cols = slice(c * LANES, (c + 1) * LANES)
        product = jnp.transpose(g_ref[:, cols].astype(f32) * o_ref[:, cols].astype(f32))
        halves.append(jnp.sum(product[:HD], axis=0, keepdims=True))
        halves.append(jnp.sum(product[HD:], axis=0, keepdims=True))
    inner = [jnp.concatenate(halves[:SHARE], axis=1), jnp.concatenate(halves[SHARE:], axis=1)]

    def chunk(begin, size, masked):
        keys = k_ref[pl.ds(begin, size), :]
        values = v_ref[pl.ds(begin, size), :]
        bias = mask_bias(block, begin, size, start_ref) if masked else None
        key_sum, value_sum = None, None
        for h in range(2):
            scores = dot_nt(keys, queries[h]) - lse_ref[0, 0, h, :1, :]
            if masked:
                scores = scores + bias
            probs = jnp.exp(scores)
            probs_grad = dot_nt(values, grads[h])
            scores_grad = (probs * (probs_grad - inner[h])).astype(bf16)
            value_part = dot(probs.astype(bf16), grads[h])
            key_part = dot(scores_grad, queries[h])
            key_sum = key_part if key_sum is None else key_sum + key_part
            value_sum = value_part if value_sum is None else value_sum + value_part
            dq_acc[h] += dot_tn(scores_grad, keys)
        dkv_acc[0, pl.ds(begin, size), :] += key_sum
        dkv_acc[1, pl.ds(begin, size), :] += value_sum

    visit_chunks(block, chunk)
    cosine, sine = cos_ref[...], sin_ref[...]
    for c, part in enumerate(unstack_heads(dq_acc[0], dq_acc[1])):
        part = part * 0.125
        turned = part * cosine - half_swap(part) * sine
        dq_ref[:, c * LANES : (c + 1) * LANES] = turned.astype(bf16)

    @pl.when(step == blocks - 1)
    def _():
        length = blocks * ROWS
        own = lax.axis_index("el")
        for chip in range(dkv_acc.shape[1] // (2 * length)):
            mine = pl.multiple_of((2 * chip + own) * length, length)
            other = pl.multiple_of((2 * chip + 1 - own) * length, length)
            for i in range(2):
                keep_ref[chip, i] = dkv_acc[i, pl.ds(mine, length), :].astype(bf16)
                send_ref[chip, i] = dkv_acc[i, pl.ds(other, length), :].astype(bf16)


def attend_back_and_swap(blocks, pairs, columns, *refs):
    away_ref = refs[9]
    here_ref = refs[-5]
    send_sem, recv_sem = refs[-2:]
    at = pl.program_id(0) * blocks + pl.program_id(1)
    peer = {"dl": 1 - lax.axis_index("dl")}
    exchange = pltpu.make_async_remote_copy(
        src_ref=away_ref.at[:, :, columns],
        dst_ref=here_ref.at[:, :, columns],
        send_sem=send_sem,
        recv_sem=recv_sem,
        device_id=peer,
        device_id_type=pl.DeviceIdType.MESH,
    )

    @pl.when(at == 0)
    def _():
        barrier = pltpu.get_barrier_semaphore()
        pl.semaphore_signal(barrier, inc=1, device_id=peer, device_id_type=pl.DeviceIdType.MESH)
        pl.semaphore_wait(barrier, 1)
        exchange.start()

    attend_back_kernel(blocks, *refs[:9], *refs[-8:-5], *refs[-4:-2])

    @pl.when(at == pairs * blocks - 1)
    def _():
        exchange.wait()


def attend_back(
    group, span, query, grad, mixed, kv, lse, start_row, cosine, sine, away, collective, kept
):
    length = query.shape[0]
    total = kv.shape[0]
    blocks = length // ROWS
    first = group * blocks
    chips = total // (2 * length)
    base, pairs = span
    side = pl.BlockSpec((chips, 2, length, LANES), lambda p, i: (0, 0, 0, p))
    heads = pl.BlockSpec((ROWS, PAIR_Q), lambda p, i: (i, base + p))
    table = pl.BlockSpec((ROWS, LANES), lambda p, i: (first + i, 0))
    swaps = [] if away is None else [away[0]]
    if away is None:
        kernel = lambda *refs: attend_back_kernel(blocks, *refs[:9], *refs[-5:])
        extra = {}
    else:
        kernel = functools.partial(attend_back_and_swap, blocks, pairs, away[1])
        extra = dict(collective_id=collective, has_side_effects=True)
    anywhere = pl.BlockSpec(memory_space=pl.ANY)
    return call(
        kernel,
        "attend_back",
        16 * pairs,
        extra,
        grid=(pairs, blocks),
        in_specs=[
            heads,
            heads,
            heads,
            pl.BlockSpec((total, LANES), lambda p, i: (0, base + p)),
            pl.BlockSpec((total, LANES), lambda p, i: (0, PAIRS + base + p)),
            pl.BlockSpec((1, 1, 2, 8, STACK), lambda p, i: (base + p, i, 0, 0, 0)),
            pl.BlockSpec((1, 8, ROWS), lambda p, i: (group, 0, i)),
            table,
            table,
        ]
        + [anywhere] * len(swaps + kept),
        out_specs=[
            heads,
            side,
            side,
        ]
        + [anywhere] * len(swaps),
        input_output_aliases={9 + len(swaps): 0} if kept else {},
        out_shape=[
            shaped(query.shape, bf16),
            shaped((chips, 2, length, pairs * LANES), bf16),
            shaped((chips, 2, length, pairs * LANES), bf16),
        ]
        + [shaped(one.shape, one.dtype) for one in swaps],
        scratch_shapes=[
            pltpu.VMEM((2, STACK, LANES), f32),
            pltpu.VMEM((2, total, LANES), f32),
        ]
        + [pltpu.SemaphoreType.DMA] * (2 * len(swaps)),
    )(query, grad, mixed, kv, kv, lse, start_row, cosine, sine, *swaps, *kept)


def branch_kernel(a_ref, x_ref, wo_ref, gain_ref, wr_ref, m_ref, n_ref, ps_ref):
    middle = x_ref[...].astype(f32) + dot(a_ref[...], wo_ref[...])
    m_ref[...] = middle
    factor = lax.rsqrt(jnp.mean(middle * middle, axis=1, keepdims=True) + epsilon)
    normed = (middle * factor * gain_ref[...]).astype(bf16)
    n_ref[...] = normed
    add_up(ps_ref, fold_rows(router(normed, wr_ref[...])))


def branch(group, attended, x, wo, gain, wr):
    length = attended.shape[0]
    return call(
        branch_kernel,
        "branch",
        6,
        grid=(length // ROWS,),
        in_specs=[
            row_block(H * HD),
            row_block(D, group * length // ROWS),
            resident((H * HD, D)),
            resident((1, D)),
            resident((D, LANES)),
        ],
        out_specs=[row_block(D), row_block(D), pl.BlockSpec((8, LANES), lambda i: (0, 0))],
        out_shape=[
            shaped((length, D), f32),
            shaped((length, D), bf16),
            shaped((8, LANES), f32),
        ],
    )(attended, x, wo, gain, wr)


def router(normed, weight):
    count = EXP_DEV * 2 * lax.axis_size("eh")
    logits = dot(normed, weight)
    logits = jnp.where(lane_of(logits.shape) < count, logits, -1e30)
    powers = jnp.exp(logits - jnp.max(logits, axis=1, keepdims=True))
    return powers / jnp.sum(powers, axis=1, keepdims=True)


def experts_kernel(
    x_ref, c_ref, t_ref, wr_ref, wg_ref, wu_ref, wd_ref, *refs
):
    mix_ref, rows_ref, x_out, c_out, hid_ref, gate_ref, up_ref = refs[-7:]
    x, cot = x_ref[...], c_ref[...]
    x_out[...] = x
    c_out[...] = cot
    level = t_ref[0].astype(f32)
    picked = jnp.where(level > 0.5, router(x, wr_ref[...]), 0.0)
    share = picked / jnp.sum(picked, axis=1, keepdims=True)
    share = jnp.where(level > 1.5, share, 0.0)
    lane = lane_of(share.shape)
    base = EXP_DEV * expert_rank()
    share = pltpu.roll(share, lax.rem(LANES - base, LANES), 1)
    mix, rows = None, None
    gate_grads = jnp.zeros(share.shape, bf16)
    for e in range(EXP_DEV):
        gate = dot(x, wg_ref[e])
        up = dot(x, wu_ref[e])
        hidden_grad = dot(cot, wd_ref[e])
        sigmoid = jax.nn.sigmoid(gate)
        active = gate * sigmoid
        hidden = active * up
        inner = jnp.sum(hidden * hidden_grad, axis=1, keepdims=True)
        coarse = inner.astype(bf16)
        fine = (inner - coarse.astype(f32)).astype(bf16)
        gate_grads = jnp.where(lane == base + e, coarse, gate_grads)
        gate_grads = jnp.where(lane == LANES // 2 + base + e, fine, gate_grads)
        weight = share[:, e : e + 1]
        scaled = (hidden * weight).astype(bf16)
        hidden_grad = hidden_grad * weight
        up_grad = (hidden_grad * active).astype(bf16)
        gate_grad = (hidden_grad * up * sigmoid * (1.0 + gate * (1.0 - sigmoid))).astype(bf16)
        cols = slice(e * FF, (e + 1) * FF)
        hid_ref[:, cols] = scaled
        gate_ref[:, cols] = gate_grad
        up_ref[:, cols] = up_grad
    for e in range(EXP_DEV):
        cols = slice(e * FF, (e + 1) * FF)
        mix_part = dot_nt(hid_ref[:, cols], wd_ref[e])
        rows_part = dot_nt(gate_ref[:, cols], wg_ref[e]) + dot_nt(up_ref[:, cols], wu_ref[e])
        mix = mix_part if mix is None else mix + mix_part
        rows = rows_part if rows is None else rows + rows_part
    mix_ref[...] = mix.astype(bf16)
    rows_ref[:, :D] = rows.astype(bf16)
    rows_ref[:, D:] = gate_grads


def experts_pass(group, groups, x, cot, level, wr, wg, wu, wd, kept):
    count = x.shape[0]
    first = group * count // ROWS
    whole = groups * count
    side = pl.BlockSpec(memory_space=pl.ANY)
    widths = [D, D, EXP_DEV * FF, EXP_DEV * FF, EXP_DEV * FF]
    return call(
        experts_kernel,
        "experts",
        113,
        grid=(count // ROWS,),
        in_specs=[
            row_block(D),
            row_block(D),
            pl.BlockSpec((1, ROWS, LANES), lambda i: (group, i, 0)),
            resident((D, LANES)),
            resident((EXP_DEV, D, FF)),
            resident((EXP_DEV, D, FF)),
            resident((EXP_DEV, D, FF)),
        ]
        + [side] * len(kept),
        out_specs=[row_block(D), row_block(D + LANES)]
        + [row_block(width, first) for width in widths],
        out_shape=[
            shaped((count, D), bf16),
            shaped((count, D + LANES), bf16),
        ]
        + [shaped((whole, width), bf16) for width in widths],
        input_output_aliases={7 + i: 2 + i for i in range(len(kept))},
    )(x, cot, level, wr, wg, wu, wd, *kept)


def norm_back(grad, normed, factor, gain):
    scaled = grad * gain
    return factor * (scaled - normed * jnp.mean(scaled * normed, axis=1, keepdims=True))


def fold_rows(values):
    return jnp.sum(values.reshape(values.shape[0] // 8, 8, values.shape[1]), axis=0)


def add_up(ref, part):
    @pl.when(pl.program_id(0) == 0)
    def _():
        ref[...] = part

    @pl.when(pl.program_id(0) > 0)
    def _():
        ref[...] += part


def middle_kernel(
    r_ref, t_ref, m_ref, n_ref, c_ref, gain_ref, wr_ref, wo_ref,
    mg_ref, b_ref, ag_ref, l_ref, dg_ref,
):
    probs = router(n_ref[...], wr_ref[...])
    level = t_ref[0].astype(f32)
    sel = jnp.where(level > 0.5, 1.0, 0.0)
    gate_grad = r_ref[:, D:].astype(f32)
    gate_grad = gate_grad + pltpu.roll(gate_grad, LANES // 2, 1)
    gate_grad = jnp.where(level > 1.5, gate_grad, 0.0)
    picked = probs * sel
    total = jnp.sum(picked, axis=1, keepdims=True)
    share = picked / total
    inner = jnp.sum(gate_grad * share, axis=1, keepdims=True)
    probs_grad = (gate_grad - inner) / total * sel
    logits_grad = probs * (probs_grad - jnp.sum(probs_grad * probs, axis=1, keepdims=True))
    coarse = logits_grad.astype(bf16)
    fine = (logits_grad - coarse.astype(f32)).astype(bf16)
    l_ref[:, :LANES] = coarse
    l_ref[:, LANES:] = fine
    grad = r_ref[:, :D].astype(f32) + dot_nt(coarse, wr_ref[...]) + dot_nt(fine, wr_ref[...])
    middle = m_ref[...]
    factor = lax.rsqrt(jnp.mean(middle * middle, axis=1, keepdims=True) + epsilon)
    normed = middle * factor
    add_up(dg_ref, fold_rows(grad * normed))
    middle_grad = c_ref[...].astype(f32) + norm_back(grad, normed, factor, gain_ref[...])
    mg_ref[...] = middle_grad
    low = middle_grad.astype(bf16)
    b_ref[...] = low
    ag_ref[...] = dot_nt(low, wo_ref[...]).astype(bf16)


def middle_back(group, rows, level, middle, normed, cot, gain, wr, wo):
    length = rows.shape[0]
    first = group * length // ROWS
    corner = lambda width: pl.BlockSpec((8, width), lambda i: (0, 0))
    return call(
        middle_kernel,
        "middle_back",
        8,
        grid=(length // ROWS,),
        in_specs=[
            row_block(D + LANES),
            pl.BlockSpec((1, ROWS, LANES), lambda i: (group, i, 0)),
            row_block(D), row_block(D), row_block(D, first),
            resident((1, D)), resident((D, LANES)), resident((H * HD, D)),
        ],
        out_specs=[
            row_block(D), row_block(D), row_block(H * HD), row_block(2 * LANES),
            corner(D),
        ],
        out_shape=[
            shaped((length, D), f32),
            shaped((length, D), bf16),
            shaped((length, H * HD), bf16),
            shaped((length, 2 * LANES), bf16),
            shaped((8, D), f32),
        ],
    )(rows, level, middle, normed, cot, gain, wr, wo)


def input_kernel(
    dq_ref, dk_ref, dv_ref, x_ref, mg_ref, cos_ref, sin_ref, gain_ref, wq_ref, wk_ref, wv_ref,
    out_ref, dk_out, dg_ref,
):
    cosine, sine = cos_ref[...], sin_ref[...]
    for c in range(KVH * HD // LANES):
        part = dk_ref[0, :, c * LANES : (c + 1) * LANES].astype(f32)
        turned = part * cosine - half_swap(part) * sine
        dk_out[:, c * LANES : (c + 1) * LANES] = turned.astype(bf16)
    grad = dot_nt(dq_ref[...], wq_ref[...])
    grad = grad + dot_nt(dk_out[...], wk_ref[...])
    grad = grad + dot_nt(dv_ref[0], wv_ref[...])
    x = x_ref[...].astype(f32)
    factor = lax.rsqrt(jnp.mean(x * x, axis=1, keepdims=True) + epsilon)
    normed = x * factor
    add_up(dg_ref, fold_rows(grad * normed))
    out_ref[...] = mg_ref[...] + norm_back(grad, normed, factor, gain_ref[...])


def input_back(group, groups, dq, dkv, x, middle_grad, cosine, sine, gain, wq, wk, wv, kept):
    length = dq.shape[0]
    first = group * length // ROWS
    kernel = lambda *refs: input_kernel(*refs[:11], *refs[-3:])
    return call(
        kernel,
        "input_back",
        8,
        grid=(length // ROWS,),
        in_specs=[
            row_block(H * HD),
            pl.BlockSpec((1, ROWS, KVH * HD), lambda i: (0, i, 0)),
            pl.BlockSpec((1, ROWS, KVH * HD), lambda i: (1, i, 0)),
            row_block(D, first),
            row_block(D),
            row_block(LANES, first),
            row_block(LANES, first),
            resident((1, D)),
            resident((D, H * HD)),
            resident((D, KVH * HD)),
            resident((D, KVH * HD)),
        ]
        + [pl.BlockSpec(memory_space=pl.ANY)] * len(kept),
        out_specs=[
            row_block(D, first),
            row_block(KVH * HD),
            pl.BlockSpec((8, D), lambda i: (0, 0)),
        ],
        out_shape=[
            shaped((groups * length, D), f32),
            shaped((length, KVH * HD), bf16),
            shaped((8, D), f32),
        ],
        input_output_aliases={11: 0} if kept else {},
    )(dq, dkv, dkv, x, middle_grad, cosine, sine, gain, wq, wk, wv, *kept)


def transpose_into(turned, lefts):
    length = lefts[0].shape[0]
    for g, left in enumerate(lefts):
        for c in range(0, D, 2 * LANES):
            part = left[:, c : c + 2 * LANES].astype(f32)
            turned[c : c + 2 * LANES, g * length : (g + 1) * length] = jnp.transpose(part).astype(
                bf16
            )


def out_kernel(groups, *refs):
    lefts, rights = refs[:groups], refs[groups : 2 * groups]
    out_ref, turned = refs[-2:]
    length = lefts[0].shape[0]

    @pl.when(pl.program_id(0) == 0)
    def _():
        transpose_into(turned, lefts)

    total = None
    for g in range(groups):
        part = dot(turned[:, g * length : (g + 1) * length], rights[g][...])
        total = part if total is None else total + part
    out_ref[...] = total.astype(bf16)


def out_gradient(lefts, rights):
    groups, length = len(lefts), lefts[0].shape[0]
    width = 4 * LANES
    return call(
        functools.partial(out_kernel, groups),
        "out_grad",
        10,
        grid=(D // width,),
        in_specs=[resident((length, D))] * groups
        + [pl.BlockSpec((length, width), lambda i: (0, i))] * groups,
        out_specs=pl.BlockSpec((D, width), lambda i: (0, i)),
        out_shape=shaped((D, D), bf16),
        scratch_shapes=[pltpu.VMEM((D, groups * length), bf16)],
    )(*lefts, *rights)


def dense_kernel(groups, sizes, *refs):
    data, chips, shard, width, full, late = sizes
    lefts, queries, keys, values = (refs[i * groups : (i + 1) * groups] for i in range(4))
    narrow_ref, late_ref, out_ref = refs[4 * groups : 4 * groups + 3]
    (turned, keep1, send1, got1, keep2, send2, got2, sum2, got3, sum3, got4, sum4, near5, far5,
     wide2, wide3, keep6, send6, got6) = refs[4 * groups + 3 : 4 * groups + 22]
    sems = refs[4 * groups + 22 :]
    half = width // 2
    length = lefts[0].shape[0]
    ranks = 2 * chips
    dh, dl, eh, el = (lax.axis_index(name) for name in ("dh", "dl", "eh", "el"))

    def near(hop, core):
        return {"eh": lax.rem(eh + hop, chips), "el": core}

    peers = [{"el": 1 - el}, {"dl": 1 - dl}]
    for hop in range(1, chips):
        peers.append(near(hop, el))
    for hop in range(1, data):
        peers.append({"dh": lax.rem(dh + hop, data)})
    barrier = pltpu.get_barrier_semaphore()
    for peer in peers:
        pl.semaphore_signal(barrier, inc=1, device_id=peer, device_id_type=pl.DeviceIdType.MESH)
    transpose_into(turned, lefts)
    pl.semaphore_wait(barrier, len(peers))

    def copy(source, target, phase, k, lane, peer):
        return pltpu.make_async_remote_copy(
            src_ref=source,
            dst_ref=target,
            send_sem=sems[2 * phase].at[k, lane],
            recv_sem=sems[2 * phase + 1].at[k, lane],
            device_id=peer,
            device_id_type=pl.DeviceIdType.MESH,
        )

    def crossed(k):
        return k < full and k % 2 == 1

    def slot(k):
        return k // 2 if k < full else (full + 1) // 2 + k - full

    def copies(phase, k):
        if phase == 0:
            return [copy(send1.at[k], got1.at[k], 0, k, 0, {"el": 1 - el})]
        if phase == 1:
            source, target = (send6, got6) if crossed(k) else (send2, got2)
            at = k // 2
            return [
                copy(source.at[at, hop - 1], target.at[at, hop - 1], 1, k, hop - 1, near(hop, el))
                for hop in range(1, chips)
            ]
        if phase == 2:
            if crossed(k):
                at = k // 2
                return [copy(wide2.at[at, 1 - dl], wide3.at[at], 2, k, 0, {"dl": 1 - dl})]
            at = slot(k)
            return [copy(sum2.at[at, 1 - dl], got3.at[at], 2, k, 0, {"dl": 1 - dl})]
        if phase == 3:
            found = []
            for hop in range(1, data):
                away = lax.rem(dh + hop, data)
                found.append(
                    copy(sum3.at[k, away], got4.at[k, hop - 1], 3, k, hop - 1, {"dh": away})
                )
            return found
        if phase == 4:
            return [
                copy(sum4.at[k], near5.at[k, eh], 4, k, hop - 1, near(hop, el))
                for hop in range(1, chips)
            ]
        return [copy(near5.at[k], far5.at[k], 5, k, 0, {"el": 1 - el})]

    def start(phase, k):
        for one in copies(phase, k):
            one.start()

    def arrived(phase, k):
        for one in copies(phase, k):
            one.wait_recv()

    def finish_shard(k):
        base = k * width if k < full else full * width + (k - full) * LANES

        def put(side, chip, block):
            place = side * chips + chip
            place = place * LANES if k < full else place * late * LANES
            at = pl.multiple_of(base + place, LANES)
            out_ref[:, pl.ds(at, LANES)] = block.astype(f32)

        for chip in range(chips):
            put(el, chip, near5[k, chip])
            put(1 - el, chip, far5[k, chip])

    def piece(column):
        size = KVH * HD
        if column >= H * HD + 2 * size:
            if column > H * HD + 2 * size:
                return jnp.zeros((D, size), bf16)
            part = jnp.transpose(narrow_ref[...])
            return jnp.concatenate([part, jnp.zeros((D, size - LANES), f32)], axis=1).astype(bf16)
        total = None
        for g in range(groups):
            if column < H * HD:
                block = queries[g][:, column : column + size]
            elif column < H * HD + size:
                block = keys[g][...]
            else:
                block = values[g][1]
            one = dot(turned[:, g * length : (g + 1) * length], block)
            total = one if total is None else total + one
        return total.astype(bf16)

    def stage_compute(k):
        if k < full:
            part = [piece(k * width + c) for c in range(0, width, KVH * HD)]
            part = part[0] if len(part) == 1 else jnp.concatenate(part, axis=1)

            @pl.when(el == 0)
            def _():
                keep1[k] = part[:, :half]
                send1[k] = part[:, half:]

            @pl.when(el == 1)
            def _():
                keep1[k] = part[:, half:]
                send1[k] = part[:, :half]

            start(0, k)

    def hand_out(block, chip, keep, send):
        hop = lax.rem(chip + chips - eh, chips)

        @pl.when(hop == 0)
        def _():
            keep[...] = block

        @pl.when(hop > 0)
        def _():
            send[hop - 1] = block

    def chip_columns(chip):
        return slice(chip * LANES, (chip + 1) * LANES)

    def stage_core(k):
        arrived(0, k)
        met = (keep1[k].astype(f32) + got1[k].astype(f32)).astype(bf16)
        at = k // 2
        if crossed(k):
            for far in range(data):
                for side in range(2):
                    first = (2 * far + side) * shard
                    wide2[at, side, far] = met[first : first + shard]
            start(2, k)
        else:
            for chip in range(chips):
                hand_out(met[:, chip_columns(chip)], chip, keep2.at[at], send2.at[at])
            start(1, k)

    def stage_second(k):
        at = k // 2
        if crossed(k):
            arrived(2, k)
            met = (wide2[at, dl].astype(f32) + wide3[at].astype(f32)).astype(bf16)
            for chip in range(chips):
                hand_out(met[:, :, chip_columns(chip)], chip, keep6.at[at], send6.at[at])
            start(1, k)
        else:
            arrived(1, k)
            total = keep2[at].astype(f32)
            for hop in range(1, chips):
                total = total + got2[at, hop - 1].astype(f32)
            spread(k, total.astype(bf16))

    def spread(k, total):
        for far in range(data):
            for side in range(2):
                first = (2 * far + side) * shard
                sum2[slot(k), side, far] = total[first : first + shard]
        start(2, k)

    def stage_third(k):
        if crossed(k):
            at = k // 2
            arrived(1, k)
            total = keep6[at].astype(f32)
            for hop in range(1, chips):
                total = total + got6[at, hop - 1].astype(f32)
        else:
            at = slot(k)
            arrived(2, k)
            total = sum2[at, dl].astype(f32) + got3[at].astype(f32)
        sum3[k] = total.astype(bf16)
        start(3, k)

    def stage_far(k):
        arrived(3, k)
        total = sum3[k, dh].astype(f32)
        for hop in range(1, data):
            total = total + got4[k, hop - 1].astype(f32)
        total = total.astype(bf16)
        sum4[k] = total
        near5[k, eh] = total
        start(4, k)

    def stage_gather(k):
        arrived(4, k)
        start(5, k)

    def stage_last(k):
        arrived(5, k)
        finish_shard(k)

    everything = list(range(full, full + late)) + list(range(full))
    for k in range(full, full + late):
        first = (k - full) * LANES
        spread(k, late_ref[:, first : first + LANES])
    stages = (
        stage_compute,
        stage_core,
        stage_second,
        stage_third,
        stage_far,
        stage_gather,
        stage_last,
    )
    for step in range(full + len(stages) - 1):
        for delay, stage in enumerate(stages):
            if 0 <= step - delay < full:
                stage(step - delay)
        if step < 4:
            for k in range(full, full + late):
                stages[3 + step](k)
    for k in everything:
        for phase in range(6):
            if k < full or phase > 1:
                for one in copies(phase, k):
                    one.wait_send()


def dense_gradient(lefts, queries, keys, values, narrow, late_part):
    groups = len(lefts)
    data, chips = lax.axis_size("dh"), lax.axis_size("eh")
    shard = D // (2 * data)
    width = 2 * chips * LANES
    columns = H * HD + 2 * KVH * HD
    full = -(-(columns + LANES) // width)
    late = late_part.shape[1] // LANES
    total = full + late
    half, ranks = width // 2, 2 * chips
    sizes = (data, chips, shard, width, full, late)
    lanes = [1, chips - 1, 1, data - 1, chips - 1, 1]
    even, odd = (full + 1) // 2, full // 2
    sems = []
    for count in lanes:
        sems += [pltpu.SemaphoreType.DMA((total, count))] * 2
    operands = [*lefts, *queries, *keys, *values, narrow, late_part]
    whole = pl.BlockSpec(memory_space=pltpu.VMEM)
    return pl.pallas_call(
        functools.partial(dense_kernel, groups, sizes),
        name="dense_grad",
        in_specs=[whole] * len(operands),
        out_specs=whole,
        out_shape=shaped((shard, full * width + late * ranks * LANES), f32),
        scratch_shapes=[
            pltpu.VMEM((D, groups * lefts[0].shape[0]), bf16),
            pltpu.VMEM((full, D, half), bf16),
            pltpu.VMEM((full, D, half), bf16),
            pltpu.VMEM((full, D, half), bf16),
            pltpu.VMEM((even, D, LANES), bf16),
            pltpu.VMEM((even, chips - 1, D, LANES), bf16),
            pltpu.VMEM((even, chips - 1, D, LANES), bf16),
            pltpu.VMEM((even + late, 2, data, shard, LANES), bf16),
            pltpu.VMEM((even + late, data, shard, LANES), bf16),
            pltpu.VMEM((total, data, shard, LANES), bf16),
            pltpu.VMEM((total, data - 1, shard, LANES), bf16),
            pltpu.VMEM((total, shard, LANES), bf16),
            pltpu.VMEM((total, chips, shard, LANES), bf16),
            pltpu.VMEM((total, chips, shard, LANES), bf16),
            pltpu.VMEM((odd, 2, data, shard, half), bf16),
            pltpu.VMEM((odd, data, shard, half), bf16),
            pltpu.VMEM((odd, data, shard, LANES), bf16),
            pltpu.VMEM((odd, chips - 1, data, shard, LANES), bf16),
            pltpu.VMEM((odd, chips - 1, data, shard, LANES), bf16),
        ]
        + sems,
        cost_estimate=pl.CostEstimate(
            flops=int(80 * 9e8), bytes_accessed=0, transcendentals=0
        ),
        compiler_params=pltpu.CompilerParams(
            vmem_limit_bytes=VMEM_LIMIT, collective_id=0, has_side_effects=True
        ),
    )(*operands)


def widen(values):
    return jnp.pad(values, ((0, 0), (0, LANES - values.shape[1])))


def swap(values, axis):
    return lax.ppermute(values, axis, [(0, 1), (1, 0)])


def pick(values, index):
    return lax.dynamic_index_in_dim(values, index, 1, keepdims=False)


def pair_slices(values, shard):
    parts = values.reshape(-1, 2, shard, values.shape[1])
    own = lax.axis_index("dl")
    return pick(parts, own), pick(parts, 1 - own)


def pair_parts(values, shard):
    own, away = pair_slices(values, shard)
    return own, swap(away, "dl")


def far_sum(own, met):
    met = (own + met).reshape(-1, own.shape[2])
    return lax.psum_scatter(met, "dh", scatter_dimension=0, tiled=True)


def take(values, axis, index):
    return lax.dynamic_index_in_dim(values, index, axis, keepdims=False)


def chip_sum(met):
    chips = lax.axis_size("eh")
    chip = lax.axis_index("eh")
    total = take(met, 0, chip)
    for hop in range(1, chips):
        order = [(i, (i + hop) % chips) for i in range(chips)]
        away = take(met, 0, lax.rem(chip + hop, chips))
        total = total + lax.ppermute(away, "eh", order)
    return total


def cut(array, index, size):
    return lax.dynamic_slice_in_dim(array, index * size, size, 1)


def column_core_sum(values):
    half = values.shape[1] // 2
    own = lax.axis_index("el")
    return cut(values, own, half) + swap(cut(values, 1 - own, half), "el")


def column_chip_sum(met):
    chips, chip = lax.axis_size("eh"), lax.axis_index("eh")
    size = met.shape[1] // chips
    total = cut(met, chip, size)
    for hop in range(1, chips):
        order = [(i, (i + hop) % chips) for i in range(chips)]
        away = cut(met, lax.rem(chip + hop, chips), size)
        total = total + lax.ppermute(away, "eh", order)
    return total


def sum_steps():
    for axis in ("el", "eh", "dl", "dh"):
        count = lax.axis_size(axis)
        hop = 1
        while hop < count:
            order = [(i, i ^ hop) for i in range(count)]
            yield lambda v, axis=axis, order=order: v + lax.ppermute(v, axis, order)
            hop *= 2


def together(*values):
    return lax.optimization_barrier(values)


def on_device(
    tokens,
    segments,
    routes,
    cotangent,
    attention_gain,
    query_weight,
    key_weight,
    value_weight,
    out_weight,
    mixture_gain,
    router_weight,
    gate_weight,
    up_weight,
    down_weight,
):
    groups, length, _ = tokens.shape
    each = range(groups)
    rows = groups * length
    ranks = lax.axis_size("eh") * 2
    dp_ranks = lax.axis_size("dh") * 2
    rank = expert_rank()
    experts = EXP_DEV * ranks
    capacity = (rows * TOPK * 5 // (4 * experts) + 7) // 8 * 8
    all_tokens = rows * dp_ranks * ranks
    first_row = rank * length
    shard = D // dp_ranks

    seg_full = jnp.concatenate([jnp.full((groups, PROMPT), -1, jnp.int32), segments], axis=1)
    seg_own = lax.dynamic_slice_in_dim(seg_full, first_row, length, 1)
    earlier = jnp.sum((segments[:, None, :] < seg_own[:, :, None]).astype(jnp.int32), axis=2)
    position = first_row + jnp.arange(length, dtype=jnp.int32)[None, :]
    place = position - earlier
    start = jnp.where(position >= PROMPT, PROMPT + earlier, 0)
    half = HD // 2
    lane = jnp.arange(LANES, dtype=jnp.int32)
    frequency = jnp.exp(-math.log(rope_base) * (lane % half).astype(f32) / half)
    angles = place.astype(f32).reshape(rows, 1) * frequency
    cosine = jnp.cos(angles)
    sine = jnp.sin(angles) * jnp.where(lane % HD < half, -1.0, 1.0)
    start_row = jnp.broadcast_to(start[:, None, :], (groups, 8, length))

    names = jnp.concatenate([routes[g] for g in each], axis=1).astype(bf16)
    names = widen(names)
    cot_rows = cotangent.reshape(rows, D)
    cot_all = [lax.all_gather(cotangent[g], EXPERT, axis=0, tiled=True) for g in each]

    x = tokens.reshape(rows, D)
    gain_a = attention_gain.reshape(1, D)
    gain_b = mixture_gain.reshape(1, D)
    router_wide = widen(router_weight)
    normed, query, kv = [None] * groups, [None] * groups, [None] * groups
    for g in each:
        normed[g], kv_own = key_value(
            g, length, x, gain_a, key_weight, value_weight, cosine, sine, names
        )
        kv[g] = lax.all_gather(kv_own, EXPERT, axis=0, tiled=True)
    for g in each:
        query[g] = project_query(g, normed[g], query_weight, cosine, sine)
    level = naming(kv[groups - 1], capacity, groups, ranks)
    level_own = lax.dynamic_slice_in_dim(level, first_row, length, 1)
    kv[0], query = together(kv[0], query)
    attended, lse = [None] * groups, [None] * groups
    middle, hidden_low, hidden_all = [None] * groups, [None] * groups, [None] * groups
    probs_local = 0.0
    for g in each:
        attended[g], lse[g] = attend(g, query[g], kv[g], start_row)
        if g == groups - 1:
            attended[g], cot_all[0] = together(attended[g], cot_all[0])
        middle[g], hidden_low[g], probs_part = branch(
            g, attended[g], x, out_weight, gain_b, router_wide
        )
        probs_local += jnp.sum(probs_part, axis=0)
        hidden_all[g] = lax.all_gather(hidden_low[g], EXPERT, axis=0, tiled=True)

    counts = jnp.sum((level_own > 0.5).astype(f32), axis=(0, 1))
    stats = jnp.stack([counts, probs_local])[:, :experts]
    steps = sum_steps()

    def beside(value, stats):
        step = next(steps, None)
        return (value, stats) if step is None else together(value, step(stats))

    kept, rows_back, mixture = [], [], []
    for g in each:
        if g > 0:
            kept[0], cot_all[g] = together(kept[0], cot_all[g])
            hidden_all[g], stats = beside(hidden_all[g], stats)
        mix, rows_grad, *kept = experts_pass(
            g, groups, hidden_all[g], cot_all[g], level, router_wide,
            gate_weight, up_weight, down_weight, kept,
        )
        rows_back.append(lax.psum_scatter(rows_grad, EXPERT, scatter_dimension=0, tiled=True))
        mixture.append(mix)
        if g < groups - 1:
            mixture[g] = lax.psum_scatter(mix, EXPERT, scatter_dimension=0, tiled=True)
    x_all, cot_both, hidden, gate_back, up_back = kept
    hidden, mixture[0] = together(hidden, mixture[0])
    hidden, stats = beside(hidden, stats)
    down_local = dot_tn(cot_both, hidden).astype(bf16)
    x_all, down_local = together(x_all, down_local)
    gate_back, stats = beside(gate_back, stats)
    gate_local = dot_tn(x_all, gate_back).astype(bf16)
    up_back, gate_local = together(up_back, gate_local)
    gate_own, gate_met = pair_parts(gate_local, shard)
    up_back, mix = together(up_back, mixture[-1])
    mixture[-1] = lax.psum_scatter(mix, EXPERT, scatter_dimension=0, tiled=True)
    up_back, stats = beside(up_back, stats)
    up_local = dot_tn(x_all, up_back).astype(bf16)
    rows_back[0], up_local = together(rows_back[0], up_local)
    rows_back[0], stats = beside(rows_back[0], stats)
    for step in steps:
        stats = step(stats)
    expert_load = stats[0] * experts / (all_tokens * TOPK)
    prob_mean = stats[1] * experts / all_tokens
    balance_loss = jnp.sum(expert_load * prob_mean) / experts

    def by_expert(part):
        return jnp.stack([part[:, e * FF : (e + 1) * FF] for e in range(EXP_DEV)]).astype(f32)

    middle_grad, branch_grad, attended_grad, logits_grad, dq, dkv = (
        [None] * groups for _ in range(6)
    )
    gain_b_local, last = 0.0, groups - 1
    down_far = lax.psum_scatter(down_local, "dh", scatter_dimension=0, tiled=True)
    for g in each:
        middle_grad[g], branch_grad[g], attended_grad[g], logits_grad[g], gain_part = middle_back(
            g, rows_back[g], level_own, middle[g], hidden_low[g], cot_rows,
            gain_b, router_wide, out_weight,
        )
        gain_b_local += jnp.sum(gain_part, axis=0)
    out_local = out_gradient(attended, branch_grad)
    fill = -D % (ranks * LANES)
    out_local = jnp.pad(out_local, ((0, 0), (0, fill)))
    attended_grad[0], out_local = together(attended_grad[0], out_local)
    cut_at = 3 * FF
    up_own, up_away = pair_slices(up_local, shard)
    swaps = [(up_away, slice(0, cut_at)), (up_away, slice(cut_at, EXP_DEV * FF))]
    out_met = column_core_sum(out_local)
    for g in each:
        pieces, kept = [], []
        here = [] if g == 0 else here
        spans = [(0, PAIRS)] if g < last else [(0, PAIRS // 2), (PAIRS // 2, PAIRS // 2)]
        for at, span in enumerate(spans):
            if g == last and at == 0:
                dq[0], gate_own = together(dq[0], gate_own)
                attended_grad[g], out_met, dq[0], gate_own, gate_met, down_far = together(
                    attended_grad[g], out_met, dq[0], gate_own, gate_met, down_far
                )
                gate_part = far_sum(gate_own, gate_met)
                down_own, down_away = pair_slices(down_far, shard)
                swaps.append((down_away, slice(0, EXP_DEV * FF)))
                out_part = column_chip_sum(out_met)
            if g == last and at == 1:
                up_met = jnp.concatenate([here[0][..., :cut_at], here[1][..., cut_at:]], axis=2)
                up_met = up_own + up_met
                kept, dkv[0], pieces[0], up_met, mixture[last] = together(
                    kept, dkv[0], pieces[0], up_met, mixture[last]
                )
                up_part = lax.psum_scatter(
                    up_met.reshape(-1, up_met.shape[2]), "dh", scatter_dimension=0, tiled=True
                )
            turn = len(here)
            grad, keep_part, send_part, *arrived = attend_back(
                g, span, query[g], attended_grad[g], attended[g], kv[g], lse[g], start_row,
                cosine, sine, swaps[turn] if turn < len(swaps) else None, 1 + turn, kept,
            )
            here += arrived
            kept = [grad]
            if g == last and at == 1:
                keep_part, dq[0] = together(keep_part, dq[0])
                down_part = (down_own + here[2])[0]
            pieces.append(keep_part + swap(send_part, "el"))
            if g == last and at == 1:
                pieces[1], dq[0] = together(pieces[1], dq[0])
        dq[g] = kept[0]
        pieces = [chip_sum(piece) for piece in pieces]
        dkv[g] = pieces[0] if len(pieces) == 1 else jnp.concatenate(pieces, axis=2)
    output = jnp.stack(
        [(middle[g] + mixture[g].astype(f32)).astype(bf16) for g in each]
    )

    kept, turned_dk, gain_a_local = [], [None] * groups, 0.0
    for g in each:
        input_grad, turned_dk[g], gain_part = input_back(
            g, groups, dq[g], dkv[g], x, middle_grad[g], cosine, sine,
            gain_a, query_weight, key_weight, value_weight, kept,
        )
        kept = [input_grad]
        gain_a_local += jnp.sum(gain_part, axis=0)
    router_parts = sum(dot_tn(logits_grad[g], hidden_low[g]) for g in each)
    router_local = (router_parts[:LANES] + router_parts[LANES:])[:experts]
    narrow = jnp.concatenate(
        [
            router_local,
            gain_a_local[None, :],
            gain_b_local[None, :],
            jnp.zeros((LANES - experts - 2, D), f32),
        ],
        axis=0,
    )
    narrow, up_part = together(narrow, up_part)
    dense = dense_gradient(normed, dq, turned_dk, dkv, narrow, out_part)
    first = dense.shape[1] - D - fill
    out_grad = dense[:, first : first + D]
    down_weight_grad, gate_weight_grad, up_weight_grad = (
        by_expert(part) for part in (down_part, gate_part, up_part)
    )
    spans = [H * HD, KVH * HD, KVH * HD, experts, 1, 1]
    pieces, begin = [], 0
    for span in spans:
        pieces.append(dense[:, begin : begin + span])
        begin += span
    query_grad, key_grad, value_grad, router_grad, gain_a_grad, gain_b_grad = pieces
    return (
        output,
        input_grad.reshape(groups, length, D),
        gain_a_grad[:, 0],
        query_grad,
        key_grad,
        value_grad,
        out_grad,
        gain_b_grad[:, 0],
        router_grad,
        gate_weight_grad,
        up_weight_grad,
        down_weight_grad,
        expert_load,
        prob_mean,
        balance_loss,
    )


def solution(mesh):
    dp_ranks, ranks = mesh.devices.shape
    fine = Mesh(
        mesh.devices.reshape(dp_ranks // 2, 2, ranks // 2, 2), ("dh", "dl", "eh", "el")
    )
    return jax.shard_map(
        on_device,
        mesh=fine,
        in_specs=(
            P(DATA, EXPERT, None),
            P(DATA, None),
            P(DATA, EXPERT, None),
            P(DATA, EXPERT, None),
            P(),
            P(),
            P(),
            P(),
            P(),
            P(),
            P(),
            P(EXPERT, None, None),
            P(EXPERT, None, None),
            P(EXPERT, None, None),
        ),
        out_specs=(
            P(DATA, EXPERT, None),
            P(DATA, EXPERT, None),
            P(DATA),
            P(DATA, None),
            P(DATA, None),
            P(DATA, None),
            P(DATA, None),
            P(DATA),
            P(DATA, None),
            P(EXPERT, DATA, None),
            P(EXPERT, DATA, None),
            P(EXPERT, DATA, None),
            P(),
            P(),
            P(),
        ),
        check_vma=False,
    )
```

```python
import functools
import math

import jax
import jax.numpy as jnp
from jax import lax
from jax.experimental import pallas as pl
from jax.experimental.pallas import tpu as pltpu
from jax.sharding import Mesh
from jax.sharding import PartitionSpec as P

D = 1536
H = 24
KVH = 8
HD = 64
FF = 512
TOPK = 8
EXP_DEV = 5
PROMPT = 1024
LANES = 128
PAIRS = KVH // 2
SHARE = H // KVH
PAIR_Q = 2 * SHARE * HD
ROWS = 256
STACK = SHARE * ROWS
EXPERT = ("eh", "el")
DATA = ("dh", "dl")
VMEM_LIMIT = 63 * 1024 * 1024

epsilon = 1e-05
rope_base = 10000.0
f32 = jnp.float32
bf16 = jnp.bfloat16


def dot(a, b):
    return lax.dot_general(a, b, (((1,), (0,)), ((), ())), preferred_element_type=f32)


def dot_nt(a, b):
    return lax.dot_general(a, b, (((1,), (1,)), ((), ())), preferred_element_type=f32)


def dot_tn(a, b):
    return lax.dot_general(a, b, (((0,), (0,)), ((), ())), preferred_element_type=f32)


def expert_rank():
    return lax.axis_index("eh") * 2 + lax.axis_index("el")


def call(kernel, name, micros, extra=None, **more):
    cost = pl.CostEstimate(flops=int(micros * 2.5e8), bytes_accessed=0, transcendentals=0)
    return pl.pallas_call(
        kernel,
        name=name,
        cost_estimate=cost,
        compiler_params=pltpu.CompilerParams(vmem_limit_bytes=VMEM_LIMIT, **(extra or {})),
        **more,
    )


def shaped(shape, dtype):
    return jax.ShapeDtypeStruct(shape, dtype)


def lane_of(shape):
    return lax.broadcasted_iota(jnp.int32, shape, len(shape) - 1)


def half_swap(values):
    lower = lane_of(values.shape) % HD < HD // 2
    return jnp.where(
        lower, pltpu.roll(values, LANES - HD // 2, 1), pltpu.roll(values, HD // 2, 1)
    )


def resident(shape):
    zeros = (0,) * len(shape)
    return pl.BlockSpec(shape, lambda *_: zeros, pipeline_mode=pl.Buffered(1))


def row_block(width, first=0):
    return pl.BlockSpec((ROWS, width), lambda i: (first + i, 0))


def naming_kernel(capacity, groups, r_ref, o_ref, earlier_ref):
    length = r_ref.shape[0]
    rows = groups * length
    lane = lane_of((rows, LANES))
    packed = r_ref[...].astype(jnp.int32)
    chosen = jnp.concatenate(
        [packed[:, g * TOPK : (g + 1) * TOPK] for g in range(groups)], axis=0
    )
    named = jnp.zeros((rows, LANES), f32)
    for k in range(TOPK):
        named = jnp.where(chosen[:, k : k + 1] == lane, 1.0, named)

    @pl.when(pl.program_id(0) == 0)
    def _():
        earlier = lax.broadcasted_iota(jnp.int32, (rows, rows), 1) < lax.broadcasted_iota(
            jnp.int32, (rows, rows), 0
        )
        earlier_ref[...] = jnp.where(earlier, 1.0, 0.0).astype(bf16)

    slot = dot(earlier_ref[...], named.astype(bf16))
    level = named * jnp.where(slot < capacity, 2.0, 1.0)
    o_ref[...] = level.reshape(groups, length, LANES).astype(bf16)


def naming(kv, capacity, groups, ranks):
    total = kv.shape[0]
    length = total // ranks
    return call(
        functools.partial(naming_kernel, capacity, groups),
        "naming",
        9,
        grid=(ranks,),
        in_specs=[pl.BlockSpec((length, LANES), lambda s: (s, 2 * PAIRS))],
        out_specs=pl.BlockSpec((groups, length, LANES), lambda s: (0, s, 0)),
        out_shape=shaped((groups, total, LANES), bf16),
        scratch_shapes=[pltpu.VMEM((groups * length, groups * length), bf16)],
    )(kv)


def key_value_kernel(x_ref, gain_ref, wk_ref, wv_ref, cos_ref, sin_ref, r_ref, n_ref, kv_ref):
    x = x_ref[...].astype(f32)
    factor = lax.rsqrt(jnp.mean(x * x, axis=1, keepdims=True) + epsilon)
    normed = (x * factor * gain_ref[...]).astype(bf16)
    n_ref[...] = normed
    cosine, sine = cos_ref[...], sin_ref[...]
    key = dot(normed, wk_ref[...])
    for c in range(KVH * HD // LANES):
        part = key[:, c * LANES : (c + 1) * LANES]
        turned = part * cosine + half_swap(part) * sine
        kv_ref[:, c * LANES : (c + 1) * LANES] = turned.astype(bf16)
    kv_ref[:, KVH * HD : 2 * KVH * HD] = dot(normed, wv_ref[...]).astype(bf16)
    kv_ref[:, 2 * KVH * HD :] = r_ref[...]


def key_value(group, length, x, gain, wk, wv, cosine, sine, names):
    first = group * length // ROWS
    width = 2 * KVH * HD + LANES
    return call(
        key_value_kernel,
        "key_value",
        5,
        grid=(length // ROWS,),
        in_specs=[
            row_block(D, first),
            resident((1, D)),
            resident((D, KVH * HD)),
            resident((D, KVH * HD)),
            row_block(LANES, first),
            row_block(LANES, first),
            row_block(LANES),
        ],
        out_specs=[row_block(D), row_block(width)],
        out_shape=[shaped((length, D), bf16), shaped((length, width), bf16)],
    )(x, gain, wk, wv, cosine, sine, names)


def query_kernel(n_ref, wq_ref, cos_ref, sin_ref, q_ref):
    cosine, sine = cos_ref[...], sin_ref[...]
    query = dot(n_ref[...], wq_ref[...])
    for c in range(H * HD // LANES):
        part = query[:, c * LANES : (c + 1) * LANES]
        turned = part * cosine + half_swap(part) * sine
        q_ref[:, c * LANES : (c + 1) * LANES] = turned.astype(bf16) * jnp.asarray(0.125, bf16)


def project_query(group, normed, wq, cosine, sine):
    length = normed.shape[0]
    first = group * length // ROWS
    return call(
        query_kernel,
        "query",
        6,
        grid=(length // ROWS,),
        in_specs=[
            row_block(D),
            resident((D, H * HD)),
            row_block(LANES, first),
            row_block(LANES, first),
        ],
        out_specs=row_block(H * HD),
        out_shape=shaped((length, H * HD), bf16),
    )(normed, wq, cosine, sine)


def stack_heads(ref):
    low = lane_of((ROWS, LANES)) < HD
    parts = [ref[:, c * LANES : (c + 1) * LANES].astype(f32) for c in range(SHARE)]
    rolled0, rolled2 = pltpu.roll(parts[0], HD, 1), pltpu.roll(parts[2], HD, 1)
    zero = jnp.zeros((ROWS, LANES), f32)
    first = [parts[0], rolled0, parts[1]]
    second = [parts[1], rolled2, parts[2]]
    return (
        jnp.concatenate([jnp.where(low, v, zero).astype(bf16) for v in first], axis=0),
        jnp.concatenate([jnp.where(low, zero, v).astype(bf16) for v in second], axis=0),
    )


def unstack_heads(first, second):
    low = lane_of((ROWS, LANES)) < HD
    return (
        jnp.where(low, first[:ROWS], pltpu.roll(first[ROWS : 2 * ROWS], HD, 1)),
        jnp.where(low, first[2 * ROWS :], second[:ROWS]),
        jnp.where(low, pltpu.roll(second[ROWS : 2 * ROWS], HD, 1), second[2 * ROWS :]),
    )


def visit_chunks(block, chunk):
    prompt_blocks = PROMPT // ROWS

    @pl.when(block >= prompt_blocks)
    def _():
        for c in range(PROMPT // (2 * ROWS)):
            chunk(c * 2 * ROWS, 2 * ROWS, False)

    @pl.when(block < prompt_blocks)
    def _():
        def step(c, carry):
            chunk(pl.multiple_of(c * ROWS, ROWS), ROWS, False)
            return carry

        lax.fori_loop(0, block, step, 0)

    @pl.when(block > prompt_blocks)
    def _():
        chunk(pl.multiple_of((block - 1) * ROWS, ROWS), ROWS, True)

    chunk(pl.multiple_of(block * ROWS, ROWS), ROWS, True)


def mask_bias(block, begin, size, start_ref):
    place = begin + lax.broadcasted_iota(jnp.int32, (size, ROWS), 0)
    own = block * ROWS + lax.broadcasted_iota(jnp.int32, (size, ROWS), 1)
    ok = (place <= own) & (place >= start_ref[0, :1, :])
    bias = jnp.where(ok, 0.0, -1e30)
    return jnp.concatenate([bias] * SHARE, axis=1)


def attend_kernel(blocks, q_ref, k_ref, v_ref, start_ref, o_ref, lse_ref, vt_ref, m_ref, l_ref, acc_ref):
    block = expert_rank() * blocks + pl.program_id(1)

    @pl.when(pl.program_id(1) == 0)
    def _():
        vt_ref[...] = jnp.transpose(v_ref[...].astype(f32)).astype(bf16)

    queries = stack_heads(q_ref)
    m_ref[...] = jnp.full_like(m_ref, -1e30)
    l_ref[...] = jnp.zeros_like(l_ref)
    acc_ref[...] = jnp.zeros_like(acc_ref)

    def chunk(begin, size, masked):
        keys = k_ref[pl.ds(begin, size), :]
        values = vt_ref[:, pl.ds(begin, size)]
        bias = mask_bias(block, begin, size, start_ref) if masked else None
        for h in range(2):
            scores = dot_nt(keys, queries[h])
            if masked:
                scores = scores + bias
            before = m_ref[h, :1]
            peak = jnp.maximum(before, jnp.max(scores, axis=0, keepdims=True))
            weight = jnp.exp(scores - peak)
            shrink = jnp.exp(before - peak)
            m_ref[h, :1] = peak
            l_ref[h, :1] = l_ref[h, :1] * shrink + jnp.sum(weight, axis=0, keepdims=True)
            acc_ref[h] = acc_ref[h] * shrink + dot(values, weight.astype(bf16))

    visit_chunks(block, chunk)
    mixed = [jnp.transpose(acc_ref[h] / l_ref[h, :1]) for h in range(2)]
    for c, part in enumerate(unstack_heads(*mixed)):
        o_ref[:, c * LANES : (c + 1) * LANES] = part.astype(bf16)
    for h in range(2):
        total = m_ref[h, :1] + jnp.log(l_ref[h, :1])
        lse_ref[0, 0, h] = jnp.broadcast_to(total, (8, STACK))


def attend(group, query, kv, start_row):
    length = query.shape[0]
    total = kv.shape[0]
    blocks = length // ROWS
    heads = pl.BlockSpec((ROWS, PAIR_Q), lambda p, i: (i, p))
    return call(
        functools.partial(attend_kernel, blocks),
        "attend",
        45,
        grid=(PAIRS, blocks),
        in_specs=[
            heads,
            pl.BlockSpec((total, LANES), lambda p, i: (0, p)),
            pl.BlockSpec((total, LANES), lambda p, i: (0, PAIRS + p)),
            pl.BlockSpec((1, 8, ROWS), lambda p, i: (group, 0, i)),
        ],
        out_specs=[
            heads,
            pl.BlockSpec((1, 1, 2, 8, STACK), lambda p, i: (p, i, 0, 0, 0)),
        ],
        out_shape=[
            shaped(query.shape, bf16),
            shaped((PAIRS, blocks, 2, 8, STACK), f32),
        ],
        scratch_shapes=[
            pltpu.VMEM((LANES, total), bf16),
            pltpu.VMEM((2, 8, STACK), f32),
            pltpu.VMEM((2, 8, STACK), f32),
            pltpu.VMEM((2, LANES, STACK), f32),
        ],
    )(query, kv, kv, start_row)


def attend_back_kernel(
    blocks,
    q_ref,
    g_ref,
    o_ref,
    k_ref,
    v_ref,
    lse_ref,
    start_ref,
    cos_ref,
    sin_ref,
    dq_ref,
    keep_ref,
    send_ref,
    dq_acc,
    dkv_acc,
):
    step = pl.program_id(1)
    block = expert_rank() * blocks + step

    @pl.when(step == 0)
    def _():
        dkv_acc[...] = jnp.zeros_like(dkv_acc)

    dq_acc[...] = jnp.zeros_like(dq_acc)
    queries = stack_heads(q_ref)
    grads = stack_heads(g_ref)
    halves = []
    for c in range(SHARE):
        cols = slice(c * LANES, (c + 1) * LANES)
        product = jnp.transpose(g_ref[:, cols].astype(f32) * o_ref[:, cols].astype(f32))
        halves.append(jnp.sum(product[:HD], axis=0, keepdims=True))
        halves.append(jnp.sum(product[HD:], axis=0, keepdims=True))
    inner = [jnp.concatenate(halves[:SHARE], axis=1), jnp.concatenate(halves[SHARE:], axis=1)]

    def chunk(begin, size, masked):
        keys = k_ref[pl.ds(begin, size), :]
        values = v_ref[pl.ds(begin, size), :]
        bias = mask_bias(block, begin, size, start_ref) if masked else None
        key_sum, value_sum = None, None
        for h in range(2):
            scores = dot_nt(keys, queries[h]) - lse_ref[0, 0, h, :1, :]
            if masked:
                scores = scores + bias
            probs = jnp.exp(scores)
            probs_grad = dot_nt(values, grads[h])
            scores_grad = (probs * (probs_grad - inner[h])).astype(bf16)
            value_part = dot(probs.astype(bf16), grads[h])
            key_part = dot(scores_grad, queries[h])
            key_sum = key_part if key_sum is None else key_sum + key_part
            value_sum = value_part if value_sum is None else value_sum + value_part
            dq_acc[h] += dot_tn(scores_grad, keys)
        dkv_acc[0, pl.ds(begin, size), :] += key_sum
        dkv_acc[1, pl.ds(begin, size), :] += value_sum

    visit_chunks(block, chunk)
    cosine, sine = cos_ref[...], sin_ref[...]
    for c, part in enumerate(unstack_heads(dq_acc[0], dq_acc[1])):
        part = part * 0.125
        turned = part * cosine - half_swap(part) * sine
        dq_ref[:, c * LANES : (c + 1) * LANES] = turned.astype(bf16)

    @pl.when(step == blocks - 1)
    def _():
        length = blocks * ROWS
        own = lax.axis_index("el")
        for chip in range(dkv_acc.shape[1] // (2 * length)):
            mine = pl.multiple_of((2 * chip + own) * length, length)
            other = pl.multiple_of((2 * chip + 1 - own) * length, length)
            for i in range(2):
                keep_ref[chip, i] = dkv_acc[i, pl.ds(mine, length), :].astype(bf16)
                send_ref[chip, i] = dkv_acc[i, pl.ds(other, length), :].astype(bf16)


def attend_back_and_swap(blocks, pairs, columns, *refs):
    away_ref = refs[9]
    here_ref = refs[-5]
    send_sem, recv_sem = refs[-2:]
    at = pl.program_id(0) * blocks + pl.program_id(1)
    peer = {"dl": 1 - lax.axis_index("dl")}
    exchange = pltpu.make_async_remote_copy(
        src_ref=away_ref.at[:, :, columns],
        dst_ref=here_ref.at[:, :, columns],
        send_sem=send_sem,
        recv_sem=recv_sem,
        device_id=peer,
        device_id_type=pl.DeviceIdType.MESH,
    )

    @pl.when(at == 0)
    def _():
        barrier = pltpu.get_barrier_semaphore()
        pl.semaphore_signal(barrier, inc=1, device_id=peer, device_id_type=pl.DeviceIdType.MESH)
        pl.semaphore_wait(barrier, 1)
        exchange.start()

    attend_back_kernel(blocks, *refs[:9], *refs[-8:-5], *refs[-4:-2])

    @pl.when(at == pairs * blocks - 1)
    def _():
        exchange.wait()


def attend_back(
    group, span, query, grad, mixed, kv, lse, start_row, cosine, sine, away, collective, kept
):
    length = query.shape[0]
    total = kv.shape[0]
    blocks = length // ROWS
    first = group * blocks
    chips = total // (2 * length)
    base, pairs = span
    side = pl.BlockSpec((chips, 2, length, LANES), lambda p, i: (0, 0, 0, p))
    heads = pl.BlockSpec((ROWS, PAIR_Q), lambda p, i: (i, base + p))
    table = pl.BlockSpec((ROWS, LANES), lambda p, i: (first + i, 0))
    swaps = [] if away is None else [away[0], *away[2]]
    arriving = [] if away is None else [away[0]]
    if away is None:
        kernel = lambda *refs: attend_back_kernel(blocks, *refs[:9], *refs[-5:])
        extra = {}
    else:
        kernel = functools.partial(attend_back_and_swap, blocks, pairs, away[1])
        extra = dict(collective_id=collective, has_side_effects=True)
    anywhere = pl.BlockSpec(memory_space=pl.ANY)
    return call(
        kernel,
        "attend_back",
        16 * pairs,
        extra,
        grid=(pairs, blocks),
        in_specs=[
            heads,
            heads,
            heads,
            pl.BlockSpec((total, LANES), lambda p, i: (0, base + p)),
            pl.BlockSpec((total, LANES), lambda p, i: (0, PAIRS + base + p)),
            pl.BlockSpec((1, 1, 2, 8, STACK), lambda p, i: (base + p, i, 0, 0, 0)),
            pl.BlockSpec((1, 8, ROWS), lambda p, i: (group, 0, i)),
            table,
            table,
        ]
        + [anywhere] * len(swaps + kept),
        out_specs=[
            heads,
            side,
            side,
        ]
        + [anywhere] * len(arriving),
        input_output_aliases={
            **({9 + len(swaps): 0} if kept else {}),
            **({10: 3} if len(swaps) > 1 else {}),
        },
        out_shape=[
            shaped(query.shape, bf16),
            shaped((chips, 2, length, pairs * LANES), bf16),
            shaped((chips, 2, length, pairs * LANES), bf16),
        ]
        + [shaped(one.shape, one.dtype) for one in arriving],
        scratch_shapes=[
            pltpu.VMEM((2, STACK, LANES), f32),
            pltpu.VMEM((2, total, LANES), f32),
        ]
        + [pltpu.SemaphoreType.DMA] * (2 * len(arriving)),
    )(query, grad, mixed, kv, kv, lse, start_row, cosine, sine, *swaps, *kept)


def branch_kernel(a_ref, x_ref, wo_ref, gain_ref, wr_ref, m_ref, n_ref, ps_ref):
    middle = x_ref[...].astype(f32) + dot(a_ref[...], wo_ref[...])
    m_ref[...] = middle
    factor = lax.rsqrt(jnp.mean(middle * middle, axis=1, keepdims=True) + epsilon)
    normed = (middle * factor * gain_ref[...]).astype(bf16)
    n_ref[...] = normed
    add_up(ps_ref, fold_rows(router(normed, wr_ref[...])))


def branch(group, attended, x, wo, gain, wr):
    length = attended.shape[0]
    return call(
        branch_kernel,
        "branch",
        6,
        grid=(length // ROWS,),
        in_specs=[
            row_block(H * HD),
            row_block(D, group * length // ROWS),
            resident((H * HD, D)),
            resident((1, D)),
            resident((D, LANES)),
        ],
        out_specs=[row_block(D), row_block(D), pl.BlockSpec((8, LANES), lambda i: (0, 0))],
        out_shape=[
            shaped((length, D), f32),
            shaped((length, D), bf16),
            shaped((8, LANES), f32),
        ],
    )(attended, x, wo, gain, wr)


def router(normed, weight):
    count = EXP_DEV * 2 * lax.axis_size("eh")
    logits = dot(normed, weight)
    logits = jnp.where(lane_of(logits.shape) < count, logits, -1e30)
    powers = jnp.exp(logits - jnp.max(logits, axis=1, keepdims=True))
    return powers / jnp.sum(powers, axis=1, keepdims=True)


def experts_kernel(x_ref, c_ref, t_ref, wr_ref, *refs):
    outs, weights, sems = refs[-11:-4], refs[-4:-1], refs[-1]
    step = pl.program_id(0)

    def loads(e):
        return [
            pltpu.make_async_copy(refs[i].at[e], weights[i].at[e], sems.at[i, e]) for i in range(3)
        ]

    @pl.when(step == 0)
    def _():
        for e in range(EXP_DEV):
            for load in loads(e):
                load.start()
        experts_rows(x_ref, c_ref, t_ref, wr_ref, *weights, *outs, loads)

    @pl.when(step > 0)
    def _():
        experts_rows(x_ref, c_ref, t_ref, wr_ref, *weights, *outs, lambda e: [])


def experts_rows(
    x_ref, c_ref, t_ref, wr_ref, wg_ref, wu_ref, wd_ref,
    mix_ref, rows_ref, x_out, c_out, hid_ref, gate_ref, up_ref, loads,
):
    x, cot = x_ref[...], c_ref[...]
    x_out[...] = x
    c_out[...] = cot
    level = t_ref[0].astype(f32)
    picked = jnp.where(level > 0.5, router(x, wr_ref[...]), 0.0)
    share = picked / jnp.sum(picked, axis=1, keepdims=True)
    share = jnp.where(level > 1.5, share, 0.0)
    lane = lane_of(share.shape)
    base = EXP_DEV * expert_rank()
    share = pltpu.roll(share, lax.rem(LANES - base, LANES), 1)
    mix, rows = None, None
    gate_grads = jnp.zeros(share.shape, bf16)
    for e in range(EXP_DEV):
        for load in loads(e):
            load.wait()
        gate = dot(x, wg_ref[e])
        up = dot(x, wu_ref[e])
        hidden_grad = dot(cot, wd_ref[e])
        sigmoid = jax.nn.sigmoid(gate)
        active = gate * sigmoid
        hidden = active * up
        inner = jnp.sum(hidden * hidden_grad, axis=1, keepdims=True)
        coarse = inner.astype(bf16)
        fine = (inner - coarse.astype(f32)).astype(bf16)
        gate_grads = jnp.where(lane == base + e, coarse, gate_grads)
        gate_grads = jnp.where(lane == LANES // 2 + base + e, fine, gate_grads)
        weight = share[:, e : e + 1]
        scaled = (hidden * weight).astype(bf16)
        hidden_grad = hidden_grad * weight
        up_grad = (hidden_grad * active).astype(bf16)
        gate_grad = (hidden_grad * up * sigmoid * (1.0 + gate * (1.0 - sigmoid))).astype(bf16)
        cols = slice(e * FF, (e + 1) * FF)
        hid_ref[:, cols] = scaled
        gate_ref[:, cols] = gate_grad
        up_ref[:, cols] = up_grad
    for e in range(EXP_DEV):
        cols = slice(e * FF, (e + 1) * FF)
        mix_part = dot_nt(hid_ref[:, cols], wd_ref[e])
        rows_part = dot_nt(gate_ref[:, cols], wg_ref[e]) + dot_nt(up_ref[:, cols], wu_ref[e])
        mix = mix_part if mix is None else mix + mix_part
        rows = rows_part if rows is None else rows + rows_part
    mix_ref[...] = mix.astype(bf16)
    rows_ref[:, :D] = rows.astype(bf16)
    rows_ref[:, D:] = gate_grads


def experts_pass(group, groups, x, cot, level, wr, wg, wu, wd, kept):
    count = x.shape[0]
    first = group * count // ROWS
    whole = groups * count
    side = pl.BlockSpec(memory_space=pl.ANY)
    widths = [D, D, EXP_DEV * FF, EXP_DEV * FF, EXP_DEV * FF]
    return call(
        experts_kernel,
        "experts",
        113,
        grid=(count // ROWS,),
        in_specs=[
            row_block(D),
            row_block(D),
            pl.BlockSpec((1, ROWS, LANES), lambda i: (group, i, 0)),
            resident((D, LANES)),
        ]
        + [side] * (3 + len(kept)),
        out_specs=[row_block(D), row_block(D + LANES)]
        + [row_block(width, first) for width in widths],
        out_shape=[
            shaped((count, D), bf16),
            shaped((count, D + LANES), bf16),
        ]
        + [shaped((whole, width), bf16) for width in widths],
        input_output_aliases={7 + i: 2 + i for i in range(len(kept))},
        scratch_shapes=[pltpu.VMEM((EXP_DEV, D, FF), bf16)] * 3
        + [pltpu.SemaphoreType.DMA((3, EXP_DEV))],
    )(x, cot, level, wr, wg, wu, wd, *kept)


def norm_back(grad, normed, factor, gain):
    scaled = grad * gain
    return factor * (scaled - normed * jnp.mean(scaled * normed, axis=1, keepdims=True))


def fold_rows(values):
    return jnp.sum(values.reshape(values.shape[0] // 8, 8, values.shape[1]), axis=0)


def add_up(ref, part):
    @pl.when(pl.program_id(0) == 0)
    def _():
        ref[...] = part

    @pl.when(pl.program_id(0) > 0)
    def _():
        ref[...] += part


def middle_kernel(
    r_ref, t_ref, m_ref, n_ref, c_ref, gain_ref, wr_ref, wo_ref,
    mg_ref, b_ref, ag_ref, l_ref, dg_ref,
):
    probs = router(n_ref[...], wr_ref[...])
    level = t_ref[0].astype(f32)
    sel = jnp.where(level > 0.5, 1.0, 0.0)
    gate_grad = r_ref[:, D:].astype(f32)
    gate_grad = gate_grad + pltpu.roll(gate_grad, LANES // 2, 1)
    gate_grad = jnp.where(level > 1.5, gate_grad, 0.0)
    picked = probs * sel
    total = jnp.sum(picked, axis=1, keepdims=True)
    share = picked / total
    inner = jnp.sum(gate_grad * share, axis=1, keepdims=True)
    probs_grad = (gate_grad - inner) / total * sel
    logits_grad = probs * (probs_grad - jnp.sum(probs_grad * probs, axis=1, keepdims=True))
    coarse = logits_grad.astype(bf16)
    fine = (logits_grad - coarse.astype(f32)).astype(bf16)
    l_ref[:, :LANES] = coarse
    l_ref[:, LANES:] = fine
    grad = r_ref[:, :D].astype(f32) + dot_nt(coarse, wr_ref[...]) + dot_nt(fine, wr_ref[...])
    middle = m_ref[...]
    factor = lax.rsqrt(jnp.mean(middle * middle, axis=1, keepdims=True) + epsilon)
    normed = middle * factor
    add_up(dg_ref, fold_rows(grad * normed))
    middle_grad = c_ref[...].astype(f32) + norm_back(grad, normed, factor, gain_ref[...])
    mg_ref[...] = middle_grad
    low = middle_grad.astype(bf16)
    b_ref[...] = low
    ag_ref[...] = dot_nt(low, wo_ref[...]).astype(bf16)


def middle_back(group, rows, level, middle, normed, cot, gain, wr, wo):
    length = rows.shape[0]
    first = group * length // ROWS
    corner = lambda width: pl.BlockSpec((8, width), lambda i: (0, 0))
    return call(
        middle_kernel,
        "middle_back",
        8,
        grid=(length // ROWS,),
        in_specs=[
            row_block(D + LANES),
            pl.BlockSpec((1, ROWS, LANES), lambda i: (group, i, 0)),
            row_block(D), row_block(D), row_block(D, first),
            resident((1, D)), resident((D, LANES)), resident((H * HD, D)),
        ],
        out_specs=[
            row_block(D), row_block(D), row_block(H * HD), row_block(2 * LANES),
            corner(D),
        ],
        out_shape=[
            shaped((length, D), f32),
            shaped((length, D), bf16),
            shaped((length, H * HD), bf16),
            shaped((length, 2 * LANES), bf16),
            shaped((8, D), f32),
        ],
    )(rows, level, middle, normed, cot, gain, wr, wo)


def input_kernel(
    dq_ref, dk_ref, dv_ref, x_ref, mg_ref, cos_ref, sin_ref, gain_ref, wq_ref, wk_ref, wv_ref,
    out_ref, dk_out, dg_ref,
):
    cosine, sine = cos_ref[...], sin_ref[...]
    for c in range(KVH * HD // LANES):
        part = dk_ref[0, :, c * LANES : (c + 1) * LANES].astype(f32)
        turned = part * cosine - half_swap(part) * sine
        dk_out[:, c * LANES : (c + 1) * LANES] = turned.astype(bf16)
    grad = dot_nt(dq_ref[...], wq_ref[...])
    grad = grad + dot_nt(dk_out[...], wk_ref[...])
    grad = grad + dot_nt(dv_ref[0], wv_ref[...])
    x = x_ref[...].astype(f32)
    factor = lax.rsqrt(jnp.mean(x * x, axis=1, keepdims=True) + epsilon)
    normed = x * factor
    add_up(dg_ref, fold_rows(grad * normed))
    out_ref[...] = mg_ref[...] + norm_back(grad, normed, factor, gain_ref[...])


def input_back(group, groups, dq, dkv, x, middle_grad, cosine, sine, gain, wq, wk, wv, kept):
    length = dq.shape[0]
    first = group * length // ROWS
    kernel = lambda *refs: input_kernel(*refs[:11], *refs[-3:])
    return call(
        kernel,
        "input_back",
        8,
        grid=(length // ROWS,),
        in_specs=[
            row_block(H * HD),
            pl.BlockSpec((1, ROWS, KVH * HD), lambda i: (0, i, 0)),
            pl.BlockSpec((1, ROWS, KVH * HD), lambda i: (1, i, 0)),
            row_block(D, first),
            row_block(D),
            row_block(LANES, first),
            row_block(LANES, first),
            resident((1, D)),
            resident((D, H * HD)),
            resident((D, KVH * HD)),
            resident((D, KVH * HD)),
        ]
        + [pl.BlockSpec(memory_space=pl.ANY)] * len(kept),
        out_specs=[
            row_block(D, first),
            row_block(KVH * HD),
            pl.BlockSpec((8, D), lambda i: (0, 0)),
        ],
        out_shape=[
            shaped((groups * length, D), f32),
            shaped((length, KVH * HD), bf16),
            shaped((8, D), f32),
        ],
        input_output_aliases={11: 0} if kept else {},
    )(dq, dkv, dkv, x, middle_grad, cosine, sine, gain, wq, wk, wv, *kept)


def transpose_into(turned, lefts):
    length = lefts[0].shape[0]
    for g, left in enumerate(lefts):
        for c in range(0, D, 2 * LANES):
            part = left[:, c : c + 2 * LANES].astype(f32)
            turned[c : c + 2 * LANES, g * length : (g + 1) * length] = jnp.transpose(part).astype(
                bf16
            )


def out_kernel(groups, *refs):
    lefts, rights = refs[:groups], refs[groups : 2 * groups]
    out_ref, turned = refs[-2:]
    length = lefts[0].shape[0]

    @pl.when(pl.program_id(0) == 0)
    def _():
        transpose_into(turned, lefts)

    total = None
    for g in range(groups):
        part = dot(turned[:, g * length : (g + 1) * length], rights[g][...])
        total = part if total is None else total + part
    out_ref[...] = total.astype(bf16)


def out_gradient(lefts, rights):
    groups, length = len(lefts), lefts[0].shape[0]
    width = 4 * LANES
    return call(
        functools.partial(out_kernel, groups),
        "out_grad",
        10,
        grid=(D // width,),
        in_specs=[resident((length, D))] * groups
        + [pl.BlockSpec((length, width), lambda i: (0, i))] * groups,
        out_specs=pl.BlockSpec((D, width), lambda i: (0, i)),
        out_shape=shaped((D, D), bf16),
        scratch_shapes=[pltpu.VMEM((D, groups * length), bf16)],
    )(*lefts, *rights)


def dense_kernel(groups, sizes, *refs):
    data, chips, shard, width, full, late = sizes
    lefts, queries, keys, values = (refs[i * groups : (i + 1) * groups] for i in range(4))
    narrow_ref, late_ref, out_ref = refs[4 * groups : 4 * groups + 3]
    (turned, keep1, send1, got1, keep2, send2, got2, sum2, got3, sum3, got4, sum4, near5, far5,
     wide2, wide3, keep6, send6, got6) = refs[4 * groups + 3 : 4 * groups + 22]
    sems = refs[4 * groups + 22 :]
    half = width // 2
    length = lefts[0].shape[0]
    ranks = 2 * chips
    dh, dl, eh, el = (lax.axis_index(name) for name in ("dh", "dl", "eh", "el"))

    def near(hop, core):
        return {"eh": lax.rem(eh + hop, chips), "el": core}

    peers = [{"el": 1 - el}, {"dl": 1 - dl}]
    for hop in range(1, chips):
        peers.append(near(hop, el))
    for hop in range(1, data):
        peers.append({"dh": lax.rem(dh + hop, data)})
    barrier = pltpu.get_barrier_semaphore()
    for peer in peers:
        pl.semaphore_signal(barrier, inc=1, device_id=peer, device_id_type=pl.DeviceIdType.MESH)
    transpose_into(turned, lefts)
    pl.semaphore_wait(barrier, len(peers))

    def copy(source, target, phase, k, lane, peer):
        return pltpu.make_async_remote_copy(
            src_ref=source,
            dst_ref=target,
            send_sem=sems[2 * phase].at[k, lane],
            recv_sem=sems[2 * phase + 1].at[k, lane],
            device_id=peer,
            device_id_type=pl.DeviceIdType.MESH,
        )

    def crossed(k):
        return k < full and k % 2 == 1

    def slot(k):
        return k // 2 if k < full else (full + 1) // 2 + k - full

    def copies(phase, k):
        if phase == 0:
            return [copy(send1.at[k], got1.at[k], 0, k, 0, {"el": 1 - el})]
        if phase == 1:
            source, target = (send6, got6) if crossed(k) else (send2, got2)
            at = k // 2
            return [
                copy(source.at[at, hop - 1], target.at[at, hop - 1], 1, k, hop - 1, near(hop, el))
                for hop in range(1, chips)
            ]
        if phase == 2:
            if crossed(k):
                at = k // 2
                return [copy(wide2.at[at, 1 - dl], wide3.at[at], 2, k, 0, {"dl": 1 - dl})]
            at = slot(k)
            return [copy(sum2.at[at, 1 - dl], got3.at[at], 2, k, 0, {"dl": 1 - dl})]
        if phase == 3:
            found = []
            for hop in range(1, data):
                away = lax.rem(dh + hop, data)
                found.append(
                    copy(sum3.at[k, away], got4.at[k, hop - 1], 3, k, hop - 1, {"dh": away})
                )
            return found
        if phase == 4:
            return [
                copy(sum4.at[k], near5.at[k, eh], 4, k, hop - 1, near(hop, el))
                for hop in range(1, chips)
            ]
        return [copy(near5.at[k], far5.at[k], 5, k, 0, {"el": 1 - el})]

    def start(phase, k):
        for one in copies(phase, k):
            one.start()

    def arrived(phase, k):
        for one in copies(phase, k):
            one.wait_recv()

    def finish_shard(k):
        base = k * width if k < full else full * width + (k - full) * LANES

        def put(side, chip, block):
            place = side * chips + chip
            place = place * LANES if k < full else place * late * LANES
            at = pl.multiple_of(base + place, LANES)
            out_ref[:, pl.ds(at, LANES)] = block.astype(f32)

        for chip in range(chips):
            put(el, chip, near5[k, chip])
            put(1 - el, chip, far5[k, chip])

    def piece(column):
        size = KVH * HD
        if column >= H * HD + 2 * size:
            if column > H * HD + 2 * size:
                return jnp.zeros((D, size), bf16)
            part = jnp.transpose(narrow_ref[...])
            return jnp.concatenate([part, jnp.zeros((D, size - LANES), f32)], axis=1).astype(bf16)
        total = None
        for g in range(groups):
            if column < H * HD:
                block = queries[g][:, column : column + size]
            elif column < H * HD + size:
                block = keys[g][...]
            else:
                block = values[g][1]
            one = dot(turned[:, g * length : (g + 1) * length], block)
            total = one if total is None else total + one
        return total.astype(bf16)

    def stage_compute(k):
        if k < full:
            part = [piece(k * width + c) for c in range(0, width, KVH * HD)]
            part = part[0] if len(part) == 1 else jnp.concatenate(part, axis=1)

            @pl.when(el == 0)
            def _():
                keep1[k] = part[:, :half]
                send1[k] = part[:, half:]

            @pl.when(el == 1)
            def _():
                keep1[k] = part[:, half:]
                send1[k] = part[:, :half]

            start(0, k)

    def hand_out(block, chip, keep, send):
        hop = lax.rem(chip + chips - eh, chips)

        @pl.when(hop == 0)
        def _():
            keep[...] = block

        @pl.when(hop > 0)
        def _():
            send[hop - 1] = block

    def chip_columns(chip):
        return slice(chip * LANES, (chip + 1) * LANES)

    def stage_core(k):
        arrived(0, k)
        met = (keep1[k].astype(f32) + got1[k].astype(f32)).astype(bf16)
        at = k // 2
        if crossed(k):
            for far in range(data):
                for side in range(2):
                    first = (2 * far + side) * shard
                    wide2[at, side, far] = met[first : first + shard]
            start(2, k)
        else:
            for chip in range(chips):
                hand_out(met[:, chip_columns(chip)], chip, keep2.at[at], send2.at[at])
            start(1, k)

    def stage_second(k):
        at = k // 2
        if crossed(k):
            arrived(2, k)
            met = (wide2[at, dl].astype(f32) + wide3[at].astype(f32)).astype(bf16)
            for chip in range(chips):
                hand_out(met[:, :, chip_columns(chip)], chip, keep6.at[at], send6.at[at])
            start(1, k)
        else:
            arrived(1, k)
            total = keep2[at].astype(f32)
            for hop in range(1, chips):
                total = total + got2[at, hop - 1].astype(f32)
            spread(k, total.astype(bf16))

    def spread(k, total):
        for far in range(data):
            for side in range(2):
                first = (2 * far + side) * shard
                sum2[slot(k), side, far] = total[first : first + shard]
        start(2, k)

    def stage_third(k):
        if crossed(k):
            at = k // 2
            arrived(1, k)
            total = keep6[at].astype(f32)
            for hop in range(1, chips):
                total = total + got6[at, hop - 1].astype(f32)
        else:
            at = slot(k)
            arrived(2, k)
            total = sum2[at, dl].astype(f32) + got3[at].astype(f32)
        sum3[k] = total.astype(bf16)
        start(3, k)

    def stage_far(k):
        arrived(3, k)
        total = sum3[k, dh].astype(f32)
        for hop in range(1, data):
            total = total + got4[k, hop - 1].astype(f32)
        total = total.astype(bf16)
        sum4[k] = total
        near5[k, eh] = total
        start(4, k)

    def stage_gather(k):
        arrived(4, k)
        start(5, k)

    def stage_last(k):
        arrived(5, k)
        finish_shard(k)

    everything = list(range(full, full + late)) + list(range(full))
    for k in range(full, full + late):
        first = (k - full) * LANES
        spread(k, late_ref[:, first : first + LANES])
    stages = (
        stage_compute,
        stage_core,
        stage_second,
        stage_third,
        stage_far,
        stage_gather,
        stage_last,
    )
    for step in range(full + len(stages) - 1):
        for delay, stage in enumerate(stages):
            if 0 <= step - delay < full:
                stage(step - delay)
        if step < 4:
            for k in range(full, full + late):
                stages[3 + step](k)
    for k in everything:
        for phase in range(6):
            if k < full or phase > 1:
                for one in copies(phase, k):
                    one.wait_send()


def dense_gradient(lefts, queries, keys, values, narrow, late_part):
    groups = len(lefts)
    data, chips = lax.axis_size("dh"), lax.axis_size("eh")
    shard = D // (2 * data)
    width = 2 * chips * LANES
    columns = H * HD + 2 * KVH * HD
    full = -(-(columns + LANES) // width)
    late = late_part.shape[1] // LANES
    total = full + late
    half, ranks = width // 2, 2 * chips
    sizes = (data, chips, shard, width, full, late)
    lanes = [1, chips - 1, 1, data - 1, chips - 1, 1]
    even, odd = (full + 1) // 2, full // 2
    sems = []
    for count in lanes:
        sems += [pltpu.SemaphoreType.DMA((total, count))] * 2
    operands = [*lefts, *queries, *keys, *values, narrow, late_part]
    whole = pl.BlockSpec(memory_space=pltpu.VMEM)
    return pl.pallas_call(
        functools.partial(dense_kernel, groups, sizes),
        name="dense_grad",
        in_specs=[whole] * len(operands),
        out_specs=whole,
        out_shape=shaped((shard, full * width + late * ranks * LANES), f32),
        scratch_shapes=[
            pltpu.VMEM((D, groups * lefts[0].shape[0]), bf16),
            pltpu.VMEM((full, D, half), bf16),
            pltpu.VMEM((full, D, half), bf16),
            pltpu.VMEM((full, D, half), bf16),
            pltpu.VMEM((even, D, LANES), bf16),
            pltpu.VMEM((even, chips - 1, D, LANES), bf16),
            pltpu.VMEM((even, chips - 1, D, LANES), bf16),
            pltpu.VMEM((even + late, 2, data, shard, LANES), bf16),
            pltpu.VMEM((even + late, data, shard, LANES), bf16),
            pltpu.VMEM((total, data, shard, LANES), bf16),
            pltpu.VMEM((total, data - 1, shard, LANES), bf16),
            pltpu.VMEM((total, shard, LANES), bf16),
            pltpu.VMEM((total, chips, shard, LANES), bf16),
            pltpu.VMEM((total, chips, shard, LANES), bf16),
            pltpu.VMEM((odd, 2, data, shard, half), bf16),
            pltpu.VMEM((odd, data, shard, half), bf16),
            pltpu.VMEM((odd, data, shard, LANES), bf16),
            pltpu.VMEM((odd, chips - 1, data, shard, LANES), bf16),
            pltpu.VMEM((odd, chips - 1, data, shard, LANES), bf16),
        ]
        + sems,
        cost_estimate=pl.CostEstimate(
            flops=int(80 * 9e8), bytes_accessed=0, transcendentals=0
        ),
        compiler_params=pltpu.CompilerParams(
            vmem_limit_bytes=VMEM_LIMIT, collective_id=0, has_side_effects=True
        ),
    )(*operands)


def widen(values):
    return jnp.pad(values, ((0, 0), (0, LANES - values.shape[1])))


def swap(values, axis):
    return lax.ppermute(values, axis, [(0, 1), (1, 0)])


def pick(values, index):
    return lax.dynamic_index_in_dim(values, index, 1, keepdims=False)


def pair_slices(values, shard):
    parts = values.reshape(-1, 2, shard, values.shape[1])
    own = lax.axis_index("dl")
    return pick(parts, own), pick(parts, 1 - own)


def pair_parts(values, shard):
    own, away = pair_slices(values, shard)
    return own, swap(away, "dl")


def far_sum(own, met):
    met = (own + met).reshape(-1, own.shape[2])
    return lax.psum_scatter(met, "dh", scatter_dimension=0, tiled=True)


def take(values, axis, index):
    return lax.dynamic_index_in_dim(values, index, axis, keepdims=False)


def chip_sum(met):
    chips = lax.axis_size("eh")
    chip = lax.axis_index("eh")
    total = take(met, 0, chip)
    for hop in range(1, chips):
        order = [(i, (i + hop) % chips) for i in range(chips)]
        away = take(met, 0, lax.rem(chip + hop, chips))
        total = total + lax.ppermute(away, "eh", order)
    return total


def cut(array, index, size):
    return lax.dynamic_slice_in_dim(array, index * size, size, 1)


def column_core_sum(values):
    half = values.shape[1] // 2
    own = lax.axis_index("el")
    return cut(values, own, half) + swap(cut(values, 1 - own, half), "el")


def column_chip_sum(met):
    chips, chip = lax.axis_size("eh"), lax.axis_index("eh")
    size = met.shape[1] // chips
    total = cut(met, chip, size)
    for hop in range(1, chips):
        order = [(i, (i + hop) % chips) for i in range(chips)]
        away = cut(met, lax.rem(chip + hop, chips), size)
        total = total + lax.ppermute(away, "eh", order)
    return total


def sum_steps():
    for axis in ("el", "eh", "dl", "dh"):
        count = lax.axis_size(axis)
        hop = 1
        while hop < count:
            order = [(i, i ^ hop) for i in range(count)]
            yield lambda v, axis=axis, order=order: v + lax.ppermute(v, axis, order)
            hop *= 2


def together(*values):
    return lax.optimization_barrier(values)


def on_device(
    tokens,
    segments,
    routes,
    cotangent,
    attention_gain,
    query_weight,
    key_weight,
    value_weight,
    out_weight,
    mixture_gain,
    router_weight,
    gate_weight,
    up_weight,
    down_weight,
):
    groups, length, _ = tokens.shape
    each = range(groups)
    rows = groups * length
    ranks = lax.axis_size("eh") * 2
    dp_ranks = lax.axis_size("dh") * 2
    rank = expert_rank()
    experts = EXP_DEV * ranks
    capacity = (rows * TOPK * 5 // (4 * experts) + 7) // 8 * 8
    all_tokens = rows * dp_ranks * ranks
    first_row = rank * length
    shard = D // dp_ranks

    seg_full = jnp.concatenate([jnp.full((groups, PROMPT), -1, jnp.int32), segments], axis=1)
    seg_own = lax.dynamic_slice_in_dim(seg_full, first_row, length, 1)
    earlier = jnp.sum((segments[:, None, :] < seg_own[:, :, None]).astype(jnp.int32), axis=2)
    position = first_row + jnp.arange(length, dtype=jnp.int32)[None, :]
    place = position - earlier
    start = jnp.where(position >= PROMPT, PROMPT + earlier, 0)
    half = HD // 2
    lane = jnp.arange(LANES, dtype=jnp.int32)
    frequency = jnp.exp(-math.log(rope_base) * (lane % half).astype(f32) / half)
    angles = place.astype(f32).reshape(rows, 1) * frequency
    cosine = jnp.cos(angles)
    sine = jnp.sin(angles) * jnp.where(lane % HD < half, -1.0, 1.0)
    start_row = jnp.broadcast_to(start[:, None, :], (groups, 8, length))

    names = jnp.concatenate([routes[g] for g in each], axis=1).astype(bf16)
    names = widen(names)
    cot_rows = cotangent.reshape(rows, D)
    cot_all = [lax.all_gather(cotangent[g], EXPERT, axis=0, tiled=True) for g in each]

    x = tokens.reshape(rows, D)
    gain_a = attention_gain.reshape(1, D)
    gain_b = mixture_gain.reshape(1, D)
    router_wide = widen(router_weight)
    normed, query, kv = [None] * groups, [None] * groups, [None] * groups
    for g in each:
        normed[g], kv_own = key_value(
            g, length, x, gain_a, key_weight, value_weight, cosine, sine, names
        )
        kv[g] = lax.all_gather(kv_own, EXPERT, axis=0, tiled=True)
    for g in each:
        query[g] = project_query(g, normed[g], query_weight, cosine, sine)
    level = naming(kv[groups - 1], capacity, groups, ranks)
    level_own = lax.dynamic_slice_in_dim(level, first_row, length, 1)
    kv[0], query = together(kv[0], query)
    attended, lse = [None] * groups, [None] * groups
    middle, hidden_low, hidden_all = [None] * groups, [None] * groups, [None] * groups
    probs_local = 0.0
    for g in each:
        attended[g], lse[g] = attend(g, query[g], kv[g], start_row)
        if g == groups - 1:
            attended[g], cot_all[0] = together(attended[g], cot_all[0])
        middle[g], hidden_low[g], probs_part = branch(
            g, attended[g], x, out_weight, gain_b, router_wide
        )
        probs_local += jnp.sum(probs_part, axis=0)
        hidden_all[g] = lax.all_gather(hidden_low[g], EXPERT, axis=0, tiled=True)

    counts = jnp.sum((level_own > 0.5).astype(f32), axis=(0, 1))
    stats = jnp.stack([counts, probs_local])[:, :experts]
    steps = sum_steps()

    def beside(value, stats):
        step = next(steps, None)
        return (value, stats) if step is None else together(value, step(stats))

    kept, rows_back, mixture = [], [], []
    for g in each:
        if g > 0:
            kept[0], cot_all[g] = together(kept[0], cot_all[g])
            hidden_all[g], stats = beside(hidden_all[g], stats)
        mix, rows_grad, *kept = experts_pass(
            g, groups, hidden_all[g], cot_all[g], level, router_wide,
            gate_weight, up_weight, down_weight, kept,
        )
        rows_back.append(lax.psum_scatter(rows_grad, EXPERT, scatter_dimension=0, tiled=True))
        mixture.append(mix)
        if g < groups - 1:
            mixture[g] = lax.psum_scatter(mix, EXPERT, scatter_dimension=0, tiled=True)
    x_all, cot_both, hidden, gate_back, up_back = kept
    hidden, mixture[0] = together(hidden, mixture[0])
    hidden, stats = beside(hidden, stats)
    down_local = dot_tn(cot_both, hidden).astype(bf16)
    x_all, down_local = together(x_all, down_local)
    gate_back, stats = beside(gate_back, stats)
    gate_local = dot_tn(x_all, gate_back).astype(bf16)
    up_back, gate_local = together(up_back, gate_local)
    gate_own, gate_met = pair_parts(gate_local, shard)
    up_back, mix = together(up_back, mixture[-1])
    mixture[-1] = lax.psum_scatter(mix, EXPERT, scatter_dimension=0, tiled=True)
    up_back, stats = beside(up_back, stats)
    up_local = dot_tn(x_all, up_back).astype(bf16)
    rows_back[0], up_local = together(rows_back[0], up_local)
    rows_back[0], stats = beside(rows_back[0], stats)
    for step in steps:
        stats = step(stats)
    expert_load = stats[0] * experts / (all_tokens * TOPK)
    prob_mean = stats[1] * experts / all_tokens
    balance_loss = jnp.sum(expert_load * prob_mean) / experts

    def by_expert(part):
        return jnp.stack([part[:, e * FF : (e + 1) * FF] for e in range(EXP_DEV)]).astype(f32)

    middle_grad, branch_grad, attended_grad, logits_grad, dq, dkv = (
        [None] * groups for _ in range(6)
    )
    gain_b_local, last = 0.0, groups - 1
    down_far = lax.psum_scatter(down_local, "dh", scatter_dimension=0, tiled=True)
    for g in each:
        middle_grad[g], branch_grad[g], attended_grad[g], logits_grad[g], gain_part = middle_back(
            g, rows_back[g], level_own, middle[g], hidden_low[g], cot_rows,
            gain_b, router_wide, out_weight,
        )
        gain_b_local += jnp.sum(gain_part, axis=0)
    out_local = out_gradient(attended, branch_grad)
    fill = -D % (ranks * LANES)
    out_local = jnp.pad(out_local, ((0, 0), (0, fill)))
    attended_grad[0], out_local = together(attended_grad[0], out_local)
    cut_at = 13 * LANES
    up_own, up_away = pair_slices(up_local, shard)
    swaps = [(up_away, slice(0, cut_at), []), (up_away, slice(cut_at, EXP_DEV * FF), None)]
    out_met = column_core_sum(out_local)
    for g in each:
        pieces, kept = [], []
        here = [] if g == 0 else here
        spans = [(0, PAIRS)] if g < last else [(0, PAIRS // 2), (PAIRS // 2, PAIRS // 2)]
        for at, span in enumerate(spans):
            if g == last and at == 0:
                dq[0], gate_own = together(dq[0], gate_own)
                attended_grad[g], out_met, dq[0], gate_own, gate_met, down_far = together(
                    attended_grad[g], out_met, dq[0], gate_own, gate_met, down_far
                )
                gate_part = far_sum(gate_own, gate_met)
                down_own, down_away = pair_slices(down_far, shard)
                swaps.append((down_away, slice(0, EXP_DEV * FF), []))
                out_part = column_chip_sum(out_met)
            if g == last and at == 1:
                up_met = up_own + here[1]
                kept, dkv[0], pieces[0], up_met, mixture[last] = together(
                    kept, dkv[0], pieces[0], up_met, mixture[last]
                )
                up_part = lax.psum_scatter(
                    up_met.reshape(-1, up_met.shape[2]), "dh", scatter_dimension=0, tiled=True
                )
            turn = len(here)
            if turn == 1:
                swaps[1] = (*swaps[1][:2], here)
            grad, keep_part, send_part, *arrived = attend_back(
                g, span, query[g], attended_grad[g], attended[g], kv[g], lse[g], start_row,
                cosine, sine, swaps[turn] if turn < len(swaps) else None, 1 + turn, kept,
            )
            here = here + arrived
            kept = [grad]
            if g == last and at == 1:
                keep_part, dq[0] = together(keep_part, dq[0])
                down_part = (down_own + here[2])[0]
            pieces.append(keep_part + swap(send_part, "el"))
            if g == last and at == 1:
                pieces[1], dq[0] = together(pieces[1], dq[0])
        dq[g] = kept[0]
        pieces = [chip_sum(piece) for piece in pieces]
        dkv[g] = pieces[0] if len(pieces) == 1 else jnp.concatenate(pieces, axis=2)
    output = jnp.stack(
        [(middle[g] + mixture[g].astype(f32)).astype(bf16) for g in each]
    )

    kept, turned_dk, gain_a_local = [], [None] * groups, 0.0
    for g in each:
        input_grad, turned_dk[g], gain_part = input_back(
            g, groups, dq[g], dkv[g], x, middle_grad[g], cosine, sine,
            gain_a, query_weight, key_weight, value_weight, kept,
        )
        kept = [input_grad]
        gain_a_local += jnp.sum(gain_part, axis=0)
    router_parts = sum(dot_tn(logits_grad[g], hidden_low[g]) for g in each)
    router_local = (router_parts[:LANES] + router_parts[LANES:])[:experts]
    narrow = jnp.concatenate(
        [
            router_local,
            gain_a_local[None, :],
            gain_b_local[None, :],
            jnp.zeros((LANES - experts - 2, D), f32),
        ],
        axis=0,
    )
    narrow, up_part = together(narrow, up_part)
    dense = dense_gradient(normed, dq, turned_dk, dkv, narrow, out_part)
    first = dense.shape[1] - D - fill
    out_grad = dense[:, first : first + D]
    down_weight_grad, gate_weight_grad, up_weight_grad = (
        by_expert(part) for part in (down_part, gate_part, up_part)
    )
    spans = [H * HD, KVH * HD, KVH * HD, experts, 1, 1]
    pieces, begin = [], 0
    for span in spans:
        pieces.append(dense[:, begin : begin + span])
        begin += span
    query_grad, key_grad, value_grad, router_grad, gain_a_grad, gain_b_grad = pieces
    return (
        output,
        input_grad.reshape(groups, length, D),
        gain_a_grad[:, 0],
        query_grad,
        key_grad,
        value_grad,
        out_grad,
        gain_b_grad[:, 0],
        router_grad,
        gate_weight_grad,
        up_weight_grad,
        down_weight_grad,
        expert_load,
        prob_mean,
        balance_loss,
    )


def solution(mesh):
    dp_ranks, ranks = mesh.devices.shape
    fine = Mesh(
        mesh.devices.reshape(dp_ranks // 2, 2, ranks // 2, 2), ("dh", "dl", "eh", "el")
    )
    return jax.shard_map(
        on_device,
        mesh=fine,
        in_specs=(
            P(DATA, EXPERT, None),
            P(DATA, None),
            P(DATA, EXPERT, None),
            P(DATA, EXPERT, None),
            P(),
            P(),
            P(),
            P(),
            P(),
            P(),
            P(),
            P(EXPERT, None, None),
            P(EXPERT, None, None),
            P(EXPERT, None, None),
        ),
        out_specs=(
            P(DATA, EXPERT, None),
            P(DATA, EXPERT, None),
            P(DATA),
            P(DATA, None),
            P(DATA, None),
            P(DATA, None),
            P(DATA, None),
            P(DATA),
            P(DATA, None),
            P(EXPERT, DATA, None),
            P(EXPERT, DATA, None),
            P(EXPERT, DATA, None),
            P(),
            P(),
            P(),
        ),
        check_vma=False,
    )
```

```python
import functools
import math

import jax
import jax.numpy as jnp
from jax import lax
from jax.experimental import pallas as pl
from jax.experimental.pallas import tpu as pltpu
from jax.sharding import Mesh
from jax.sharding import PartitionSpec as P

D = 1536
H = 24
KVH = 8
HD = 64
FF = 512
TOPK = 8
EXP_DEV = 5
PROMPT = 1024
LANES = 128
PAIRS = KVH // 2
SHARE = H // KVH
PAIR_Q = 2 * SHARE * HD
ROWS = 256
STACK = SHARE * ROWS
EXPERT = ("eh", "el")
DATA = ("dh", "dl")
VMEM_LIMIT = 63 * 1024 * 1024

epsilon = 1e-05
rope_base = 10000.0
f32 = jnp.float32
bf16 = jnp.bfloat16


def dot(a, b):
    return lax.dot_general(a, b, (((1,), (0,)), ((), ())), preferred_element_type=f32)


def dot_nt(a, b):
    return lax.dot_general(a, b, (((1,), (1,)), ((), ())), preferred_element_type=f32)


def dot_tn(a, b):
    return lax.dot_general(a, b, (((0,), (0,)), ((), ())), preferred_element_type=f32)


def expert_rank():
    return lax.axis_index("eh") * 2 + lax.axis_index("el")


def call(kernel, name, micros, extra=None, **more):
    cost = pl.CostEstimate(flops=int(micros * 2.5e8), bytes_accessed=0, transcendentals=0)
    return pl.pallas_call(
        kernel,
        name=name,
        cost_estimate=cost,
        compiler_params=pltpu.CompilerParams(vmem_limit_bytes=VMEM_LIMIT, **(extra or {})),
        **more,
    )


def shaped(shape, dtype):
    return jax.ShapeDtypeStruct(shape, dtype)


def lane_of(shape):
    return lax.broadcasted_iota(jnp.int32, shape, len(shape) - 1)


def half_swap(values):
    lower = lane_of(values.shape) % HD < HD // 2
    return jnp.where(
        lower, pltpu.roll(values, LANES - HD // 2, 1), pltpu.roll(values, HD // 2, 1)
    )


def resident(shape):
    zeros = (0,) * len(shape)
    return pl.BlockSpec(shape, lambda *_: zeros, pipeline_mode=pl.Buffered(1))


def row_block(width, first=0):
    return pl.BlockSpec((ROWS, width), lambda i: (first + i, 0))


def naming_kernel(capacity, groups, r_ref, o_ref):
    length = r_ref.shape[0]
    rows = groups * length
    lane = lane_of((rows, LANES))
    packed = r_ref[...].astype(jnp.int32)
    chosen = jnp.concatenate(
        [packed[:, g * TOPK : (g + 1) * TOPK] for g in range(groups)], axis=0
    )
    named = jnp.zeros((rows, LANES), f32)
    for k in range(TOPK):
        named = jnp.where(chosen[:, k : k + 1] == lane, 1.0, named)
    earlier = lax.broadcasted_iota(jnp.int32, (rows, rows), 1) < lax.broadcasted_iota(
        jnp.int32, (rows, rows), 0
    )
    slot = dot(jnp.where(earlier, 1.0, 0.0).astype(bf16), named.astype(bf16))
    level = named * jnp.where(slot < capacity, 2.0, 1.0)
    o_ref[...] = level.reshape(groups, length, LANES).astype(bf16)


def naming(kv, capacity, groups, ranks):
    total = kv.shape[0]
    length = total // ranks
    return call(
        functools.partial(naming_kernel, capacity, groups),
        "naming",
        9,
        grid=(ranks,),
        in_specs=[pl.BlockSpec((length, LANES), lambda s: (s, 2 * PAIRS))],
        out_specs=pl.BlockSpec((groups, length, LANES), lambda s: (0, s, 0)),
        out_shape=shaped((groups, total, LANES), bf16),
    )(kv)


def key_value_kernel(x_ref, gain_ref, wk_ref, wv_ref, cos_ref, sin_ref, r_ref, n_ref, kv_ref):
    x = x_ref[...].astype(f32)
    factor = lax.rsqrt(jnp.mean(x * x, axis=1, keepdims=True) + epsilon)
    normed = (x * factor * gain_ref[...]).astype(bf16)
    n_ref[...] = normed
    cosine, sine = cos_ref[...], sin_ref[...]
    key = dot(normed, wk_ref[...])
    for c in range(KVH * HD // LANES):
        part = key[:, c * LANES : (c + 1) * LANES]
        turned = part * cosine + half_swap(part) * sine
        kv_ref[:, c * LANES : (c + 1) * LANES] = turned.astype(bf16)
    kv_ref[:, KVH * HD : 2 * KVH * HD] = dot(normed, wv_ref[...]).astype(bf16)
    kv_ref[:, 2 * KVH * HD :] = r_ref[...]


def key_value(group, length, x, gain, wk, wv, cosine, sine, names):
    first = group * length // ROWS
    width = 2 * KVH * HD + LANES
    return call(
        key_value_kernel,
        "key_value",
        5,
        grid=(length // ROWS,),
        in_specs=[
            row_block(D, first),
            resident((1, D)),
            resident((D, KVH * HD)),
            resident((D, KVH * HD)),
            row_block(LANES, first),
            row_block(LANES, first),
            row_block(LANES),
        ],
        out_specs=[row_block(D), row_block(width)],
        out_shape=[shaped((length, D), bf16), shaped((length, width), bf16)],
    )(x, gain, wk, wv, cosine, sine, names)


def query_kernel(n_ref, wq_ref, cos_ref, sin_ref, q_ref):
    cosine, sine = cos_ref[...], sin_ref[...]
    query = dot(n_ref[...], wq_ref[...])
    for c in range(H * HD // LANES):
        part = query[:, c * LANES : (c + 1) * LANES]
        turned = part * cosine + half_swap(part) * sine
        q_ref[:, c * LANES : (c + 1) * LANES] = turned.astype(bf16) * jnp.asarray(0.125, bf16)


def project_query(group, normed, wq, cosine, sine):
    length = normed.shape[0]
    first = group * length // ROWS
    return call(
        query_kernel,
        "query",
        6,
        grid=(length // ROWS,),
        in_specs=[
            row_block(D),
            resident((D, H * HD)),
            row_block(LANES, first),
            row_block(LANES, first),
        ],
        out_specs=row_block(H * HD),
        out_shape=shaped((length, H * HD), bf16),
    )(normed, wq, cosine, sine)


def stack_heads(ref):
    low = lane_of((ROWS, LANES)) < HD
    parts = [ref[:, c * LANES : (c + 1) * LANES].astype(f32) for c in range(SHARE)]
    rolled0, rolled2 = pltpu.roll(parts[0], HD, 1), pltpu.roll(parts[2], HD, 1)
    zero = jnp.zeros((ROWS, LANES), f32)
    first = [parts[0], rolled0, parts[1]]
    second = [parts[1], rolled2, parts[2]]
    return (
        jnp.concatenate([jnp.where(low, v, zero).astype(bf16) for v in first], axis=0),
        jnp.concatenate([jnp.where(low, zero, v).astype(bf16) for v in second], axis=0),
    )


def unstack_heads(first, second):
    low = lane_of((ROWS, LANES)) < HD
    return (
        jnp.where(low, first[:ROWS], pltpu.roll(first[ROWS : 2 * ROWS], HD, 1)),
        jnp.where(low, first[2 * ROWS :], second[:ROWS]),
        jnp.where(low, pltpu.roll(second[ROWS : 2 * ROWS], HD, 1), second[2 * ROWS :]),
    )


def visit_chunks(block, chunk):
    prompt_blocks = PROMPT // ROWS

    @pl.when(block >= prompt_blocks)
    def _():
        for c in range(PROMPT // (2 * ROWS)):
            chunk(c * 2 * ROWS, 2 * ROWS, False)

    @pl.when(block < prompt_blocks)
    def _():
        def step(c, carry):
            chunk(pl.multiple_of(c * ROWS, ROWS), ROWS, False)
            return carry

        lax.fori_loop(0, block, step, 0)

    @pl.when(block > prompt_blocks)
    def _():
        chunk(pl.multiple_of((block - 1) * ROWS, ROWS), ROWS, True)

    chunk(pl.multiple_of(block * ROWS, ROWS), ROWS, True)


def mask_bias(block, begin, size, start_ref):
    place = begin + lax.broadcasted_iota(jnp.int32, (size, ROWS), 0)
    own = block * ROWS + lax.broadcasted_iota(jnp.int32, (size, ROWS), 1)
    ok = (place <= own) & (place >= start_ref[0, :1, :])
    bias = jnp.where(ok, 0.0, -1e30)
    return jnp.concatenate([bias] * SHARE, axis=1)


def attend_kernel(blocks, q_ref, k_ref, v_ref, start_ref, o_ref, lse_ref, vt_ref, m_ref, l_ref, acc_ref):
    block = expert_rank() * blocks + pl.program_id(1)

    @pl.when(pl.program_id(1) == 0)
    def _():
        vt_ref[...] = jnp.transpose(v_ref[...].astype(f32)).astype(bf16)

    queries = stack_heads(q_ref)
    m_ref[...] = jnp.full_like(m_ref, -1e30)
    l_ref[...] = jnp.zeros_like(l_ref)
    acc_ref[...] = jnp.zeros_like(acc_ref)

    def chunk(begin, size, masked):
        keys = k_ref[pl.ds(begin, size), :]
        values = vt_ref[:, pl.ds(begin, size)]
        bias = mask_bias(block, begin, size, start_ref) if masked else None
        for h in range(2):
            scores = dot_nt(keys, queries[h])
            if masked:
                scores = scores + bias
            before = m_ref[h, :1]
            peak = jnp.maximum(before, jnp.max(scores, axis=0, keepdims=True))
            weight = jnp.exp(scores - peak)
            shrink = jnp.exp(before - peak)
            m_ref[h, :1] = peak
            l_ref[h, :1] = l_ref[h, :1] * shrink + jnp.sum(weight, axis=0, keepdims=True)
            acc_ref[h] = acc_ref[h] * shrink + dot(values, weight.astype(bf16))

    visit_chunks(block, chunk)
    mixed = [jnp.transpose(acc_ref[h] / l_ref[h, :1]) for h in range(2)]
    for c, part in enumerate(unstack_heads(*mixed)):
        o_ref[:, c * LANES : (c + 1) * LANES] = part.astype(bf16)
    for h in range(2):
        total = m_ref[h, :1] + jnp.log(l_ref[h, :1])
        lse_ref[0, 0, h] = jnp.broadcast_to(total, (8, STACK))


def attend(group, query, kv, start_row):
    length = query.shape[0]
    total = kv.shape[0]
    blocks = length // ROWS
    heads = pl.BlockSpec((ROWS, PAIR_Q), lambda p, i: (i, p))
    return call(
        functools.partial(attend_kernel, blocks),
        "attend",
        45,
        grid=(PAIRS, blocks),
        in_specs=[
            heads,
            pl.BlockSpec((total, LANES), lambda p, i: (0, p)),
            pl.BlockSpec((total, LANES), lambda p, i: (0, PAIRS + p)),
            pl.BlockSpec((1, 8, ROWS), lambda p, i: (group, 0, i)),
        ],
        out_specs=[
            heads,
            pl.BlockSpec((1, 1, 2, 8, STACK), lambda p, i: (p, i, 0, 0, 0)),
        ],
        out_shape=[
            shaped(query.shape, bf16),
            shaped((PAIRS, blocks, 2, 8, STACK), f32),
        ],
        scratch_shapes=[
            pltpu.VMEM((LANES, total), bf16),
            pltpu.VMEM((2, 8, STACK), f32),
            pltpu.VMEM((2, 8, STACK), f32),
            pltpu.VMEM((2, LANES, STACK), f32),
        ],
    )(query, kv, kv, start_row)


def attend_back_kernel(
    blocks,
    q_ref,
    g_ref,
    o_ref,
    k_ref,
    v_ref,
    lse_ref,
    start_ref,
    cos_ref,
    sin_ref,
    dq_ref,
    keep_ref,
    send_ref,
    dq_acc,
    dkv_acc,
):
    step = pl.program_id(1)
    block = expert_rank() * blocks + step

    @pl.when(step == 0)
    def _():
        dkv_acc[...] = jnp.zeros_like(dkv_acc)

    dq_acc[...] = jnp.zeros_like(dq_acc)
    queries = stack_heads(q_ref)
    grads = stack_heads(g_ref)
    halves = []
    for c in range(SHARE):
        cols = slice(c * LANES, (c + 1) * LANES)
        product = jnp.transpose(g_ref[:, cols].astype(f32) * o_ref[:, cols].astype(f32))
        halves.append(jnp.sum(product[:HD], axis=0, keepdims=True))
        halves.append(jnp.sum(product[HD:], axis=0, keepdims=True))
    inner = [jnp.concatenate(halves[:SHARE], axis=1), jnp.concatenate(halves[SHARE:], axis=1)]

    def chunk(begin, size, masked):
        keys = k_ref[pl.ds(begin, size), :]
        values = v_ref[pl.ds(begin, size), :]
        bias = mask_bias(block, begin, size, start_ref) if masked else None
        key_sum, value_sum = None, None
        for h in range(2):
            scores = dot_nt(keys, queries[h]) - lse_ref[0, 0, h, :1, :]
            if masked:
                scores = scores + bias
            probs = jnp.exp(scores)
            probs_grad = dot_nt(values, grads[h])
            scores_grad = (probs * (probs_grad - inner[h])).astype(bf16)
            value_part = dot(probs.astype(bf16), grads[h])
            key_part = dot(scores_grad, queries[h])
            key_sum = key_part if key_sum is None else key_sum + key_part
            value_sum = value_part if value_sum is None else value_sum + value_part
            dq_acc[h] += dot_tn(scores_grad, keys)
        dkv_acc[0, pl.ds(begin, size), :] += key_sum
        dkv_acc[1, pl.ds(begin, size), :] += value_sum

    visit_chunks(block, chunk)
    cosine, sine = cos_ref[...], sin_ref[...]
    for c, part in enumerate(unstack_heads(dq_acc[0], dq_acc[1])):
        part = part * 0.125
        turned = part * cosine - half_swap(part) * sine
        dq_ref[:, c * LANES : (c + 1) * LANES] = turned.astype(bf16)

    @pl.when(step == blocks - 1)
    def _():
        length = blocks * ROWS
        own = lax.axis_index("el")
        for chip in range(dkv_acc.shape[1] // (2 * length)):
            mine = pl.multiple_of((2 * chip + own) * length, length)
            other = pl.multiple_of((2 * chip + 1 - own) * length, length)
            for i in range(2):
                keep_ref[chip, i] = dkv_acc[i, pl.ds(mine, length), :].astype(bf16)
                send_ref[chip, i] = dkv_acc[i, pl.ds(other, length), :].astype(bf16)


def attend_back_and_swap(blocks, pairs, columns, *refs):
    away_ref = refs[9]
    here_ref = refs[-5]
    send_sem, recv_sem = refs[-2:]
    at = pl.program_id(0) * blocks + pl.program_id(1)
    peer = {"dl": 1 - lax.axis_index("dl")}
    exchange = pltpu.make_async_remote_copy(
        src_ref=away_ref.at[:, :, columns],
        dst_ref=here_ref.at[:, :, columns],
        send_sem=send_sem,
        recv_sem=recv_sem,
        device_id=peer,
        device_id_type=pl.DeviceIdType.MESH,
    )

    @pl.when(at == 0)
    def _():
        barrier = pltpu.get_barrier_semaphore()
        pl.semaphore_signal(barrier, inc=1, device_id=peer, device_id_type=pl.DeviceIdType.MESH)
        pl.semaphore_wait(barrier, 1)
        exchange.start()

    attend_back_kernel(blocks, *refs[:9], *refs[-8:-5], *refs[-4:-2])

    @pl.when(at == pairs * blocks - 1)
    def _():
        exchange.wait()


def attend_back(
    group, span, query, grad, mixed, kv, lse, start_row, cosine, sine, away, collective, kept
):
    length = query.shape[0]
    total = kv.shape[0]
    blocks = length // ROWS
    first = group * blocks
    chips = total // (2 * length)
    base, pairs = span
    side = pl.BlockSpec((chips, 2, length, LANES), lambda p, i: (0, 0, 0, p))
    heads = pl.BlockSpec((ROWS, PAIR_Q), lambda p, i: (i, base + p))
    table = pl.BlockSpec((ROWS, LANES), lambda p, i: (first + i, 0))
    swaps = [] if away is None else [away[0], *away[2]]
    arriving = [] if away is None else [away[0]]
    if away is None:
        kernel = lambda *refs: attend_back_kernel(blocks, *refs[:9], *refs[-5:])
        extra = {}
    else:
        kernel = functools.partial(attend_back_and_swap, blocks, pairs, away[1])
        extra = dict(collective_id=collective, has_side_effects=True)
    anywhere = pl.BlockSpec(memory_space=pl.ANY)
    return call(
        kernel,
        "attend_back",
        16 * pairs,
        extra,
        grid=(pairs, blocks),
        in_specs=[
            heads,
            heads,
            heads,
            pl.BlockSpec((total, LANES), lambda p, i: (0, base + p)),
            pl.BlockSpec((total, LANES), lambda p, i: (0, PAIRS + base + p)),
            pl.BlockSpec((1, 1, 2, 8, STACK), lambda p, i: (base + p, i, 0, 0, 0)),
            pl.BlockSpec((1, 8, ROWS), lambda p, i: (group, 0, i)),
            table,
            table,
        ]
        + [anywhere] * len(swaps + kept),
        out_specs=[
            heads,
            side,
            side,
        ]
        + [anywhere] * len(arriving),
        input_output_aliases={
            **({9 + len(swaps): 0} if kept else {}),
            **({10: 3} if len(swaps) > 1 else {}),
        },
        out_shape=[
            shaped(query.shape, bf16),
            shaped((chips, 2, length, pairs * LANES), bf16),
            shaped((chips, 2, length, pairs * LANES), bf16),
        ]
        + [shaped(one.shape, one.dtype) for one in arriving],
        scratch_shapes=[
            pltpu.VMEM((2, STACK, LANES), f32),
            pltpu.VMEM((2, total, LANES), f32),
        ]
        + [pltpu.SemaphoreType.DMA] * (2 * len(arriving)),
    )(query, grad, mixed, kv, kv, lse, start_row, cosine, sine, *swaps, *kept)


def branch_kernel(a_ref, x_ref, wo_ref, gain_ref, wr_ref, m_ref, n_ref, ps_ref):
    middle = x_ref[...].astype(f32) + dot(a_ref[...], wo_ref[...])
    m_ref[...] = middle
    factor = lax.rsqrt(jnp.mean(middle * middle, axis=1, keepdims=True) + epsilon)
    normed = (middle * factor * gain_ref[...]).astype(bf16)
    n_ref[...] = normed
    add_up(ps_ref, fold_rows(router(normed, wr_ref[...])))


def branch(group, attended, x, wo, gain, wr):
    length = attended.shape[0]
    return call(
        branch_kernel,
        "branch",
        6,
        grid=(length // ROWS,),
        in_specs=[
            row_block(H * HD),
            row_block(D, group * length // ROWS),
            resident((H * HD, D)),
            resident((1, D)),
            resident((D, LANES)),
        ],
        out_specs=[row_block(D), row_block(D), pl.BlockSpec((8, LANES), lambda i: (0, 0))],
        out_shape=[
            shaped((length, D), f32),
            shaped((length, D), bf16),
            shaped((8, LANES), f32),
        ],
    )(attended, x, wo, gain, wr)


def router(normed, weight):
    count = EXP_DEV * 2 * lax.axis_size("eh")
    logits = dot(normed, weight)
    logits = jnp.where(lane_of(logits.shape) < count, logits, -1e30)
    powers = jnp.exp(logits - jnp.max(logits, axis=1, keepdims=True))
    return powers / jnp.sum(powers, axis=1, keepdims=True)


def experts_kernel(
    x_ref, c_ref, t_ref, wr_ref, wg_ref, wu_ref, wd_ref, *refs
):
    mix_ref, rows_ref, x_out, c_out, hid_ref, gate_ref, up_ref = refs[-7:]
    x, cot = x_ref[...], c_ref[...]
    x_out[...] = x
    c_out[...] = cot
    level = t_ref[0].astype(f32)
    picked = jnp.where(level > 0.5, router(x, wr_ref[...]), 0.0)
    share = picked / jnp.sum(picked, axis=1, keepdims=True)
    share = jnp.where(level > 1.5, share, 0.0)
    lane = lane_of(share.shape)
    base = EXP_DEV * expert_rank()
    share = pltpu.roll(share, lax.rem(LANES - base, LANES), 1)
    mix, rows = None, None
    gate_grads = jnp.zeros(share.shape, bf16)
    for e in range(EXP_DEV):
        gate = dot(x, wg_ref[e])
        up = dot(x, wu_ref[e])
        hidden_grad = dot(cot, wd_ref[e])
        sigmoid = jax.nn.sigmoid(gate)
        active = gate * sigmoid
        hidden = active * up
        inner = jnp.sum(hidden * hidden_grad, axis=1, keepdims=True)
        coarse = inner.astype(bf16)
        fine = (inner - coarse.astype(f32)).astype(bf16)
        gate_grads = jnp.where(lane == base + e, coarse, gate_grads)
        gate_grads = jnp.where(lane == LANES // 2 + base + e, fine, gate_grads)
        weight = share[:, e : e + 1]
        scaled = (hidden * weight).astype(bf16)
        hidden_grad = hidden_grad * weight
        up_grad = (hidden_grad * active).astype(bf16)
        gate_grad = (hidden_grad * up * sigmoid * (1.0 + gate * (1.0 - sigmoid))).astype(bf16)
        cols = slice(e * FF, (e + 1) * FF)
        hid_ref[:, cols] = scaled
        gate_ref[:, cols] = gate_grad
        up_ref[:, cols] = up_grad
    for e in range(EXP_DEV):
        cols = slice(e * FF, (e + 1) * FF)
        mix_part = dot_nt(hid_ref[:, cols], wd_ref[e])
        rows_part = dot_nt(gate_ref[:, cols], wg_ref[e]) + dot_nt(up_ref[:, cols], wu_ref[e])
        mix = mix_part if mix is None else mix + mix_part
        rows = rows_part if rows is None else rows + rows_part
    mix_ref[...] = mix.astype(bf16)
    rows_ref[:, :D] = rows.astype(bf16)
    rows_ref[:, D:] = gate_grads


def experts_pass(group, groups, x, cot, level, wr, wg, wu, wd, kept):
    count = x.shape[0]
    first = group * count // ROWS
    whole = groups * count
    side = pl.BlockSpec(memory_space=pl.ANY)
    widths = [D, D, EXP_DEV * FF, EXP_DEV * FF, EXP_DEV * FF]
    return call(
        experts_kernel,
        "experts",
        113,
        grid=(count // ROWS,),
        in_specs=[
            row_block(D),
            row_block(D),
            pl.BlockSpec((1, ROWS, LANES), lambda i: (group, i, 0)),
            resident((D, LANES)),
            resident((EXP_DEV, D, FF)),
            resident((EXP_DEV, D, FF)),
            resident((EXP_DEV, D, FF)),
        ]
        + [side] * len(kept),
        out_specs=[row_block(D), row_block(D + LANES)]
        + [row_block(width, first) for width in widths],
        out_shape=[
            shaped((count, D), bf16),
            shaped((count, D + LANES), bf16),
        ]
        + [shaped((whole, width), bf16) for width in widths],
        input_output_aliases={7 + i: 2 + i for i in range(len(kept))},
    )(x, cot, level, wr, wg, wu, wd, *kept)


def norm_back(grad, normed, factor, gain):
    scaled = grad * gain
    return factor * (scaled - normed * jnp.mean(scaled * normed, axis=1, keepdims=True))


def fold_rows(values):
    return jnp.sum(values.reshape(values.shape[0] // 8, 8, values.shape[1]), axis=0)


def add_up(ref, part):
    @pl.when(pl.program_id(0) == 0)
    def _():
        ref[...] = part

    @pl.when(pl.program_id(0) > 0)
    def _():
        ref[...] += part


def middle_kernel(
    r_ref, t_ref, m_ref, n_ref, c_ref, gain_ref, wr_ref, wo_ref,
    mg_ref, b_ref, ag_ref, l_ref, dg_ref,
):
    probs = router(n_ref[...], wr_ref[...])
    level = t_ref[0].astype(f32)
    sel = jnp.where(level > 0.5, 1.0, 0.0)
    gate_grad = r_ref[:, D:].astype(f32)
    gate_grad = gate_grad + pltpu.roll(gate_grad, LANES // 2, 1)
    gate_grad = jnp.where(level > 1.5, gate_grad, 0.0)
    picked = probs * sel
    total = jnp.sum(picked, axis=1, keepdims=True)
    share = picked / total
    inner = jnp.sum(gate_grad * share, axis=1, keepdims=True)
    probs_grad = (gate_grad - inner) / total * sel
    logits_grad = probs * (probs_grad - jnp.sum(probs_grad * probs, axis=1, keepdims=True))
    coarse = logits_grad.astype(bf16)
    fine = (logits_grad - coarse.astype(f32)).astype(bf16)
    l_ref[:, :LANES] = coarse
    l_ref[:, LANES:] = fine
    grad = r_ref[:, :D].astype(f32) + dot_nt(coarse, wr_ref[...]) + dot_nt(fine, wr_ref[...])
    middle = m_ref[...]
    factor = lax.rsqrt(jnp.mean(middle * middle, axis=1, keepdims=True) + epsilon)
    normed = middle * factor
    add_up(dg_ref, fold_rows(grad * normed))
    middle_grad = c_ref[...].astype(f32) + norm_back(grad, normed, factor, gain_ref[...])
    mg_ref[...] = middle_grad
    low = middle_grad.astype(bf16)
    b_ref[...] = low
    ag_ref[...] = dot_nt(low, wo_ref[...]).astype(bf16)


def middle_back(group, rows, level, middle, normed, cot, gain, wr, wo):
    length = rows.shape[0]
    first = group * length // ROWS
    corner = lambda width: pl.BlockSpec((8, width), lambda i: (0, 0))
    return call(
        middle_kernel,
        "middle_back",
        8,
        grid=(length // ROWS,),
        in_specs=[
            row_block(D + LANES),
            pl.BlockSpec((1, ROWS, LANES), lambda i: (group, i, 0)),
            row_block(D), row_block(D), row_block(D, first),
            resident((1, D)), resident((D, LANES)), resident((H * HD, D)),
        ],
        out_specs=[
            row_block(D), row_block(D), row_block(H * HD), row_block(2 * LANES),
            corner(D),
        ],
        out_shape=[
            shaped((length, D), f32),
            shaped((length, D), bf16),
            shaped((length, H * HD), bf16),
            shaped((length, 2 * LANES), bf16),
            shaped((8, D), f32),
        ],
    )(rows, level, middle, normed, cot, gain, wr, wo)


def input_kernel(
    dq_ref, dk_ref, dv_ref, x_ref, mg_ref, cos_ref, sin_ref, gain_ref, wq_ref, wk_ref, wv_ref,
    out_ref, dk_out, dg_ref,
):
    cosine, sine = cos_ref[...], sin_ref[...]
    for c in range(KVH * HD // LANES):
        part = dk_ref[0, :, c * LANES : (c + 1) * LANES].astype(f32)
        turned = part * cosine - half_swap(part) * sine
        dk_out[:, c * LANES : (c + 1) * LANES] = turned.astype(bf16)
    grad = dot_nt(dq_ref[...], wq_ref[...])
    grad = grad + dot_nt(dk_out[...], wk_ref[...])
    grad = grad + dot_nt(dv_ref[0], wv_ref[...])
    x = x_ref[...].astype(f32)
    factor = lax.rsqrt(jnp.mean(x * x, axis=1, keepdims=True) + epsilon)
    normed = x * factor
    add_up(dg_ref, fold_rows(grad * normed))
    out_ref[...] = mg_ref[...] + norm_back(grad, normed, factor, gain_ref[...])


def input_back(group, groups, dq, dkv, x, middle_grad, cosine, sine, gain, wq, wk, wv, kept):
    length = dq.shape[0]
    first = group * length // ROWS
    kernel = lambda *refs: input_kernel(*refs[:11], *refs[-3:])
    return call(
        kernel,
        "input_back",
        8,
        grid=(length // ROWS,),
        in_specs=[
            row_block(H * HD),
            pl.BlockSpec((1, ROWS, KVH * HD), lambda i: (0, i, 0)),
            pl.BlockSpec((1, ROWS, KVH * HD), lambda i: (1, i, 0)),
            row_block(D, first),
            row_block(D),
            row_block(LANES, first),
            row_block(LANES, first),
            resident((1, D)),
            resident((D, H * HD)),
            resident((D, KVH * HD)),
            resident((D, KVH * HD)),
        ]
        + [pl.BlockSpec(memory_space=pl.ANY)] * len(kept),
        out_specs=[
            row_block(D, first),
            row_block(KVH * HD),
            pl.BlockSpec((8, D), lambda i: (0, 0)),
        ],
        out_shape=[
            shaped((groups * length, D), f32),
            shaped((length, KVH * HD), bf16),
            shaped((8, D), f32),
        ],
        input_output_aliases={11: 0} if kept else {},
    )(dq, dkv, dkv, x, middle_grad, cosine, sine, gain, wq, wk, wv, *kept)


def transpose_into(turned, lefts):
    length = lefts[0].shape[0]
    for g, left in enumerate(lefts):
        for c in range(0, D, 2 * LANES):
            part = left[:, c : c + 2 * LANES].astype(f32)
            turned[c : c + 2 * LANES, g * length : (g + 1) * length] = jnp.transpose(part).astype(
                bf16
            )


def out_kernel(groups, *refs):
    lefts, rights = refs[:groups], refs[groups : 2 * groups]
    out_ref, turned = refs[-2:]
    length = lefts[0].shape[0]

    @pl.when(pl.program_id(0) == 0)
    def _():
        transpose_into(turned, lefts)

    total = None
    for g in range(groups):
        part = dot(turned[:, g * length : (g + 1) * length], rights[g][...])
        total = part if total is None else total + part
    out_ref[...] = total.astype(bf16)


def out_gradient(lefts, rights):
    groups, length = len(lefts), lefts[0].shape[0]
    width = 4 * LANES
    return call(
        functools.partial(out_kernel, groups),
        "out_grad",
        10,
        grid=(D // width,),
        in_specs=[resident((length, D))] * groups
        + [pl.BlockSpec((length, width), lambda i: (0, i))] * groups,
        out_specs=pl.BlockSpec((D, width), lambda i: (0, i)),
        out_shape=shaped((D, D), bf16),
        scratch_shapes=[pltpu.VMEM((D, groups * length), bf16)],
    )(*lefts, *rights)


def dense_kernel(groups, sizes, *refs):
    data, chips, shard, width, full, late = sizes
    lefts, queries, keys, values = (refs[i * groups : (i + 1) * groups] for i in range(4))
    narrow_ref, late_ref, out_ref = refs[4 * groups : 4 * groups + 3]
    (turned, keep1, send1, got1, keep2, send2, got2, sum2, got3, sum3, got4, sum4, near5, far5,
     wide2, wide3, keep6, send6, got6) = refs[4 * groups + 3 : 4 * groups + 22]
    sems = refs[4 * groups + 22 :]
    half = width // 2
    length = lefts[0].shape[0]
    ranks = 2 * chips
    dh, dl, eh, el = (lax.axis_index(name) for name in ("dh", "dl", "eh", "el"))

    def near(hop, core):
        return {"eh": lax.rem(eh + hop, chips), "el": core}

    peers = [{"el": 1 - el}, {"dl": 1 - dl}]
    for hop in range(1, chips):
        peers.append(near(hop, el))
    for hop in range(1, data):
        peers.append({"dh": lax.rem(dh + hop, data)})
    barrier = pltpu.get_barrier_semaphore()
    for peer in peers:
        pl.semaphore_signal(barrier, inc=1, device_id=peer, device_id_type=pl.DeviceIdType.MESH)
    transpose_into(turned, lefts)
    pl.semaphore_wait(barrier, len(peers))

    def copy(source, target, phase, k, lane, peer):
        return pltpu.make_async_remote_copy(
            src_ref=source,
            dst_ref=target,
            send_sem=sems[2 * phase].at[k, lane],
            recv_sem=sems[2 * phase + 1].at[k, lane],
            device_id=peer,
            device_id_type=pl.DeviceIdType.MESH,
        )

    def crossed(k):
        return k < full and k % 2 == 1

    def slot(k):
        return k // 2 if k < full else (full + 1) // 2 + k - full

    def copies(phase, k):
        if phase == 0:
            return [copy(send1.at[k], got1.at[k], 0, k, 0, {"el": 1 - el})]
        if phase == 1:
            source, target = (send6, got6) if crossed(k) else (send2, got2)
            at = k // 2
            return [
                copy(source.at[at, hop - 1], target.at[at, hop - 1], 1, k, hop - 1, near(hop, el))
                for hop in range(1, chips)
            ]
        if phase == 2:
            if crossed(k):
                at = k // 2
                return [copy(wide2.at[at, 1 - dl], wide3.at[at], 2, k, 0, {"dl": 1 - dl})]
            at = slot(k)
            return [copy(sum2.at[at, 1 - dl], got3.at[at], 2, k, 0, {"dl": 1 - dl})]
        if phase == 3:
            found = []
            for hop in range(1, data):
                away = lax.rem(dh + hop, data)
                found.append(
                    copy(sum3.at[k, away], got4.at[k, hop - 1], 3, k, hop - 1, {"dh": away})
                )
            return found
        if phase == 4:
            return [
                copy(sum4.at[k], near5.at[k, eh], 4, k, hop - 1, near(hop, el))
                for hop in range(1, chips)
            ]
        return [copy(near5.at[k], far5.at[k], 5, k, 0, {"el": 1 - el})]

    def start(phase, k):
        for one in copies(phase, k):
            one.start()

    def arrived(phase, k):
        for one in copies(phase, k):
            one.wait_recv()

    def finish_shard(k):
        base = k * width if k < full else full * width + (k - full) * LANES

        def put(side, chip, block):
            place = side * chips + chip
            place = place * LANES if k < full else place * late * LANES
            at = pl.multiple_of(base + place, LANES)
            out_ref[:, pl.ds(at, LANES)] = block.astype(f32)

        for chip in range(chips):
            put(el, chip, near5[k, chip])
            put(1 - el, chip, far5[k, chip])

    def piece(column):
        size = KVH * HD
        if column >= H * HD + 2 * size:
            if column > H * HD + 2 * size:
                return jnp.zeros((D, size), bf16)
            part = jnp.transpose(narrow_ref[...])
            return jnp.concatenate([part, jnp.zeros((D, size - LANES), f32)], axis=1).astype(bf16)
        total = None
        for g in range(groups):
            if column < H * HD:
                block = queries[g][:, column : column + size]
            elif column < H * HD + size:
                block = keys[g][...]
            else:
                block = values[g][1]
            one = dot(turned[:, g * length : (g + 1) * length], block)
            total = one if total is None else total + one
        return total.astype(bf16)

    def stage_compute(k):
        if k < full:
            part = [piece(k * width + c) for c in range(0, width, KVH * HD)]
            part = part[0] if len(part) == 1 else jnp.concatenate(part, axis=1)

            @pl.when(el == 0)
            def _():
                keep1[k] = part[:, :half]
                send1[k] = part[:, half:]

            @pl.when(el == 1)
            def _():
                keep1[k] = part[:, half:]
                send1[k] = part[:, :half]

            start(0, k)

    def hand_out(block, chip, keep, send):
        hop = lax.rem(chip + chips - eh, chips)

        @pl.when(hop == 0)
        def _():
            keep[...] = block

        @pl.when(hop > 0)
        def _():
            send[hop - 1] = block

    def chip_columns(chip):
        return slice(chip * LANES, (chip + 1) * LANES)

    def stage_core(k):
        arrived(0, k)
        met = (keep1[k].astype(f32) + got1[k].astype(f32)).astype(bf16)
        at = k // 2
        if crossed(k):
            for far in range(data):
                for side in range(2):
                    first = (2 * far + side) * shard
                    wide2[at, side, far] = met[first : first + shard]
            start(2, k)
        else:
            for chip in range(chips):
                hand_out(met[:, chip_columns(chip)], chip, keep2.at[at], send2.at[at])
            start(1, k)

    def stage_second(k):
        at = k // 2
        if crossed(k):
            arrived(2, k)
            met = (wide2[at, dl].astype(f32) + wide3[at].astype(f32)).astype(bf16)
            for chip in range(chips):
                hand_out(met[:, :, chip_columns(chip)], chip, keep6.at[at], send6.at[at])
            start(1, k)
        else:
            arrived(1, k)
            total = keep2[at].astype(f32)
            for hop in range(1, chips):
                total = total + got2[at, hop - 1].astype(f32)
            spread(k, total.astype(bf16))

    def spread(k, total):
        for far in range(data):
            for side in range(2):
                first = (2 * far + side) * shard
                sum2[slot(k), side, far] = total[first : first + shard]
        start(2, k)

    def stage_third(k):
        if crossed(k):
            at = k // 2
            arrived(1, k)
            total = keep6[at].astype(f32)
            for hop in range(1, chips):
                total = total + got6[at, hop - 1].astype(f32)
        else:
            at = slot(k)
            arrived(2, k)
            total = sum2[at, dl].astype(f32) + got3[at].astype(f32)
        sum3[k] = total.astype(bf16)
        start(3, k)

    def stage_far(k):
        arrived(3, k)
        total = sum3[k, dh].astype(f32)
        for hop in range(1, data):
            total = total + got4[k, hop - 1].astype(f32)
        total = total.astype(bf16)
        sum4[k] = total
        near5[k, eh] = total
        start(4, k)

    def stage_gather(k):
        arrived(4, k)
        start(5, k)

    def stage_last(k):
        arrived(5, k)
        finish_shard(k)

    everything = list(range(full, full + late)) + list(range(full))
    for k in range(full, full + late):
        first = (k - full) * LANES
        spread(k, late_ref[:, first : first + LANES])
    stages = (
        stage_compute,
        stage_core,
        stage_second,
        stage_third,
        stage_far,
        stage_gather,
        stage_last,
    )
    for step in range(full + len(stages) - 1):
        for delay, stage in enumerate(stages):
            if 0 <= step - delay < full:
                stage(step - delay)
        if step < 4:
            for k in range(full, full + late):
                stages[3 + step](k)
    for k in everything:
        for phase in range(6):
            if k < full or phase > 1:
                for one in copies(phase, k):
                    one.wait_send()


def dense_gradient(lefts, queries, keys, values, narrow, late_part):
    groups = len(lefts)
    data, chips = lax.axis_size("dh"), lax.axis_size("eh")
    shard = D // (2 * data)
    width = 2 * chips * LANES
    columns = H * HD + 2 * KVH * HD
    full = -(-(columns + LANES) // width)
    late = late_part.shape[1] // LANES
    total = full + late
    half, ranks = width // 2, 2 * chips
    sizes = (data, chips, shard, width, full, late)
    lanes = [1, chips - 1, 1, data - 1, chips - 1, 1]
    even, odd = (full + 1) // 2, full // 2
    sems = []
    for count in lanes:
        sems += [pltpu.SemaphoreType.DMA((total, count))] * 2
    operands = [*lefts, *queries, *keys, *values, narrow, late_part]
    whole = pl.BlockSpec(memory_space=pltpu.VMEM)
    return pl.pallas_call(
        functools.partial(dense_kernel, groups, sizes),
        name="dense_grad",
        in_specs=[whole] * len(operands),
        out_specs=whole,
        out_shape=shaped((shard, full * width + late * ranks * LANES), f32),
        scratch_shapes=[
            pltpu.VMEM((D, groups * lefts[0].shape[0]), bf16),
            pltpu.VMEM((full, D, half), bf16),
            pltpu.VMEM((full, D, half), bf16),
            pltpu.VMEM((full, D, half), bf16),
            pltpu.VMEM((even, D, LANES), bf16),
            pltpu.VMEM((even, chips - 1, D, LANES), bf16),
            pltpu.VMEM((even, chips - 1, D, LANES), bf16),
            pltpu.VMEM((even + late, 2, data, shard, LANES), bf16),
            pltpu.VMEM((even + late, data, shard, LANES), bf16),
            pltpu.VMEM((total, data, shard, LANES), bf16),
            pltpu.VMEM((total, data - 1, shard, LANES), bf16),
            pltpu.VMEM((total, shard, LANES), bf16),
            pltpu.VMEM((total, chips, shard, LANES), bf16),
            pltpu.VMEM((total, chips, shard, LANES), bf16),
            pltpu.VMEM((odd, 2, data, shard, half), bf16),
            pltpu.VMEM((odd, data, shard, half), bf16),
            pltpu.VMEM((odd, data, shard, LANES), bf16),
            pltpu.VMEM((odd, chips - 1, data, shard, LANES), bf16),
            pltpu.VMEM((odd, chips - 1, data, shard, LANES), bf16),
        ]
        + sems,
        cost_estimate=pl.CostEstimate(
            flops=int(80 * 9e8), bytes_accessed=0, transcendentals=0
        ),
        compiler_params=pltpu.CompilerParams(
            vmem_limit_bytes=VMEM_LIMIT, collective_id=0, has_side_effects=True
        ),
    )(*operands)


def widen(values):
    return jnp.pad(values, ((0, 0), (0, LANES - values.shape[1])))


def swap(values, axis):
    return lax.ppermute(values, axis, [(0, 1), (1, 0)])


def pick(values, index):
    return lax.dynamic_index_in_dim(values, index, 1, keepdims=False)


def pair_slices(values, shard):
    parts = values.reshape(-1, 2, shard, values.shape[1])
    own = lax.axis_index("dl")
    return pick(parts, own), pick(parts, 1 - own)


def pair_parts(values, shard):
    own, away = pair_slices(values, shard)
    return own, swap(away, "dl")


def far_sum(own, met):
    met = (own + met).reshape(-1, own.shape[2])
    return lax.psum_scatter(met, "dh", scatter_dimension=0, tiled=True)


def take(values, axis, index):
    return lax.dynamic_index_in_dim(values, index, axis, keepdims=False)


def chip_sum(met):
    chips = lax.axis_size("eh")
    chip = lax.axis_index("eh")
    total = take(met, 0, chip)
    for hop in range(1, chips):
        order = [(i, (i + hop) % chips) for i in range(chips)]
        away = take(met, 0, lax.rem(chip + hop, chips))
        total = total + lax.ppermute(away, "eh", order)
    return total


def cut(array, index, size):
    return lax.dynamic_slice_in_dim(array, index * size, size, 1)


def column_core_sum(values):
    half = values.shape[1] // 2
    own = lax.axis_index("el")
    return cut(values, own, half) + swap(cut(values, 1 - own, half), "el")


def column_chip_sum(met):
    chips, chip = lax.axis_size("eh"), lax.axis_index("eh")
    size = met.shape[1] // chips
    total = cut(met, chip, size)
    for hop in range(1, chips):
        order = [(i, (i + hop) % chips) for i in range(chips)]
        away = cut(met, lax.rem(chip + hop, chips), size)
        total = total + lax.ppermute(away, "eh", order)
    return total


def sum_steps():
    for axis in ("el", "eh", "dl", "dh"):
        count = lax.axis_size(axis)
        hop = 1
        while hop < count:
            order = [(i, i ^ hop) for i in range(count)]
            yield lambda v, axis=axis, order=order: v + lax.ppermute(v, axis, order)
            hop *= 2


def together(*values):
    return lax.optimization_barrier(values)


def on_device(
    tokens,
    segments,
    routes,
    cotangent,
    attention_gain,
    query_weight,
    key_weight,
    value_weight,
    out_weight,
    mixture_gain,
    router_weight,
    gate_weight,
    up_weight,
    down_weight,
):
    groups, length, _ = tokens.shape
    each = range(groups)
    rows = groups * length
    ranks = lax.axis_size("eh") * 2
    dp_ranks = lax.axis_size("dh") * 2
    rank = expert_rank()
    experts = EXP_DEV * ranks
    capacity = (rows * TOPK * 5 // (4 * experts) + 7) // 8 * 8
    all_tokens = rows * dp_ranks * ranks
    first_row = rank * length
    shard = D // dp_ranks

    seg_full = jnp.concatenate([jnp.full((groups, PROMPT), -1, jnp.int32), segments], axis=1)
    seg_own = lax.dynamic_slice_in_dim(seg_full, first_row, length, 1)
    earlier = jnp.sum((segments[:, None, :] < seg_own[:, :, None]).astype(jnp.int32), axis=2)
    position = first_row + jnp.arange(length, dtype=jnp.int32)[None, :]
    place = position - earlier
    start = jnp.where(position >= PROMPT, PROMPT + earlier, 0)
    half = HD // 2
    lane = jnp.arange(LANES, dtype=jnp.int32)
    frequency = jnp.exp(-math.log(rope_base) * (lane % half).astype(f32) / half)
    angles = place.astype(f32).reshape(rows, 1) * frequency
    cosine = jnp.cos(angles)
    sine = jnp.sin(angles) * jnp.where(lane % HD < half, -1.0, 1.0)
    start_row = jnp.broadcast_to(start[:, None, :], (groups, 8, length))

    names = jnp.concatenate([routes[g] for g in each], axis=1).astype(bf16)
    names = widen(names)
    cot_rows = cotangent.reshape(rows, D)
    cot_all = [lax.all_gather(cotangent[g], EXPERT, axis=0, tiled=True) for g in each]

    x = tokens.reshape(rows, D)
    gain_a = attention_gain.reshape(1, D)
    gain_b = mixture_gain.reshape(1, D)
    router_wide = widen(router_weight)
    normed, query, kv = [None] * groups, [None] * groups, [None] * groups
    for g in each:
        normed[g], kv_own = key_value(
            g, length, x, gain_a, key_weight, value_weight, cosine, sine, names
        )
        kv[g] = lax.all_gather(kv_own, EXPERT, axis=0, tiled=True)
    for g in each:
        query[g] = project_query(g, normed[g], query_weight, cosine, sine)
    level = naming(kv[groups - 1], capacity, groups, ranks)
    level_own = lax.dynamic_slice_in_dim(level, first_row, length, 1)
    kv[0], query = together(kv[0], query)
    attended, lse = [None] * groups, [None] * groups
    middle, hidden_low, hidden_all = [None] * groups, [None] * groups, [None] * groups
    probs_local = 0.0
    for g in each:
        attended[g], lse[g] = attend(g, query[g], kv[g], start_row)
        if g == groups - 1:
            attended[g], cot_all[0] = together(attended[g], cot_all[0])
        middle[g], hidden_low[g], probs_part = branch(
            g, attended[g], x, out_weight, gain_b, router_wide
        )
        probs_local += jnp.sum(probs_part, axis=0)
        hidden_all[g] = lax.all_gather(hidden_low[g], EXPERT, axis=0, tiled=True)

    counts = jnp.sum((level_own > 0.5).astype(f32), axis=(0, 1))
    stats = jnp.stack([counts, probs_local])[:, :experts]
    steps = sum_steps()

    def beside(value, stats):
        step = next(steps, None)
        return (value, stats) if step is None else together(value, step(stats))

    kept, rows_back, mixture = [], [], []
    for g in each:
        if g > 0:
            kept[0], cot_all[g] = together(kept[0], cot_all[g])
            hidden_all[g], stats = beside(hidden_all[g], stats)
        mix, rows_grad, *kept = experts_pass(
            g, groups, hidden_all[g], cot_all[g], level, router_wide,
            gate_weight, up_weight, down_weight, kept,
        )
        rows_back.append(lax.psum_scatter(rows_grad, EXPERT, scatter_dimension=0, tiled=True))
        mixture.append(mix)
        if g < groups - 1:
            mixture[g] = lax.psum_scatter(mix, EXPERT, scatter_dimension=0, tiled=True)
    x_all, cot_both, hidden, gate_back, up_back = kept
    hidden, mixture[0] = together(hidden, mixture[0])
    hidden, stats = beside(hidden, stats)
    down_local = dot_tn(cot_both, hidden).astype(bf16)
    x_all, down_local = together(x_all, down_local)
    gate_back, stats = beside(gate_back, stats)
    gate_local = dot_tn(x_all, gate_back).astype(bf16)
    up_back, gate_local = together(up_back, gate_local)
    gate_own, gate_met = pair_parts(gate_local, shard)
    up_back, mix = together(up_back, mixture[-1])
    mixture[-1] = lax.psum_scatter(mix, EXPERT, scatter_dimension=0, tiled=True)
    up_back, stats = beside(up_back, stats)
    up_local = dot_tn(x_all, up_back).astype(bf16)
    rows_back[0], up_local = together(rows_back[0], up_local)
    rows_back[0], stats = beside(rows_back[0], stats)
    for step in steps:
        stats = step(stats)
    expert_load = stats[0] * experts / (all_tokens * TOPK)
    prob_mean = stats[1] * experts / all_tokens
    balance_loss = jnp.sum(expert_load * prob_mean) / experts

    def by_expert(part):
        return jnp.stack([part[:, e * FF : (e + 1) * FF] for e in range(EXP_DEV)]).astype(f32)

    middle_grad, branch_grad, attended_grad, logits_grad, dq, dkv = (
        [None] * groups for _ in range(6)
    )
    gain_b_local, last = 0.0, groups - 1
    down_far = lax.psum_scatter(down_local, "dh", scatter_dimension=0, tiled=True)
    for g in each:
        middle_grad[g], branch_grad[g], attended_grad[g], logits_grad[g], gain_part = middle_back(
            g, rows_back[g], level_own, middle[g], hidden_low[g], cot_rows,
            gain_b, router_wide, out_weight,
        )
        gain_b_local += jnp.sum(gain_part, axis=0)
    out_local = out_gradient(attended, branch_grad)
    fill = -D % (ranks * LANES)
    out_local = jnp.pad(out_local, ((0, 0), (0, fill)))
    attended_grad[0], out_local = together(attended_grad[0], out_local)
    cut_at = 13 * LANES
    up_own, up_away = pair_slices(up_local, shard)
    swaps = [(up_away, slice(0, cut_at), []), (up_away, slice(cut_at, EXP_DEV * FF), None)]
    out_met = column_core_sum(out_local)
    for g in each:
        pieces, kept = [], []
        here = [] if g == 0 else here
        spans = [(0, PAIRS)] if g < last else [(0, PAIRS // 2), (PAIRS // 2, PAIRS // 2)]
        for at, span in enumerate(spans):
            if g == last and at == 0:
                dq[0], gate_own = together(dq[0], gate_own)
                attended_grad[g], out_met, dq[0], gate_own, gate_met, down_far = together(
                    attended_grad[g], out_met, dq[0], gate_own, gate_met, down_far
                )
                gate_part = far_sum(gate_own, gate_met)
                down_own, down_away = pair_slices(down_far, shard)
                swaps.append((down_away, slice(0, EXP_DEV * FF), []))
                out_part = column_chip_sum(out_met)
            if g == last and at == 1:
                up_met = up_own + here[1]
                kept, dkv[0], pieces[0], up_met, mixture[last] = together(
                    kept, dkv[0], pieces[0], up_met, mixture[last]
                )
                up_part = lax.psum_scatter(
                    up_met.reshape(-1, up_met.shape[2]), "dh", scatter_dimension=0, tiled=True
                )
            turn = len(here)
            if turn == 1:
                swaps[1] = (*swaps[1][:2], here)
            grad, keep_part, send_part, *arrived = attend_back(
                g, span, query[g], attended_grad[g], attended[g], kv[g], lse[g], start_row,
                cosine, sine, swaps[turn] if turn < len(swaps) else None, 1 + turn, kept,
            )
            here = here + arrived
            kept = [grad]
            if g == last and at == 1:
                keep_part, dq[0] = together(keep_part, dq[0])
                down_part = (down_own + here[2])[0]
            pieces.append(keep_part + swap(send_part, "el"))
            if g == last and at == 1:
                pieces[1], dq[0] = together(pieces[1], dq[0])
        dq[g] = kept[0]
        pieces = [chip_sum(piece) for piece in pieces]
        dkv[g] = pieces[0] if len(pieces) == 1 else jnp.concatenate(pieces, axis=2)
    output = jnp.stack(
        [(middle[g] + mixture[g].astype(f32)).astype(bf16) for g in each]
    )

    kept, turned_dk, gain_a_local = [], [None] * groups, 0.0
    for g in each:
        input_grad, turned_dk[g], gain_part = input_back(
            g, groups, dq[g], dkv[g], x, middle_grad[g], cosine, sine,
            gain_a, query_weight, key_weight, value_weight, kept,
        )
        kept = [input_grad]
        gain_a_local += jnp.sum(gain_part, axis=0)
    router_parts = sum(dot_tn(logits_grad[g], hidden_low[g]) for g in each)
    router_local = (router_parts[:LANES] + router_parts[LANES:])[:experts]
    narrow = jnp.concatenate(
        [
            router_local,
            gain_a_local[None, :],
            gain_b_local[None, :],
            jnp.zeros((LANES - experts - 2, D), f32),
        ],
        axis=0,
    )
    narrow, up_part = together(narrow, up_part)
    dense = dense_gradient(normed, dq, turned_dk, dkv, narrow, out_part)
    first = dense.shape[1] - D - fill
    out_grad = dense[:, first : first + D]
    down_weight_grad, gate_weight_grad, up_weight_grad = (
        by_expert(part) for part in (down_part, gate_part, up_part)
    )
    spans = [H * HD, KVH * HD, KVH * HD, experts, 1, 1]
    pieces, begin = [], 0
    for span in spans:
        pieces.append(dense[:, begin : begin + span])
        begin += span
    query_grad, key_grad, value_grad, router_grad, gain_a_grad, gain_b_grad = pieces
    return (
        output,
        input_grad.reshape(groups, length, D),
        gain_a_grad[:, 0],
        query_grad,
        key_grad,
        value_grad,
        out_grad,
        gain_b_grad[:, 0],
        router_grad,
        gate_weight_grad,
        up_weight_grad,
        down_weight_grad,
        expert_load,
        prob_mean,
        balance_loss,
    )


def solution(mesh):
    dp_ranks, ranks = mesh.devices.shape
    fine = Mesh(
        mesh.devices.reshape(dp_ranks // 2, 2, ranks // 2, 2), ("dh", "dl", "eh", "el")
    )
    return jax.shard_map(
        on_device,
        mesh=fine,
        in_specs=(
            P(DATA, EXPERT, None),
            P(DATA, None),
            P(DATA, EXPERT, None),
            P(DATA, EXPERT, None),
            P(),
            P(),
            P(),
            P(),
            P(),
            P(),
            P(),
            P(EXPERT, None, None),
            P(EXPERT, None, None),
            P(EXPERT, None, None),
        ),
        out_specs=(
            P(DATA, EXPERT, None),
            P(DATA, EXPERT, None),
            P(DATA),
            P(DATA, None),
            P(DATA, None),
            P(DATA, None),
            P(DATA, None),
            P(DATA),
            P(DATA, None),
            P(EXPERT, DATA, None),
            P(EXPERT, DATA, None),
            P(EXPERT, DATA, None),
            P(),
            P(),
            P(),
        ),
        check_vma=False,
    )
```

```python
import functools
import math

import jax
import jax.numpy as jnp
from jax import lax
from jax.experimental import pallas as pl
from jax.experimental.pallas import tpu as pltpu
from jax.sharding import Mesh
from jax.sharding import PartitionSpec as P

D = 1536
H = 24
KVH = 8
HD = 64
FF = 512
TOPK = 8
EXP_DEV = 5
PROMPT = 1024
LANES = 128
PAIRS = KVH // 2
SHARE = H // KVH
PAIR_Q = 2 * SHARE * HD
ROWS = 256
STACK = SHARE * ROWS
EXPERT = ("eh", "el")
DATA = ("dh", "dl")
VMEM_LIMIT = 63 * 1024 * 1024

epsilon = 1e-05
rope_base = 10000.0
f32 = jnp.float32
bf16 = jnp.bfloat16


def dot(a, b):
    return lax.dot_general(a, b, (((1,), (0,)), ((), ())), preferred_element_type=f32)


def dot_nt(a, b):
    return lax.dot_general(a, b, (((1,), (1,)), ((), ())), preferred_element_type=f32)


def dot_tn(a, b):
    return lax.dot_general(a, b, (((0,), (0,)), ((), ())), preferred_element_type=f32)


def expert_rank():
    return lax.axis_index("eh") * 2 + lax.axis_index("el")


def call(kernel, name, micros, extra=None, **more):
    cost = pl.CostEstimate(flops=int(micros * 2.5e8), bytes_accessed=0, transcendentals=0)
    return pl.pallas_call(
        kernel,
        name=name,
        cost_estimate=cost,
        compiler_params=pltpu.CompilerParams(vmem_limit_bytes=VMEM_LIMIT, **(extra or {})),
        **more,
    )


def shaped(shape, dtype):
    return jax.ShapeDtypeStruct(shape, dtype)


def lane_of(shape):
    return lax.broadcasted_iota(jnp.int32, shape, len(shape) - 1)


def half_swap(values):
    lower = lane_of(values.shape) % HD < HD // 2
    return jnp.where(
        lower, pltpu.roll(values, LANES - HD // 2, 1), pltpu.roll(values, HD // 2, 1)
    )


def resident(shape):
    zeros = (0,) * len(shape)
    return pl.BlockSpec(shape, lambda *_: zeros, pipeline_mode=pl.Buffered(1))


def row_block(width, first=0):
    return pl.BlockSpec((ROWS, width), lambda i: (first + i, 0))


def naming_kernel(capacity, groups, r_ref, o_ref):
    length = r_ref.shape[0]
    rows = groups * length
    lane = lane_of((rows, LANES))
    packed = r_ref[...].astype(jnp.int32)
    chosen = jnp.concatenate(
        [packed[:, g * TOPK : (g + 1) * TOPK] for g in range(groups)], axis=0
    )
    named = jnp.zeros((rows, LANES), f32)
    for k in range(TOPK):
        named = jnp.where(chosen[:, k : k + 1] == lane, 1.0, named)
    earlier = lax.broadcasted_iota(jnp.int32, (rows, rows), 1) < lax.broadcasted_iota(
        jnp.int32, (rows, rows), 0
    )
    slot = dot(jnp.where(earlier, 1.0, 0.0).astype(bf16), named.astype(bf16))
    level = named * jnp.where(slot < capacity, 2.0, 1.0)
    o_ref[...] = level.reshape(groups, length, LANES).astype(bf16)


def naming(kv, capacity, groups, ranks):
    total = kv.shape[0]
    length = total // ranks
    return call(
        functools.partial(naming_kernel, capacity, groups),
        "naming",
        9,
        grid=(ranks,),
        in_specs=[pl.BlockSpec((length, LANES), lambda s: (s, 2 * PAIRS))],
        out_specs=pl.BlockSpec((groups, length, LANES), lambda s: (0, s, 0)),
        out_shape=shaped((groups, total, LANES), bf16),
    )(kv)


def key_value_kernel(x_ref, gain_ref, wk_ref, wv_ref, cos_ref, sin_ref, r_ref, n_ref, kv_ref):
    x = x_ref[...].astype(f32)
    factor = lax.rsqrt(jnp.mean(x * x, axis=1, keepdims=True) + epsilon)
    normed = (x * factor * gain_ref[...]).astype(bf16)
    n_ref[...] = normed
    cosine, sine = cos_ref[...], sin_ref[...]
    key = dot(normed, wk_ref[...])
    for c in range(KVH * HD // LANES):
        part = key[:, c * LANES : (c + 1) * LANES]
        turned = part * cosine + half_swap(part) * sine
        kv_ref[:, c * LANES : (c + 1) * LANES] = turned.astype(bf16)
    kv_ref[:, KVH * HD : 2 * KVH * HD] = dot(normed, wv_ref[...]).astype(bf16)
    kv_ref[:, 2 * KVH * HD :] = r_ref[...]


def key_value(group, length, x, gain, wk, wv, cosine, sine, names):
    first = group * length // ROWS
    width = 2 * KVH * HD + LANES
    return call(
        key_value_kernel,
        "key_value",
        5,
        grid=(length // ROWS,),
        in_specs=[
            row_block(D, first),
            resident((1, D)),
            resident((D, KVH * HD)),
            resident((D, KVH * HD)),
            row_block(LANES, first),
            row_block(LANES, first),
            row_block(LANES),
        ],
        out_specs=[row_block(D), row_block(width)],
        out_shape=[shaped((length, D), bf16), shaped((length, width), bf16)],
    )(x, gain, wk, wv, cosine, sine, names)


def query_kernel(n_ref, wq_ref, cos_ref, sin_ref, q_ref):
    cosine, sine = cos_ref[...], sin_ref[...]
    query = dot(n_ref[...], wq_ref[...])
    for c in range(H * HD // LANES):
        part = query[:, c * LANES : (c + 1) * LANES]
        turned = part * cosine + half_swap(part) * sine
        q_ref[:, c * LANES : (c + 1) * LANES] = turned.astype(bf16) * jnp.asarray(0.125, bf16)


def project_query(group, normed, wq, cosine, sine):
    length = normed.shape[0]
    first = group * length // ROWS
    return call(
        query_kernel,
        "query",
        6,
        grid=(length // ROWS,),
        in_specs=[
            row_block(D),
            resident((D, H * HD)),
            row_block(LANES, first),
            row_block(LANES, first),
        ],
        out_specs=row_block(H * HD),
        out_shape=shaped((length, H * HD), bf16),
    )(normed, wq, cosine, sine)


def stack_heads(ref):
    low = lane_of((ROWS, LANES)) < HD
    parts = [ref[:, c * LANES : (c + 1) * LANES].astype(f32) for c in range(SHARE)]
    rolled0, rolled2 = pltpu.roll(parts[0], HD, 1), pltpu.roll(parts[2], HD, 1)
    zero = jnp.zeros((ROWS, LANES), f32)
    first = [parts[0], rolled0, parts[1]]
    second = [parts[1], rolled2, parts[2]]
    return (
        jnp.concatenate([jnp.where(low, v, zero).astype(bf16) for v in first], axis=0),
        jnp.concatenate([jnp.where(low, zero, v).astype(bf16) for v in second], axis=0),
    )


def unstack_heads(first, second):
    low = lane_of((ROWS, LANES)) < HD
    return (
        jnp.where(low, first[:ROWS], pltpu.roll(first[ROWS : 2 * ROWS], HD, 1)),
        jnp.where(low, first[2 * ROWS :], second[:ROWS]),
        jnp.where(low, pltpu.roll(second[ROWS : 2 * ROWS], HD, 1), second[2 * ROWS :]),
    )


def visit_chunks(block, chunk):
    prompt_blocks = PROMPT // ROWS

    @pl.when(block >= prompt_blocks)
    def _():
        for c in range(PROMPT // (2 * ROWS)):
            chunk(c * 2 * ROWS, 2 * ROWS, False)

    @pl.when(block < prompt_blocks)
    def _():
        def step(c, carry):
            chunk(pl.multiple_of(c * ROWS, ROWS), ROWS, False)
            return carry

        lax.fori_loop(0, block, step, 0)

    @pl.when(block > prompt_blocks)
    def _():
        chunk(pl.multiple_of((block - 1) * ROWS, ROWS), ROWS, True)

    chunk(pl.multiple_of(block * ROWS, ROWS), ROWS, True)


def mask_bias(block, begin, size, start_ref):
    place = begin + lax.broadcasted_iota(jnp.int32, (size, ROWS), 0)
    own = block * ROWS + lax.broadcasted_iota(jnp.int32, (size, ROWS), 1)
    ok = (place <= own) & (place >= start_ref[0, :1, :])
    bias = jnp.where(ok, 0.0, -1e30)
    return jnp.concatenate([bias] * SHARE, axis=1)


def attend_kernel(blocks, q_ref, k_ref, v_ref, start_ref, o_ref, lse_ref, vt_ref, m_ref, l_ref, acc_ref):
    block = expert_rank() * blocks + pl.program_id(1)

    @pl.when(pl.program_id(1) == 0)
    def _():
        vt_ref[...] = jnp.transpose(v_ref[...].astype(f32)).astype(bf16)

    queries = stack_heads(q_ref)
    m_ref[...] = jnp.full_like(m_ref, -1e30)
    l_ref[...] = jnp.zeros_like(l_ref)
    acc_ref[...] = jnp.zeros_like(acc_ref)

    def chunk(begin, size, masked):
        keys = k_ref[pl.ds(begin, size), :]
        values = vt_ref[:, pl.ds(begin, size)]
        bias = mask_bias(block, begin, size, start_ref) if masked else None
        for h in range(2):
            scores = dot_nt(keys, queries[h])
            if masked:
                scores = scores + bias
            before = m_ref[h, :1]
            peak = jnp.maximum(before, jnp.max(scores, axis=0, keepdims=True))
            weight = jnp.exp(scores - peak)
            shrink = jnp.exp(before - peak)
            m_ref[h, :1] = peak
            l_ref[h, :1] = l_ref[h, :1] * shrink + jnp.sum(weight, axis=0, keepdims=True)
            acc_ref[h] = acc_ref[h] * shrink + dot(values, weight.astype(bf16))

    visit_chunks(block, chunk)
    mixed = [jnp.transpose(acc_ref[h] / l_ref[h, :1]) for h in range(2)]
    for c, part in enumerate(unstack_heads(*mixed)):
        o_ref[:, c * LANES : (c + 1) * LANES] = part.astype(bf16)
    for h in range(2):
        total = m_ref[h, :1] + jnp.log(l_ref[h, :1])
        lse_ref[0, 0, h] = jnp.broadcast_to(total, (8, STACK))


def attend(group, query, kv, start_row):
    length = query.shape[0]
    total = kv.shape[0]
    blocks = length // ROWS
    heads = pl.BlockSpec((ROWS, PAIR_Q), lambda p, i: (i, p))
    return call(
        functools.partial(attend_kernel, blocks),
        "attend",
        45,
        grid=(PAIRS, blocks),
        in_specs=[
            heads,
            pl.BlockSpec((total, LANES), lambda p, i: (0, p)),
            pl.BlockSpec((total, LANES), lambda p, i: (0, PAIRS + p)),
            pl.BlockSpec((1, 8, ROWS), lambda p, i: (group, 0, i)),
        ],
        out_specs=[
            heads,
            pl.BlockSpec((1, 1, 2, 8, STACK), lambda p, i: (p, i, 0, 0, 0)),
        ],
        out_shape=[
            shaped(query.shape, bf16),
            shaped((PAIRS, blocks, 2, 8, STACK), f32),
        ],
        scratch_shapes=[
            pltpu.VMEM((LANES, total), bf16),
            pltpu.VMEM((2, 8, STACK), f32),
            pltpu.VMEM((2, 8, STACK), f32),
            pltpu.VMEM((2, LANES, STACK), f32),
        ],
    )(query, kv, kv, start_row)


def attend_back_kernel(
    blocks,
    q_ref,
    g_ref,
    o_ref,
    k_ref,
    v_ref,
    lse_ref,
    start_ref,
    cos_ref,
    sin_ref,
    dq_ref,
    keep_ref,
    send_ref,
    dq_acc,
    dkv_acc,
):
    step = pl.program_id(1)
    block = expert_rank() * blocks + step

    @pl.when(step == 0)
    def _():
        dkv_acc[...] = jnp.zeros_like(dkv_acc)

    dq_acc[...] = jnp.zeros_like(dq_acc)
    queries = stack_heads(q_ref)
    grads = stack_heads(g_ref)
    halves = []
    for c in range(SHARE):
        cols = slice(c * LANES, (c + 1) * LANES)
        product = jnp.transpose(g_ref[:, cols].astype(f32) * o_ref[:, cols].astype(f32))
        halves.append(jnp.sum(product[:HD], axis=0, keepdims=True))
        halves.append(jnp.sum(product[HD:], axis=0, keepdims=True))
    inner = [jnp.concatenate(halves[:SHARE], axis=1), jnp.concatenate(halves[SHARE:], axis=1)]

    def chunk(begin, size, masked):
        keys = k_ref[pl.ds(begin, size), :]
        values = v_ref[pl.ds(begin, size), :]
        bias = mask_bias(block, begin, size, start_ref) if masked else None
        key_sum, value_sum = None, None
        for h in range(2):
            scores = dot_nt(keys, queries[h]) - lse_ref[0, 0, h, :1, :]
            if masked:
                scores = scores + bias
            probs = jnp.exp(scores)
            probs_grad = dot_nt(values, grads[h])
            scores_grad = (probs * (probs_grad - inner[h])).astype(bf16)
            value_part = dot(probs.astype(bf16), grads[h])
            key_part = dot(scores_grad, queries[h])
            key_sum = key_part if key_sum is None else key_sum + key_part
            value_sum = value_part if value_sum is None else value_sum + value_part
            dq_acc[h] += dot_tn(scores_grad, keys)
        dkv_acc[0, pl.ds(begin, size), :] += key_sum
        dkv_acc[1, pl.ds(begin, size), :] += value_sum

    visit_chunks(block, chunk)
    cosine, sine = cos_ref[...], sin_ref[...]
    for c, part in enumerate(unstack_heads(dq_acc[0], dq_acc[1])):
        part = part * 0.125
        turned = part * cosine - half_swap(part) * sine
        dq_ref[:, c * LANES : (c + 1) * LANES] = turned.astype(bf16)

    @pl.when(step == blocks - 1)
    def _():
        length = blocks * ROWS
        own = lax.axis_index("el")
        for chip in range(dkv_acc.shape[1] // (2 * length)):
            mine = pl.multiple_of((2 * chip + own) * length, length)
            other = pl.multiple_of((2 * chip + 1 - own) * length, length)
            for i in range(2):
                keep_ref[chip, i] = dkv_acc[i, pl.ds(mine, length), :].astype(bf16)
                send_ref[chip, i] = dkv_acc[i, pl.ds(other, length), :].astype(bf16)


def attend_back_and_swap(blocks, pairs, columns, *refs):
    away_ref = refs[9]
    here_ref = refs[-5]
    send_sem, recv_sem = refs[-2:]
    at = pl.program_id(0) * blocks + pl.program_id(1)
    peer = {"dl": 1 - lax.axis_index("dl")}
    exchange = pltpu.make_async_remote_copy(
        src_ref=away_ref.at[:, :, columns],
        dst_ref=here_ref.at[:, :, columns],
        send_sem=send_sem,
        recv_sem=recv_sem,
        device_id=peer,
        device_id_type=pl.DeviceIdType.MESH,
    )

    @pl.when(at == 0)
    def _():
        barrier = pltpu.get_barrier_semaphore()
        pl.semaphore_signal(barrier, inc=1, device_id=peer, device_id_type=pl.DeviceIdType.MESH)
        pl.semaphore_wait(barrier, 1)
        exchange.start()

    attend_back_kernel(blocks, *refs[:9], *refs[-8:-5], *refs[-4:-2])

    @pl.when(at == pairs * blocks - 1)
    def _():
        exchange.wait()


def attend_back(
    group, span, query, grad, mixed, kv, lse, start_row, cosine, sine, away, collective, kept
):
    length = query.shape[0]
    total = kv.shape[0]
    blocks = length // ROWS
    first = group * blocks
    chips = total // (2 * length)
    base, pairs = span
    side = pl.BlockSpec((chips, 2, length, LANES), lambda p, i: (0, 0, 0, p))
    heads = pl.BlockSpec((ROWS, PAIR_Q), lambda p, i: (i, base + p))
    table = pl.BlockSpec((ROWS, LANES), lambda p, i: (first + i, 0))
    swaps = [] if away is None else [away[0], *away[2]]
    arriving = [] if away is None else [away[0]]
    if away is None:
        kernel = lambda *refs: attend_back_kernel(blocks, *refs[:9], *refs[-5:])
        extra = {}
    else:
        kernel = functools.partial(attend_back_and_swap, blocks, pairs, away[1])
        extra = dict(collective_id=collective, has_side_effects=True)
    anywhere = pl.BlockSpec(memory_space=pl.ANY)
    return call(
        kernel,
        "attend_back",
        16 * pairs,
        extra,
        grid=(pairs, blocks),
        in_specs=[
            heads,
            heads,
            heads,
            pl.BlockSpec((total, LANES), lambda p, i: (0, base + p)),
            pl.BlockSpec((total, LANES), lambda p, i: (0, PAIRS + base + p)),
            pl.BlockSpec((1, 1, 2, 8, STACK), lambda p, i: (base + p, i, 0, 0, 0)),
            pl.BlockSpec((1, 8, ROWS), lambda p, i: (group, 0, i)),
            table,
            table,
        ]
        + [anywhere] * len(swaps + kept),
        out_specs=[
            heads,
            side,
            side,
        ]
        + [anywhere] * len(arriving),
        input_output_aliases={
            **({9 + len(swaps): 0} if kept else {}),
            **({10: 3} if len(swaps) > 1 else {}),
        },
        out_shape=[
            shaped(query.shape, bf16),
            shaped((chips, 2, length, pairs * LANES), bf16),
            shaped((chips, 2, length, pairs * LANES), bf16),
        ]
        + [shaped(one.shape, one.dtype) for one in arriving],
        scratch_shapes=[
            pltpu.VMEM((2, STACK, LANES), f32),
            pltpu.VMEM((2, total, LANES), f32),
        ]
        + [pltpu.SemaphoreType.DMA] * (2 * len(arriving)),
    )(query, grad, mixed, kv, kv, lse, start_row, cosine, sine, *swaps, *kept)


def branch_kernel(a_ref, x_ref, wo_ref, gain_ref, wr_ref, m_ref, n_ref, ps_ref):
    middle = x_ref[...].astype(f32) + dot(a_ref[...], wo_ref[...])
    m_ref[...] = middle
    factor = lax.rsqrt(jnp.mean(middle * middle, axis=1, keepdims=True) + epsilon)
    normed = (middle * factor * gain_ref[...]).astype(bf16)
    n_ref[...] = normed
    add_up(ps_ref, fold_rows(router(normed, wr_ref[...])))


def branch(group, attended, x, wo, gain, wr):
    length = attended.shape[0]
    return call(
        branch_kernel,
        "branch",
        6,
        grid=(length // ROWS,),
        in_specs=[
            row_block(H * HD),
            row_block(D, group * length // ROWS),
            resident((H * HD, D)),
            resident((1, D)),
            resident((D, LANES)),
        ],
        out_specs=[row_block(D), row_block(D), pl.BlockSpec((8, LANES), lambda i: (0, 0))],
        out_shape=[
            shaped((length, D), f32),
            shaped((length, D), bf16),
            shaped((8, LANES), f32),
        ],
    )(attended, x, wo, gain, wr)


def router(normed, weight):
    count = EXP_DEV * 2 * lax.axis_size("eh")
    logits = dot(normed, weight)
    logits = jnp.where(lane_of(logits.shape) < count, logits, -1e30)
    powers = jnp.exp(logits - jnp.max(logits, axis=1, keepdims=True))
    return powers / jnp.sum(powers, axis=1, keepdims=True)


def experts_kernel(x_ref, c_ref, t_ref, wr_ref, *refs):
    outs, weights, sems = refs[-11:-4], refs[-4:-1], refs[-1]
    step = pl.program_id(0)

    def loads(e):
        return [
            pltpu.make_async_copy(refs[i].at[e], weights[i].at[e], sems.at[i, e]) for i in range(3)
        ]

    @pl.when(step == 0)
    def _():
        for e in range(EXP_DEV):
            for load in loads(e):
                load.start()
        experts_rows(x_ref, c_ref, t_ref, wr_ref, *weights, *outs, loads)

    @pl.when(step > 0)
    def _():
        experts_rows(x_ref, c_ref, t_ref, wr_ref, *weights, *outs, lambda e: [])


def experts_rows(
    x_ref, c_ref, t_ref, wr_ref, wg_ref, wu_ref, wd_ref,
    mix_ref, rows_ref, x_out, c_out, hid_ref, gate_ref, up_ref, loads,
):
    x, cot = x_ref[...], c_ref[...]
    x_out[...] = x
    c_out[...] = cot
    level = t_ref[0].astype(f32)
    picked = jnp.where(level > 0.5, router(x, wr_ref[...]), 0.0)
    share = picked / jnp.sum(picked, axis=1, keepdims=True)
    share = jnp.where(level > 1.5, share, 0.0)
    lane = lane_of(share.shape)
    base = EXP_DEV * expert_rank()
    share = pltpu.roll(share, lax.rem(LANES - base, LANES), 1)
    mix, rows = None, None
    gate_grads = jnp.zeros(share.shape, bf16)
    for e in range(EXP_DEV):
        for load in loads(e):
            load.wait()
        gate = dot(x, wg_ref[e])
        up = dot(x, wu_ref[e])
        hidden_grad = dot(cot, wd_ref[e])
        sigmoid = jax.nn.sigmoid(gate)
        active = gate * sigmoid
        hidden = active * up
        inner = jnp.sum(hidden * hidden_grad, axis=1, keepdims=True)
        coarse = inner.astype(bf16)
        fine = (inner - coarse.astype(f32)).astype(bf16)
        gate_grads = jnp.where(lane == base + e, coarse, gate_grads)
        gate_grads = jnp.where(lane == LANES // 2 + base + e, fine, gate_grads)
        weight = share[:, e : e + 1]
        scaled = (hidden * weight).astype(bf16)
        hidden_grad = hidden_grad * weight
        up_grad = (hidden_grad * active).astype(bf16)
        gate_grad = (hidden_grad * up * sigmoid * (1.0 + gate * (1.0 - sigmoid))).astype(bf16)
        cols = slice(e * FF, (e + 1) * FF)
        hid_ref[:, cols] = scaled
        gate_ref[:, cols] = gate_grad
        up_ref[:, cols] = up_grad
    for e in range(EXP_DEV):
        cols = slice(e * FF, (e + 1) * FF)
        mix_part = dot_nt(hid_ref[:, cols], wd_ref[e])
        rows_part = dot_nt(gate_ref[:, cols], wg_ref[e]) + dot_nt(up_ref[:, cols], wu_ref[e])
        mix = mix_part if mix is None else mix + mix_part
        rows = rows_part if rows is None else rows + rows_part
    mix_ref[...] = mix.astype(bf16)
    rows_ref[:, :D] = rows.astype(bf16)
    rows_ref[:, D:] = gate_grads


def experts_pass(group, groups, x, cot, level, wr, wg, wu, wd, kept):
    count = x.shape[0]
    first = group * count // ROWS
    whole = groups * count
    side = pl.BlockSpec(memory_space=pl.ANY)
    widths = [D, D, EXP_DEV * FF, EXP_DEV * FF, EXP_DEV * FF]
    def ready(*refs):
        experts_rows(*refs[:7], *refs[-7:], lambda e: [])

    return call(
        ready if kept else experts_kernel,
        "experts",
        113,
        grid=(count // ROWS,),
        in_specs=[
            row_block(D),
            row_block(D),
            pl.BlockSpec((1, ROWS, LANES), lambda i: (group, i, 0)),
            resident((D, LANES)),
        ]
        + ([resident((EXP_DEV, D, FF))] if kept else [side]) * 3
        + [side] * len(kept),
        out_specs=[row_block(D), row_block(D + LANES)]
        + [row_block(width, first) for width in widths],
        out_shape=[
            shaped((count, D), bf16),
            shaped((count, D + LANES), bf16),
        ]
        + [shaped((whole, width), bf16) for width in widths],
        input_output_aliases={7 + i: 2 + i for i in range(len(kept))},
        scratch_shapes=[]
        if kept
        else [pltpu.VMEM((EXP_DEV, D, FF), bf16)] * 3 + [pltpu.SemaphoreType.DMA((3, EXP_DEV))],
    )(x, cot, level, wr, wg, wu, wd, *kept)


def norm_back(grad, normed, factor, gain):
    scaled = grad * gain
    return factor * (scaled - normed * jnp.mean(scaled * normed, axis=1, keepdims=True))


def fold_rows(values):
    return jnp.sum(values.reshape(values.shape[0] // 8, 8, values.shape[1]), axis=0)


def add_up(ref, part):
    @pl.when(pl.program_id(0) == 0)
    def _():
        ref[...] = part

    @pl.when(pl.program_id(0) > 0)
    def _():
        ref[...] += part


def middle_kernel(
    r_ref, t_ref, m_ref, n_ref, c_ref, gain_ref, wr_ref, wo_ref,
    mg_ref, b_ref, ag_ref, l_ref, dg_ref,
):
    probs = router(n_ref[...], wr_ref[...])
    level = t_ref[0].astype(f32)
    sel = jnp.where(level > 0.5, 1.0, 0.0)
    gate_grad = r_ref[:, D:].astype(f32)
    gate_grad = gate_grad + pltpu.roll(gate_grad, LANES // 2, 1)
    gate_grad = jnp.where(level > 1.5, gate_grad, 0.0)
    picked = probs * sel
    total = jnp.sum(picked, axis=1, keepdims=True)
    share = picked / total
    inner = jnp.sum(gate_grad * share, axis=1, keepdims=True)
    probs_grad = (gate_grad - inner) / total * sel
    logits_grad = probs * (probs_grad - jnp.sum(probs_grad * probs, axis=1, keepdims=True))
    coarse = logits_grad.astype(bf16)
    fine = (logits_grad - coarse.astype(f32)).astype(bf16)
    l_ref[:, :LANES] = coarse
    l_ref[:, LANES:] = fine
    grad = r_ref[:, :D].astype(f32) + dot_nt(coarse, wr_ref[...]) + dot_nt(fine, wr_ref[...])
    middle = m_ref[...]
    factor = lax.rsqrt(jnp.mean(middle * middle, axis=1, keepdims=True) + epsilon)
    normed = middle * factor
    add_up(dg_ref, fold_rows(grad * normed))
    middle_grad = c_ref[...].astype(f32) + norm_back(grad, normed, factor, gain_ref[...])
    mg_ref[...] = middle_grad
    low = middle_grad.astype(bf16)
    b_ref[...] = low
    ag_ref[...] = dot_nt(low, wo_ref[...]).astype(bf16)


def middle_back(group, rows, level, middle, normed, cot, gain, wr, wo):
    length = rows.shape[0]
    first = group * length // ROWS
    corner = lambda width: pl.BlockSpec((8, width), lambda i: (0, 0))
    return call(
        middle_kernel,
        "middle_back",
        8,
        grid=(length // ROWS,),
        in_specs=[
            row_block(D + LANES),
            pl.BlockSpec((1, ROWS, LANES), lambda i: (group, i, 0)),
            row_block(D), row_block(D), row_block(D, first),
            resident((1, D)), resident((D, LANES)), resident((H * HD, D)),
        ],
        out_specs=[
            row_block(D), row_block(D), row_block(H * HD), row_block(2 * LANES),
            corner(D),
        ],
        out_shape=[
            shaped((length, D), f32),
            shaped((length, D), bf16),
            shaped((length, H * HD), bf16),
            shaped((length, 2 * LANES), bf16),
            shaped((8, D), f32),
        ],
    )(rows, level, middle, normed, cot, gain, wr, wo)


def input_kernel(
    dq_ref, dk_ref, dv_ref, x_ref, mg_ref, cos_ref, sin_ref, gain_ref, wq_ref, wk_ref, wv_ref,
    out_ref, dk_out, dg_ref,
):
    cosine, sine = cos_ref[...], sin_ref[...]
    for c in range(KVH * HD // LANES):
        part = dk_ref[0, :, c * LANES : (c + 1) * LANES].astype(f32)
        turned = part * cosine - half_swap(part) * sine
        dk_out[:, c * LANES : (c + 1) * LANES] = turned.astype(bf16)
    grad = dot_nt(dq_ref[...], wq_ref[...])
    grad = grad + dot_nt(dk_out[...], wk_ref[...])
    grad = grad + dot_nt(dv_ref[0], wv_ref[...])
    x = x_ref[...].astype(f32)
    factor = lax.rsqrt(jnp.mean(x * x, axis=1, keepdims=True) + epsilon)
    normed = x * factor
    add_up(dg_ref, fold_rows(grad * normed))
    out_ref[...] = mg_ref[...] + norm_back(grad, normed, factor, gain_ref[...])


def input_back(group, groups, dq, dkv, x, middle_grad, cosine, sine, gain, wq, wk, wv, kept):
    length = dq.shape[0]
    first = group * length // ROWS
    kernel = lambda *refs: input_kernel(*refs[:11], *refs[-3:])
    return call(
        kernel,
        "input_back",
        8,
        grid=(length // ROWS,),
        in_specs=[
            row_block(H * HD),
            pl.BlockSpec((1, ROWS, KVH * HD), lambda i: (0, i, 0)),
            pl.BlockSpec((1, ROWS, KVH * HD), lambda i: (1, i, 0)),
            row_block(D, first),
            row_block(D),
            row_block(LANES, first),
            row_block(LANES, first),
            resident((1, D)),
            resident((D, H * HD)),
            resident((D, KVH * HD)),
            resident((D, KVH * HD)),
        ]
        + [pl.BlockSpec(memory_space=pl.ANY)] * len(kept),
        out_specs=[
            row_block(D, first),
            row_block(KVH * HD),
            pl.BlockSpec((8, D), lambda i: (0, 0)),
        ],
        out_shape=[
            shaped((groups * length, D), f32),
            shaped((length, KVH * HD), bf16),
            shaped((8, D), f32),
        ],
        input_output_aliases={11: 0} if kept else {},
    )(dq, dkv, dkv, x, middle_grad, cosine, sine, gain, wq, wk, wv, *kept)


def transpose_into(turned, lefts):
    length = lefts[0].shape[0]
    for g, left in enumerate(lefts):
        for c in range(0, D, 2 * LANES):
            part = left[:, c : c + 2 * LANES].astype(f32)
            turned[c : c + 2 * LANES, g * length : (g + 1) * length] = jnp.transpose(part).astype(
                bf16
            )


def out_kernel(groups, *refs):
    lefts, rights = refs[:groups], refs[groups : 2 * groups]
    out_ref, turned = refs[-2:]
    length = lefts[0].shape[0]

    @pl.when(pl.program_id(0) == 0)
    def _():
        transpose_into(turned, lefts)

    total = None
    for g in range(groups):
        part = dot(turned[:, g * length : (g + 1) * length], rights[g][...])
        total = part if total is None else total + part
    out_ref[...] = total.astype(bf16)


def out_gradient(lefts, rights):
    groups, length = len(lefts), lefts[0].shape[0]
    width = 4 * LANES
    return call(
        functools.partial(out_kernel, groups),
        "out_grad",
        10,
        grid=(D // width,),
        in_specs=[resident((length, D))] * groups
        + [pl.BlockSpec((length, width), lambda i: (0, i))] * groups,
        out_specs=pl.BlockSpec((D, width), lambda i: (0, i)),
        out_shape=shaped((D, D), bf16),
        scratch_shapes=[pltpu.VMEM((D, groups * length), bf16)],
    )(*lefts, *rights)


def dense_kernel(groups, sizes, *refs):
    data, chips, shard, width, full, late = sizes
    lefts, queries, keys, values = (refs[i * groups : (i + 1) * groups] for i in range(4))
    narrow_ref, late_ref, out_ref = refs[4 * groups : 4 * groups + 3]
    (turned, keep1, send1, got1, keep2, send2, got2, sum2, got3, sum3, got4, sum4, near5, far5,
     wide2, wide3, keep6, send6, got6) = refs[4 * groups + 3 : 4 * groups + 22]
    sems = refs[4 * groups + 22 :]
    half = width // 2
    length = lefts[0].shape[0]
    ranks = 2 * chips
    dh, dl, eh, el = (lax.axis_index(name) for name in ("dh", "dl", "eh", "el"))

    def near(hop, core):
        return {"eh": lax.rem(eh + hop, chips), "el": core}

    peers = [{"el": 1 - el}, {"dl": 1 - dl}]
    for hop in range(1, chips):
        peers.append(near(hop, el))
    for hop in range(1, data):
        peers.append({"dh": lax.rem(dh + hop, data)})
    barrier = pltpu.get_barrier_semaphore()
    for peer in peers:
        pl.semaphore_signal(barrier, inc=1, device_id=peer, device_id_type=pl.DeviceIdType.MESH)
    transpose_into(turned, lefts)
    pl.semaphore_wait(barrier, len(peers))

    def copy(source, target, phase, k, lane, peer):
        return pltpu.make_async_remote_copy(
            src_ref=source,
            dst_ref=target,
            send_sem=sems[2 * phase].at[k, lane],
            recv_sem=sems[2 * phase + 1].at[k, lane],
            device_id=peer,
            device_id_type=pl.DeviceIdType.MESH,
        )

    def crossed(k):
        return k < full and k % 2 == 1

    def slot(k):
        return k // 2 if k < full else (full + 1) // 2 + k - full

    def copies(phase, k):
        if phase == 0:
            return [copy(send1.at[k], got1.at[k], 0, k, 0, {"el": 1 - el})]
        if phase == 1:
            source, target = (send6, got6) if crossed(k) else (send2, got2)
            at = k // 2
            return [
                copy(source.at[at, hop - 1], target.at[at, hop - 1], 1, k, hop - 1, near(hop, el))
                for hop in range(1, chips)
            ]
        if phase == 2:
            if crossed(k):
                at = k // 2
                return [copy(wide2.at[at, 1 - dl], wide3.at[at], 2, k, 0, {"dl": 1 - dl})]
            at = slot(k)
            return [copy(sum2.at[at, 1 - dl], got3.at[at], 2, k, 0, {"dl": 1 - dl})]
        if phase == 3:
            found = []
            for hop in range(1, data):
                away = lax.rem(dh + hop, data)
                found.append(
                    copy(sum3.at[k, away], got4.at[k, hop - 1], 3, k, hop - 1, {"dh": away})
                )
            return found
        if phase == 4:
            return [
                copy(sum4.at[k], near5.at[k, eh], 4, k, hop - 1, near(hop, el))
                for hop in range(1, chips)
            ]
        return [copy(near5.at[k], far5.at[k], 5, k, 0, {"el": 1 - el})]

    def start(phase, k):
        for one in copies(phase, k):
            one.start()

    def arrived(phase, k):
        for one in copies(phase, k):
            one.wait_recv()

    def finish_shard(k):
        base = k * width if k < full else full * width + (k - full) * LANES

        def put(side, chip, block):
            place = side * chips + chip
            place = place * LANES if k < full else place * late * LANES
            at = pl.multiple_of(base + place, LANES)
            out_ref[:, pl.ds(at, LANES)] = block.astype(f32)

        for chip in range(chips):
            put(el, chip, near5[k, chip])
            put(1 - el, chip, far5[k, chip])

    def piece(column):
        size = KVH * HD
        if column >= H * HD + 2 * size:
            if column > H * HD + 2 * size:
                return jnp.zeros((D, size), bf16)
            part = jnp.transpose(narrow_ref[...])
            return jnp.concatenate([part, jnp.zeros((D, size - LANES), f32)], axis=1).astype(bf16)
        total = None
        for g in range(groups):
            if column < H * HD:
                block = queries[g][:, column : column + size]
            elif column < H * HD + size:
                block = keys[g][...]
            else:
                block = values[g][1]
            one = dot(turned[:, g * length : (g + 1) * length], block)
            total = one if total is None else total + one
        return total.astype(bf16)

    def stage_compute(k):
        if k < full:
            part = [piece(k * width + c) for c in range(0, width, KVH * HD)]
            part = part[0] if len(part) == 1 else jnp.concatenate(part, axis=1)

            @pl.when(el == 0)
            def _():
                keep1[k] = part[:, :half]
                send1[k] = part[:, half:]

            @pl.when(el == 1)
            def _():
                keep1[k] = part[:, half:]
                send1[k] = part[:, :half]

            start(0, k)

    def hand_out(block, chip, keep, send):
        hop = lax.rem(chip + chips - eh, chips)

        @pl.when(hop == 0)
        def _():
            keep[...] = block

        @pl.when(hop > 0)
        def _():
            send[hop - 1] = block

    def chip_columns(chip):
        return slice(chip * LANES, (chip + 1) * LANES)

    def stage_core(k):
        arrived(0, k)
        met = (keep1[k].astype(f32) + got1[k].astype(f32)).astype(bf16)
        at = k // 2
        if crossed(k):
            for far in range(data):
                for side in range(2):
                    first = (2 * far + side) * shard
                    wide2[at, side, far] = met[first : first + shard]
            start(2, k)
        else:
            for chip in range(chips):
                hand_out(met[:, chip_columns(chip)], chip, keep2.at[at], send2.at[at])
            start(1, k)

    def stage_second(k):
        at = k // 2
        if crossed(k):
            arrived(2, k)
            met = (wide2[at, dl].astype(f32) + wide3[at].astype(f32)).astype(bf16)
            for chip in range(chips):
                hand_out(met[:, :, chip_columns(chip)], chip, keep6.at[at], send6.at[at])
            start(1, k)
        else:
            arrived(1, k)
            total = keep2[at].astype(f32)
            for hop in range(1, chips):
                total = total + got2[at, hop - 1].astype(f32)
            spread(k, total.astype(bf16))

    def spread(k, total):
        for far in range(data):
            for side in range(2):
                first = (2 * far + side) * shard
                sum2[slot(k), side, far] = total[first : first + shard]
        start(2, k)

    def stage_third(k):
        if crossed(k):
            at = k // 2
            arrived(1, k)
            total = keep6[at].astype(f32)
            for hop in range(1, chips):
                total = total + got6[at, hop - 1].astype(f32)
        else:
            at = slot(k)
            arrived(2, k)
            total = sum2[at, dl].astype(f32) + got3[at].astype(f32)
        sum3[k] = total.astype(bf16)
        start(3, k)

    def stage_far(k):
        arrived(3, k)
        total = sum3[k, dh].astype(f32)
        for hop in range(1, data):
            total = total + got4[k, hop - 1].astype(f32)
        total = total.astype(bf16)
        sum4[k] = total
        near5[k, eh] = total
        start(4, k)

    def stage_gather(k):
        arrived(4, k)
        start(5, k)

    def stage_last(k):
        arrived(5, k)
        finish_shard(k)

    everything = list(range(full, full + late)) + list(range(full))
    for k in range(full, full + late):
        first = (k - full) * LANES
        spread(k, late_ref[:, first : first + LANES])
    stages = (
        stage_compute,
        stage_core,
        stage_second,
        stage_third,
        stage_far,
        stage_gather,
        stage_last,
    )
    for step in range(full + len(stages) - 1):
        for delay, stage in enumerate(stages):
            if 0 <= step - delay < full:
                stage(step - delay)
        if step < 4:
            for k in range(full, full + late):
                stages[3 + step](k)
    for k in everything:
        for phase in range(6):
            if k < full or phase > 1:
                for one in copies(phase, k):
                    one.wait_send()


def dense_gradient(lefts, queries, keys, values, narrow, late_part):
    groups = len(lefts)
    data, chips = lax.axis_size("dh"), lax.axis_size("eh")
    shard = D // (2 * data)
    width = 2 * chips * LANES
    columns = H * HD + 2 * KVH * HD
    full = -(-(columns + LANES) // width)
    late = late_part.shape[1] // LANES
    total = full + late
    half, ranks = width // 2, 2 * chips
    sizes = (data, chips, shard, width, full, late)
    lanes = [1, chips - 1, 1, data - 1, chips - 1, 1]
    even, odd = (full + 1) // 2, full // 2
    sems = []
    for count in lanes:
        sems += [pltpu.SemaphoreType.DMA((total, count))] * 2
    operands = [*lefts, *queries, *keys, *values, narrow, late_part]
    whole = pl.BlockSpec(memory_space=pltpu.VMEM)
    return pl.pallas_call(
        functools.partial(dense_kernel, groups, sizes),
        name="dense_grad",
        in_specs=[whole] * len(operands),
        out_specs=whole,
        out_shape=shaped((shard, full * width + late * ranks * LANES), f32),
        scratch_shapes=[
            pltpu.VMEM((D, groups * lefts[0].shape[0]), bf16),
            pltpu.VMEM((full, D, half), bf16),
            pltpu.VMEM((full, D, half), bf16),
            pltpu.VMEM((full, D, half), bf16),
            pltpu.VMEM((even, D, LANES), bf16),
            pltpu.VMEM((even, chips - 1, D, LANES), bf16),
            pltpu.VMEM((even, chips - 1, D, LANES), bf16),
            pltpu.VMEM((even + late, 2, data, shard, LANES), bf16),
            pltpu.VMEM((even + late, data, shard, LANES), bf16),
            pltpu.VMEM((total, data, shard, LANES), bf16),
            pltpu.VMEM((total, data - 1, shard, LANES), bf16),
            pltpu.VMEM((total, shard, LANES), bf16),
            pltpu.VMEM((total, chips, shard, LANES), bf16),
            pltpu.VMEM((total, chips, shard, LANES), bf16),
            pltpu.VMEM((odd, 2, data, shard, half), bf16),
            pltpu.VMEM((odd, data, shard, half), bf16),
            pltpu.VMEM((odd, data, shard, LANES), bf16),
            pltpu.VMEM((odd, chips - 1, data, shard, LANES), bf16),
            pltpu.VMEM((odd, chips - 1, data, shard, LANES), bf16),
        ]
        + sems,
        cost_estimate=pl.CostEstimate(
            flops=int(80 * 9e8), bytes_accessed=0, transcendentals=0
        ),
        compiler_params=pltpu.CompilerParams(
            vmem_limit_bytes=VMEM_LIMIT, collective_id=0, has_side_effects=True
        ),
    )(*operands)


def widen(values):
    return jnp.pad(values, ((0, 0), (0, LANES - values.shape[1])))


def swap(values, axis):
    return lax.ppermute(values, axis, [(0, 1), (1, 0)])


def pick(values, index):
    return lax.dynamic_index_in_dim(values, index, 1, keepdims=False)


def pair_slices(values, shard):
    parts = values.reshape(-1, 2, shard, values.shape[1])
    own = lax.axis_index("dl")
    return pick(parts, own), pick(parts, 1 - own)


def pair_parts(values, shard):
    own, away = pair_slices(values, shard)
    return own, swap(away, "dl")


def far_sum(own, met):
    met = (own + met).reshape(-1, own.shape[2])
    return lax.psum_scatter(met, "dh", scatter_dimension=0, tiled=True)


def take(values, axis, index):
    return lax.dynamic_index_in_dim(values, index, axis, keepdims=False)


def chip_sum(met):
    chips = lax.axis_size("eh")
    chip = lax.axis_index("eh")
    total = take(met, 0, chip)
    for hop in range(1, chips):
        order = [(i, (i + hop) % chips) for i in range(chips)]
        away = take(met, 0, lax.rem(chip + hop, chips))
        total = total + lax.ppermute(away, "eh", order)
    return total


def cut(array, index, size):
    return lax.dynamic_slice_in_dim(array, index * size, size, 1)


def column_core_sum(values):
    half = values.shape[1] // 2
    own = lax.axis_index("el")
    return cut(values, own, half) + swap(cut(values, 1 - own, half), "el")


def column_chip_sum(met):
    chips, chip = lax.axis_size("eh"), lax.axis_index("eh")
    size = met.shape[1] // chips
    total = cut(met, chip, size)
    for hop in range(1, chips):
        order = [(i, (i + hop) % chips) for i in range(chips)]
        away = cut(met, lax.rem(chip + hop, chips), size)
        total = total + lax.ppermute(away, "eh", order)
    return total


def sum_steps():
    for axis in ("el", "eh", "dl", "dh"):
        count = lax.axis_size(axis)
        hop = 1
        while hop < count:
            order = [(i, i ^ hop) for i in range(count)]
            yield lambda v, axis=axis, order=order: v + lax.ppermute(v, axis, order)
            hop *= 2


def together(*values):
    return lax.optimization_barrier(values)


def on_device(
    tokens,
    segments,
    routes,
    cotangent,
    attention_gain,
    query_weight,
    key_weight,
    value_weight,
    out_weight,
    mixture_gain,
    router_weight,
    gate_weight,
    up_weight,
    down_weight,
):
    groups, length, _ = tokens.shape
    each = range(groups)
    rows = groups * length
    ranks = lax.axis_size("eh") * 2
    dp_ranks = lax.axis_size("dh") * 2
    rank = expert_rank()
    experts = EXP_DEV * ranks
    capacity = (rows * TOPK * 5 // (4 * experts) + 7) // 8 * 8
    all_tokens = rows * dp_ranks * ranks
    first_row = rank * length
    shard = D // dp_ranks

    seg_full = jnp.concatenate([jnp.full((groups, PROMPT), -1, jnp.int32), segments], axis=1)
    seg_own = lax.dynamic_slice_in_dim(seg_full, first_row, length, 1)
    earlier = jnp.sum((segments[:, None, :] < seg_own[:, :, None]).astype(jnp.int32), axis=2)
    position = first_row + jnp.arange(length, dtype=jnp.int32)[None, :]
    place = position - earlier
    start = jnp.where(position >= PROMPT, PROMPT + earlier, 0)
    half = HD // 2
    lane = jnp.arange(LANES, dtype=jnp.int32)
    frequency = jnp.exp(-math.log(rope_base) * (lane % half).astype(f32) / half)
    angles = place.astype(f32).reshape(rows, 1) * frequency
    cosine = jnp.cos(angles)
    sine = jnp.sin(angles) * jnp.where(lane % HD < half, -1.0, 1.0)
    start_row = jnp.broadcast_to(start[:, None, :], (groups, 8, length))

    names = jnp.concatenate([routes[g] for g in each], axis=1).astype(bf16)
    names = widen(names)
    cot_rows = cotangent.reshape(rows, D)
    cot_all = [lax.all_gather(cotangent[g], EXPERT, axis=0, tiled=True) for g in each]

    x = tokens.reshape(rows, D)
    gain_a = attention_gain.reshape(1, D)
    gain_b = mixture_gain.reshape(1, D)
    router_wide = widen(router_weight)
    normed, query, kv = [None] * groups, [None] * groups, [None] * groups
    for g in each:
        normed[g], kv_own = key_value(
            g, length, x, gain_a, key_weight, value_weight, cosine, sine, names
        )
        kv[g] = lax.all_gather(kv_own, EXPERT, axis=0, tiled=True)
    for g in each:
        query[g] = project_query(g, normed[g], query_weight, cosine, sine)
    level = naming(kv[groups - 1], capacity, groups, ranks)
    level_own = lax.dynamic_slice_in_dim(level, first_row, length, 1)
    kv[0], query = together(kv[0], query)
    attended, lse = [None] * groups, [None] * groups
    middle, hidden_low, hidden_all = [None] * groups, [None] * groups, [None] * groups
    probs_local = 0.0
    for g in each:
        attended[g], lse[g] = attend(g, query[g], kv[g], start_row)
        if g == groups - 1:
            attended[g], cot_all[0] = together(attended[g], cot_all[0])
        middle[g], hidden_low[g], probs_part = branch(
            g, attended[g], x, out_weight, gain_b, router_wide
        )
        probs_local += jnp.sum(probs_part, axis=0)
        hidden_all[g] = lax.all_gather(hidden_low[g], EXPERT, axis=0, tiled=True)

    counts = jnp.sum((level_own > 0.5).astype(f32), axis=(0, 1))
    stats = jnp.stack([counts, probs_local])[:, :experts]
    steps = sum_steps()

    def beside(value, stats):
        step = next(steps, None)
        return (value, stats) if step is None else together(value, step(stats))

    kept, rows_back, mixture = [], [], []
    for g in each:
        if g > 0:
            kept[0], cot_all[g] = together(kept[0], cot_all[g])
            hidden_all[g], stats = beside(hidden_all[g], stats)
        mix, rows_grad, *kept = experts_pass(
            g, groups, hidden_all[g], cot_all[g], level, router_wide,
            gate_weight, up_weight, down_weight, kept,
        )
        rows_back.append(lax.psum_scatter(rows_grad, EXPERT, scatter_dimension=0, tiled=True))
        mixture.append(mix)
        if g < groups - 1:
            mixture[g] = lax.psum_scatter(mix, EXPERT, scatter_dimension=0, tiled=True)
    x_all, cot_both, hidden, gate_back, up_back = kept
    hidden, mixture[0] = together(hidden, mixture[0])
    hidden, stats = beside(hidden, stats)
    down_local = dot_tn(cot_both, hidden).astype(bf16)
    x_all, down_local = together(x_all, down_local)
    gate_back, stats = beside(gate_back, stats)
    gate_local = dot_tn(x_all, gate_back).astype(bf16)
    up_back, gate_local = together(up_back, gate_local)
    gate_own, gate_met = pair_parts(gate_local, shard)
    up_back, mix = together(up_back, mixture[-1])
    mixture[-1] = lax.psum_scatter(mix, EXPERT, scatter_dimension=0, tiled=True)
    up_back, stats = beside(up_back, stats)
    up_local = dot_tn(x_all, up_back).astype(bf16)
    rows_back[0], up_local = together(rows_back[0], up_local)
    rows_back[0], stats = beside(rows_back[0], stats)
    for step in steps:
        stats = step(stats)
    expert_load = stats[0] * experts / (all_tokens * TOPK)
    prob_mean = stats[1] * experts / all_tokens
    balance_loss = jnp.sum(expert_load * prob_mean) / experts

    def by_expert(part):
        return jnp.stack([part[:, e * FF : (e + 1) * FF] for e in range(EXP_DEV)]).astype(f32)

    middle_grad, branch_grad, attended_grad, logits_grad, dq, dkv = (
        [None] * groups for _ in range(6)
    )
    gain_b_local, last = 0.0, groups - 1
    down_far = lax.psum_scatter(down_local, "dh", scatter_dimension=0, tiled=True)
    for g in each:
        middle_grad[g], branch_grad[g], attended_grad[g], logits_grad[g], gain_part = middle_back(
            g, rows_back[g], level_own, middle[g], hidden_low[g], cot_rows,
            gain_b, router_wide, out_weight,
        )
        gain_b_local += jnp.sum(gain_part, axis=0)
    out_local = out_gradient(attended, branch_grad)
    fill = -D % (ranks * LANES)
    out_local = jnp.pad(out_local, ((0, 0), (0, fill)))
    attended_grad[0], out_local = together(attended_grad[0], out_local)
    cut_at = 13 * LANES
    up_own, up_away = pair_slices(up_local, shard)
    swaps = [(up_away, slice(0, cut_at), []), (up_away, slice(cut_at, EXP_DEV * FF), None)]
    out_met = column_core_sum(out_local)
    for g in each:
        pieces, kept = [], []
        here = [] if g == 0 else here
        spans = [(0, PAIRS)] if g < last else [(0, PAIRS // 2), (PAIRS // 2, PAIRS // 2)]
        for at, span in enumerate(spans):
            if g == last and at == 0:
                dq[0], gate_own = together(dq[0], gate_own)
                attended_grad[g], out_met, dq[0], gate_own, gate_met, down_far = together(
                    attended_grad[g], out_met, dq[0], gate_own, gate_met, down_far
                )
                gate_part = far_sum(gate_own, gate_met)
                down_own, down_away = pair_slices(down_far, shard)
                swaps.append((down_away, slice(0, EXP_DEV * FF), []))
                out_part = column_chip_sum(out_met)
            if g == last and at == 1:
                up_met = up_own + here[1]
                kept, dkv[0], pieces[0], up_met, mixture[last] = together(
                    kept, dkv[0], pieces[0], up_met, mixture[last]
                )
                up_part = lax.psum_scatter(
                    up_met.reshape(-1, up_met.shape[2]), "dh", scatter_dimension=0, tiled=True
                )
            turn = len(here)
            if turn == 1:
                swaps[1] = (*swaps[1][:2], here)
            grad, keep_part, send_part, *arrived = attend_back(
                g, span, query[g], attended_grad[g], attended[g], kv[g], lse[g], start_row,
                cosine, sine, swaps[turn] if turn < len(swaps) else None, 1 + turn, kept,
            )
            here = here + arrived
            kept = [grad]
            if g == last and at == 1:
                keep_part, dq[0] = together(keep_part, dq[0])
                down_part = (down_own + here[2])[0]
            pieces.append(keep_part + swap(send_part, "el"))
            if g == last and at == 1:
                pieces[1], dq[0] = together(pieces[1], dq[0])
        dq[g] = kept[0]
        pieces = [chip_sum(piece) for piece in pieces]
        dkv[g] = pieces[0] if len(pieces) == 1 else jnp.concatenate(pieces, axis=2)
    output = jnp.stack(
        [(middle[g] + mixture[g].astype(f32)).astype(bf16) for g in each]
    )

    kept, turned_dk, gain_a_local = [], [None] * groups, 0.0
    for g in each:
        input_grad, turned_dk[g], gain_part = input_back(
            g, groups, dq[g], dkv[g], x, middle_grad[g], cosine, sine,
            gain_a, query_weight, key_weight, value_weight, kept,
        )
        kept = [input_grad]
        gain_a_local += jnp.sum(gain_part, axis=0)
    router_parts = sum(dot_tn(logits_grad[g], hidden_low[g]) for g in each)
    router_local = (router_parts[:LANES] + router_parts[LANES:])[:experts]
    narrow = jnp.concatenate(
        [
            router_local,
            gain_a_local[None, :],
            gain_b_local[None, :],
            jnp.zeros((LANES - experts - 2, D), f32),
        ],
        axis=0,
    )
    narrow, up_part = together(narrow, up_part)
    dense = dense_gradient(normed, dq, turned_dk, dkv, narrow, out_part)
    first = dense.shape[1] - D - fill
    out_grad = dense[:, first : first + D]
    down_weight_grad, gate_weight_grad, up_weight_grad = (
        by_expert(part) for part in (down_part, gate_part, up_part)
    )
    spans = [H * HD, KVH * HD, KVH * HD, experts, 1, 1]
    pieces, begin = [], 0
    for span in spans:
        pieces.append(dense[:, begin : begin + span])
        begin += span
    query_grad, key_grad, value_grad, router_grad, gain_a_grad, gain_b_grad = pieces
    return (
        output,
        input_grad.reshape(groups, length, D),
        gain_a_grad[:, 0],
        query_grad,
        key_grad,
        value_grad,
        out_grad,
        gain_b_grad[:, 0],
        router_grad,
        gate_weight_grad,
        up_weight_grad,
        down_weight_grad,
        expert_load,
        prob_mean,
        balance_loss,
    )


def solution(mesh):
    dp_ranks, ranks = mesh.devices.shape
    fine = Mesh(
        mesh.devices.reshape(dp_ranks // 2, 2, ranks // 2, 2), ("dh", "dl", "eh", "el")
    )
    return jax.shard_map(
        on_device,
        mesh=fine,
        in_specs=(
            P(DATA, EXPERT, None),
            P(DATA, None),
            P(DATA, EXPERT, None),
            P(DATA, EXPERT, None),
            P(),
            P(),
            P(),
            P(),
            P(),
            P(),
            P(),
            P(EXPERT, None, None),
            P(EXPERT, None, None),
            P(EXPERT, None, None),
        ),
        out_specs=(
            P(DATA, EXPERT, None),
            P(DATA, EXPERT, None),
            P(DATA),
            P(DATA, None),
            P(DATA, None),
            P(DATA, None),
            P(DATA, None),
            P(DATA),
            P(DATA, None),
            P(EXPERT, DATA, None),
            P(EXPERT, DATA, None),
            P(EXPERT, DATA, None),
            P(),
            P(),
            P(),
        ),
        check_vma=False,
    )
```
